32 devices in a mesh: groups: 2 (over y), dev: 8 (over z, x), sub: 2 (over core).
Axes of the slice: x: 2, y: 2, z: 4, core: 2. Of those that a mesh axis runs over, the one named last changes fastest.
Arguments:
- tokens: bfloat16 [2048, 2048], P(('groups', 'dev')), parts along dimension 0, may hold values from -6 to 6
- query_key_value: bfloat16 [2048, 3, 2048], P(('groups', 'dev'), None, 'sub'), parts along dimension 0, may hold values from -6 to 6
- out_weight: bfloat16 [2048, 2048], P('dev', 'sub'), may hold values from -0.125 to 0.125
- modulation: float32 [8, 2048], P('groups'), parts along dimension 0, may hold values from -3 to 3
- router_weight: bfloat16 [2048, 64], replicated, may hold values from -0.125 to 0.125
- expert_ids: int32 [2048, 4], P(('groups', 'dev')), parts along dimension 0, may hold values from 0 to 63, all different within a row; in each aligned block of 128 rows (0 to 127, 128 to 255, ...) at most 12 rows name the same one
- gate_up_weight: bfloat16 [128, 2, 2048, 384], P('dev', None, None, 'sub'), may hold values from -0.125 to 0.125
- down_weight: bfloat16 [128, 384, 2048], P('dev', None, 'sub'), may hold values from -0.21875 to 0.21875
Outputs:
- block_out: bfloat16 [2048, 2048], P(('groups', 'dev'), 'sub'), parts along dimension 0
The draws below stay inside these ranges and needn't reach their ends.
There are 2 independent parts, one for each index of `groups`. The reference program is written for one: setup_inputs(seed, part) draws one part's arguments, and reference() takes and returns one part's arrays. A program takes and returns all parts, laid end to end along the dimension named above; an argument that names none is the same for every part. Nothing has to cross between parts.
Inputs may be any that keep to these rules, and one draw needn't show every extreme that they name: `expert_ids`: each token names 4 different experts. Within each aligned block of 128 rows no expert is named by more than 12 rows, a bound that some block reaches.
All inputs are finite; a program needn't handle non-finite values.
Results may differ from the reference program's by a relative error of at most 0.008.
Values may be sent and summed in bfloat16 or wider, within the bound.
A program may use at most 128 MiB of HBM per device.

```python
import math
import jax
import jax.numpy as jnp
import numpy as np
from jax import lax

D = 2048
HEADS = 16
HEAD = 128
FF = 768
EXPERTS = 64
TOPK = 4
TOK_DEV = 128
CAP = 12
TOKENS = 1024
N_DEV = 8


def draw_query_key_value(key, part):
    base_key = jax.random.fold_in(jax.random.fold_in(key, 7331), 0)
    width = HEADS * HEAD
    values = jnp.clip(jax.random.normal(base_key, (TOKENS, 3, width), jnp.float32), -6.0, 6.0)
    return values.astype(jnp.bfloat16)


def steps_of(stream_key, dims, cuts, smallest, top_value):
    def one(axis_at, blocks):
        heights = jax.random.uniform(jax.random.fold_in(jax.random.fold_in(stream_key, 6), axis_at), (blocks,), jnp.float32, smallest / len(cuts), top_value / len(cuts))
        return jnp.repeat(jnp.exp(heights), dims[axis_at] // blocks).reshape((-1,) + (1,) * (len(dims) - axis_at - 1))

    loudness = one(*cuts[0])
    for cut in cuts[1:]:
        loudness = loudness * one(*cut)
    return loudness


def routed_block(own_key, own, number, rows, amount, top, most, lean):
    ranking = jax.random.permutation(own_key, amount)
    crowded, ordinary = load_shares(amount, rows * top, most, lean, True), load_shares(amount, rows * top, most, lean, False)
    places = jnp.arange(amount)

    def named(tallies, turn):
        used = int((tallies > 0).sum())
        fixed = max(1, used // 4)
        shifted = fixed + (places - fixed + turn * (used - fixed)) % max(1, amount - fixed)
        return jnp.zeros((amount,), jnp.int32).at[ranking[jnp.where(places < fixed, places, shifted)]].set(jnp.asarray(tallies, jnp.int32))

    tallies = jnp.where(number % 4 == 0, named(crowded, number // 4), named(ordinary, number - number // 4 - 1))
    mixed = jax.random.permutation(jax.random.fold_in(own, 3), amount)
    giver, receiver = mixed[0:amount // 2 * 2:2], mixed[1:amount // 2 * 2:2]
    room = jnp.minimum(tallies[giver] - 1, most - tallies[receiver]) // 2
    room = jnp.where((giver == ranking[0]) | (receiver == ranking[0]) | (tallies[receiver] == 0), 0, jnp.maximum(room, 0))
    shifted = jax.random.randint(jax.random.fold_in(own, 4), (amount // 2,), 0, 1 << 20) % (room + 1)
    tallies = tallies.at[giver].add(-shifted).at[receiver].add(shifted)
    members = jnp.searchsorted(jnp.cumsum(tallies), jnp.arange(rows * top), side="right").astype(jnp.int32)
    listing = members.reshape(top, rows).T
    listing = listing[jax.random.permutation(jax.random.fold_in(own, 1), rows)]
    turn = jax.random.randint(jax.random.fold_in(own, 2), (rows, 1), 0, top)
    return jnp.take_along_axis(listing, (jnp.arange(top)[None, :] + turn) % top, axis=1)


def load_shares(number_of, total, most, slope, full):
    portions = [(1 << 20) // math.isqrt(rank ** slope) + 1 for rank in range(1, number_of + 1)]
    largest = most if full else min(most, max(-(-total // number_of), total * portions[0] // sum(portions)))
    least = 1 if total - largest >= number_of - 1 else 0
    given, rest = [largest] + [least] * (number_of - 1), total - largest - least * (number_of - 1)
    while rest > 0:
        candidates = [i for i in range(1, number_of) if given[i] < largest] or [i for i in range(1, number_of) if given[i] < most]
        whole, remaining = sum([portions[i] for i in candidates]), rest
        for i in candidates:
            more = min(most - given[i], max(1, remaining * portions[i] // whole), rest)
            given[i] = given[i] + more
            rest = rest - more
    return np.array(given)


def gaussian(stream_key, dims, deviation, limit, cuts=(), kind=jnp.bfloat16):
    entries = jax.random.normal(stream_key, dims, jnp.float32) * deviation
    if len(cuts) > 0:
        entries = steps_of(stream_key, dims, cuts, -0.22, 0.18) * entries
    return jnp.clip(entries, min=-limit, max=limit).astype(kind)


def setup_inputs(seed: int = 0, part: int = 0) -> dict:
    key_list = jax.random.split(jax.random.key(seed), 9)
    part_splits = jax.random.split(jax.random.fold_in(key_list[8], part), 9)
    tokens = gaussian(part_splits[0], (TOKENS, D), 1.0, 6.0, ((0, 8),))
    query_key_value = draw_query_key_value(jax.random.fold_in(jax.random.fold_in(key_list[8], part), 71), part)
    out_weight = gaussian(key_list[2], (D, HEADS * HEAD), (HEADS * HEAD) ** -0.5, 0.125, ((0, 8), (1, 2)))
    modulation = gaussian(part_splits[3], (4, D), 0.5, 3.0, (), jnp.float32)
    router_weight = gaussian(key_list[4], (D, EXPERTS), D ** -0.5, 0.125)
    expert_ids_keys = jax.random.split(jax.random.fold_in(part_splits[5], 1), TOKENS // TOK_DEV)
    expert_ids_turns = jax.random.permutation(jax.random.fold_in(part_splits[5], 3), TOKENS // TOK_DEV)
    expert_ids = jax.vmap(lambda own, number: routed_block(jax.random.fold_in(part_splits[5], 2), own, number, TOK_DEV, EXPERTS, TOPK, CAP, 1))(expert_ids_keys, expert_ids_turns).reshape((TOKENS, TOPK))
    gate_up_weight = gaussian(key_list[6], (2 * EXPERTS, 2, D, FF // 2), D ** -0.5, 0.125, ((0, 8), (3, 2)))
    down_weight = gaussian(key_list[7], (2 * EXPERTS, FF // 2, D), FF ** -0.5, 0.21875, ((0, 8), (2, 2)))
    return {"tokens": tokens, "query_key_value": query_key_value, "out_weight": out_weight, "modulation": modulation, "router_weight": router_weight, "expert_ids": expert_ids, "gate_up_weight": gate_up_weight, "down_weight": down_weight}


EPS = 1e-06
NEG = -1e+30

def window_attention(query, keys, values, index, total):
    count = query.shape[0]
    rows = jnp.arange(count, dtype=jnp.int32)[:, None]
    cols = jnp.arange(3 * count, dtype=jnp.int32)[None, :] - count
    place = index * count + cols
    allowed = (jnp.abs(cols - rows) <= count) & (place >= 0) & (place < total)
    scores = jnp.einsum('qhd,khd->hqk', query.astype(jnp.float32), keys.astype(jnp.float32)) / math.sqrt(query.shape[2])
    scores = jnp.where(allowed[None], scores, NEG)
    top = lax.optimization_barrier(jnp.max(scores, -1, keepdims=True))
    weight = jnp.exp(scores - top)
    weight = (weight / lax.optimization_barrier(jnp.sum(weight, -1, keepdims=True))).astype(jnp.bfloat16)
    mixed = jnp.einsum('hqk,khd->qhd', weight.astype(jnp.float32), values.astype(jnp.float32))
    return mixed.astype(jnp.bfloat16)

def attend(query_key_value):
    blocks = TOKENS // TOK_DEV
    packed = query_key_value.reshape(blocks, TOK_DEV, 3, HEADS, HEAD)
    empty = jnp.zeros((1, TOK_DEV, 3, HEADS, HEAD), packed.dtype)
    padded = jnp.concatenate([empty, packed, empty], 0)

    def block(index):
        near = lax.dynamic_slice_in_dim(padded, index, 3, 0).reshape(3 * TOK_DEV, 3, HEADS, HEAD)
        query = lax.dynamic_index_in_dim(packed, index, 0, keepdims=False)[:, 0]
        return window_attention(query, near[:, 1], near[:, 2], index, TOKENS)
    result = lax.map(block, jnp.arange(blocks, dtype=jnp.int32))
    return result.reshape(TOKENS, HEADS * HEAD)

def normalize(state, modulation):
    scale = lax.rsqrt(lax.optimization_barrier(jnp.mean(state * state, -1, keepdims=True)) + EPS)
    return (state * scale * (1.0 + modulation[2]) + modulation[1]).astype(jnp.bfloat16)

def route(normed, router_weight, expert_ids):
    logits = jnp.dot(normed, router_weight, preferred_element_type=jnp.float32)
    experts = router_weight.shape[1]
    match = expert_ids[:, :, None] == jnp.arange(experts, dtype=jnp.int32)[None, None, :]
    picked = lax.optimization_barrier(jnp.sum(jnp.where(match, logits[:, None, :], 0.0), -1))
    lifted = jax.nn.sigmoid(picked)
    return lifted / lax.optimization_barrier(jnp.sum(lifted, -1, keepdims=True))

def experts_sum(normed, gates, expert_ids, gate_up_weight, down_weight):
    room = N_DEV * CAP

    def step(total, expert):
        match = expert_ids == expert
        chosen = jnp.any(match, 1)
        rows = jnp.nonzero(chosen, size=room, fill_value=0)[0].astype(jnp.int32)
        live = jnp.arange(room, dtype=jnp.int32) < jnp.sum(chosen.astype(jnp.int32))
        weight = lax.optimization_barrier(jnp.sum(jnp.where(match, gates, 0.0), 1))[rows]
        weight = jnp.where(live, weight, 0.0)
        pair = lax.dynamic_slice_in_dim(gate_up_weight, 2 * expert, 2, 0)
        down_pair = lax.dynamic_slice_in_dim(down_weight, 2 * expert, 2, 0)
        inputs = normed[rows]
        output = jnp.zeros((room, normed.shape[1]), jnp.float32)
        for half in range(2):
            gate = jnp.dot(inputs, pair[half, 0], preferred_element_type=jnp.float32)
            up = jnp.dot(inputs, pair[half, 1], preferred_element_type=jnp.float32)
            hidden = (jax.nn.silu(gate) * up).astype(jnp.bfloat16)
            piece = jnp.dot(hidden, down_pair[half], preferred_element_type=jnp.float32).astype(jnp.bfloat16)
            output = output + piece.astype(jnp.float32)
        return (total.at[rows].add(weight[:, None] * output), None)
    total = jnp.zeros((normed.shape[0], normed.shape[1]), jnp.float32)
    total, _ = lax.scan(step, total, jnp.arange(EXPERTS, dtype=jnp.int32))
    return total

def reference(tokens, query_key_value, out_weight, modulation, router_weight, expert_ids, gate_up_weight, down_weight):
    mixed = attend(query_key_value)
    proj = lax.dot_general(mixed, out_weight, (((1,), (1,)), ((), ())), preferred_element_type=jnp.float32)
    state = tokens.astype(jnp.float32) + (1.0 + modulation[0]) * proj
    normed = normalize(state, modulation)
    gates = route(normed, router_weight, expert_ids)
    routed = experts_sum(normed, gates, expert_ids, gate_up_weight, down_weight)
    return (state + (1.0 + modulation[3]) * routed).astype(jnp.bfloat16)
```

```python
import functools
import math

import jax
import jax.numpy as jnp
from jax import lax
from jax.experimental import pallas as pl
from jax.experimental.pallas import tpu as pltpu
from jax.sharding import PartitionSpec as P

HEAD = 128
CAP = 12


EPS = 1e-06
NEG = -1e30


def extended(cells, sides, width):
    for axis, dim in sides:
        count = lax.axis_size(axis)
        ends = count - 1
        head = lax.slice_in_dim(cells, 0, width, axis=dim)
        tail = lax.slice_in_dim(cells, cells.shape[dim] - width, cells.shape[dim], axis=dim)
        cells = jnp.concatenate(
            [
                lax.ppermute(tail, axis, [(i, (i + 1) % count) for i in range(ends)]),
                cells,
                lax.ppermute(head, axis, [((i + 1) % count, i) for i in range(ends)]),
            ],
            axis=dim,
        )
    return cells


def window_attention(query, keys, values, index, total):
    count = query.shape[0]
    rows = jnp.arange(count, dtype=jnp.int32)[:, None]
    cols = jnp.arange(3 * count, dtype=jnp.int32)[None, :] - count
    place = index * count + cols
    allowed = (jnp.abs(cols - rows) <= count) & (place >= 0) & (place < total)
    scores = jnp.einsum(
        "qhd,khd->hqk", query, keys, preferred_element_type=jnp.float32
    ) / math.sqrt(query.shape[2])
    scores = jnp.where(allowed[None], scores, NEG)
    top = jnp.max(scores, -1, keepdims=True)
    weight = jnp.exp(scores - top)
    weight = (weight / jnp.sum(weight, -1, keepdims=True)).astype(jnp.bfloat16)
    mixed = jnp.einsum("hqk,khd->qhd", weight, values, preferred_element_type=jnp.float32)
    return mixed.astype(jnp.bfloat16)


def normalize(state, modulation):
    scale = lax.rsqrt(jnp.mean(state * state, -1, keepdims=True) + EPS)
    return (state * scale * (1.0 + modulation[2]) + modulation[1]).astype(jnp.bfloat16)


def route(normed, router_weight, expert_ids):
    logits = jnp.dot(normed, router_weight, preferred_element_type=jnp.float32)
    experts = router_weight.shape[1]
    match = expert_ids[:, :, None] == jnp.arange(experts, dtype=jnp.int32)[None, None, :]
    picked = jnp.sum(jnp.where(match, logits[:, None, :], 0.0), -1)
    lifted = jax.nn.sigmoid(picked)
    return lifted / jnp.sum(lifted, -1, keepdims=True)


LANES = 128
SLOT = 16
COLS = 2
CHUNKS = 4
VMEM_BYTES = 66 * 1000 * 1000
MESH = pl.DeviceIdType.MESH


def choose(index, table):
    value = jnp.int32(table[0])
    for i in range(1, len(table)):
        value = jnp.where(index == i, table[i], value)
    return value


def line_order(lines, nearest):
    rows = []
    for z in range(lines):
        lower = z < lines - 1 - z
        others = [line for line in range(lines) if line != z]
        sign = 1 if nearest else -1
        rows.append(sorted(others, key=lambda line: (sign * abs(line - z), (line > z) == lower)))
    return [[rows[z][j] for z in range(lines)] for j in range(lines - 1)]


def expert_kernel(
    devices, weight_copies,
    normed, meta, state, modulation, wide,
    out,
    tok, got_packed, got_rows, got_sum, disp, gu, dn, raised, hid_own, hid_other,
    got_meta, pick, gated, squeeze, grow, acc,
    meta_s, meta_r, z_s, z_r, x_s, x_r, core_s, core_r, hid_s, hid_r, rx_s, rx_r, rz_s, rz_r,
):
    me = lax.axis_index("dev")
    part = lax.axis_index("sub")
    other = 1 - part
    z = me // COLS
    x = me % COLS
    lines = devices // COLS
    count, width = normed.shape
    half = width // 2
    local = raised.shape[0]
    hidden = gu.shape[2]
    both_hidden = 2 * hidden
    slots = local * SLOT
    pack = local * CAP
    rows = devices * SLOT
    chunks, wide_chunk = tok.shape[1], tok.shape[3]

    def remote(src, dst, send, recv, where):
        return pltpu.make_async_remote_copy(
            src_ref=src, dst_ref=dst, send_sem=send, recv_sem=recv,
            device_id=where, device_id_type=MESH,
        )

    above = jnp.minimum(me + COLS, devices - 1)
    below = jnp.maximum(me - COLS, 0)
    x_to = {"dev": z * COLS + (1 - x)}
    core_to = {"sub": other}
    not_top = z < lines - 1
    not_bottom = z > 0
    near_lines = [choose(z, table) for table in line_order(lines, True)]
    far_lines = [choose(z, table) for table in line_order(lines, False)]

    def lanes_of(c):
        return pl.ds(pl.multiple_of(c * wide_chunk, wide_chunk), wide_chunk)

    def own_lanes(c):
        return pl.ds(pl.multiple_of(part * half + c * wide_chunk, wide_chunk), wide_chunk)

    def slot_rows(s):
        return pl.ds(pl.multiple_of(s * SLOT, SLOT), SLOT)

    def meta_copy(line):
        return remote(
            meta.at[pl.ds(pl.multiple_of(line * COLS * local, COLS * local), COLS * local)],
            got_meta.at[z], meta_s.at[line], meta_r.at[z], {"dev": line * COLS + x},
        )

    def meta_arrival(line):
        return remote(got_meta.at[line], got_meta.at[line], meta_s.at[line], meta_r.at[line], x_to)

    def z_copy(line, c, way, src=None):
        dst = tok.at[line, c]
        where = {"dev": jnp.where(way == 0, above, below)}
        return remote(
            dst if src is None else src, dst, z_s.at[line, c, way], z_r.at[line, c], where
        )

    def packed_out(line, c):
        return wide.at[line, pl.ds(slots, pack), lanes_of(c)]

    def x_copy(line, c):
        return remote(
            packed_out(line, c), got_packed.at[line, c], x_s.at[line, c], x_r.at[line, c], x_to
        )

    def core_copy(which, s, c):
        place = disp.at[which, c, :, slot_rows(s), :]
        return remote(place, place, core_s.at[s, c], core_r.at[s, c], core_to)

    def own_send(c):
        src = normed.at[:, own_lanes(c)]

        @pl.when(not_top)
        def _():
            z_copy(z, c, 0, src).start()

        @pl.when(not_bottom)
        def _():
            z_copy(z, c, 1, src).start()

    own_send(0)
    for line in near_lines:
        meta_copy(line).start()

    before = (
        lax.broadcasted_iota(jnp.int32, (count, count), 0)
        < lax.broadcasted_iota(jnp.int32, (count, count), 1)
    ).astype(jnp.float32).astype(jnp.bfloat16)
    place = lax.broadcasted_iota(jnp.int32, (local, SLOT, count), 1).astype(jnp.float32)

    def routing(line, ours, theirs):
        for first, gate in ((True, ours), (False, theirs)):
            chosen = jnp.where(gate > 0.0, 1.0, 0.0)
            rank = jnp.dot(chosen.astype(jnp.bfloat16), before, preferred_element_type=jnp.float32)
            rank = jnp.where(gate > 0.0, rank, -1.0)
            hit = jnp.broadcast_to(rank[:, None, :], place.shape) == place
            one = jnp.where(hit, 1.0, 0.0).reshape(slots, count).astype(jnp.bfloat16)
            value = jnp.where(hit, jnp.broadcast_to(gate[:, None, :], place.shape), 0.0)
            value = value.reshape(slots, count).astype(jnp.bfloat16)
            if first:
                pick[line, :slots] = one
                gated[line, :slots] = value
            else:
                pick[line, slots:] = jnp.dot(
                    squeeze[...], one, preferred_element_type=jnp.float32
                ).astype(jnp.bfloat16)
                gated[line, slots:] = jnp.dot(
                    squeeze[...], value, preferred_element_type=jnp.float32
                ).astype(jnp.bfloat16)

    def expert_rows(base, column):
        return pl.ds(pl.multiple_of(base + column * local, local), local)

    def spread(line, c, block):
        moved = jnp.dot(pick[line], block, preferred_element_type=jnp.float32).astype(jnp.bfloat16)
        s = line * COLS + x
        wide[line, slots:slots + pack, lanes_of(c)] = moved[slots:]
        x_copy(line, c).start()
        disp[part, c, :, slot_rows(s), :] = moved[:slots].reshape(local, SLOT, wide_chunk)
        core_copy(part, s, c).start()

    def own_step(c):
        spread(z, c, normed[:, own_lanes(c)])

    def line_step(line, c):
        low = line < z

        @pl.when(c == 0)
        def _():
            meta_arrival(line).wait_recv()
            routing(
                line, got_meta[line, expert_rows(0, x)], got_meta[line, expert_rows(0, 1 - x)]
            )

        way = jnp.where(low, 0, 1)
        z_copy(line, c, way).wait_recv()

        @pl.when(jnp.where(low, not_top, not_bottom))
        def _():
            z_copy(line, c, way).start()

        spread(line, c, tok[line, c])

    def x_step(line, c):
        x_copy(line, c).wait_recv()
        s = line * COLS + (1 - x)
        disp[part, c, :, slot_rows(s), :] = jnp.dot(
            grow[...], got_packed[line, c], preferred_element_type=jnp.float32
        ).astype(jnp.bfloat16).reshape(local, SLOT, wide_chunk)
        core_copy(part, s, c).start()

    def across_rows(left, right):
        return lax.dot_general(
            left, right, (((1,), (1,)), ((), ())), preferred_element_type=jnp.float32
        )

    def raise_part(e, c):
        total = raised[e]
        for side in range(2):
            lanes = pl.ds(pl.multiple_of(side * half + c * wide_chunk, wide_chunk), wide_chunk)
            weight = jnp.concatenate(
                [gu[2 * e, 0, :, lanes], gu[2 * e + 1, 0, :, lanes],
                 gu[2 * e, 1, :, lanes], gu[2 * e + 1, 1, :, lanes]], axis=0
            )
            total = total + across_rows(disp[side, c, e], weight)
        return total

    def hid_copy(e):
        return remote(hid_own.at[e], hid_other.at[e], hid_s.at[e], hid_r.at[e], core_to)

    def arrived(c):
        for s in range(devices):
            core_copy(other, s, c).wait_recv()

    routing(
        z, meta[expert_rows(z * COLS * local, x)], meta[expert_rows(z * COLS * local, 1 - x)]
    )
    own_step(0)

    def weight_wait(h, carry):
        for copy in weight_copies(h):
            copy.wait()
        return carry

    lax.fori_loop(0, 2 * local, weight_wait, 0)

    def step(t, carry):
        ready = t - lines

        def raise_some(i):
            first, last = i * local // (2 * lines), (i + 1) * local // (2 * lines)

            @pl.when(ready >= 0)
            def _():
                if i == 0:
                    arrived(ready)
                for e in range(first, last):
                    raised[e] = raise_part(e, ready)

        @pl.when(t + 1 < chunks)
        def _():
            own_send(t + 1)
            own_step(t + 1)

        raise_some(0)
        for j, line in enumerate(near_lines):
            c = t - jnp.abs(line - z) + 1

            @pl.when((c >= 0) & (c < chunks))
            def _():
                line_step(line, c)

            raise_some(1 + j)

        @pl.when(t < chunks)
        def _():
            x_step(z, t)

        raise_some(lines)
        for j, line in enumerate(near_lines):
            c = t - jnp.abs(line - z)

            @pl.when((c >= 0) & (c < chunks))
            def _():
                x_step(line, c)

            raise_some(lines + 1 + j)
        return carry

    lax.fori_loop(0, chunks + lines - 1, step, 0)
    arrived(chunks - 1)

    def last_raise(e, carry):
        total = raise_part(e, chunks - 1)
        gate = total[:, :both_hidden]
        hid_own[e] = (gate * jax.nn.sigmoid(gate) * total[:, both_hidden:]).astype(jnp.bfloat16)
        hid_copy(e).start()
        return carry

    lax.fori_loop(0, local, last_raise, 0)

    group = 2 * wide_chunk

    def lower(g):
        lanes = slice(g * group, (g + 1) * group)

        def one(e, carry):
            if g == 0:
                hid_copy(e).wait_recv()
            mine = pl.ds(pl.multiple_of(part * hidden, SLOT), hidden)
            theirs = pl.ds(pl.multiple_of(other * hidden, SLOT), hidden)
            left = jnp.concatenate([hid_own[e], hid_other[e]], axis=1)
            right = jnp.concatenate(
                [dn[2 * e, mine, lanes], dn[2 * e + 1, mine, lanes],
                 dn[2 * e, theirs, lanes], dn[2 * e + 1, theirs, lanes]], axis=0
            )
            wide[e, :rows, lanes] = jnp.dot(
                left, right, preferred_element_type=jnp.float32
            ).astype(jnp.bfloat16)
            return carry

        lax.fori_loop(0, local, one, 0)

    def result_rows(s, q):
        return wide[:local, slot_rows(s), lanes_of(q)].reshape(slots, wide_chunk)

    def rx_copy(line, q):
        return remote(
            wide.at[lines + line, pl.ds(slots, pack), lanes_of(q)], got_rows.at[line, q],
            rx_s.at[line, q], rx_r.at[line, q], x_to,
        )

    def rz_copy(line, q, way):
        where = {"dev": jnp.where(way == 0, above, below)}
        return remote(
            tok.at[line, q], got_sum.at[way, line, q],
            rz_s.at[line, q], rz_r.at[way, line, q], where,
        )

    def give(line, q):
        packed = jnp.dot(
            squeeze[...], result_rows(line * COLS + (1 - x), q), preferred_element_type=jnp.float32
        )
        wide[lines + line, slots:slots + pack, lanes_of(q)] = packed.astype(jnp.bfloat16)
        rx_copy(line, q).start()

    def gather_here(line, q):
        rx_copy(line, q).wait_recv()
        pieces = jnp.concatenate([result_rows(line * COLS + x, q), got_rows[line, q]], axis=0)
        acc[...] = lax.dot_general(
            gated[line], pieces, (((0,), (0,)), ((), ())), preferred_element_type=jnp.float32
        )

    def add_line(line, q, way):
        rz_copy(line, q, way).wait_recv()
        acc[...] += got_sum[way, line, q].astype(jnp.float32)

    def pass_on(line, q):
        gather_here(line, q)
        way = jnp.where(line > z, 0, 1)

        @pl.when(jnp.where(line > z, not_bottom, not_top))
        def _():
            add_line(line, q, way)

        tok[line, q] = acc[...].astype(jnp.bfloat16)
        rz_copy(line, q, way).start()

    for g in range(half // group):
        lower(g)
        for q in range(2 * g, 2 * g + 2):
            give(far_lines[0], q)
    for line in far_lines[1:] + [z]:
        lax.fori_loop(0, chunks, lambda q, carry, line=line: (give(line, q), carry)[1], 0)
    for line in near_lines:
        low = line < z

        @pl.when(jnp.where(low, not_top, not_bottom))
        def _():
            for c in range(chunks):
                z_copy(line, c, jnp.where(low, 0, 1)).wait_send()

    for line in far_lines:
        lax.fori_loop(0, chunks, lambda q, carry, line=line: (pass_on(line, q), carry)[1], 0)
    for q in range(chunks):
        gather_here(z, q)

        @pl.when(not_bottom)
        def _():
            add_line(z, q, 0)

        @pl.when(not_top)
        def _():
            add_line(z, q, 1)

        own = own_lanes(q)
        lanes = slice(q * wide_chunk, (q + 1) * wide_chunk)
        out[:, lanes] = (
            state[:, own] + (1.0 + modulation[3:4, own]) * acc[...]
        ).astype(out.dtype)

    for c in range(chunks):

        @pl.when(not_top)
        def _():
            z_copy(z, c, 0, normed.at[:, own_lanes(c)]).wait_send()

        @pl.when(not_bottom)
        def _():
            z_copy(z, c, 1, normed.at[:, own_lanes(c)]).wait_send()

        for line in near_lines:
            rz_copy(line, c, jnp.where(line > z, 0, 1)).wait_send()
        for line in range(lines):
            x_copy(line, c).wait_send()
            rx_copy(line, c).wait_send()
        for s in range(devices):
            core_copy(part, s, c).wait_send()
    for line in near_lines:
        meta_copy(line).wait_send()

    def hid_drain(e, carry):
        hid_copy(e).wait_send()
        return carry

    lax.fori_loop(0, local, hid_drain, 0)


def front_kernel(
    devices, start_weights,
    sources, held, own_sem,
    normed, state, meta,
    near, wide, mixed, mine_out, their_out,
    near_s, near_r, far_s, far_r, ag_s, ag_r, y_r, sum_s, sum_r,
):
    packed_hbm, weight_hbm = sources[1], sources[2]
    tokens, packed, weight, modulation, router, ids = held

    def own_copy(i):
        return pltpu.make_async_copy(sources[i], held[i], own_sem.at[i])

    for i in (1, 2, 0, 3, 4, 5):
        own_copy(i).start()
    me = lax.axis_index("dev")
    part = lax.axis_index("sub")
    group = lax.axis_index("groups")
    z = me // COLS
    x = me % COLS
    across = z * COLS + (1 - x)
    lines = devices // COLS
    count, width = tokens.shape
    shard = weight.shape[0]
    extra = shard * 3 // 8 // SLOT * SLOT
    main = shard - extra
    not_top = z < lines - 1
    not_bottom = z > 0
    up_to = {"dev": jnp.minimum(me + COLS, devices - 1)}
    down_to = {"dev": jnp.maximum(me - COLS, 0)}
    x_to = {"dev": across}
    y_to = {"groups": 1 - group}
    core_to = {"sub": 1 - part}

    barrier = pltpu.get_barrier_semaphore()
    for step in range(1, devices):
        pl.semaphore_signal(
            barrier, inc=1, device_id={"dev": (me + step) % devices}, device_id_type=MESH
        )
    pl.semaphore_signal(barrier, inc=1, device_id=core_to, device_id_type=MESH)
    pl.semaphore_signal(barrier, inc=1, device_id=y_to, device_id_type=MESH)
    pl.semaphore_wait(barrier, devices + 1)

    def remote(src, dst, send, recv, where):
        return pltpu.make_async_remote_copy(
            src_ref=src, dst_ref=dst, send_sem=send, recv_sem=recv,
            device_id=where, device_id_type=MESH,
        )

    def near_copy(i):
        return remote(packed_hbm.at[1 + i], near.at[x, i], near_s.at[i], near_r.at[i], x_to)

    def far_copy(i, where):
        return remote(near.at[1 - x, i], near.at[x, i], far_s.at[i], far_r.at[i], where)

    def piece(s, way, where, src=None):
        start, size = (main, extra) if way == 3 else (extra, main)
        dst = wide.at[s, pl.ds(pl.multiple_of(group * start, SLOT), size)]
        recv = y_r.at[s] if way == 3 else ag_r.at[s]
        return remote(dst if src is None else src, dst, ag_s.at[s, way], recv, where)

    far_up = (x == 0) & not_top
    far_down = (x == 1) & not_bottom
    have_far = ((x == 0) & not_bottom) | ((x == 1) & not_top)
    mine = weight_hbm.at[pl.ds(pl.multiple_of(group * extra, SLOT), main)]

    for i in range(2):
        near_copy(i).start()

    @pl.when(not_top)
    def _():
        piece(me, 0, up_to, mine).start()

    @pl.when(not_bottom)
    def _():
        piece(me, 1, down_to, mine).start()

    piece(me, 2, x_to, mine).start()
    start_weights()

    @pl.when(jnp.logical_not(have_far))
    def _():
        near[x] = jnp.zeros_like(near[x])

    for i in range(2):
        near_copy(i).wait_recv()

        @pl.when(far_up)
        def _():
            far_copy(i, up_to).start()

        @pl.when(far_down)
        def _():
            far_copy(i, down_to).start()

    def both(d, act):
        @pl.when(z - d >= 0)
        def _():
            act(z - d, True)

        @pl.when(z + d < lines)
        def _():
            act(z + d, False)

    def project(s, block):
        mine_out[s] = lax.dot_general(
            mixed[...], block, (((1,), (1,)), ((), ())), preferred_element_type=jnp.float32
        )
        sum_copy(s).start()

    def sum_copy(s):
        return remote(mine_out.at[s], their_out.at[s], sum_s.at[s], sum_r.at[s], core_to)

    def take_line(zz, low):
        s = zz * COLS + x
        piece(s, 2, x_to).wait_recv()

        @pl.when(not_top if low else not_bottom)
        def _():
            piece(s, 0 if low else 1, up_to if low else down_to).start()

        piece(s, 2, x_to).start()
        piece(s, 3, y_to).start()

    def take_across(zz, low):
        s = zz * COLS + (1 - x)
        piece(s, 2, x_to).wait_recv()
        piece(s, 3, y_to).start()

    def take_y(s):
        dst = wide.at[s, pl.ds(pl.multiple_of((1 - group) * main, SLOT), extra)]
        remote(dst, dst, ag_s.at[s, 3], y_r.at[s], y_to).wait_recv()
        project(s, wide[s])

    def line_y(zz, low):
        take_y(zz * COLS + x)

    def across_y(zz, low):
        take_y(zz * COLS + (1 - x))

    both(1, take_line)
    take_across(z, False)
    for d in range(2, min(3, lines)):
        both(d, take_line)
    for i in range(6):
        own_copy(i).wait()

    @pl.when(have_far)
    def _():
        for i in range(2):
            far_copy(i, x_to).wait_recv()

    row = lax.broadcasted_iota(jnp.int32, (count, count), 0)
    col = lax.broadcasted_iota(jnp.int32, (count, count), 1)
    see_before = (col >= row) & (me > 0)
    see_after = (col <= row) & (me < devices - 1)
    for h in range(mixed.shape[1] // HEAD):
        lanes = slice(h * HEAD, (h + 1) * HEAD)
        query = packed[0, :, lanes]

        def score(keys):
            return lax.dot_general(
                query, keys, (((1,), (1,)), ((), ())), preferred_element_type=jnp.float32
            ) / math.sqrt(HEAD)

        scores = jnp.concatenate(
            [
                jnp.where(see_before, score(near[0, 0, :, lanes]), NEG),
                score(packed[1, :, lanes]),
                jnp.where(see_after, score(near[1, 0, :, lanes]), NEG),
            ],
            axis=1,
        )
        top = jnp.max(scores, -1, keepdims=True)
        share = jnp.exp(scores - top)
        share = (share / jnp.sum(share, -1, keepdims=True)).astype(jnp.bfloat16)
        values = jnp.concatenate(
            [near[0, 1, :, lanes], packed[2, :, lanes], near[1, 1, :, lanes]], axis=0
        )
        mixed[:, lanes] = jnp.dot(
            share, values, preferred_element_type=jnp.float32
        ).astype(jnp.bfloat16)

    project(me, weight[...])
    for d in range(3, lines):
        both(d, take_line)
    for d in range(1, lines):
        both(d, line_y)
        both(d, take_across)
        if d == 1:
            take_y(across)
    for d in range(1, lines):
        both(d, across_y)

    square = jnp.zeros((count, 1), jnp.float32)
    for s in range(devices):
        sum_copy(s).wait_recv()
        lanes = slice(s * shard, (s + 1) * shard)
        value = tokens[:, lanes].astype(jnp.float32) + (1.0 + modulation[0:1, lanes]) * (
            mine_out[s] + their_out[s]
        )
        state[:, lanes] = value
        square = square + jnp.sum(value * value, -1, keepdims=True)
    scale = lax.rsqrt(square / width + EPS)
    for s in range(devices):
        lanes = slice(s * shard, (s + 1) * shard)
        normed[:, lanes] = (
            state[:, lanes] * scale * (1.0 + modulation[2:3, lanes]) + modulation[1:2, lanes]
        ).astype(jnp.bfloat16)
    logits = lax.dot_general(
        router[...], normed[...], (((1,), (1,)), ((), ())), preferred_element_type=jnp.float32
    )
    name = lax.broadcasted_iota(jnp.int32, logits.shape, 0)
    named = name == ids[0:1]
    for k in range(1, ids.shape[0]):
        named = named | (name == ids[k:k + 1])
    lifted = jnp.where(named, jax.nn.sigmoid(logits), 0.0)
    meta[...] = lifted / jnp.sum(lifted, 0, keepdims=True)

    for i in range(2):
        near_copy(i).wait_send()

        @pl.when(far_up | far_down)
        def _():
            far_copy(i, x_to).wait_send()

    @pl.when(not_top)
    def _():
        piece(me, 0, up_to, mine).wait_send()

    @pl.when(not_bottom)
    def _():
        piece(me, 1, down_to, mine).wait_send()

    piece(me, 2, x_to, mine).wait_send()
    piece(across, 3, y_to).wait_send()
    for d in range(1, lines):

        def sent(zz, low):
            s = zz * COLS + x

            @pl.when(not_top if low else not_bottom)
            def _():
                piece(s, 0 if low else 1, up_to).wait_send()

            piece(s, 2, x_to).wait_send()
            piece(s, 3, y_to).wait_send()
            piece(zz * COLS + (1 - x), 3, y_to).wait_send()

        both(d, sent)
    for s in range(devices):
        sum_copy(s).wait_send()


def block_kernel(devices, *refs):
    sources, gate_up, down, out = refs[:6], refs[6], refs[7], refs[8]
    held, normed, state, meta = refs[9:15], refs[15], refs[16], refs[17]
    front_buffers, expert_buffers = refs[18:23], refs[23:39]
    own_sem, gu_sem, dn_sem = refs[39:42]
    front_sems, expert_sems = refs[42:51], refs[51:]
    gu, dn, raised = expert_buffers[5:8]
    squeeze, grow = expert_buffers[13:15]
    halves = gate_up.shape[0]

    def weight_copies(h):
        return (
            pltpu.make_async_copy(gate_up.at[h], gu.at[h], gu_sem.at[h]),
            pltpu.make_async_copy(down.at[h], dn.at[h], dn_sem.at[h]),
        )

    def start_weights():
        def one(h, carry):
            for copy in weight_copies(h):
                copy.start()
            return carry

        lax.fori_loop(0, halves, one, 0)
        raised[...] = jnp.zeros_like(raised)
        for ref, axis in ((squeeze, 0), (grow, 1)):
            packed = lax.broadcasted_iota(jnp.int32, ref.shape, axis)
            slot = lax.broadcasted_iota(jnp.int32, ref.shape, 1 - axis)
            inner = slot & (SLOT - 1)
            same = (packed == (slot - inner) // SLOT * CAP + inner) & (inner < CAP)
            ref[...] = jnp.where(same, 1.0, 0.0).astype(jnp.bfloat16)

    front_kernel(
        devices, start_weights, sources, held, own_sem, normed, state, meta,
        *front_buffers, *front_sems,
    )
    expert_kernel(
        devices, weight_copies, normed, meta, state, held[3], front_buffers[1], out,
        *expert_buffers, *expert_sems,
    )


def block_call(
    tokens, query_key_value, out_weight, modulation, router_weight, expert_ids,
    gate_up_weight, down_weight,
):
    devices = lax.axis_size("dev")
    count, width = tokens.shape
    half = down_weight.shape[2]
    halves = gate_up_weight.shape[0]
    local = halves // 2
    gate_up_weight = gate_up_weight.swapaxes(2, 3)
    hidden = gate_up_weight.shape[2]
    lines = devices // COLS
    rows = devices * SLOT
    slots, pack = local * SLOT, local * CAP
    part = half // CHUNKS
    shard = out_weight.shape[0]
    own = (
        tokens, query_key_value.transpose(1, 0, 2), out_weight, modulation,
        router_weight.T, expert_ids.T,
    )
    hbm = pl.BlockSpec(memory_space=pl.ANY)
    dma = pltpu.SemaphoreType.DMA
    return pl.pallas_call(
        functools.partial(block_kernel, devices),
        out_shape=jax.ShapeDtypeStruct((count, half), jnp.bfloat16),
        in_specs=[hbm] * 8,
        out_specs=pl.BlockSpec(memory_space=pltpu.VMEM),
        scratch_shapes=[
            *[pltpu.VMEM(array.shape, array.dtype) for array in own],
            pltpu.VMEM((count, width), jnp.bfloat16),
            pltpu.VMEM((count, width), jnp.float32),
            pltpu.VMEM((router_weight.shape[1], count), jnp.float32),
            pltpu.VMEM((2, 2, count, half), jnp.bfloat16),
            pltpu.VMEM((devices, shard, half), jnp.bfloat16),
            pltpu.VMEM((count, half), jnp.bfloat16),
            pltpu.VMEM((devices, count, shard), jnp.float32),
            pltpu.VMEM((devices, count, shard), jnp.float32),
            pltpu.VMEM((lines, CHUNKS, count, part), jnp.bfloat16),
            pltpu.VMEM((lines, CHUNKS, pack, part), jnp.bfloat16),
            pltpu.VMEM((lines, CHUNKS, pack, part), jnp.bfloat16),
            pltpu.VMEM((2, lines, CHUNKS, count, part), jnp.bfloat16),
            pltpu.VMEM((2, CHUNKS, local, rows, part), jnp.bfloat16),
            pltpu.VMEM(gate_up_weight.shape, jnp.bfloat16),
            pltpu.VMEM(down_weight.shape, jnp.bfloat16),
            pltpu.VMEM((local, rows, 4 * hidden), jnp.float32),
            pltpu.VMEM((local, rows, 2 * hidden), jnp.bfloat16),
            pltpu.VMEM((local, rows, 2 * hidden), jnp.bfloat16),
            pltpu.VMEM((lines, COLS * local, count), jnp.float32),
            pltpu.VMEM((lines, slots + pack, count), jnp.bfloat16),
            pltpu.VMEM((lines, slots + pack, count), jnp.bfloat16),
            pltpu.VMEM((pack, slots), jnp.bfloat16),
            pltpu.VMEM((slots, pack), jnp.bfloat16),
            pltpu.VMEM((count, part), jnp.float32),
            dma((6,)), dma((halves,)), dma((halves,)),
            dma((2,)), dma((2,)), dma((2,)), dma((2,)),
            dma((devices, 4)), dma((devices,)), dma((devices,)),
            dma((devices,)), dma((devices,)),
            dma((lines,)), dma((lines,)),
            dma((lines, CHUNKS, 2)), dma((lines, CHUNKS)),
            dma((lines, CHUNKS)), dma((lines, CHUNKS)),
            dma((devices, CHUNKS)), dma((devices, CHUNKS)),
            dma((local,)), dma((local,)),
            dma((lines, CHUNKS)), dma((lines, CHUNKS)),
            dma((lines, CHUNKS)), dma((2, lines, CHUNKS)),
        ],
        compiler_params=pltpu.CompilerParams(
            collective_id=1, has_side_effects=True, vmem_limit_bytes=VMEM_BYTES
        ),
    )(*own, gate_up_weight, down_weight)


def body(
    tokens,
    query_key_value,
    out_weight,
    modulation,
    router_weight,
    expert_ids,
    gate_up_weight,
    down_weight,
):
    count = tokens.shape[0]
    width = tokens.shape[1]
    parts = lax.axis_size("sub")
    part = lax.axis_index("sub")
    position = lax.axis_index("dev")
    devices = lax.axis_size("dev")
    total = count * devices
    local_width = query_key_value.shape[2]
    weight_bytes = 2 * (gate_up_weight.size + down_weight.size)
    token_bytes = 12 * devices * count * width
    fits = weight_bytes + token_bytes < VMEM_BYTES and CAP <= SLOT
    paired = parts == 2 and lax.axis_size("groups") == 2 and devices % COLS == 0
    experts_here = gate_up_weight.shape[0] // 2
    tiled = out_weight.shape[0] % (2 * LANES) == 0 and count == LANES
    tiled = tiled and down_weight.shape[2] % (2 * CHUNKS * LANES) == 0 and experts_here == devices
    tiled = tiled and experts_here * (SLOT + CAP) <= out_weight.shape[0] and SLOT * devices == LANES
    tiled = tiled and gate_up_weight.shape[3] % 64 == 0
    if fits and paired and tiled:
        return block_call(
            tokens, query_key_value, out_weight, modulation, router_weight, expert_ids,
            gate_up_weight, down_weight,
        )
    heads_here = local_width // HEAD
    query = query_key_value[:, 0].reshape(count, heads_here, HEAD)
    pair = query_key_value[:, 1:]
    near = extended(pair, (("dev", 0),), count)
    keys = near[:, 0].reshape(3 * count, heads_here, HEAD)
    values = near[:, 1].reshape(3 * count, heads_here, HEAD)
    mixed = window_attention(query, keys, values, position, total).reshape(count, local_width)
    partial_proj = lax.dot_general(
        mixed,
        lax.all_gather(out_weight, "dev", axis=0, tiled=True),
        (((1,), (1,)), ((), ())),
        preferred_element_type=jnp.float32,
    )
    proj = lax.psum(partial_proj, "sub")
    state = tokens.astype(jnp.float32) + (1.0 + modulation[0]) * proj
    normed = normalize(state, modulation)
    gates = route(normed, router_weight, expert_ids)
    experts = router_weight.shape[1]
    topk = expert_ids.shape[1]
    flat = expert_ids.reshape(-1)
    picks = flat.shape[0]
    onehot = (flat[:, None] == jnp.arange(experts, dtype=jnp.int32)[None, :]).astype(jnp.int32)
    rank = jnp.sum((jnp.cumsum(onehot, 0) - 1) * onehot, 1)
    target = flat * CAP + rank
    hit = target[None, :] == jnp.arange(experts * CAP, dtype=jnp.int32)[:, None]
    filled = jnp.any(hit, 1)
    anchor = jnp.sum(jnp.where(hit, jnp.arange(picks, dtype=jnp.int32)[None, :], 0), 1) // topk
    slice_width = width // parts
    sent = lax.dynamic_slice_in_dim(normed, part * slice_width, slice_width, 1)
    sent_width = sent.shape[1]
    rows_out = jnp.where(filled[:, None], sent[anchor], jnp.zeros((), jnp.bfloat16))
    halves_here = gate_up_weight.shape[0]
    doubled = jnp.broadcast_to(
        rows_out.reshape(experts, 1, CAP, sent_width), (experts, 2, CAP, sent_width)
    )
    outgoing = doubled.reshape(devices, halves_here, CAP, sent_width)
    up_form = "sxcd,xgdf->sxcgf"
    down_form = "sxcf,xfd->sxcd"
    incoming = lax.all_to_all(outgoing, "dev", split_axis=0, concat_axis=0, tiled=True)
    both = jnp.einsum(
        up_form,
        lax.all_gather(incoming, "sub", axis=3, tiled=True),
        gate_up_weight,
        preferred_element_type=jnp.float32,
    )
    hidden = (jax.nn.silu(both[..., 0, :]) * both[..., 1, :]).astype(jnp.bfloat16)
    gathered = lax.all_gather(hidden, "sub", axis=hidden.ndim - 1, tiled=True)
    result = jnp.einsum(down_form, gathered, down_weight, preferred_element_type=jnp.float32)
    returned = lax.all_to_all(
        result.astype(jnp.bfloat16), "dev", split_axis=0, concat_axis=0, tiled=True
    )
    own_width = returned.shape[-1]
    arranged = returned.reshape(experts, 2, CAP, own_width)
    answers = arranged[flat, :, rank, :].reshape(count, topk, 2, own_width).astype(jnp.float32)
    combined = answers[:, :, 0] + answers[:, :, 1]
    routed = jnp.einsum("tk,tkd->td", gates, combined)
    own = lax.dynamic_slice_in_dim(state, part * slice_width, slice_width, 1)
    lift = lax.dynamic_slice_in_dim(modulation[3], part * slice_width, slice_width, 0)
    return (own + (1.0 + lift) * routed).astype(jnp.bfloat16)


def solution(mesh):
    return jax.shard_map(
        body,
        mesh=mesh,
        in_specs=(
            P(("groups", "dev"), None),
            P(("groups", "dev"), None, "sub"),
            P("dev", "sub"),
            P("groups", None),
            P(),
            P(("groups", "dev"), None),
            P("dev", None, None, "sub"),
            P("dev", None, "sub"),
        ),
        out_specs=P(("groups", "dev"), "sub"),
        check_vma=False,
    )
```

```python
import functools
import math

import jax
import jax.numpy as jnp
from jax import lax
from jax.experimental import pallas as pl
from jax.experimental.pallas import tpu as pltpu
from jax.sharding import PartitionSpec as P

HEAD = 128
CAP = 12


EPS = 1e-06
NEG = -1e30


def extended(cells, sides, width):
    for axis, dim in sides:
        count = lax.axis_size(axis)
        ends = count - 1
        head = lax.slice_in_dim(cells, 0, width, axis=dim)
        tail = lax.slice_in_dim(cells, cells.shape[dim] - width, cells.shape[dim], axis=dim)
        cells = jnp.concatenate(
            [
                lax.ppermute(tail, axis, [(i, (i + 1) % count) for i in range(ends)]),
                cells,
                lax.ppermute(head, axis, [((i + 1) % count, i) for i in range(ends)]),
            ],
            axis=dim,
        )
    return cells


def window_attention(query, keys, values, index, total):
    count = query.shape[0]
    rows = jnp.arange(count, dtype=jnp.int32)[:, None]
    cols = jnp.arange(3 * count, dtype=jnp.int32)[None, :] - count
    place = index * count + cols
    allowed = (jnp.abs(cols - rows) <= count) & (place >= 0) & (place < total)
    scores = jnp.einsum(
        "qhd,khd->hqk", query, keys, preferred_element_type=jnp.float32
    ) / math.sqrt(query.shape[2])
    scores = jnp.where(allowed[None], scores, NEG)
    top = jnp.max(scores, -1, keepdims=True)
    weight = jnp.exp(scores - top)
    weight = (weight / jnp.sum(weight, -1, keepdims=True)).astype(jnp.bfloat16)
    mixed = jnp.einsum("hqk,khd->qhd", weight, values, preferred_element_type=jnp.float32)
    return mixed.astype(jnp.bfloat16)


def normalize(state, modulation):
    scale = lax.rsqrt(jnp.mean(state * state, -1, keepdims=True) + EPS)
    return (state * scale * (1.0 + modulation[2]) + modulation[1]).astype(jnp.bfloat16)


def route(normed, router_weight, expert_ids):
    logits = jnp.dot(normed, router_weight, preferred_element_type=jnp.float32)
    experts = router_weight.shape[1]
    match = expert_ids[:, :, None] == jnp.arange(experts, dtype=jnp.int32)[None, None, :]
    picked = jnp.sum(jnp.where(match, logits[:, None, :], 0.0), -1)
    lifted = jax.nn.sigmoid(picked)
    return lifted / jnp.sum(lifted, -1, keepdims=True)


LANES = 128
SLOT = 16
COLS = 2
CHUNKS = 4
PIECES = 2
VMEM_BYTES = 66 * 1000 * 1000
MESH = pl.DeviceIdType.MESH


def choose(index, table):
    value = jnp.int32(table[0])
    for i in range(1, len(table)):
        value = jnp.where(index == i, table[i], value)
    return value


def line_order(lines, nearest):
    rows = []
    for z in range(lines):
        lower = z < lines - 1 - z
        others = [line for line in range(lines) if line != z]
        sign = 1 if nearest else -1
        rows.append(sorted(others, key=lambda line: (sign * abs(line - z), (line > z) == lower)))
    return [[rows[z][j] for z in range(lines)] for j in range(lines - 1)]


def expert_kernel(
    devices, weight_copies,
    normed, meta, state, modulation, wide,
    out,
    tok, got_packed, got_rows, got_sum, disp, gu, dn, raised, hid_own, hid_other,
    got_meta, pick, gated, squeeze, grow, acc,
    meta_s, meta_r, z_s, z_r, x_s, x_r, core_s, core_r, hid_s, hid_r, rx_s, rx_r, rz_s, rz_r,
):
    me = lax.axis_index("dev")
    part = lax.axis_index("sub")
    other = 1 - part
    z = me // COLS
    x = me % COLS
    lines = devices // COLS
    count, width = normed.shape
    half = width // 2
    local = raised.shape[0]
    hidden = gu.shape[2]
    both_hidden = 2 * hidden
    slots = local * SLOT
    pack = local * CAP
    rows = devices * SLOT
    chunks, wide_chunk = tok.shape[1], tok.shape[3]

    def remote(src, dst, send, recv, where):
        return pltpu.make_async_remote_copy(
            src_ref=src, dst_ref=dst, send_sem=send, recv_sem=recv,
            device_id=where, device_id_type=MESH,
        )

    above = jnp.minimum(me + COLS, devices - 1)
    below = jnp.maximum(me - COLS, 0)
    x_to = {"dev": z * COLS + (1 - x)}
    core_to = {"sub": other}
    not_top = z < lines - 1
    not_bottom = z > 0
    near_lines = [choose(z, table) for table in line_order(lines, True)]
    far_lines = [choose(z, table) for table in line_order(lines, False)]

    def lanes_of(c):
        return pl.ds(pl.multiple_of(c * wide_chunk, wide_chunk), wide_chunk)

    def own_lanes(c):
        return pl.ds(pl.multiple_of(part * half + c * wide_chunk, wide_chunk), wide_chunk)

    def slot_rows(s):
        return pl.ds(pl.multiple_of(s * SLOT, SLOT), SLOT)

    def meta_copy(line):
        return remote(
            meta.at[pl.ds(pl.multiple_of(line * COLS * local, COLS * local), COLS * local)],
            got_meta.at[z], meta_s.at[line], meta_r.at[z], {"dev": line * COLS + x},
        )

    def meta_arrival(line):
        return remote(got_meta.at[line], got_meta.at[line], meta_s.at[line], meta_r.at[line], x_to)

    def z_copy(line, c, way, src=None):
        dst = tok.at[line, c]
        where = {"dev": jnp.where(way == 0, above, below)}
        return remote(
            dst if src is None else src, dst, z_s.at[line, c, way], z_r.at[line, c], where
        )

    def packed_out(line, c):
        return wide.at[line, pl.ds(slots, pack), lanes_of(c)]

    def x_copy(line, c):
        return remote(
            packed_out(line, c), got_packed.at[line, c], x_s.at[line, c], x_r.at[line, c], x_to
        )

    def core_copy(which, s, c):
        place = disp.at[which, c, :, slot_rows(s), :]
        return remote(place, place, core_s.at[s, c], core_r.at[s, c], core_to)

    def own_send(c):
        src = normed.at[:, own_lanes(c)]

        @pl.when(not_top)
        def _():
            z_copy(z, c, 0, src).start()

        @pl.when(not_bottom)
        def _():
            z_copy(z, c, 1, src).start()

    own_send(0)
    for line in near_lines:
        meta_copy(line).start()

    before = (
        lax.broadcasted_iota(jnp.int32, (count, count), 0)
        < lax.broadcasted_iota(jnp.int32, (count, count), 1)
    ).astype(jnp.float32).astype(jnp.bfloat16)
    place = lax.broadcasted_iota(jnp.int32, (local, SLOT, count), 1).astype(jnp.float32)

    def routing(line, ours, theirs):
        for first, gate in ((True, ours), (False, theirs)):
            chosen = jnp.where(gate > 0.0, 1.0, 0.0)
            rank = jnp.dot(chosen.astype(jnp.bfloat16), before, preferred_element_type=jnp.float32)
            rank = jnp.where(gate > 0.0, rank, -1.0)
            hit = jnp.broadcast_to(rank[:, None, :], place.shape) == place
            one = jnp.where(hit, 1.0, 0.0).reshape(slots, count).astype(jnp.bfloat16)
            value = jnp.where(hit, jnp.broadcast_to(gate[:, None, :], place.shape), 0.0)
            value = value.reshape(slots, count).astype(jnp.bfloat16)
            if first:
                pick[line, :slots] = one
                gated[line, :slots] = value
            else:
                pick[line, slots:] = jnp.dot(
                    squeeze[...], one, preferred_element_type=jnp.float32
                ).astype(jnp.bfloat16)
                gated[line, slots:] = jnp.dot(
                    squeeze[...], value, preferred_element_type=jnp.float32
                ).astype(jnp.bfloat16)

    def expert_rows(base, column):
        return pl.ds(pl.multiple_of(base + column * local, local), local)

    def spread(line, c, block):
        moved = jnp.dot(pick[line], block, preferred_element_type=jnp.float32).astype(jnp.bfloat16)
        s = line * COLS + x
        wide[line, slots:slots + pack, lanes_of(c)] = moved[slots:]
        x_copy(line, c).start()
        disp[part, c, :, slot_rows(s), :] = moved[:slots].reshape(local, SLOT, wide_chunk)
        core_copy(part, s, c).start()

    def own_step(c):
        spread(z, c, normed[:, own_lanes(c)])

    def line_step(line, c):
        low = line < z

        @pl.when(c == 0)
        def _():
            meta_arrival(line).wait_recv()
            routing(
                line, got_meta[line, expert_rows(0, x)], got_meta[line, expert_rows(0, 1 - x)]
            )

        way = jnp.where(low, 0, 1)
        z_copy(line, c, way).wait_recv()

        @pl.when(jnp.where(low, not_top, not_bottom))
        def _():
            z_copy(line, c, way).start()

        spread(line, c, tok[line, c])

    def x_step(line, c):
        x_copy(line, c).wait_recv()
        s = line * COLS + (1 - x)
        disp[part, c, :, slot_rows(s), :] = jnp.dot(
            grow[...], got_packed[line, c], preferred_element_type=jnp.float32
        ).astype(jnp.bfloat16).reshape(local, SLOT, wide_chunk)
        core_copy(part, s, c).start()

    def across_rows(left, right):
        return lax.dot_general(
            left, right, (((1,), (1,)), ((), ())), preferred_element_type=jnp.float32
        )

    def raise_part(e, c):
        total = raised[e]
        for side in range(2):
            lanes = pl.ds(pl.multiple_of(side * half + c * wide_chunk, wide_chunk), wide_chunk)
            weight = jnp.concatenate(
                [gu[2 * e, 0, :, lanes], gu[2 * e + 1, 0, :, lanes],
                 gu[2 * e, 1, :, lanes], gu[2 * e + 1, 1, :, lanes]], axis=0
            )
            total = total + across_rows(disp[side, c, e], weight)
        return total

    def hid_copy(e):
        return remote(hid_own.at[e], hid_other.at[e], hid_s.at[e], hid_r.at[e], core_to)

    def arrived(c):
        for s in range(devices):
            core_copy(other, s, c).wait_recv()

    routing(
        z, meta[expert_rows(z * COLS * local, x)], meta[expert_rows(z * COLS * local, 1 - x)]
    )
    own_step(0)

    def weight_wait(h, carry):
        for copy in weight_copies(h):
            copy.wait()
        return carry

    lax.fori_loop(0, 2 * local, weight_wait, 0)

    def step(t, carry):
        ready = t - lines

        def raise_some(i):
            first, last = i * local // (2 * lines), (i + 1) * local // (2 * lines)

            @pl.when(ready >= 0)
            def _():
                if i == 0:
                    arrived(ready)
                for e in range(first, last):
                    raised[e] = raise_part(e, ready)

        @pl.when(t + 1 < chunks)
        def _():
            own_send(t + 1)
            own_step(t + 1)

        raise_some(0)
        for j, line in enumerate(near_lines):
            c = t - jnp.abs(line - z) + 1

            @pl.when((c >= 0) & (c < chunks))
            def _():
                line_step(line, c)

            raise_some(1 + j)

        @pl.when(t < chunks)
        def _():
            x_step(z, t)

        raise_some(lines)
        for j, line in enumerate(near_lines):
            c = t - jnp.abs(line - z)

            @pl.when((c >= 0) & (c < chunks))
            def _():
                x_step(line, c)

            raise_some(lines + 1 + j)
        return carry

    lax.fori_loop(0, chunks + lines - 1, step, 0)
    arrived(chunks - 1)

    def last_raise(e, carry):
        total = raise_part(e, chunks - 1)
        gate = total[:, :both_hidden]
        hid_own[e] = (gate * jax.nn.sigmoid(gate) * total[:, both_hidden:]).astype(jnp.bfloat16)
        hid_copy(e).start()
        return carry

    lax.fori_loop(0, local, last_raise, 0)

    group = 2 * wide_chunk

    def lower(g):
        lanes = slice(g * group, (g + 1) * group)

        def one(e, carry):
            if g == 0:
                hid_copy(e).wait_recv()
            mine = pl.ds(pl.multiple_of(part * hidden, SLOT), hidden)
            theirs = pl.ds(pl.multiple_of(other * hidden, SLOT), hidden)
            left = jnp.concatenate([hid_own[e], hid_other[e]], axis=1)
            right = jnp.concatenate(
                [dn[2 * e, mine, lanes], dn[2 * e + 1, mine, lanes],
                 dn[2 * e, theirs, lanes], dn[2 * e + 1, theirs, lanes]], axis=0
            )
            wide[e, :rows, lanes] = jnp.dot(
                left, right, preferred_element_type=jnp.float32
            ).astype(jnp.bfloat16)
            return carry

        lax.fori_loop(0, local, one, 0)

    def result_rows(s, q):
        return wide[:local, slot_rows(s), lanes_of(q)].reshape(slots, wide_chunk)

    def rx_copy(line, q):
        return remote(
            wide.at[lines + line, pl.ds(slots, pack), lanes_of(q)], got_rows.at[line, q],
            rx_s.at[line, q], rx_r.at[line, q], x_to,
        )

    def rz_copy(line, q, way):
        where = {"dev": jnp.where(way == 0, above, below)}
        return remote(
            tok.at[line, q], got_sum.at[way, line, q],
            rz_s.at[line, q], rz_r.at[way, line, q], where,
        )

    def give(line, q):
        packed = jnp.dot(
            squeeze[...], result_rows(line * COLS + (1 - x), q), preferred_element_type=jnp.float32
        )
        wide[lines + line, slots:slots + pack, lanes_of(q)] = packed.astype(jnp.bfloat16)
        rx_copy(line, q).start()

    def gather_here(line, q):
        rx_copy(line, q).wait_recv()
        pieces = jnp.concatenate([result_rows(line * COLS + x, q), got_rows[line, q]], axis=0)
        acc[...] = lax.dot_general(
            gated[line], pieces, (((0,), (0,)), ((), ())), preferred_element_type=jnp.float32
        )

    def add_line(line, q, way):
        rz_copy(line, q, way).wait_recv()
        acc[...] += got_sum[way, line, q].astype(jnp.float32)

    def pass_on(line, q):
        gather_here(line, q)
        way = jnp.where(line > z, 0, 1)

        @pl.when(jnp.where(line > z, not_bottom, not_top))
        def _():
            add_line(line, q, way)

        tok[line, q] = acc[...].astype(jnp.bfloat16)
        rz_copy(line, q, way).start()

    for g in range(half // group):
        lower(g)
        for q in range(2 * g, 2 * g + 2):
            give(far_lines[0], q)
    for line in far_lines[1:] + [z]:
        lax.fori_loop(0, chunks, lambda q, carry, line=line: (give(line, q), carry)[1], 0)
    for line in near_lines:
        low = line < z

        @pl.when(jnp.where(low, not_top, not_bottom))
        def _():
            for c in range(chunks):
                z_copy(line, c, jnp.where(low, 0, 1)).wait_send()

    for line in far_lines:
        lax.fori_loop(0, chunks, lambda q, carry, line=line: (pass_on(line, q), carry)[1], 0)
    for q in range(chunks):
        gather_here(z, q)

        @pl.when(not_bottom)
        def _():
            add_line(z, q, 0)

        @pl.when(not_top)
        def _():
            add_line(z, q, 1)

        own = own_lanes(q)
        lanes = slice(q * wide_chunk, (q + 1) * wide_chunk)
        out[:, lanes] = (
            state[:, own] + (1.0 + modulation[3:4, own]) * acc[...]
        ).astype(out.dtype)

    for c in range(chunks):

        @pl.when(not_top)
        def _():
            z_copy(z, c, 0, normed.at[:, own_lanes(c)]).wait_send()

        @pl.when(not_bottom)
        def _():
            z_copy(z, c, 1, normed.at[:, own_lanes(c)]).wait_send()

        for line in near_lines:
            rz_copy(line, c, jnp.where(line > z, 0, 1)).wait_send()
        for line in range(lines):
            x_copy(line, c).wait_send()
            rx_copy(line, c).wait_send()
        for s in range(devices):
            core_copy(part, s, c).wait_send()
    for line in near_lines:
        meta_copy(line).wait_send()

    def hid_drain(e, carry):
        hid_copy(e).wait_send()
        return carry

    lax.fori_loop(0, local, hid_drain, 0)


def front_kernel(
    devices, start_weights,
    sources, held, own_sem,
    normed, state, meta,
    near, column, mixed, mixed_in, mine_out, their_out, sent_back, got_back, their_back,
    near_s, near_r, far_s, far_r, wz_s, wz_r, wy_s, wy_r, mix_s, mix_r,
    sum_s, sum_r, back_s, back_r, share_s, share_r,
):
    packed_hbm, weight_hbm = sources[1], sources[2]
    tokens, packed, modulation, router, ids = held
    me = lax.axis_index("dev")
    part = lax.axis_index("sub")
    group = lax.axis_index("groups")
    z = me // COLS
    x = me % COLS
    lines = devices // COLS
    count, width = tokens.shape
    shard = column.shape[1]
    share = shard // 2
    piece = share // PIECES
    pairs, pair = near.shape[1], near.shape[4]
    targets = (tokens, packed, column.at[z], modulation, router, ids)

    def own_copy(i):
        return pltpu.make_async_copy(sources[i], targets[i], own_sem.at[i])

    for i in (1, 2, 0, 3, 4, 5):
        own_copy(i).start()
    not_top = z < lines - 1
    not_bottom = z > 0
    above = jnp.minimum(me + COLS, devices - 1)
    below = jnp.maximum(me - COLS, 0)
    x_to = {"dev": z * COLS + (1 - x)}
    y_to = {"groups": 1 - group}
    core_to = {"sub": 1 - part}
    near_lines = [choose(z, table) for table in line_order(lines, True)]

    barrier = pltpu.get_barrier_semaphore()

    def greet(where):
        pl.semaphore_signal(barrier, inc=1, device_id=where, device_id_type=MESH)

    for where in (x_to, y_to, core_to):
        greet(where)
    for line in near_lines:
        greet({"dev": line * COLS + x})
    pl.semaphore_wait(barrier, lines + 2)

    def remote(src, dst, send, recv, where):
        return pltpu.make_async_remote_copy(
            src_ref=src, dst_ref=dst, send_sem=send, recv_sem=recv,
            device_id=where, device_id_type=MESH,
        )

    def near_copy(k):
        src = packed_hbm.at[1:3, :, pl.ds(k * pair, pair)]
        return remote(src, near.at[x, k], near_s.at[k], near_r.at[k], x_to)

    def far_copy(k):
        where = {"dev": jnp.where(x == 0, above, below)}
        return remote(near.at[1 - x, k], near.at[x, k], far_s.at[k], far_r.at[k], where)

    give_far = ((x == 0) & not_top) | ((x == 1) & not_bottom)
    have_far = ((x == 0) & not_bottom) | ((x == 1) & not_top)

    def piece_rows(which, i):
        return pl.ds(pl.multiple_of(which * share + i * piece, SLOT), piece)

    def wz_copy(line, i, way, src=None):
        dst = column.at[line, piece_rows(group, i)]
        where = {"dev": jnp.where(way == 0, above, below)}
        return remote(
            dst if src is None else src, dst, wz_s.at[line, i, way], wz_r.at[line, i], where
        )

    def own_piece(i):
        return weight_hbm.at[piece_rows(group, i)]

    def wy_copy(line, i, which):
        block = column.at[line, piece_rows(which, i)]
        return remote(block, block, wy_s.at[line, i], wy_r.at[line, i], y_to)

    for k in range(pairs):
        near_copy(k).start()
    for i in range(PIECES):

        @pl.when(not_top)
        def _():
            wz_copy(z, i, 0, own_piece(i)).start()

        @pl.when(not_bottom)
        def _():
            wz_copy(z, i, 1, own_piece(i)).start()

    start_weights()

    @pl.when(jnp.logical_not(have_far))
    def _():
        near[x] = jnp.zeros_like(near[x])

    def way_of(line):
        return jnp.where(line < z, 0, 1)

    def more(line):
        return jnp.where(line < z, not_top, not_bottom)

    def busy(line):
        return jnp.where(line < z, x == 0, x == 1)

    def distance(line):
        return jnp.abs(line - z)

    def take(line, onward):
        for i in range(PIECES):
            wz_copy(line, i, way_of(line)).wait_recv()

            @pl.when(onward)
            def _():
                wz_copy(line, i, way_of(line)).start()

            wy_copy(line, i, group).start()

    def pass_near(k):
        near_copy(k).wait_recv()

        @pl.when(give_far)
        def _():
            far_copy(k).start()

    early = pairs // 2
    for k in range(early):
        pass_near(k)
    for line in near_lines:

        @pl.when(distance(line) == 1)
        def _():
            take(line, more(line) & jnp.logical_not(busy(line)))

    for k in range(early, pairs):
        pass_near(k)
    for line in near_lines:

        @pl.when((distance(line) == 1) & busy(line) & more(line))
        def _():
            for i in range(PIECES):
                wz_copy(line, i, way_of(line)).start()

    for i in range(6):
        own_copy(i).wait()

    row = lax.broadcasted_iota(jnp.int32, (count, count), 0)
    col = lax.broadcasted_iota(jnp.int32, (count, count), 1)
    see_before = (col >= row) & (me > 0)
    see_after = (col <= row) & (me < devices - 1)

    def mix_copy(k):
        lanes = pl.ds(k * pair, pair)
        return remote(
            mixed.at[:, lanes], mixed_in.at[:, lanes], mix_s.at[k], mix_r.at[k], x_to
        )

    for k in range(pairs):

        @pl.when(have_far)
        def _():
            far_copy(k).wait_recv()

        for h in range(pair // HEAD):
            lanes = slice(k * pair + h * HEAD, k * pair + (h + 1) * HEAD)
            inner = slice(h * HEAD, (h + 1) * HEAD)
            query = packed[0, :, lanes]

            def score(keys):
                return lax.dot_general(
                    query, keys, (((1,), (1,)), ((), ())), preferred_element_type=jnp.float32
                ) / math.sqrt(HEAD)

            scores = jnp.concatenate(
                [
                    jnp.where(see_before, score(near[0, k, 0, :, inner]), NEG),
                    score(packed[1, :, lanes]),
                    jnp.where(see_after, score(near[1, k, 0, :, inner]), NEG),
                ],
                axis=1,
            )
            top = jnp.max(scores, -1, keepdims=True)
            weight = jnp.exp(scores - top)
            weight = (weight / jnp.sum(weight, -1, keepdims=True)).astype(jnp.bfloat16)
            values = jnp.concatenate(
                [near[0, k, 1, :, inner], packed[2, :, lanes], near[1, k, 1, :, inner]], axis=0
            )
            mixed[:, lanes] = jnp.dot(
                weight, values, preferred_element_type=jnp.float32
            ).astype(jnp.bfloat16)
        mix_copy(k).start()
        if k + 1 == early:
            for line in near_lines:

                @pl.when((distance(line) == 2) & jnp.logical_not(busy(line)))
                def _():
                    take(line, more(line))

    for k in range(pairs):
        mix_copy(k).wait_recv()

    def place_of(which):
        return group if which == 0 else 1 - group

    def sum_copy(line, which):
        place = place_of(which)
        return remote(
            mine_out.at[line, place], their_out.at[line, place],
            sum_s.at[line, which], sum_r.at[line, which], core_to,
        )

    def back_copy(line, which):
        place = place_of(which)
        return remote(
            sent_back.at[line, place], got_back.at[line, place],
            back_s.at[line, which], back_r.at[line, which], x_to,
        )

    def share_copy(line, which):
        place = place_of(which)
        return remote(
            got_back.at[line, place], their_back.at[line, place],
            share_s.at[line, which], share_r.at[line, which], core_to,
        )

    def project(line, which):
        place = place_of(which)
        block = column[line, pl.ds(pl.multiple_of(place * share, SLOT), share), :]
        both = jnp.concatenate([mixed_in[...], mixed[...]], axis=0)
        product = lax.dot_general(
            both, block, (((1,), (1,)), ((), ())), preferred_element_type=jnp.float32
        )
        sent_back[line, place] = product[:count].astype(jnp.bfloat16)
        back_copy(line, which).start()
        mine_out[line, place] = product[count:]
        sum_copy(line, which).start()

    steps = [(line, which) for line in [z] + near_lines for which in range(2)]

    def relay(i):
        back_copy(*steps[i]).wait_recv()
        share_copy(*steps[i]).start()

    for i, (line, which) in enumerate(steps):
        if i >= 2:
            if which == 0:

                @pl.when((distance(line) > 2) | ((distance(line) == 2) & busy(line)))
                def _():
                    take(line, more(line))
            else:
                for n in range(PIECES):
                    wy_copy(line, n, 1 - group).wait_recv()
        project(line, which)
        if i >= 2:
            relay(i - 2)
    relay(len(steps) - 2)
    relay(len(steps) - 1)

    square = jnp.zeros((count, 1), jnp.float32)
    for line, which in steps:
        place = place_of(which)
        sum_copy(line, which).wait_recv()
        share_copy(line, which).wait_recv()
        for column_of, total in (
            (x, mine_out[line, place] + their_out[line, place]),
            (
                1 - x,
                got_back[line, place].astype(jnp.float32)
                + their_back[line, place].astype(jnp.float32),
            ),
        ):
            start = (line * COLS + column_of) * shard + place * share
            lanes = pl.ds(pl.multiple_of(start, LANES), share)
            value = tokens[:, lanes].astype(jnp.float32) + (1.0 + modulation[0:1, lanes]) * total
            state[:, lanes] = value
            square = square + jnp.sum(value * value, -1, keepdims=True)
    scale = lax.rsqrt(square / width + EPS)
    for s in range(devices):
        lanes = slice(s * shard, (s + 1) * shard)
        normed[:, lanes] = (
            state[:, lanes] * scale * (1.0 + modulation[2:3, lanes]) + modulation[1:2, lanes]
        ).astype(jnp.bfloat16)
    logits = lax.dot_general(
        router[...], normed[...], (((1,), (1,)), ((), ())), preferred_element_type=jnp.float32
    )
    name = lax.broadcasted_iota(jnp.int32, logits.shape, 0)
    named = name == ids[0:1]
    for k in range(1, ids.shape[0]):
        named = named | (name == ids[k:k + 1])
    lifted = jnp.where(named, jax.nn.sigmoid(logits), 0.0)
    meta[...] = lifted / jnp.sum(lifted, 0, keepdims=True)

    for k in range(pairs):
        near_copy(k).wait_send()
        mix_copy(k).wait_send()

        @pl.when(give_far)
        def _():
            far_copy(k).wait_send()

    for i in range(PIECES):

        @pl.when(not_top)
        def _():
            wz_copy(z, i, 0, own_piece(i)).wait_send()

        @pl.when(not_bottom)
        def _():
            wz_copy(z, i, 1, own_piece(i)).wait_send()

        for line in near_lines:

            @pl.when(more(line))
            def _():
                wz_copy(line, i, way_of(line)).wait_send()

            wy_copy(line, i, group).wait_send()
    for line, which in steps:
        sum_copy(line, which).wait_send()
        back_copy(line, which).wait_send()
        share_copy(line, which).wait_send()


def block_kernel(devices, *refs):
    sources, gate_up, down, out = refs[:6], refs[6], refs[7], refs[8]
    held, normed, state, meta, wide = refs[9:14], refs[14], refs[15], refs[16], refs[17]
    front_buffers, expert_buffers = refs[18:27], refs[27:43]
    own_sem, gu_sem, dn_sem = refs[43:46]
    front_sems, expert_sems = refs[46:62], refs[62:]
    gu, dn, raised = expert_buffers[5:8]
    squeeze, grow = expert_buffers[13:15]
    halves = gate_up.shape[0]

    def weight_copies(h):
        return (
            pltpu.make_async_copy(gate_up.at[h], gu.at[h], gu_sem.at[h]),
            pltpu.make_async_copy(down.at[h], dn.at[h], dn_sem.at[h]),
        )

    def start_weights():
        def one(h, carry):
            for copy in weight_copies(h):
                copy.start()
            return carry

        lax.fori_loop(0, halves, one, 0)
        raised[...] = jnp.zeros_like(raised)
        for ref, axis in ((squeeze, 0), (grow, 1)):
            packed = lax.broadcasted_iota(jnp.int32, ref.shape, axis)
            slot = lax.broadcasted_iota(jnp.int32, ref.shape, 1 - axis)
            inner = slot & (SLOT - 1)
            same = (packed == (slot - inner) // SLOT * CAP + inner) & (inner < CAP)
            ref[...] = jnp.where(same, 1.0, 0.0).astype(jnp.bfloat16)

    front_kernel(
        devices, start_weights, sources, held, own_sem, normed, state, meta,
        *front_buffers, *front_sems,
    )
    expert_kernel(
        devices, weight_copies, normed, meta, state, held[2], wide, out,
        *expert_buffers, *expert_sems,
    )


def block_call(
    tokens, query_key_value, out_weight, modulation, router_weight, expert_ids,
    gate_up_weight, down_weight,
):
    devices = lax.axis_size("dev")
    count, width = tokens.shape
    half = down_weight.shape[2]
    halves = gate_up_weight.shape[0]
    local = halves // 2
    gate_up_weight = gate_up_weight.swapaxes(2, 3)
    hidden = gate_up_weight.shape[2]
    lines = devices // COLS
    rows = devices * SLOT
    slots, pack = local * SLOT, local * CAP
    part = half // CHUNKS
    shard = out_weight.shape[0]
    own = (
        tokens, query_key_value.transpose(1, 0, 2), out_weight, modulation,
        router_weight.T, expert_ids.T,
    )
    hbm = pl.BlockSpec(memory_space=pl.ANY)
    dma = pltpu.SemaphoreType.DMA
    return pl.pallas_call(
        functools.partial(block_kernel, devices),
        out_shape=jax.ShapeDtypeStruct((count, half), jnp.bfloat16),
        in_specs=[hbm] * 8,
        out_specs=pl.BlockSpec(memory_space=pltpu.VMEM),
        scratch_shapes=[
            *[pltpu.VMEM(own[i].shape, own[i].dtype) for i in (0, 1, 3, 4, 5)],
            pltpu.VMEM((count, width), jnp.bfloat16),
            pltpu.VMEM((count, width), jnp.float32),
            pltpu.VMEM((router_weight.shape[1], count), jnp.float32),
            pltpu.VMEM((devices, slots + pack, half), jnp.bfloat16),
            pltpu.VMEM((2, CHUNKS, 2, count, part), jnp.bfloat16),
            pltpu.VMEM((lines, shard, half), jnp.bfloat16),
            pltpu.VMEM((count, half), jnp.bfloat16),
            pltpu.VMEM((count, half), jnp.bfloat16),
            pltpu.VMEM((lines, 2, count, shard // 2), jnp.float32),
            pltpu.VMEM((lines, 2, count, shard // 2), jnp.float32),
            pltpu.VMEM((lines, 2, count, shard // 2), jnp.bfloat16),
            pltpu.VMEM((lines, 2, count, shard // 2), jnp.bfloat16),
            pltpu.VMEM((lines, 2, count, shard // 2), jnp.bfloat16),
            pltpu.VMEM((lines, CHUNKS, count, part), jnp.bfloat16),
            pltpu.VMEM((lines, CHUNKS, pack, part), jnp.bfloat16),
            pltpu.VMEM((lines, CHUNKS, pack, part), jnp.bfloat16),
            pltpu.VMEM((2, lines, CHUNKS, count, part), jnp.bfloat16),
            pltpu.VMEM((2, CHUNKS, local, rows, part), jnp.bfloat16),
            pltpu.VMEM(gate_up_weight.shape, jnp.bfloat16),
            pltpu.VMEM(down_weight.shape, jnp.bfloat16),
            pltpu.VMEM((local, rows, 4 * hidden), jnp.float32),
            pltpu.VMEM((local, rows, 2 * hidden), jnp.bfloat16),
            pltpu.VMEM((local, rows, 2 * hidden), jnp.bfloat16),
            pltpu.VMEM((lines, COLS * local, count), jnp.float32),
            pltpu.VMEM((lines, slots + pack, count), jnp.bfloat16),
            pltpu.VMEM((lines, slots + pack, count), jnp.bfloat16),
            pltpu.VMEM((pack, slots), jnp.bfloat16),
            pltpu.VMEM((slots, pack), jnp.bfloat16),
            pltpu.VMEM((count, part), jnp.float32),
            dma((6,)), dma((halves,)), dma((halves,)),
            dma((CHUNKS,)), dma((CHUNKS,)), dma((CHUNKS,)), dma((CHUNKS,)),
            dma((lines, PIECES, 2)), dma((lines, PIECES)),
            dma((lines, PIECES)), dma((lines, PIECES)), dma((CHUNKS,)), dma((CHUNKS,)),
            dma((lines, 2)), dma((lines, 2)), dma((lines, 2)), dma((lines, 2)),
            dma((lines, 2)), dma((lines, 2)),
            dma((lines,)), dma((lines,)),
            dma((lines, CHUNKS, 2)), dma((lines, CHUNKS)),
            dma((lines, CHUNKS)), dma((lines, CHUNKS)),
            dma((devices, CHUNKS)), dma((devices, CHUNKS)),
            dma((local,)), dma((local,)),
            dma((lines, CHUNKS)), dma((lines, CHUNKS)),
            dma((lines, CHUNKS)), dma((2, lines, CHUNKS)),
        ],
        compiler_params=pltpu.CompilerParams(
            collective_id=1, has_side_effects=True, vmem_limit_bytes=VMEM_BYTES
        ),
    )(*own, gate_up_weight, down_weight)


def body(
    tokens,
    query_key_value,
    out_weight,
    modulation,
    router_weight,
    expert_ids,
    gate_up_weight,
    down_weight,
):
    count = tokens.shape[0]
    width = tokens.shape[1]
    parts = lax.axis_size("sub")
    part = lax.axis_index("sub")
    position = lax.axis_index("dev")
    devices = lax.axis_size("dev")
    total = count * devices
    local_width = query_key_value.shape[2]
    weight_bytes = 2 * (gate_up_weight.size + down_weight.size)
    token_bytes = 12 * devices * count * width
    fits = weight_bytes + token_bytes < VMEM_BYTES and CAP <= SLOT
    paired = parts == 2 and lax.axis_size("groups") == 2 and devices % COLS == 0
    experts_here = gate_up_weight.shape[0] // 2
    tiled = out_weight.shape[0] % (2 * LANES) == 0 and count == LANES
    tiled = tiled and down_weight.shape[2] // CHUNKS % HEAD == 0 and devices // COLS > 2
    tiled = tiled and down_weight.shape[2] % (2 * CHUNKS * LANES) == 0 and experts_here == devices
    tiled = tiled and SLOT * devices == LANES
    tiled = tiled and gate_up_weight.shape[3] % 64 == 0
    if fits and paired and tiled:
        return block_call(
            tokens, query_key_value, out_weight, modulation, router_weight, expert_ids,
            gate_up_weight, down_weight,
        )
    heads_here = local_width // HEAD
    query = query_key_value[:, 0].reshape(count, heads_here, HEAD)
    pair = query_key_value[:, 1:]
    near = extended(pair, (("dev", 0),), count)
    keys = near[:, 0].reshape(3 * count, heads_here, HEAD)
    values = near[:, 1].reshape(3 * count, heads_here, HEAD)
    mixed = window_attention(query, keys, values, position, total).reshape(count, local_width)
    partial_proj = lax.dot_general(
        mixed,
        lax.all_gather(out_weight, "dev", axis=0, tiled=True),
        (((1,), (1,)), ((), ())),
        preferred_element_type=jnp.float32,
    )
    proj = lax.psum(partial_proj, "sub")
    state = tokens.astype(jnp.float32) + (1.0 + modulation[0]) * proj
    normed = normalize(state, modulation)
    gates = route(normed, router_weight, expert_ids)
    experts = router_weight.shape[1]
    topk = expert_ids.shape[1]
    flat = expert_ids.reshape(-1)
    picks = flat.shape[0]
    onehot = (flat[:, None] == jnp.arange(experts, dtype=jnp.int32)[None, :]).astype(jnp.int32)
    rank = jnp.sum((jnp.cumsum(onehot, 0) - 1) * onehot, 1)
    target = flat * CAP + rank
    hit = target[None, :] == jnp.arange(experts * CAP, dtype=jnp.int32)[:, None]
    filled = jnp.any(hit, 1)
    anchor = jnp.sum(jnp.where(hit, jnp.arange(picks, dtype=jnp.int32)[None, :], 0), 1) // topk
    slice_width = width // parts
    sent = lax.dynamic_slice_in_dim(normed, part * slice_width, slice_width, 1)
    sent_width = sent.shape[1]
    rows_out = jnp.where(filled[:, None], sent[anchor], jnp.zeros((), jnp.bfloat16))
    halves_here = gate_up_weight.shape[0]
    doubled = jnp.broadcast_to(
        rows_out.reshape(experts, 1, CAP, sent_width), (experts, 2, CAP, sent_width)
    )
    outgoing = doubled.reshape(devices, halves_here, CAP, sent_width)
    up_form = "sxcd,xgdf->sxcgf"
    down_form = "sxcf,xfd->sxcd"
    incoming = lax.all_to_all(outgoing, "dev", split_axis=0, concat_axis=0, tiled=True)
    both = jnp.einsum(
        up_form,
        lax.all_gather(incoming, "sub", axis=3, tiled=True),
        gate_up_weight,
        preferred_element_type=jnp.float32,
    )
    hidden = (jax.nn.silu(both[..., 0, :]) * both[..., 1, :]).astype(jnp.bfloat16)
    gathered = lax.all_gather(hidden, "sub", axis=hidden.ndim - 1, tiled=True)
    result = jnp.einsum(down_form, gathered, down_weight, preferred_element_type=jnp.float32)
    returned = lax.all_to_all(
        result.astype(jnp.bfloat16), "dev", split_axis=0, concat_axis=0, tiled=True
    )
    own_width = returned.shape[-1]
    arranged = returned.reshape(experts, 2, CAP, own_width)
    answers = arranged[flat, :, rank, :].reshape(count, topk, 2, own_width).astype(jnp.float32)
    combined = answers[:, :, 0] + answers[:, :, 1]
    routed = jnp.einsum("tk,tkd->td", gates, combined)
    own = lax.dynamic_slice_in_dim(state, part * slice_width, slice_width, 1)
    lift = lax.dynamic_slice_in_dim(modulation[3], part * slice_width, slice_width, 0)
    return (own + (1.0 + lift) * routed).astype(jnp.bfloat16)


def solution(mesh):
    return jax.shard_map(
        body,
        mesh=mesh,
        in_specs=(
            P(("groups", "dev"), None),
            P(("groups", "dev"), None, "sub"),
            P("dev", "sub"),
            P("groups", None),
            P(),
            P(("groups", "dev"), None),
            P("dev", None, None, "sub"),
            P("dev", None, "sub"),
        ),
        out_specs=P(("groups", "dev"), "sub"),
        check_vma=False,
    )
```

```python
import functools
import math

import jax
import jax.numpy as jnp
from jax import lax
from jax.experimental import pallas as pl
from jax.experimental.pallas import tpu as pltpu
from jax.sharding import PartitionSpec as P

HEAD = 128
CAP = 12


EPS = 1e-06
NEG = -1e30


def extended(cells, sides, width):
    for axis, dim in sides:
        count = lax.axis_size(axis)
        ends = count - 1
        head = lax.slice_in_dim(cells, 0, width, axis=dim)
        tail = lax.slice_in_dim(cells, cells.shape[dim] - width, cells.shape[dim], axis=dim)
        cells = jnp.concatenate(
            [
                lax.ppermute(tail, axis, [(i, (i + 1) % count) for i in range(ends)]),
                cells,
                lax.ppermute(head, axis, [((i + 1) % count, i) for i in range(ends)]),
            ],
            axis=dim,
        )
    return cells


def window_attention(query, keys, values, index, total):
    count = query.shape[0]
    rows = jnp.arange(count, dtype=jnp.int32)[:, None]
    cols = jnp.arange(3 * count, dtype=jnp.int32)[None, :] - count
    place = index * count + cols
    allowed = (jnp.abs(cols - rows) <= count) & (place >= 0) & (place < total)
    scores = jnp.einsum(
        "qhd,khd->hqk", query, keys, preferred_element_type=jnp.float32
    ) / math.sqrt(query.shape[2])
    scores = jnp.where(allowed[None], scores, NEG)
    top = jnp.max(scores, -1, keepdims=True)
    weight = jnp.exp(scores - top)
    weight = (weight / jnp.sum(weight, -1, keepdims=True)).astype(jnp.bfloat16)
    mixed = jnp.einsum("hqk,khd->qhd", weight, values, preferred_element_type=jnp.float32)
    return mixed.astype(jnp.bfloat16)


def normalize(state, modulation):
    scale = lax.rsqrt(jnp.mean(state * state, -1, keepdims=True) + EPS)
    return (state * scale * (1.0 + modulation[2]) + modulation[1]).astype(jnp.bfloat16)


def route(normed, router_weight, expert_ids):
    logits = jnp.dot(normed, router_weight, preferred_element_type=jnp.float32)
    experts = router_weight.shape[1]
    match = expert_ids[:, :, None] == jnp.arange(experts, dtype=jnp.int32)[None, None, :]
    picked = jnp.sum(jnp.where(match, logits[:, None, :], 0.0), -1)
    lifted = jax.nn.sigmoid(picked)
    return lifted / jnp.sum(lifted, -1, keepdims=True)


LANES = 128
SLOT = 16
COLS = 2
CHUNKS = 4
PIECES = 2
VMEM_BYTES = 66 * 1000 * 1000
MESH = pl.DeviceIdType.MESH


def choose(index, table):
    value = jnp.int32(table[0])
    for i in range(1, len(table)):
        value = jnp.where(index == i, table[i], value)
    return value


def line_order(lines, nearest):
    rows = []
    for z in range(lines):
        lower = z < lines - 1 - z
        others = [line for line in range(lines) if line != z]
        sign = 1 if nearest else -1
        rows.append(sorted(others, key=lambda line: (sign * abs(line - z), (line > z) == lower)))
    return [[rows[z][j] for z in range(lines)] for j in range(lines - 1)]


def expert_kernel(
    devices, weight_copies,
    normed, meta, state, modulation, wide,
    out,
    tok, got_packed, got_rows, got_sum, disp, gu, dn, raised, hid_own, hid_other,
    got_meta, pick, gated, squeeze, grow, acc,
    meta_s, meta_r, z_s, z_r, x_s, x_r, core_s, core_r, hid_s, hid_r, rx_s, rx_r, rz_s, rz_r,
):
    me = lax.axis_index("dev")
    part = lax.axis_index("sub")
    other = 1 - part
    z = me // COLS
    x = me % COLS
    lines = devices // COLS
    count, width = normed.shape
    half = width // 2
    local = raised.shape[0]
    hidden = gu.shape[2]
    both_hidden = 2 * hidden
    slots = local * SLOT
    pack = local * CAP
    rows = devices * SLOT
    chunks, wide_chunk = tok.shape[1], tok.shape[3]

    def remote(src, dst, send, recv, where):
        return pltpu.make_async_remote_copy(
            src_ref=src, dst_ref=dst, send_sem=send, recv_sem=recv,
            device_id=where, device_id_type=MESH,
        )

    above = jnp.minimum(me + COLS, devices - 1)
    below = jnp.maximum(me - COLS, 0)
    x_to = {"dev": z * COLS + (1 - x)}
    core_to = {"sub": other}
    not_top = z < lines - 1
    not_bottom = z > 0
    near_lines = [choose(z, table) for table in line_order(lines, True)]
    far_lines = [choose(z, table) for table in line_order(lines, False)]

    def lanes_of(c):
        return pl.ds(pl.multiple_of(c * wide_chunk, wide_chunk), wide_chunk)

    def own_lanes(c):
        return pl.ds(pl.multiple_of(part * half + c * wide_chunk, wide_chunk), wide_chunk)

    def slot_rows(s):
        return pl.ds(pl.multiple_of(s * SLOT, SLOT), SLOT)

    def meta_copy(line):
        return remote(
            meta.at[pl.ds(pl.multiple_of(line * COLS * local, COLS * local), COLS * local)],
            got_meta.at[z], meta_s.at[line], meta_r.at[z], {"dev": line * COLS + x},
        )

    def meta_arrival(line):
        return remote(got_meta.at[line], got_meta.at[line], meta_s.at[line], meta_r.at[line], x_to)

    def z_copy(line, c, way, src=None):
        dst = tok.at[line, c]
        where = {"dev": jnp.where(way == 0, above, below)}
        return remote(
            dst if src is None else src, dst, z_s.at[line, c, way], z_r.at[line, c], where
        )

    def packed_out(line, c):
        return wide.at[line, pl.ds(slots, pack), lanes_of(c)]

    def x_copy(line, c):
        return remote(
            packed_out(line, c), got_packed.at[line, c], x_s.at[line, c], x_r.at[line, c], x_to
        )

    def core_copy(which, s, c):
        place = disp.at[which, c, :, slot_rows(s), :]
        return remote(place, place, core_s.at[s, c], core_r.at[s, c], core_to)

    def own_send(c):
        src = normed.at[:, own_lanes(c)]

        @pl.when(not_top)
        def _():
            z_copy(z, c, 0, src).start()

        @pl.when(not_bottom)
        def _():
            z_copy(z, c, 1, src).start()

    own_send(0)
    for line in near_lines:
        meta_copy(line).start()

    before = (
        lax.broadcasted_iota(jnp.int32, (count, count), 0)
        < lax.broadcasted_iota(jnp.int32, (count, count), 1)
    ).astype(jnp.float32).astype(jnp.bfloat16)
    place = lax.broadcasted_iota(jnp.int32, (local, SLOT, count), 1).astype(jnp.float32)

    def routing(line, ours, theirs):
        for first, gate in ((True, ours), (False, theirs)):
            chosen = jnp.where(gate > 0.0, 1.0, 0.0)
            rank = jnp.dot(chosen.astype(jnp.bfloat16), before, preferred_element_type=jnp.float32)
            rank = jnp.where(gate > 0.0, rank, -1.0)
            hit = jnp.broadcast_to(rank[:, None, :], place.shape) == place
            one = jnp.where(hit, 1.0, 0.0).reshape(slots, count).astype(jnp.bfloat16)
            value = jnp.where(hit, jnp.broadcast_to(gate[:, None, :], place.shape), 0.0)
            value = value.reshape(slots, count).astype(jnp.bfloat16)
            if first:
                pick[line, :slots] = one
                gated[line, :slots] = value
            else:
                pick[line, slots:] = jnp.dot(
                    squeeze[...], one, preferred_element_type=jnp.float32
                ).astype(jnp.bfloat16)
                gated[line, slots:] = jnp.dot(
                    squeeze[...], value, preferred_element_type=jnp.float32
                ).astype(jnp.bfloat16)

    def expert_rows(base, column):
        return pl.ds(pl.multiple_of(base + column * local, local), local)

    def spread(line, c, block):
        moved = jnp.dot(pick[line], block, preferred_element_type=jnp.float32).astype(jnp.bfloat16)
        s = line * COLS + x
        wide[line, slots:slots + pack, lanes_of(c)] = moved[slots:]
        x_copy(line, c).start()
        disp[part, c, :, slot_rows(s), :] = moved[:slots].reshape(local, SLOT, wide_chunk)
        core_copy(part, s, c).start()

    def own_step(c):
        spread(z, c, normed[:, own_lanes(c)])

    def line_step(line, c):
        low = line < z

        @pl.when(c == 0)
        def _():
            meta_arrival(line).wait_recv()
            routing(
                line, got_meta[line, expert_rows(0, x)], got_meta[line, expert_rows(0, 1 - x)]
            )

        way = jnp.where(low, 0, 1)
        z_copy(line, c, way).wait_recv()

        @pl.when(jnp.where(low, not_top, not_bottom))
        def _():
            z_copy(line, c, way).start()

        spread(line, c, tok[line, c])

    def x_step(line, c):
        x_copy(line, c).wait_recv()
        s = line * COLS + (1 - x)
        disp[part, c, :, slot_rows(s), :] = jnp.dot(
            grow[...], got_packed[line, c], preferred_element_type=jnp.float32
        ).astype(jnp.bfloat16).reshape(local, SLOT, wide_chunk)
        core_copy(part, s, c).start()

    def across_rows(left, right):
        return lax.dot_general(
            left, right, (((1,), (1,)), ((), ())), preferred_element_type=jnp.float32
        )

    def raise_part(e, c):
        total = raised[e]
        for side in range(2):
            lanes = pl.ds(pl.multiple_of(side * half + c * wide_chunk, wide_chunk), wide_chunk)
            weight = jnp.concatenate(
                [gu[2 * e, 0, :, lanes], gu[2 * e + 1, 0, :, lanes],
                 gu[2 * e, 1, :, lanes], gu[2 * e + 1, 1, :, lanes]], axis=0
            )
            total = total + across_rows(disp[side, c, e], weight)
        return total

    def hid_copy(e):
        return remote(hid_own.at[e], hid_other.at[e], hid_s.at[e], hid_r.at[e], core_to)

    def arrived(c):
        for s in range(devices):
            core_copy(other, s, c).wait_recv()

    routing(
        z, meta[expert_rows(z * COLS * local, x)], meta[expert_rows(z * COLS * local, 1 - x)]
    )
    own_step(0)

    def weight_wait(h, carry):
        for copy in weight_copies(h):
            copy.wait()
        return carry

    lax.fori_loop(0, 2 * local, weight_wait, 0)

    def step(t, carry):
        ready = t - lines

        def raise_some(i):
            first, last = i * local // (2 * lines), (i + 1) * local // (2 * lines)

            @pl.when(ready >= 0)
            def _():
                if i == 0:
                    arrived(ready)
                for e in range(first, last):
                    raised[e] = raise_part(e, ready)

        @pl.when(t + 1 < chunks)
        def _():
            own_send(t + 1)
            own_step(t + 1)

        raise_some(0)
        for j, line in enumerate(near_lines):
            c = t - jnp.abs(line - z) + 1

            @pl.when((c >= 0) & (c < chunks))
            def _():
                line_step(line, c)

            raise_some(1 + j)

        @pl.when(t < chunks)
        def _():
            x_step(z, t)

        raise_some(lines)
        for j, line in enumerate(near_lines):
            c = t - jnp.abs(line - z)

            @pl.when((c >= 0) & (c < chunks))
            def _():
                x_step(line, c)

            raise_some(lines + 1 + j)
        return carry

    lax.fori_loop(0, chunks + lines - 1, step, 0)
    arrived(chunks - 1)

    def last_raise(e, carry):
        total = raise_part(e, chunks - 1)
        gate = total[:, :both_hidden]
        hid_own[e] = (gate * jax.nn.sigmoid(gate) * total[:, both_hidden:]).astype(jnp.bfloat16)
        hid_copy(e).start()
        return carry

    lax.fori_loop(0, local, last_raise, 0)

    group = 2 * wide_chunk

    def lower(g):
        lanes = slice(g * group, (g + 1) * group)

        def one(e, carry):
            if g == 0:
                hid_copy(e).wait_recv()
            mine = pl.ds(pl.multiple_of(part * hidden, SLOT), hidden)
            theirs = pl.ds(pl.multiple_of(other * hidden, SLOT), hidden)
            left = jnp.concatenate([hid_own[e], hid_other[e]], axis=1)
            right = jnp.concatenate(
                [dn[2 * e, mine, lanes], dn[2 * e + 1, mine, lanes],
                 dn[2 * e, theirs, lanes], dn[2 * e + 1, theirs, lanes]], axis=0
            )
            wide[e, :rows, lanes] = jnp.dot(
                left, right, preferred_element_type=jnp.float32
            ).astype(jnp.bfloat16)
            return carry

        lax.fori_loop(0, local, one, 0)

    def result_rows(s, q):
        return wide[:local, slot_rows(s), lanes_of(q)].reshape(slots, wide_chunk)

    def rx_copy(line, q):
        return remote(
            wide.at[lines + line, pl.ds(slots, pack), lanes_of(q)], got_rows.at[line, q],
            rx_s.at[line, q], rx_r.at[line, q], x_to,
        )

    def rz_copy(line, q, way):
        where = {"dev": jnp.where(way == 0, above, below)}
        return remote(
            tok.at[line, q], got_sum.at[way, line, q],
            rz_s.at[line, q], rz_r.at[way, line, q], where,
        )

    def give(line, q):
        packed = jnp.dot(
            squeeze[...], result_rows(line * COLS + (1 - x), q), preferred_element_type=jnp.float32
        )
        wide[lines + line, slots:slots + pack, lanes_of(q)] = packed.astype(jnp.bfloat16)
        rx_copy(line, q).start()

    def gather_here(line, q):
        rx_copy(line, q).wait_recv()
        pieces = jnp.concatenate([result_rows(line * COLS + x, q), got_rows[line, q]], axis=0)
        acc[...] = lax.dot_general(
            gated[line], pieces, (((0,), (0,)), ((), ())), preferred_element_type=jnp.float32
        )

    def add_line(line, q, way):
        rz_copy(line, q, way).wait_recv()
        acc[...] += got_sum[way, line, q].astype(jnp.float32)

    def pass_on(line, q):
        gather_here(line, q)
        way = jnp.where(line > z, 0, 1)

        @pl.when(jnp.where(line > z, not_bottom, not_top))
        def _():
            add_line(line, q, way)

        tok[line, q] = acc[...].astype(jnp.bfloat16)
        rz_copy(line, q, way).start()

    for g in range(half // group):
        lower(g)
        for q in range(2 * g, 2 * g + 2):
            give(far_lines[0], q)
    for line in far_lines[1:] + [z]:
        lax.fori_loop(0, chunks, lambda q, carry, line=line: (give(line, q), carry)[1], 0)
    for line in near_lines:
        low = line < z

        @pl.when(jnp.where(low, not_top, not_bottom))
        def _():
            for c in range(chunks):
                z_copy(line, c, jnp.where(low, 0, 1)).wait_send()

    for line in far_lines:
        lax.fori_loop(0, chunks, lambda q, carry, line=line: (pass_on(line, q), carry)[1], 0)
    for q in range(chunks):
        gather_here(z, q)

        @pl.when(not_bottom)
        def _():
            add_line(z, q, 0)

        @pl.when(not_top)
        def _():
            add_line(z, q, 1)

        own = own_lanes(q)
        lanes = slice(q * wide_chunk, (q + 1) * wide_chunk)
        out[:, lanes] = (
            state[:, own] + (1.0 + modulation[3:4, own]) * acc[...]
        ).astype(out.dtype)

    for c in range(chunks):

        @pl.when(not_top)
        def _():
            z_copy(z, c, 0, normed.at[:, own_lanes(c)]).wait_send()

        @pl.when(not_bottom)
        def _():
            z_copy(z, c, 1, normed.at[:, own_lanes(c)]).wait_send()

        for line in near_lines:
            rz_copy(line, c, jnp.where(line > z, 0, 1)).wait_send()
        for line in range(lines):
            x_copy(line, c).wait_send()
            rx_copy(line, c).wait_send()
        for s in range(devices):
            core_copy(part, s, c).wait_send()
    for line in near_lines:
        meta_copy(line).wait_send()

    def hid_drain(e, carry):
        hid_copy(e).wait_send()
        return carry

    lax.fori_loop(0, local, hid_drain, 0)


def front_kernel(
    devices, start_weights,
    sources, held, own_sem,
    normed, state, meta,
    near, relayed, column, mixed, mixed_in, mine_out, their_out, sent_back, got_back, their_back,
    near_s, near_r, far_s, far_r, way_s, way_r, side_s, wz_s, wz_r, wy_s, wy_r, mix_s, mix_r,
    sum_s, sum_r, back_s, back_r, share_s, share_r,
):
    packed_hbm, weight_hbm = sources[1], sources[2]
    tokens, packed, modulation, router, ids = held
    me = lax.axis_index("dev")
    part = lax.axis_index("sub")
    group = lax.axis_index("groups")
    z = me // COLS
    x = me % COLS
    lines = devices // COLS
    count, width = tokens.shape
    shard = column.shape[1]
    share = shard // 2
    piece = share // PIECES
    pairs, pair = near.shape[1], near.shape[4]
    targets = (tokens, packed, column.at[z], modulation, router, ids)

    def own_copy(i):
        return pltpu.make_async_copy(sources[i], targets[i], own_sem.at[i])

    for i in (1, 2, 0, 3, 4, 5):
        own_copy(i).start()
    not_top = z < lines - 1
    not_bottom = z > 0
    above = jnp.minimum(me + COLS, devices - 1)
    below = jnp.maximum(me - COLS, 0)
    x_to = {"dev": z * COLS + (1 - x)}
    y_to = {"groups": 1 - group}
    core_to = {"sub": 1 - part}
    near_lines = [choose(z, table) for table in line_order(lines, True)]

    barrier = pltpu.get_barrier_semaphore()

    def greet(where):
        pl.semaphore_signal(barrier, inc=1, device_id=where, device_id_type=MESH)

    for where in (x_to, y_to, core_to):
        greet(where)
    for line in near_lines:
        greet({"dev": line * COLS + x})
    pl.semaphore_wait(barrier, lines + 2)

    def remote(src, dst, send, recv, where):
        return pltpu.make_async_remote_copy(
            src_ref=src, dst_ref=dst, send_sem=send, recv_sem=recv,
            device_id=where, device_id_type=MESH,
        )

    def near_copy(k):
        src = packed_hbm.at[1:3, :, pl.ds(k * pair, pair)]
        return remote(src, near.at[x, k], near_s.at[k], near_r.at[k], x_to)

    def far_copy(k):
        where = {"dev": jnp.where(x == 0, above, below)}
        return remote(near.at[1 - x, k], near.at[x, k], far_s.at[k], far_r.at[k], where)

    give_far = ((x == 0) & not_top) | ((x == 1) & not_bottom)
    have_far = ((x == 0) & not_bottom) | ((x == 1) & not_top)

    early = pairs // 2
    give_side = ((x == 1) & not_top) | ((x == 0) & not_bottom)
    have_side = ((x == 1) & not_bottom) | ((x == 0) & not_top)

    def way_copy(k):
        src = packed_hbm.at[1:3, :, pl.ds(k * pair, pair)]
        where = {"dev": jnp.where(x == 1, above, below)}
        return remote(src, relayed.at[k - early], way_s.at[k - early], way_r.at[k - early], where)

    def side_copy(k):
        return remote(
            relayed.at[k - early], near.at[1 - x, k], side_s.at[k - early], far_r.at[k], x_to
        )

    def piece_rows(which, i):
        return pl.ds(pl.multiple_of(which * share + i * piece, SLOT), piece)

    def wz_copy(line, i, way, src=None):
        dst = column.at[line, piece_rows(group, i)]
        where = {"dev": jnp.where(way == 0, above, below)}
        return remote(
            dst if src is None else src, dst, wz_s.at[line, i, way], wz_r.at[line, i], where
        )

    def own_piece(i):
        return weight_hbm.at[piece_rows(group, i)]

    def wy_copy(line, i, which):
        block = column.at[line, piece_rows(which, i)]
        return remote(block, block, wy_s.at[line, i], wy_r.at[line, i], y_to)

    for k in range(pairs):
        near_copy(k).start()
    for i in range(PIECES):

        @pl.when(not_top)
        def _():
            wz_copy(z, i, 0, own_piece(i)).start()

        @pl.when(not_bottom)
        def _():
            wz_copy(z, i, 1, own_piece(i)).start()

    @pl.when(give_side)
    def _():
        for k in range(early, pairs):
            way_copy(k).start()

    start_weights()

    @pl.when(jnp.logical_not(have_far))
    def _():
        near[x] = jnp.zeros_like(near[x])

    def way_of(line):
        return jnp.where(line < z, 0, 1)

    def more(line):
        return jnp.where(line < z, not_top, not_bottom)

    def busy(line):
        return jnp.where(line < z, x == 0, x == 1)

    def distance(line):
        return jnp.abs(line - z)

    def take(line, onward, pieces=range(PIECES)):
        for i in pieces:
            wz_copy(line, i, way_of(line)).wait_recv()

            @pl.when(onward)
            def _():
                wz_copy(line, i, way_of(line)).start()

            wy_copy(line, i, group).start()

    def take_next(only_busy, pieces):
        for line in near_lines:

            @pl.when((distance(line) == 1) & (busy(line) if only_busy else jnp.logical_not(busy(line))))
            def _():
                take(line, more(line), pieces)

    take_next(True, range(1))
    take_next(False, range(1))
    for k in range(early):
        near_copy(k).wait_recv()

        @pl.when(give_far)
        def _():
            far_copy(k).start()

    take_next(True, range(1, PIECES))
    take_next(False, range(1, PIECES))

    @pl.when(have_side)
    def _():
        for k in range(early, pairs):
            way_copy(k).wait_recv()
            side_copy(k).start()

    for k in range(early, pairs):
        near_copy(k).wait_recv()
    for i in range(6):
        own_copy(i).wait()

    row = lax.broadcasted_iota(jnp.int32, (count, count), 0)
    col = lax.broadcasted_iota(jnp.int32, (count, count), 1)
    see_before = (col >= row) & (me > 0)
    see_after = (col <= row) & (me < devices - 1)

    def mix_copy(k):
        lanes = pl.ds(k * pair, pair)
        return remote(
            mixed.at[:, lanes], mixed_in.at[:, lanes], mix_s.at[k], mix_r.at[k], x_to
        )

    for k in range(pairs):

        @pl.when(have_far)
        def _():
            far_copy(k).wait_recv()

        for h in range(pair // HEAD):
            lanes = slice(k * pair + h * HEAD, k * pair + (h + 1) * HEAD)
            inner = slice(h * HEAD, (h + 1) * HEAD)
            query = packed[0, :, lanes]

            def score(keys):
                return lax.dot_general(
                    query, keys, (((1,), (1,)), ((), ())), preferred_element_type=jnp.float32
                ) / math.sqrt(HEAD)

            scores = jnp.concatenate(
                [
                    jnp.where(see_before, score(near[0, k, 0, :, inner]), NEG),
                    score(packed[1, :, lanes]),
                    jnp.where(see_after, score(near[1, k, 0, :, inner]), NEG),
                ],
                axis=1,
            )
            top = jnp.max(scores, -1, keepdims=True)
            weight = jnp.exp(scores - top)
            weight = (weight / jnp.sum(weight, -1, keepdims=True)).astype(jnp.bfloat16)
            values = jnp.concatenate(
                [near[0, k, 1, :, inner], packed[2, :, lanes], near[1, k, 1, :, inner]], axis=0
            )
            mixed[:, lanes] = jnp.dot(
                weight, values, preferred_element_type=jnp.float32
            ).astype(jnp.bfloat16)
        mix_copy(k).start()
        if k + 1 == early:
            for line in near_lines:

                @pl.when(distance(line) == 2)
                def _():
                    take(line, more(line))

    for k in range(pairs):
        mix_copy(k).wait_recv()

    def place_of(which):
        return group if which == 0 else 1 - group

    def sum_copy(line, which):
        place = place_of(which)
        return remote(
            mine_out.at[line, place], their_out.at[line, place],
            sum_s.at[line, which], sum_r.at[line, which], core_to,
        )

    def back_copy(line, which):
        place = place_of(which)
        return remote(
            sent_back.at[line, place], got_back.at[line, place],
            back_s.at[line, which], back_r.at[line, which], x_to,
        )

    def share_copy(line, which):
        place = place_of(which)
        return remote(
            got_back.at[line, place], their_back.at[line, place],
            share_s.at[line, which], share_r.at[line, which], core_to,
        )

    def project(line, which):
        place = place_of(which)
        block = column[line, pl.ds(pl.multiple_of(place * share, SLOT), share), :]
        both = jnp.concatenate([mixed_in[...], mixed[...]], axis=0)
        product = lax.dot_general(
            both, block, (((1,), (1,)), ((), ())), preferred_element_type=jnp.float32
        )
        sent_back[line, place] = product[:count].astype(jnp.bfloat16)
        back_copy(line, which).start()
        mine_out[line, place] = product[count:]
        sum_copy(line, which).start()

    steps = [(line, which) for line in [z] + near_lines for which in range(2)]

    def relay(i):
        back_copy(*steps[i]).wait_recv()
        share_copy(*steps[i]).start()

    for i, (line, which) in enumerate(steps):
        if which == 0 and i == 4:
            for late in near_lines[1:]:

                @pl.when(distance(late) > 2)
                def _():
                    take(late, more(late))
        if which == 1 and i > 1:
            if i == len(steps) - 1:
                for n in range(i - 1):
                    relay(n)
            for n in range(PIECES):
                wy_copy(line, n, 1 - group).wait_recv()
        project(line, which)
    relay(len(steps) - 2)
    relay(len(steps) - 1)

    square = jnp.zeros((count, 1), jnp.float32)
    for line, which in steps:
        place = place_of(which)
        sum_copy(line, which).wait_recv()
        share_copy(line, which).wait_recv()
        for column_of, total in (
            (x, mine_out[line, place] + their_out[line, place]),
            (
                1 - x,
                got_back[line, place].astype(jnp.float32)
                + their_back[line, place].astype(jnp.float32),
            ),
        ):
            start = (line * COLS + column_of) * shard + place * share
            lanes = pl.ds(pl.multiple_of(start, LANES), share)
            value = tokens[:, lanes].astype(jnp.float32) + (1.0 + modulation[0:1, lanes]) * total
            state[:, lanes] = value
            square = square + jnp.sum(value * value, -1, keepdims=True)
    scale = lax.rsqrt(square / width + EPS)
    for s in range(devices):
        lanes = slice(s * shard, (s + 1) * shard)
        normed[:, lanes] = (
            state[:, lanes] * scale * (1.0 + modulation[2:3, lanes]) + modulation[1:2, lanes]
        ).astype(jnp.bfloat16)
    logits = lax.dot_general(
        router[...], normed[...], (((1,), (1,)), ((), ())), preferred_element_type=jnp.float32
    )
    name = lax.broadcasted_iota(jnp.int32, logits.shape, 0)
    named = name == ids[0:1]
    for k in range(1, ids.shape[0]):
        named = named | (name == ids[k:k + 1])
    lifted = jnp.where(named, jax.nn.sigmoid(logits), 0.0)
    meta[...] = lifted / jnp.sum(lifted, 0, keepdims=True)

    for k in range(pairs):
        near_copy(k).wait_send()
        mix_copy(k).wait_send()

        if k < early:

            @pl.when(give_far)
            def _():
                far_copy(k).wait_send()
        else:

            @pl.when(give_side)
            def _():
                way_copy(k).wait_send()

            @pl.when(have_side)
            def _():
                side_copy(k).wait_send()

    for i in range(PIECES):

        @pl.when(not_top)
        def _():
            wz_copy(z, i, 0, own_piece(i)).wait_send()

        @pl.when(not_bottom)
        def _():
            wz_copy(z, i, 1, own_piece(i)).wait_send()

        for line in near_lines:

            @pl.when(more(line))
            def _():
                wz_copy(line, i, way_of(line)).wait_send()

            wy_copy(line, i, group).wait_send()
    for line, which in steps:
        sum_copy(line, which).wait_send()
        back_copy(line, which).wait_send()
        share_copy(line, which).wait_send()


def block_kernel(devices, *refs):
    sources, gate_up, down, out = refs[:6], refs[6], refs[7], refs[8]
    held, normed, state, meta, wide = refs[9:14], refs[14], refs[15], refs[16], refs[17]
    front_buffers, expert_buffers = refs[18:28], refs[28:44]
    own_sem, gu_sem, dn_sem = refs[44:47]
    front_sems, expert_sems = refs[47:66], refs[66:]
    gu, dn, raised = expert_buffers[5:8]
    squeeze, grow = expert_buffers[13:15]
    halves = gate_up.shape[0]

    def weight_copies(h):
        return (
            pltpu.make_async_copy(gate_up.at[h], gu.at[h], gu_sem.at[h]),
            pltpu.make_async_copy(down.at[h], dn.at[h], dn_sem.at[h]),
        )

    def start_weights():
        def one(h, carry):
            for copy in weight_copies(h):
                copy.start()
            return carry

        lax.fori_loop(0, halves, one, 0)
        raised[...] = jnp.zeros_like(raised)
        for ref, axis in ((squeeze, 0), (grow, 1)):
            packed = lax.broadcasted_iota(jnp.int32, ref.shape, axis)
            slot = lax.broadcasted_iota(jnp.int32, ref.shape, 1 - axis)
            inner = slot & (SLOT - 1)
            same = (packed == (slot - inner) // SLOT * CAP + inner) & (inner < CAP)
            ref[...] = jnp.where(same, 1.0, 0.0).astype(jnp.bfloat16)

    front_kernel(
        devices, start_weights, sources, held, own_sem, normed, state, meta,
        *front_buffers, *front_sems,
    )
    expert_kernel(
        devices, weight_copies, normed, meta, state, held[2], wide, out,
        *expert_buffers, *expert_sems,
    )


def block_call(
    tokens, query_key_value, out_weight, modulation, router_weight, expert_ids,
    gate_up_weight, down_weight,
):
    devices = lax.axis_size("dev")
    count, width = tokens.shape
    half = down_weight.shape[2]
    halves = gate_up_weight.shape[0]
    local = halves // 2
    gate_up_weight = gate_up_weight.swapaxes(2, 3)
    hidden = gate_up_weight.shape[2]
    lines = devices // COLS
    rows = devices * SLOT
    slots, pack = local * SLOT, local * CAP
    part = half // CHUNKS
    shard = out_weight.shape[0]
    own = (
        tokens, query_key_value.transpose(1, 0, 2), out_weight, modulation,
        router_weight.T, expert_ids.T,
    )
    hbm = pl.BlockSpec(memory_space=pl.ANY)
    dma = pltpu.SemaphoreType.DMA
    return pl.pallas_call(
        functools.partial(block_kernel, devices),
        out_shape=jax.ShapeDtypeStruct((count, half), jnp.bfloat16),
        in_specs=[hbm] * 8,
        out_specs=pl.BlockSpec(memory_space=pltpu.VMEM),
        scratch_shapes=[
            *[pltpu.VMEM(own[i].shape, own[i].dtype) for i in (0, 1, 3, 4, 5)],
            pltpu.VMEM((count, width), jnp.bfloat16),
            pltpu.VMEM((count, width), jnp.float32),
            pltpu.VMEM((router_weight.shape[1], count), jnp.float32),
            pltpu.VMEM((devices, slots + pack, half), jnp.bfloat16),
            pltpu.VMEM((2, CHUNKS, 2, count, part), jnp.bfloat16),
            pltpu.VMEM((CHUNKS // 2, 2, count, part), jnp.bfloat16),
            pltpu.VMEM((lines, shard, half), jnp.bfloat16),
            pltpu.VMEM((count, half), jnp.bfloat16),
            pltpu.VMEM((count, half), jnp.bfloat16),
            pltpu.VMEM((lines, 2, count, shard // 2), jnp.float32),
            pltpu.VMEM((lines, 2, count, shard // 2), jnp.float32),
            pltpu.VMEM((lines, 2, count, shard // 2), jnp.bfloat16),
            pltpu.VMEM((lines, 2, count, shard // 2), jnp.bfloat16),
            pltpu.VMEM((lines, 2, count, shard // 2), jnp.bfloat16),
            pltpu.VMEM((lines, CHUNKS, count, part), jnp.bfloat16),
            pltpu.VMEM((lines, CHUNKS, pack, part), jnp.bfloat16),
            pltpu.VMEM((lines, CHUNKS, pack, part), jnp.bfloat16),
            pltpu.VMEM((2, lines, CHUNKS, count, part), jnp.bfloat16),
            pltpu.VMEM((2, CHUNKS, local, rows, part), jnp.bfloat16),
            pltpu.VMEM(gate_up_weight.shape, jnp.bfloat16),
            pltpu.VMEM(down_weight.shape, jnp.bfloat16),
            pltpu.VMEM((local, rows, 4 * hidden), jnp.float32),
            pltpu.VMEM((local, rows, 2 * hidden), jnp.bfloat16),
            pltpu.VMEM((local, rows, 2 * hidden), jnp.bfloat16),
            pltpu.VMEM((lines, COLS * local, count), jnp.float32),
            pltpu.VMEM((lines, slots + pack, count), jnp.bfloat16),
            pltpu.VMEM((lines, slots + pack, count), jnp.bfloat16),
            pltpu.VMEM((pack, slots), jnp.bfloat16),
            pltpu.VMEM((slots, pack), jnp.bfloat16),
            pltpu.VMEM((count, part), jnp.float32),
            dma((6,)), dma((halves,)), dma((halves,)),
            dma((CHUNKS,)), dma((CHUNKS,)), dma((CHUNKS,)), dma((CHUNKS,)),
            dma((CHUNKS // 2,)), dma((CHUNKS // 2,)), dma((CHUNKS // 2,)),
            dma((lines, PIECES, 2)), dma((lines, PIECES)),
            dma((lines, PIECES)), dma((lines, PIECES)), dma((CHUNKS,)), dma((CHUNKS,)),
            dma((lines, 2)), dma((lines, 2)), dma((lines, 2)), dma((lines, 2)),
            dma((lines, 2)), dma((lines, 2)),
            dma((lines,)), dma((lines,)),
            dma((lines, CHUNKS, 2)), dma((lines, CHUNKS)),
            dma((lines, CHUNKS)), dma((lines, CHUNKS)),
            dma((devices, CHUNKS)), dma((devices, CHUNKS)),
            dma((local,)), dma((local,)),
            dma((lines, CHUNKS)), dma((lines, CHUNKS)),
            dma((lines, CHUNKS)), dma((2, lines, CHUNKS)),
        ],
        compiler_params=pltpu.CompilerParams(
            collective_id=1, has_side_effects=True, vmem_limit_bytes=VMEM_BYTES
        ),
    )(*own, gate_up_weight, down_weight)


def body(
    tokens,
    query_key_value,
    out_weight,
    modulation,
    router_weight,
    expert_ids,
    gate_up_weight,
    down_weight,
):
    count = tokens.shape[0]
    width = tokens.shape[1]
    parts = lax.axis_size("sub")
    part = lax.axis_index("sub")
    position = lax.axis_index("dev")
    devices = lax.axis_size("dev")
    total = count * devices
    local_width = query_key_value.shape[2]
    weight_bytes = 2 * (gate_up_weight.size + down_weight.size)
    token_bytes = 12 * devices * count * width
    fits = weight_bytes + token_bytes < VMEM_BYTES and CAP <= SLOT
    paired = parts == 2 and lax.axis_size("groups") == 2 and devices % COLS == 0
    experts_here = gate_up_weight.shape[0] // 2
    tiled = out_weight.shape[0] % (2 * LANES) == 0 and count == LANES
    tiled = tiled and down_weight.shape[2] // CHUNKS % HEAD == 0 and devices // COLS > 2
    tiled = tiled and down_weight.shape[2] % (2 * CHUNKS * LANES) == 0 and experts_here == devices
    tiled = tiled and SLOT * devices == LANES
    tiled = tiled and gate_up_weight.shape[3] % 64 == 0
    if fits and paired and tiled:
        return block_call(
            tokens, query_key_value, out_weight, modulation, router_weight, expert_ids,
            gate_up_weight, down_weight,
        )
    heads_here = local_width // HEAD
    query = query_key_value[:, 0].reshape(count, heads_here, HEAD)
    pair = query_key_value[:, 1:]
    near = extended(pair, (("dev", 0),), count)
    keys = near[:, 0].reshape(3 * count, heads_here, HEAD)
    values = near[:, 1].reshape(3 * count, heads_here, HEAD)
    mixed = window_attention(query, keys, values, position, total).reshape(count, local_width)
    partial_proj = lax.dot_general(
        mixed,
        lax.all_gather(out_weight, "dev", axis=0, tiled=True),
        (((1,), (1,)), ((), ())),
        preferred_element_type=jnp.float32,
    )
    proj = lax.psum(partial_proj, "sub")
    state = tokens.astype(jnp.float32) + (1.0 + modulation[0]) * proj
    normed = normalize(state, modulation)
    gates = route(normed, router_weight, expert_ids)
    experts = router_weight.shape[1]
    topk = expert_ids.shape[1]
    flat = expert_ids.reshape(-1)
    picks = flat.shape[0]
    onehot = (flat[:, None] == jnp.arange(experts, dtype=jnp.int32)[None, :]).astype(jnp.int32)
    rank = jnp.sum((jnp.cumsum(onehot, 0) - 1) * onehot, 1)
    target = flat * CAP + rank
    hit = target[None, :] == jnp.arange(experts * CAP, dtype=jnp.int32)[:, None]
    filled = jnp.any(hit, 1)
    anchor = jnp.sum(jnp.where(hit, jnp.arange(picks, dtype=jnp.int32)[None, :], 0), 1) // topk
    slice_width = width // parts
    sent = lax.dynamic_slice_in_dim(normed, part * slice_width, slice_width, 1)
    sent_width = sent.shape[1]
    rows_out = jnp.where(filled[:, None], sent[anchor], jnp.zeros((), jnp.bfloat16))
    halves_here = gate_up_weight.shape[0]
    doubled = jnp.broadcast_to(
        rows_out.reshape(experts, 1, CAP, sent_width), (experts, 2, CAP, sent_width)
    )
    outgoing = doubled.reshape(devices, halves_here, CAP, sent_width)
    up_form = "sxcd,xgdf->sxcgf"
    down_form = "sxcf,xfd->sxcd"
    incoming = lax.all_to_all(outgoing, "dev", split_axis=0, concat_axis=0, tiled=True)
    both = jnp.einsum(
        up_form,
        lax.all_gather(incoming, "sub", axis=3, tiled=True),
        gate_up_weight,
        preferred_element_type=jnp.float32,
    )
    hidden = (jax.nn.silu(both[..., 0, :]) * both[..., 1, :]).astype(jnp.bfloat16)
    gathered = lax.all_gather(hidden, "sub", axis=hidden.ndim - 1, tiled=True)
    result = jnp.einsum(down_form, gathered, down_weight, preferred_element_type=jnp.float32)
    returned = lax.all_to_all(
        result.astype(jnp.bfloat16), "dev", split_axis=0, concat_axis=0, tiled=True
    )
    own_width = returned.shape[-1]
    arranged = returned.reshape(experts, 2, CAP, own_width)
    answers = arranged[flat, :, rank, :].reshape(count, topk, 2, own_width).astype(jnp.float32)
    combined = answers[:, :, 0] + answers[:, :, 1]
    routed = jnp.einsum("tk,tkd->td", gates, combined)
    own = lax.dynamic_slice_in_dim(state, part * slice_width, slice_width, 1)
    lift = lax.dynamic_slice_in_dim(modulation[3], part * slice_width, slice_width, 0)
    return (own + (1.0 + lift) * routed).astype(jnp.bfloat16)


def solution(mesh):
    return jax.shard_map(
        body,
        mesh=mesh,
        in_specs=(
            P(("groups", "dev"), None),
            P(("groups", "dev"), None, "sub"),
            P("dev", "sub"),
            P("groups", None),
            P(),
            P(("groups", "dev"), None),
            P("dev", None, None, "sub"),
            P("dev", None, "sub"),
        ),
        out_specs=P(("groups", "dev"), "sub"),
        check_vma=False,
    )
```

```python
import functools
import math

import jax
import jax.numpy as jnp
from jax import lax
from jax.experimental import pallas as pl
from jax.experimental.pallas import tpu as pltpu
from jax.sharding import PartitionSpec as P

HEAD = 128
CAP = 12


EPS = 1e-06
NEG = -1e30


def extended(cells, sides, width):
    for axis, dim in sides:
        count = lax.axis_size(axis)
        ends = count - 1
        head = lax.slice_in_dim(cells, 0, width, axis=dim)
        tail = lax.slice_in_dim(cells, cells.shape[dim] - width, cells.shape[dim], axis=dim)
        cells = jnp.concatenate(
            [
                lax.ppermute(tail, axis, [(i, (i + 1) % count) for i in range(ends)]),
                cells,
                lax.ppermute(head, axis, [((i + 1) % count, i) for i in range(ends)]),
            ],
            axis=dim,
        )
    return cells


def window_attention(query, keys, values, index, total):
    count = query.shape[0]
    rows = jnp.arange(count, dtype=jnp.int32)[:, None]
    cols = jnp.arange(3 * count, dtype=jnp.int32)[None, :] - count
    place = index * count + cols
    allowed = (jnp.abs(cols - rows) <= count) & (place >= 0) & (place < total)
    scores = jnp.einsum(
        "qhd,khd->hqk", query, keys, preferred_element_type=jnp.float32
    ) / math.sqrt(query.shape[2])
    scores = jnp.where(allowed[None], scores, NEG)
    top = jnp.max(scores, -1, keepdims=True)
    weight = jnp.exp(scores - top)
    weight = (weight / jnp.sum(weight, -1, keepdims=True)).astype(jnp.bfloat16)
    mixed = jnp.einsum("hqk,khd->qhd", weight, values, preferred_element_type=jnp.float32)
    return mixed.astype(jnp.bfloat16)


def normalize(state, modulation):
    scale = lax.rsqrt(jnp.mean(state * state, -1, keepdims=True) + EPS)
    return (state * scale * (1.0 + modulation[2]) + modulation[1]).astype(jnp.bfloat16)


def route(normed, router_weight, expert_ids):
    logits = jnp.dot(normed, router_weight, preferred_element_type=jnp.float32)
    experts = router_weight.shape[1]
    match = expert_ids[:, :, None] == jnp.arange(experts, dtype=jnp.int32)[None, None, :]
    picked = jnp.sum(jnp.where(match, logits[:, None, :], 0.0), -1)
    lifted = jax.nn.sigmoid(picked)
    return lifted / jnp.sum(lifted, -1, keepdims=True)


LANES = 128
SLOT = 16
COLS = 2
CHUNKS = 4
PIECES = 2
VMEM_BYTES = 66 * 1000 * 1000
MESH = pl.DeviceIdType.MESH


def choose(index, table):
    value = jnp.int32(table[0])
    for i in range(1, len(table)):
        value = jnp.where(index == i, table[i], value)
    return value


def line_order(lines, nearest, inner=False):
    rows = []
    for z in range(lines):
        lower = (z < lines - 1 - z) != inner
        others = [line for line in range(lines) if line != z]
        sign = 1 if nearest else -1
        rows.append(sorted(others, key=lambda line: (sign * abs(line - z), (line > z) == lower)))
    return [[rows[z][j] for z in range(lines)] for j in range(lines - 1)]


def expert_kernel(
    devices, weight_copies,
    normed, meta, state, modulation, wide,
    out,
    tok, got_packed, got_rows, got_sum, disp, gu, dn, hid_own, hid_other,
    got_meta, pick, gated, squeeze, grow, acc,
    meta_s, meta_r, z_s, z_r, x_s, x_r, core_s, core_r, hid_s, hid_r, rx_s, rx_r, rz_s, rz_r,
):
    me = lax.axis_index("dev")
    part = lax.axis_index("sub")
    other = 1 - part
    z = me // COLS
    x = me % COLS
    lines = devices // COLS
    count, width = normed.shape
    half = width // 2
    local = hid_own.shape[0]
    hidden = gu.shape[2]
    slots = local * SLOT
    pack = local * CAP
    rows = devices * SLOT
    chunks, wide_chunk = tok.shape[1], tok.shape[3]

    def remote(src, dst, send, recv, where):
        return pltpu.make_async_remote_copy(
            src_ref=src, dst_ref=dst, send_sem=send, recv_sem=recv,
            device_id=where, device_id_type=MESH,
        )

    above = jnp.minimum(me + COLS, devices - 1)
    below = jnp.maximum(me - COLS, 0)
    x_to = {"dev": z * COLS + (1 - x)}
    core_to = {"sub": other}
    not_top = z < lines - 1
    not_bottom = z > 0
    near_lines = [choose(z, table) for table in line_order(lines, True, True)]
    far_lines = [choose(z, table) for table in line_order(lines, False)]

    def lanes_of(c):
        return pl.ds(pl.multiple_of(c * wide_chunk, wide_chunk), wide_chunk)

    def own_lanes(c):
        return pl.ds(pl.multiple_of(part * half + c * wide_chunk, wide_chunk), wide_chunk)

    def slot_rows(s):
        return pl.ds(pl.multiple_of(s * SLOT, SLOT), SLOT)

    def meta_copy(line):
        return remote(
            meta.at[pl.ds(pl.multiple_of(line * COLS * local, COLS * local), COLS * local)],
            got_meta.at[z], meta_s.at[line], meta_r.at[z], {"dev": line * COLS + x},
        )

    def meta_arrival(line):
        return remote(got_meta.at[line], got_meta.at[line], meta_s.at[line], meta_r.at[line], x_to)

    def z_copy(line, c, way, src=None):
        dst = tok.at[line, c]
        where = {"dev": jnp.where(way == 0, above, below)}
        return remote(
            dst if src is None else src, dst, z_s.at[line, c, way], z_r.at[line, c], where
        )

    def packed_out(line, c):
        return wide.at[line, pl.ds(slots, pack), lanes_of(c)]

    def x_copy(line, c):
        return remote(
            packed_out(line, c), got_packed.at[line, c], x_s.at[line, c], x_r.at[line, c], x_to
        )

    def core_copy(which, s, c):
        place = disp.at[which, c, :, slot_rows(s), :]
        return remote(place, place, core_s.at[s, c], core_r.at[s, c], core_to)

    def own_send(c):
        src = normed.at[:, own_lanes(c)]

        @pl.when(not_top)
        def _():
            z_copy(z, c, 0, src).start()

        @pl.when(not_bottom)
        def _():
            z_copy(z, c, 1, src).start()

    own_send(0)
    for line in near_lines:
        meta_copy(line).start()

    before = (
        lax.broadcasted_iota(jnp.int32, (count, count), 0)
        < lax.broadcasted_iota(jnp.int32, (count, count), 1)
    ).astype(jnp.float32).astype(jnp.bfloat16)
    place = lax.broadcasted_iota(jnp.int32, (local, SLOT, count), 1).astype(jnp.float32)

    def routing(line, ours, theirs):
        for first, gate in ((True, ours), (False, theirs)):
            chosen = jnp.where(gate > 0.0, 1.0, 0.0)
            rank = jnp.dot(chosen.astype(jnp.bfloat16), before, preferred_element_type=jnp.float32)
            rank = jnp.where(gate > 0.0, rank, -1.0)
            hit = jnp.broadcast_to(rank[:, None, :], place.shape) == place
            one = jnp.where(hit, 1.0, 0.0).reshape(slots, count).astype(jnp.bfloat16)
            value = jnp.where(hit, jnp.broadcast_to(gate[:, None, :], place.shape), 0.0)
            value = value.reshape(slots, count).astype(jnp.bfloat16)
            if first:
                pick[line, :slots] = one
                gated[line, :slots] = value
            else:
                pick[line, slots:] = jnp.dot(
                    squeeze[...], one, preferred_element_type=jnp.float32
                ).astype(jnp.bfloat16)
                gated[line, slots:] = jnp.dot(
                    squeeze[...], value, preferred_element_type=jnp.float32
                ).astype(jnp.bfloat16)

    def expert_rows(base, column):
        return pl.ds(pl.multiple_of(base + column * local, local), local)

    def spread(line, c, block):
        moved = jnp.dot(pick[line], block, preferred_element_type=jnp.float32).astype(jnp.bfloat16)
        s = line * COLS + x
        wide[line, slots:slots + pack, lanes_of(c)] = moved[slots:]
        x_copy(line, c).start()
        disp[part, c, :, slot_rows(s), :] = moved[:slots].reshape(local, SLOT, wide_chunk)
        core_copy(part, s, c).start()

    def own_step(c):
        spread(z, c, normed[:, own_lanes(c)])

    def line_step(line, c):
        low = line < z

        @pl.when(c == 0)
        def _():
            meta_arrival(line).wait_recv()
            routing(
                line, got_meta[line, expert_rows(0, x)], got_meta[line, expert_rows(0, 1 - x)]
            )

        way = jnp.where(low, 0, 1)
        z_copy(line, c, way).wait_recv()

        @pl.when(jnp.where(low, not_top, not_bottom))
        def _():
            z_copy(line, c, way).start()

        spread(line, c, tok[line, c])

    def x_step(line, c):
        x_copy(line, c).wait_recv()
        s = line * COLS + (1 - x)
        disp[part, c, :, slot_rows(s), :] = jnp.dot(
            grow[...], got_packed[line, c], preferred_element_type=jnp.float32
        ).astype(jnp.bfloat16).reshape(local, SLOT, wide_chunk)
        core_copy(part, s, c).start()

    def across_rows(left, right):
        return lax.dot_general(
            left, right, (((1,), (1,)), ((), ())), preferred_element_type=jnp.float32
        )

    def raise_expert(e):
        sums = []
        for g in range(2):
            for b in range(2):
                total = None
                for c in range(chunks):
                    for side in range(2):
                        start = side * half + c * wide_chunk
                        piece = across_rows(
                            gu[2 * e + b, g, :, start:start + wide_chunk], disp[side, c, e]
                        )
                        total = piece if total is None else total + piece
                sums.append(total)
        for b in range(2):
            gate = sums[b]
            hid_own[e, b * hidden:(b + 1) * hidden] = (
                gate * jax.nn.sigmoid(gate) * sums[2 + b]
            ).astype(jnp.bfloat16)
        hid_copy(e).start()

    def hid_copy(e):
        return remote(hid_own.at[e], hid_other.at[e], hid_s.at[e], hid_r.at[e], core_to)

    def arrived(c):
        for s in range(devices):
            core_copy(other, s, c).wait_recv()

    routing(
        z, meta[expert_rows(z * COLS * local, x)], meta[expert_rows(z * COLS * local, 1 - x)]
    )
    own_step(0)

    def weight_wait(h, carry):
        for copy in weight_copies(h):
            copy.wait()
        return carry

    lax.fori_loop(0, 2 * local, weight_wait, 0)

    def step(t, carry):
        for j, line in enumerate(near_lines):
            c = t - jnp.abs(line - z) + 1

            @pl.when((c >= 0) & (c < chunks))
            def _():
                line_step(line, c)

            if j == 0:

                @pl.when(t + 1 < chunks)
                def _():
                    own_send(t + 1)
                    own_step(t + 1)

        @pl.when(t < chunks)
        def _():
            x_step(z, t)

        for j, line in enumerate(near_lines):
            c = t - jnp.abs(line - z)

            @pl.when((c >= 0) & (c < chunks))
            def _():
                x_step(line, c)

        return carry

    lax.fori_loop(0, chunks + lines - 1, step, 0)
    for c in range(chunks):
        arrived(c)

    def lower_expert(e):
        hid_copy(e).wait_recv()
        mine = pl.ds(pl.multiple_of(part * hidden, SLOT), hidden)
        theirs = pl.ds(pl.multiple_of(other * hidden, SLOT), hidden)
        left = jnp.concatenate([hid_own[e], hid_other[e]], axis=0)
        right = jnp.concatenate(
            [dn[2 * e, mine], dn[2 * e + 1, mine], dn[2 * e, theirs], dn[2 * e + 1, theirs]], axis=0
        )
        wide[e, :rows] = lax.dot_general(
            left, right, (((0,), (0,)), ((), ())), preferred_element_type=jnp.float32
        ).astype(jnp.bfloat16)

    raise_expert(0)

    def both_ways(e, carry):
        raise_expert(e)
        lower_expert(e - 1)
        return carry

    lax.fori_loop(1, local, both_ways, 0)
    lower_expert(local - 1)

    def result_rows(s, q):
        return wide[:local, slot_rows(s), lanes_of(q)].reshape(slots, wide_chunk)

    def rx_copy(line, q):
        return remote(
            wide.at[lines + line, pl.ds(slots, pack), lanes_of(q)], got_rows.at[line, q],
            rx_s.at[line, q], rx_r.at[line, q], x_to,
        )

    def rz_copy(line, q, way):
        where = {"dev": jnp.where(way == 0, above, below)}
        return remote(
            tok.at[line, q], got_sum.at[way, line, q],
            rz_s.at[line, q], rz_r.at[way, line, q], where,
        )

    def give(line, q):
        packed = jnp.dot(
            squeeze[...], result_rows(line * COLS + (1 - x), q), preferred_element_type=jnp.float32
        )
        wide[lines + line, slots:slots + pack, lanes_of(q)] = packed.astype(jnp.bfloat16)
        rx_copy(line, q).start()

    def gather_here(line, q):
        rx_copy(line, q).wait_recv()
        pieces = jnp.concatenate([result_rows(line * COLS + x, q), got_rows[line, q]], axis=0)
        acc[...] = lax.dot_general(
            gated[line], pieces, (((0,), (0,)), ((), ())), preferred_element_type=jnp.float32
        )

    def add_line(line, q, way):
        rz_copy(line, q, way).wait_recv()
        acc[...] += got_sum[way, line, q].astype(jnp.float32)

    def pass_on(line, q):
        gather_here(line, q)
        way = jnp.where(line > z, 0, 1)

        @pl.when(jnp.where(line > z, not_bottom, not_top))
        def _():
            add_line(line, q, way)

        tok[line, q] = acc[...].astype(jnp.bfloat16)
        rz_copy(line, q, way).start()

    for line in far_lines + [z]:
        lax.fori_loop(0, chunks, lambda q, carry, line=line: (give(line, q), carry)[1], 0)
    for line in near_lines:
        low = line < z

        @pl.when(jnp.where(low, not_top, not_bottom))
        def _():
            for c in range(chunks):
                z_copy(line, c, jnp.where(low, 0, 1)).wait_send()

    for line in far_lines:
        lax.fori_loop(0, chunks, lambda q, carry, line=line: (pass_on(line, q), carry)[1], 0)
    for q in range(chunks):
        gather_here(z, q)

        @pl.when(not_bottom)
        def _():
            add_line(z, q, 0)

        @pl.when(not_top)
        def _():
            add_line(z, q, 1)

        own = own_lanes(q)
        lanes = slice(q * wide_chunk, (q + 1) * wide_chunk)
        out[:, lanes] = (
            state[:, own] + (1.0 + modulation[3:4, own]) * acc[...]
        ).astype(out.dtype)

    for c in range(chunks):

        @pl.when(not_top)
        def _():
            z_copy(z, c, 0, normed.at[:, own_lanes(c)]).wait_send()

        @pl.when(not_bottom)
        def _():
            z_copy(z, c, 1, normed.at[:, own_lanes(c)]).wait_send()

        for line in near_lines:
            rz_copy(line, c, jnp.where(line > z, 0, 1)).wait_send()
        for line in range(lines):
            x_copy(line, c).wait_send()
            rx_copy(line, c).wait_send()
        for s in range(devices):
            core_copy(part, s, c).wait_send()
    for line in near_lines:
        meta_copy(line).wait_send()

    def hid_drain(e, carry):
        hid_copy(e).wait_send()
        return carry

    lax.fori_loop(0, local, hid_drain, 0)


def front_kernel(
    devices, start_weights,
    sources, held, own_sem,
    normed, state, meta,
    near, relayed, column, mixed, mixed_in, mine_out, their_out, sent_back, got_back, their_back,
    near_s, near_r, far_s, far_r, way_s, way_r, side_s, wz_s, wz_r, wy_s, wy_r, mix_s, mix_r,
    sum_s, sum_r, back_s, back_r, share_s, share_r,
):
    packed_hbm, weight_hbm = sources[1], sources[2]
    tokens, packed, modulation, router, ids = held
    me = lax.axis_index("dev")
    part = lax.axis_index("sub")
    group = lax.axis_index("groups")
    z = me // COLS
    x = me % COLS
    lines = devices // COLS
    count, width = tokens.shape
    shard = column.shape[1]
    share = shard // 2
    piece = share // PIECES
    pairs, pair = near.shape[1], near.shape[4]
    targets = (tokens, packed, column.at[z], modulation, router, ids)

    def own_copy(i):
        return pltpu.make_async_copy(sources[i], targets[i], own_sem.at[i])

    for i in (1, 2, 0, 3, 4, 5):
        own_copy(i).start()
    not_top = z < lines - 1
    not_bottom = z > 0
    above = jnp.minimum(me + COLS, devices - 1)
    below = jnp.maximum(me - COLS, 0)
    x_to = {"dev": z * COLS + (1 - x)}
    y_to = {"groups": 1 - group}
    core_to = {"sub": 1 - part}
    near_lines = [choose(z, table) for table in line_order(lines, True)]

    barrier = pltpu.get_barrier_semaphore()

    def greet(where):
        pl.semaphore_signal(barrier, inc=1, device_id=where, device_id_type=MESH)

    for where in (x_to, y_to, core_to):
        greet(where)
    for line in near_lines:
        greet({"dev": line * COLS + x})
    pl.semaphore_wait(barrier, lines + 2)

    def remote(src, dst, send, recv, where):
        return pltpu.make_async_remote_copy(
            src_ref=src, dst_ref=dst, send_sem=send, recv_sem=recv,
            device_id=where, device_id_type=MESH,
        )

    def near_copy(k):
        src = packed_hbm.at[1:3, :, pl.ds(k * pair, pair)]
        return remote(src, near.at[x, k], near_s.at[k], near_r.at[k], x_to)

    def far_copy(k):
        where = {"dev": jnp.where(x == 0, above, below)}
        return remote(near.at[1 - x, k], near.at[x, k], far_s.at[k], far_r.at[k], where)

    give_far = ((x == 0) & not_top) | ((x == 1) & not_bottom)
    have_far = ((x == 0) & not_bottom) | ((x == 1) & not_top)

    early = pairs // 2
    give_side = ((x == 1) & not_top) | ((x == 0) & not_bottom)
    have_side = ((x == 1) & not_bottom) | ((x == 0) & not_top)

    def way_copy(k):
        src = packed_hbm.at[1:3, :, pl.ds(k * pair, pair)]
        where = {"dev": jnp.where(x == 1, above, below)}
        return remote(src, relayed.at[k - early], way_s.at[k - early], way_r.at[k - early], where)

    def side_copy(k):
        return remote(
            relayed.at[k - early], near.at[1 - x, k], side_s.at[k - early], far_r.at[k], x_to
        )

    def piece_rows(which, i):
        return pl.ds(pl.multiple_of(which * share + i * piece, SLOT), piece)

    def wz_copy(line, i, way, src=None):
        dst = column.at[line, piece_rows(group, i)]
        where = {"dev": jnp.where(way == 0, above, below)}
        return remote(
            dst if src is None else src, dst, wz_s.at[line, i, way], wz_r.at[line, i], where
        )

    def own_piece(i):
        return weight_hbm.at[piece_rows(group, i)]

    def wy_copy(line, i, which):
        block = column.at[line, piece_rows(which, i)]
        return remote(block, block, wy_s.at[line, i], wy_r.at[line, i], y_to)

    for k in range(pairs):
        near_copy(k).start()
    for i in range(PIECES):

        @pl.when(not_top)
        def _():
            wz_copy(z, i, 0, own_piece(i)).start()

        @pl.when(not_bottom)
        def _():
            wz_copy(z, i, 1, own_piece(i)).start()

    @pl.when(give_side)
    def _():
        for k in range(early, pairs):
            way_copy(k).start()

    start_weights()

    @pl.when(jnp.logical_not(have_far))
    def _():
        near[x] = jnp.zeros_like(near[x])

    def way_of(line):
        return jnp.where(line < z, 0, 1)

    def more(line):
        return jnp.where(line < z, not_top, not_bottom)

    def busy(line):
        return jnp.where(line < z, x == 0, x == 1)

    def distance(line):
        return jnp.abs(line - z)

    def take(line, onward, pieces=range(PIECES)):
        for i in pieces:
            wz_copy(line, i, way_of(line)).wait_recv()

            @pl.when(onward)
            def _():
                wz_copy(line, i, way_of(line)).start()

            wy_copy(line, i, group).start()

    def take_next(only_busy, pieces):
        for line in near_lines:

            @pl.when((distance(line) == 1) & (busy(line) if only_busy else jnp.logical_not(busy(line))))
            def _():
                take(line, more(line), pieces)

    take_next(True, range(1))
    take_next(False, range(1))
    for k in range(early):
        near_copy(k).wait_recv()

        @pl.when(give_far)
        def _():
            far_copy(k).start()

    take_next(True, range(1, PIECES))
    take_next(False, range(1, PIECES))

    @pl.when(have_side)
    def _():
        for k in range(early, pairs):
            way_copy(k).wait_recv()
            side_copy(k).start()

    for k in range(early, pairs):
        near_copy(k).wait_recv()
    for i in range(6):
        own_copy(i).wait()

    row = lax.broadcasted_iota(jnp.int32, (count, count), 0)
    col = lax.broadcasted_iota(jnp.int32, (count, count), 1)
    see_before = (col >= row) & (me > 0)
    see_after = (col <= row) & (me < devices - 1)

    def mix_copy(k):
        lanes = pl.ds(k * pair, pair)
        return remote(
            mixed.at[:, lanes], mixed_in.at[:, lanes], mix_s.at[k], mix_r.at[k], x_to
        )

    for k in range(pairs):

        @pl.when(have_far)
        def _():
            far_copy(k).wait_recv()

        for h in range(pair // HEAD):
            lanes = slice(k * pair + h * HEAD, k * pair + (h + 1) * HEAD)
            inner = slice(h * HEAD, (h + 1) * HEAD)
            query = packed[0, :, lanes]

            def score(keys):
                return lax.dot_general(
                    query, keys, (((1,), (1,)), ((), ())), preferred_element_type=jnp.float32
                ) / math.sqrt(HEAD)

            scores = jnp.concatenate(
                [
                    jnp.where(see_before, score(near[0, k, 0, :, inner]), NEG),
                    score(packed[1, :, lanes]),
                    jnp.where(see_after, score(near[1, k, 0, :, inner]), NEG),
                ],
                axis=1,
            )
            top = jnp.max(scores, -1, keepdims=True)
            weight = jnp.exp(scores - top)
            weight = (weight / jnp.sum(weight, -1, keepdims=True)).astype(jnp.bfloat16)
            values = jnp.concatenate(
                [near[0, k, 1, :, inner], packed[2, :, lanes], near[1, k, 1, :, inner]], axis=0
            )
            mixed[:, lanes] = jnp.dot(
                weight, values, preferred_element_type=jnp.float32
            ).astype(jnp.bfloat16)
        mix_copy(k).start()
        if k + 1 == early:
            for line in near_lines:

                @pl.when(distance(line) == 2)
                def _():
                    take(line, more(line))

    for k in range(pairs):
        mix_copy(k).wait_recv()

    def place_of(which):
        return group if which == 0 else 1 - group

    def sum_copy(line, which):
        place = place_of(which)
        return remote(
            mine_out.at[line, place], their_out.at[line, place],
            sum_s.at[line, which], sum_r.at[line, which], core_to,
        )

    def back_copy(line, which):
        place = place_of(which)
        return remote(
            sent_back.at[line, place], got_back.at[line, place],
            back_s.at[line, which], back_r.at[line, which], x_to,
        )

    def share_copy(line, which):
        place = place_of(which)
        return remote(
            got_back.at[line, place], their_back.at[line, place],
            share_s.at[line, which], share_r.at[line, which], core_to,
        )

    def project(line, which):
        place = place_of(which)
        block = column[line, pl.ds(pl.multiple_of(place * share, SLOT), share), :]
        both = jnp.concatenate([mixed_in[...], mixed[...]], axis=0)
        product = lax.dot_general(
            both, block, (((1,), (1,)), ((), ())), preferred_element_type=jnp.float32
        )
        sent_back[line, place] = product[:count].astype(jnp.bfloat16)
        back_copy(line, which).start()
        mine_out[line, place] = product[count:]
        sum_copy(line, which).start()

    steps = [(line, which) for line in [z] + near_lines for which in range(2)]

    def relay(i):
        back_copy(*steps[i]).wait_recv()
        share_copy(*steps[i]).start()

    for i, (line, which) in enumerate(steps):
        if which == 0 and i == 4:
            for late in near_lines[1:]:

                @pl.when(distance(late) > 2)
                def _():
                    take(late, more(late))
        if which == 1 and i > 1:
            if i == len(steps) - 1:
                for n in range(i - 1):
                    relay(n)
            for n in range(PIECES):
                wy_copy(line, n, 1 - group).wait_recv()
        project(line, which)
    relay(len(steps) - 2)
    relay(len(steps) - 1)

    square = jnp.zeros((count, 1), jnp.float32)
    for line, which in steps:
        place = place_of(which)
        sum_copy(line, which).wait_recv()
        share_copy(line, which).wait_recv()
        for column_of, total in (
            (x, mine_out[line, place] + their_out[line, place]),
            (
                1 - x,
                got_back[line, place].astype(jnp.float32)
                + their_back[line, place].astype(jnp.float32),
            ),
        ):
            start = (line * COLS + column_of) * shard + place * share
            lanes = pl.ds(pl.multiple_of(start, LANES), share)
            value = tokens[:, lanes].astype(jnp.float32) + (1.0 + modulation[0:1, lanes]) * total
            state[:, lanes] = value
            square = square + jnp.sum(value * value, -1, keepdims=True)
    scale = lax.rsqrt(square / width + EPS)
    for s in range(devices):
        lanes = slice(s * shard, (s + 1) * shard)
        normed[:, lanes] = (
            state[:, lanes] * scale * (1.0 + modulation[2:3, lanes]) + modulation[1:2, lanes]
        ).astype(jnp.bfloat16)
    logits = lax.dot_general(
        router[...], normed[...], (((1,), (1,)), ((), ())), preferred_element_type=jnp.float32
    )
    name = lax.broadcasted_iota(jnp.int32, logits.shape, 0)
    named = name == ids[0:1]
    for k in range(1, ids.shape[0]):
        named = named | (name == ids[k:k + 1])
    lifted = jnp.where(named, jax.nn.sigmoid(logits), 0.0)
    meta[...] = lifted / jnp.sum(lifted, 0, keepdims=True)

    for k in range(pairs):
        near_copy(k).wait_send()
        mix_copy(k).wait_send()

        if k < early:

            @pl.when(give_far)
            def _():
                far_copy(k).wait_send()
        else:

            @pl.when(give_side)
            def _():
                way_copy(k).wait_send()

            @pl.when(have_side)
            def _():
                side_copy(k).wait_send()

    for i in range(PIECES):

        @pl.when(not_top)
        def _():
            wz_copy(z, i, 0, own_piece(i)).wait_send()

        @pl.when(not_bottom)
        def _():
            wz_copy(z, i, 1, own_piece(i)).wait_send()

        for line in near_lines:

            @pl.when(more(line))
            def _():
                wz_copy(line, i, way_of(line)).wait_send()

            wy_copy(line, i, group).wait_send()
    for line, which in steps:
        sum_copy(line, which).wait_send()
        back_copy(line, which).wait_send()
        share_copy(line, which).wait_send()


def block_kernel(devices, *refs):
    sources, gate_up, down, out = refs[:6], refs[6], refs[7], refs[8]
    held, normed, state, meta, wide = refs[9:14], refs[14], refs[15], refs[16], refs[17]
    front_buffers, expert_buffers = refs[18:28], refs[28:43]
    own_sem, gu_sem, dn_sem = refs[43:46]
    front_sems, expert_sems = refs[46:65], refs[65:]
    gu, dn = expert_buffers[5:7]
    squeeze, grow = expert_buffers[12:14]
    halves = gate_up.shape[0]

    def weight_copies(h):
        return (
            pltpu.make_async_copy(gate_up.at[h], gu.at[h], gu_sem.at[h]),
            pltpu.make_async_copy(down.at[h], dn.at[h], dn_sem.at[h]),
        )

    def start_weights():
        def one(h, carry):
            for copy in weight_copies(h):
                copy.start()
            return carry

        lax.fori_loop(0, halves, one, 0)
        for ref, axis in ((squeeze, 0), (grow, 1)):
            packed = lax.broadcasted_iota(jnp.int32, ref.shape, axis)
            slot = lax.broadcasted_iota(jnp.int32, ref.shape, 1 - axis)
            inner = slot & (SLOT - 1)
            same = (packed == (slot - inner) // SLOT * CAP + inner) & (inner < CAP)
            ref[...] = jnp.where(same, 1.0, 0.0).astype(jnp.bfloat16)

    front_kernel(
        devices, start_weights, sources, held, own_sem, normed, state, meta,
        *front_buffers, *front_sems,
    )
    expert_kernel(
        devices, weight_copies, normed, meta, state, held[2], wide, out,
        *expert_buffers, *expert_sems,
    )


def block_call(
    tokens, query_key_value, out_weight, modulation, router_weight, expert_ids,
    gate_up_weight, down_weight,
):
    devices = lax.axis_size("dev")
    count, width = tokens.shape
    half = down_weight.shape[2]
    halves = gate_up_weight.shape[0]
    local = halves // 2
    gate_up_weight = gate_up_weight.swapaxes(2, 3)
    hidden = gate_up_weight.shape[2]
    lines = devices // COLS
    rows = devices * SLOT
    slots, pack = local * SLOT, local * CAP
    part = half // CHUNKS
    shard = out_weight.shape[0]
    own = (
        tokens, query_key_value.transpose(1, 0, 2), out_weight, modulation,
        router_weight.T, expert_ids.T,
    )
    hbm = pl.BlockSpec(memory_space=pl.ANY)
    dma = pltpu.SemaphoreType.DMA
    return pl.pallas_call(
        functools.partial(block_kernel, devices),
        out_shape=jax.ShapeDtypeStruct((count, half), jnp.bfloat16),
        in_specs=[hbm] * 8,
        out_specs=pl.BlockSpec(memory_space=pltpu.VMEM),
        scratch_shapes=[
            *[pltpu.VMEM(own[i].shape, own[i].dtype) for i in (0, 1, 3, 4, 5)],
            pltpu.VMEM((count, width), jnp.bfloat16),
            pltpu.VMEM((count, width), jnp.float32),
            pltpu.VMEM((router_weight.shape[1], count), jnp.float32),
            pltpu.VMEM((devices, slots + pack, half), jnp.bfloat16),
            pltpu.VMEM((2, CHUNKS, 2, count, part), jnp.bfloat16),
            pltpu.VMEM((CHUNKS // 2, 2, count, part), jnp.bfloat16),
            pltpu.VMEM((lines, shard, half), jnp.bfloat16),
            pltpu.VMEM((count, half), jnp.bfloat16),
            pltpu.VMEM((count, half), jnp.bfloat16),
            pltpu.VMEM((lines, 2, count, shard // 2), jnp.float32),
            pltpu.VMEM((lines, 2, count, shard // 2), jnp.float32),
            pltpu.VMEM((lines, 2, count, shard // 2), jnp.bfloat16),
            pltpu.VMEM((lines, 2, count, shard // 2), jnp.bfloat16),
            pltpu.VMEM((lines, 2, count, shard // 2), jnp.bfloat16),
            pltpu.VMEM((lines, CHUNKS, count, part), jnp.bfloat16),
            pltpu.VMEM((lines, CHUNKS, pack, part), jnp.bfloat16),
            pltpu.VMEM((lines, CHUNKS, pack, part), jnp.bfloat16),
            pltpu.VMEM((2, lines, CHUNKS, count, part), jnp.bfloat16),
            pltpu.VMEM((2, CHUNKS, local, rows, part), jnp.bfloat16),
            pltpu.VMEM(gate_up_weight.shape, jnp.bfloat16),
            pltpu.VMEM(down_weight.shape, jnp.bfloat16),
            pltpu.VMEM((local, 2 * hidden, rows), jnp.bfloat16),
            pltpu.VMEM((local, 2 * hidden, rows), jnp.bfloat16),
            pltpu.VMEM((lines, COLS * local, count), jnp.float32),
            pltpu.VMEM((lines, slots + pack, count), jnp.bfloat16),
            pltpu.VMEM((lines, slots + pack, count), jnp.bfloat16),
            pltpu.VMEM((pack, slots), jnp.bfloat16),
            pltpu.VMEM((slots, pack), jnp.bfloat16),
            pltpu.VMEM((count, part), jnp.float32),
            dma((6,)), dma((halves,)), dma((halves,)),
            dma((CHUNKS,)), dma((CHUNKS,)), dma((CHUNKS,)), dma((CHUNKS,)),
            dma((CHUNKS // 2,)), dma((CHUNKS // 2,)), dma((CHUNKS // 2,)),
            dma((lines, PIECES, 2)), dma((lines, PIECES)),
            dma((lines, PIECES)), dma((lines, PIECES)), dma((CHUNKS,)), dma((CHUNKS,)),
            dma((lines, 2)), dma((lines, 2)), dma((lines, 2)), dma((lines, 2)),
            dma((lines, 2)), dma((lines, 2)),
            dma((lines,)), dma((lines,)),
            dma((lines, CHUNKS, 2)), dma((lines, CHUNKS)),
            dma((lines, CHUNKS)), dma((lines, CHUNKS)),
            dma((devices, CHUNKS)), dma((devices, CHUNKS)),
            dma((local,)), dma((local,)),
            dma((lines, CHUNKS)), dma((lines, CHUNKS)),
            dma((lines, CHUNKS)), dma((2, lines, CHUNKS)),
        ],
        compiler_params=pltpu.CompilerParams(
            collective_id=1, has_side_effects=True, vmem_limit_bytes=VMEM_BYTES
        ),
    )(*own, gate_up_weight, down_weight)


def body(
    tokens,
    query_key_value,
    out_weight,
    modulation,
    router_weight,
    expert_ids,
    gate_up_weight,
    down_weight,
):
    count = tokens.shape[0]
    width = tokens.shape[1]
    parts = lax.axis_size("sub")
    part = lax.axis_index("sub")
    position = lax.axis_index("dev")
    devices = lax.axis_size("dev")
    total = count * devices
    local_width = query_key_value.shape[2]
    weight_bytes = 2 * (gate_up_weight.size + down_weight.size)
    token_bytes = 12 * devices * count * width
    fits = weight_bytes + token_bytes < VMEM_BYTES and CAP <= SLOT
    paired = parts == 2 and lax.axis_size("groups") == 2 and devices % COLS == 0
    experts_here = gate_up_weight.shape[0] // 2
    tiled = out_weight.shape[0] % (2 * LANES) == 0 and count == LANES
    tiled = tiled and down_weight.shape[2] // CHUNKS % HEAD == 0 and devices // COLS > 2
    tiled = tiled and down_weight.shape[2] % (2 * CHUNKS * LANES) == 0 and experts_here == devices
    tiled = tiled and SLOT * devices == LANES
    tiled = tiled and gate_up_weight.shape[3] % 64 == 0
    if fits and paired and tiled:
        return block_call(
            tokens, query_key_value, out_weight, modulation, router_weight, expert_ids,
            gate_up_weight, down_weight,
        )
    heads_here = local_width // HEAD
    query = query_key_value[:, 0].reshape(count, heads_here, HEAD)
    pair = query_key_value[:, 1:]
    near = extended(pair, (("dev", 0),), count)
    keys = near[:, 0].reshape(3 * count, heads_here, HEAD)
    values = near[:, 1].reshape(3 * count, heads_here, HEAD)
    mixed = window_attention(query, keys, values, position, total).reshape(count, local_width)
    partial_proj = lax.dot_general(
        mixed,
        lax.all_gather(out_weight, "dev", axis=0, tiled=True),
        (((1,), (1,)), ((), ())),
        preferred_element_type=jnp.float32,
    )
    proj = lax.psum(partial_proj, "sub")
    state = tokens.astype(jnp.float32) + (1.0 + modulation[0]) * proj
    normed = normalize(state, modulation)
    gates = route(normed, router_weight, expert_ids)
    experts = router_weight.shape[1]
    topk = expert_ids.shape[1]
    flat = expert_ids.reshape(-1)
    picks = flat.shape[0]
    onehot = (flat[:, None] == jnp.arange(experts, dtype=jnp.int32)[None, :]).astype(jnp.int32)
    rank = jnp.sum((jnp.cumsum(onehot, 0) - 1) * onehot, 1)
    target = flat * CAP + rank
    hit = target[None, :] == jnp.arange(experts * CAP, dtype=jnp.int32)[:, None]
    filled = jnp.any(hit, 1)
    anchor = jnp.sum(jnp.where(hit, jnp.arange(picks, dtype=jnp.int32)[None, :], 0), 1) // topk
    slice_width = width // parts
    sent = lax.dynamic_slice_in_dim(normed, part * slice_width, slice_width, 1)
    sent_width = sent.shape[1]
    rows_out = jnp.where(filled[:, None], sent[anchor], jnp.zeros((), jnp.bfloat16))
    halves_here = gate_up_weight.shape[0]
    doubled = jnp.broadcast_to(
        rows_out.reshape(experts, 1, CAP, sent_width), (experts, 2, CAP, sent_width)
    )
    outgoing = doubled.reshape(devices, halves_here, CAP, sent_width)
    up_form = "sxcd,xgdf->sxcgf"
    down_form = "sxcf,xfd->sxcd"
    incoming = lax.all_to_all(outgoing, "dev", split_axis=0, concat_axis=0, tiled=True)
    both = jnp.einsum(
        up_form,
        lax.all_gather(incoming, "sub", axis=3, tiled=True),
        gate_up_weight,
        preferred_element_type=jnp.float32,
    )
    hidden = (jax.nn.silu(both[..., 0, :]) * both[..., 1, :]).astype(jnp.bfloat16)
    gathered = lax.all_gather(hidden, "sub", axis=hidden.ndim - 1, tiled=True)
    result = jnp.einsum(down_form, gathered, down_weight, preferred_element_type=jnp.float32)
    returned = lax.all_to_all(
        result.astype(jnp.bfloat16), "dev", split_axis=0, concat_axis=0, tiled=True
    )
    own_width = returned.shape[-1]
    arranged = returned.reshape(experts, 2, CAP, own_width)
    answers = arranged[flat, :, rank, :].reshape(count, topk, 2, own_width).astype(jnp.float32)
    combined = answers[:, :, 0] + answers[:, :, 1]
    routed = jnp.einsum("tk,tkd->td", gates, combined)
    own = lax.dynamic_slice_in_dim(state, part * slice_width, slice_width, 1)
    lift = lax.dynamic_slice_in_dim(modulation[3], part * slice_width, slice_width, 0)
    return (own + (1.0 + lift) * routed).astype(jnp.bfloat16)


def solution(mesh):
    return jax.shard_map(
        body,
        mesh=mesh,
        in_specs=(
            P(("groups", "dev"), None),
            P(("groups", "dev"), None, "sub"),
            P("dev", "sub"),
            P("groups", None),
            P(),
            P(("groups", "dev"), None),
            P("dev", None, None, "sub"),
            P("dev", None, "sub"),
        ),
        out_specs=P(("groups", "dev"), "sub"),
        check_vma=False,
    )
```

```python
import functools
import math

import jax
import jax.numpy as jnp
from jax import lax
from jax.experimental import pallas as pl
from jax.experimental.pallas import tpu as pltpu
from jax.sharding import PartitionSpec as P

HEAD = 128
CAP = 12


EPS = 1e-06
NEG = -1e30


def extended(cells, sides, width):
    for axis, dim in sides:
        count = lax.axis_size(axis)
        ends = count - 1
        head = lax.slice_in_dim(cells, 0, width, axis=dim)
        tail = lax.slice_in_dim(cells, cells.shape[dim] - width, cells.shape[dim], axis=dim)
        cells = jnp.concatenate(
            [
                lax.ppermute(tail, axis, [(i, (i + 1) % count) for i in range(ends)]),
                cells,
                lax.ppermute(head, axis, [((i + 1) % count, i) for i in range(ends)]),
            ],
            axis=dim,
        )
    return cells


def window_attention(query, keys, values, index, total):
    count = query.shape[0]
    rows = jnp.arange(count, dtype=jnp.int32)[:, None]
    cols = jnp.arange(3 * count, dtype=jnp.int32)[None, :] - count
    place = index * count + cols
    allowed = (jnp.abs(cols - rows) <= count) & (place >= 0) & (place < total)
    scores = jnp.einsum(
        "qhd,khd->hqk", query, keys, preferred_element_type=jnp.float32
    ) / math.sqrt(query.shape[2])
    scores = jnp.where(allowed[None], scores, NEG)
    top = jnp.max(scores, -1, keepdims=True)
    weight = jnp.exp(scores - top)
    weight = (weight / jnp.sum(weight, -1, keepdims=True)).astype(jnp.bfloat16)
    mixed = jnp.einsum("hqk,khd->qhd", weight, values, preferred_element_type=jnp.float32)
    return mixed.astype(jnp.bfloat16)


def normalize(state, modulation):
    scale = lax.rsqrt(jnp.mean(state * state, -1, keepdims=True) + EPS)
    return (state * scale * (1.0 + modulation[2]) + modulation[1]).astype(jnp.bfloat16)


def route(normed, router_weight, expert_ids):
    logits = jnp.dot(normed, router_weight, preferred_element_type=jnp.float32)
    experts = router_weight.shape[1]
    match = expert_ids[:, :, None] == jnp.arange(experts, dtype=jnp.int32)[None, None, :]
    picked = jnp.sum(jnp.where(match, logits[:, None, :], 0.0), -1)
    lifted = jax.nn.sigmoid(picked)
    return lifted / jnp.sum(lifted, -1, keepdims=True)


LANES = 128
SLOT = 16
COLS = 2
CHUNKS = 4
PIECES = 4
LAG = 2
VMEM_BYTES = 66 * 1000 * 1000
MESH = pl.DeviceIdType.MESH


def choose(index, table):
    value = jnp.int32(table[0])
    for i in range(1, len(table)):
        value = jnp.where(index == i, table[i], value)
    return value


def line_order(lines, nearest, inner=False):
    rows = []
    for z in range(lines):
        lower = (z < lines - 1 - z) != inner
        others = [line for line in range(lines) if line != z]
        sign = 1 if nearest else -1
        rows.append(sorted(others, key=lambda line: (sign * abs(line - z), (line > z) == lower)))
    return [[rows[z][j] for z in range(lines)] for j in range(lines - 1)]


def expert_kernel(
    devices, weight_copies,
    normed, meta, state, modulation, wide,
    out,
    tok, got_packed, got_rows, got_sum, disp, gu, dn, raised, hid_own, hid_other,
    got_meta, pick, gated, squeeze, grow, acc,
    meta_s, meta_r, z_s, z_r, x_s, x_r, core_s, core_r, hid_s, hid_r, rx_s, rx_r, rz_s, rz_r,
):
    me = lax.axis_index("dev")
    part = lax.axis_index("sub")
    other = 1 - part
    z = me // COLS
    x = me % COLS
    lines = devices // COLS
    count, width = normed.shape
    half = width // 2
    local = hid_own.shape[0]
    hidden = gu.shape[2]
    slots = local * SLOT
    pack = local * CAP
    rows = devices * SLOT
    chunks, wide_chunk = tok.shape[1], tok.shape[3]

    def remote(src, dst, send, recv, where):
        return pltpu.make_async_remote_copy(
            src_ref=src, dst_ref=dst, send_sem=send, recv_sem=recv,
            device_id=where, device_id_type=MESH,
        )

    above = jnp.minimum(me + COLS, devices - 1)
    below = jnp.maximum(me - COLS, 0)
    x_to = {"dev": z * COLS + (1 - x)}
    core_to = {"sub": other}
    not_top = z < lines - 1
    not_bottom = z > 0
    near_lines = [choose(z, table) for table in line_order(lines, True, True)]
    far_lines = [choose(z, table) for table in line_order(lines, False)]

    def lanes_of(c):
        return pl.ds(pl.multiple_of(c * wide_chunk, wide_chunk), wide_chunk)

    def own_lanes(c):
        return pl.ds(pl.multiple_of(part * half + c * wide_chunk, wide_chunk), wide_chunk)

    def slot_rows(s):
        return pl.ds(pl.multiple_of(s * SLOT, SLOT), SLOT)

    def meta_copy(line):
        return remote(
            meta.at[pl.ds(pl.multiple_of(line * COLS * local, COLS * local), COLS * local)],
            got_meta.at[z], meta_s.at[line], meta_r.at[z], {"dev": line * COLS + x},
        )

    def meta_arrival(line):
        return remote(got_meta.at[line], got_meta.at[line], meta_s.at[line], meta_r.at[line], x_to)

    def z_copy(line, c, way, src=None):
        dst = tok.at[line, c]
        where = {"dev": jnp.where(way == 0, above, below)}
        return remote(
            dst if src is None else src, dst, z_s.at[line, c, way], z_r.at[line, c], where
        )

    def packed_out(line, c):
        return wide.at[line, pl.ds(slots, pack), lanes_of(c)]

    def x_copy(line, c):
        return remote(
            packed_out(line, c), got_packed.at[line, c], x_s.at[line, c], x_r.at[line, c], x_to
        )

    def core_copy(which, s, c):
        place = disp.at[which, c, :, slot_rows(s), :]
        return remote(place, place, core_s.at[s, c], core_r.at[s, c], core_to)

    def own_send(c):
        src = normed.at[:, own_lanes(c)]

        @pl.when(not_top)
        def _():
            z_copy(z, c, 0, src).start()

        @pl.when(not_bottom)
        def _():
            z_copy(z, c, 1, src).start()

    own_send(0)
    for line in near_lines:
        meta_copy(line).start()
    for c in range(1, chunks):
        own_send(c)

    before = (
        lax.broadcasted_iota(jnp.int32, (count, count), 0)
        < lax.broadcasted_iota(jnp.int32, (count, count), 1)
    ).astype(jnp.float32).astype(jnp.bfloat16)
    place = lax.broadcasted_iota(jnp.int32, (local, SLOT, count), 1).astype(jnp.float32)

    def routing(line, ours, theirs):
        for first, gate in ((True, ours), (False, theirs)):
            chosen = jnp.where(gate > 0.0, 1.0, 0.0)
            rank = jnp.dot(chosen.astype(jnp.bfloat16), before, preferred_element_type=jnp.float32)
            rank = jnp.where(gate > 0.0, rank, -1.0)
            hit = jnp.broadcast_to(rank[:, None, :], place.shape) == place
            one = jnp.where(hit, 1.0, 0.0).reshape(slots, count).astype(jnp.bfloat16)
            value = jnp.where(hit, jnp.broadcast_to(gate[:, None, :], place.shape), 0.0)
            value = value.reshape(slots, count).astype(jnp.bfloat16)
            if first:
                pick[line, :slots] = one
                gated[line, :slots] = value
            else:
                pick[line, slots:] = jnp.dot(
                    squeeze[...], one, preferred_element_type=jnp.float32
                ).astype(jnp.bfloat16)
                gated[line, slots:] = jnp.dot(
                    squeeze[...], value, preferred_element_type=jnp.float32
                ).astype(jnp.bfloat16)

    def expert_rows(base, column):
        return pl.ds(pl.multiple_of(base + column * local, local), local)

    def spread(line, c, block):
        moved = jnp.dot(pick[line], block, preferred_element_type=jnp.float32).astype(jnp.bfloat16)
        s = line * COLS + x
        wide[line, slots:slots + pack, lanes_of(c)] = moved[slots:]
        x_copy(line, c).start()
        disp[part, c, :, slot_rows(s), :] = moved[:slots].reshape(local, SLOT, wide_chunk)
        core_copy(part, s, c).start()

    def own_step(c):
        spread(z, c, normed[:, own_lanes(c)])

    def line_step(line, c):
        low = line < z

        @pl.when(c == 0)
        def _():
            meta_arrival(line).wait_recv()
            routing(
                line, got_meta[line, expert_rows(0, x)], got_meta[line, expert_rows(0, 1 - x)]
            )

        way = jnp.where(low, 0, 1)
        z_copy(line, c, way).wait_recv()

        @pl.when(jnp.where(low, not_top, not_bottom))
        def _():
            z_copy(line, c, way).start()

        spread(line, c, tok[line, c])

    def x_step(line, c):
        x_copy(line, c).wait_recv()
        s = line * COLS + (1 - x)
        disp[part, c, :, slot_rows(s), :] = jnp.dot(
            grow[...], got_packed[line, c], preferred_element_type=jnp.float32
        ).astype(jnp.bfloat16).reshape(local, SLOT, wide_chunk)
        core_copy(part, s, c).start()

    def across_rows(left, right):
        return lax.dot_general(
            left, right, (((1,), (1,)), ((), ())), preferred_element_type=jnp.float32
        )

    def raise_side(e, side):
        sums = []
        for g in range(2):
            for b in range(2):
                total = None
                for c in range(chunks):
                    start = side * half + c * wide_chunk
                    piece = across_rows(
                        gu[2 * e + b, g, :, start:start + wide_chunk], disp[side, c, e]
                    )
                    total = piece if total is None else total + piece
                sums.append(total)
        return sums

    def raise_first(e, carry):
        for n, total in enumerate(raise_side(e, 1)):
            raised[e, n * hidden:(n + 1) * hidden] = total
        return carry

    def raise_second(e, carry):
        sums = [
            total + raised[e, n * hidden:(n + 1) * hidden]
            for n, total in enumerate(raise_side(e, 0))
        ]
        for b in range(2):
            gate = sums[b]
            hid_own[e, b * hidden:(b + 1) * hidden] = (
                gate * jax.nn.sigmoid(gate) * sums[2 + b]
            ).astype(jnp.bfloat16)
        hid_copy(e).start()
        return carry

    def hid_copy(e):
        return remote(hid_own.at[e], hid_other.at[e], hid_s.at[e], hid_r.at[e], core_to)

    def arrived():
        for c in range(chunks):
            for s in range(devices):
                core_copy(other, s, c).wait_recv()

    routing(
        z, meta[expert_rows(z * COLS * local, x)], meta[expert_rows(z * COLS * local, 1 - x)]
    )
    for c in range(chunks):
        own_step(c)

    def weight_wait(h, carry):
        for copy in weight_copies(h):
            copy.wait()
        return carry

    lax.fori_loop(0, 2 * local, weight_wait, 0)

    def step(t, carry):
        for line in near_lines:
            c = t - (jnp.abs(line - z) - 1) * chunks

            @pl.when((c >= 0) & (c < chunks))
            def _():
                line_step(line, c)

        @pl.when((t >= 1) & (t < 1 + chunks))
        def _():
            x_step(z, t - 1)

        for line in near_lines:
            c = t - LAG - (jnp.abs(line - z) - 1) * chunks

            @pl.when((c >= 0) & (c < chunks))
            def _():
                x_step(line, c)

        return carry

    span = chunks * (lines - 1) + LAG
    lax.fori_loop(0, span - 2, step, 0)
    first, second = local * 3 // 8, local * 5 // 8

    def early_raise(start, stop):
        @pl.when(part == 0)
        def _():
            if start == 0:
                arrived()
            lax.fori_loop(start, stop, raise_first, 0)

    early_raise(0, first)
    step(span - 2, 0)
    early_raise(first, second)
    step(span - 1, 0)
    early_raise(second, local)

    @pl.when(part == 1)
    def _():
        lax.fori_loop(0, local, raise_first, 0)
        arrived()

    lax.fori_loop(0, local, raise_second, 0)

    group = 2 * wide_chunk

    def lower(g):
        lanes = slice(g * group, (g + 1) * group)

        def one(e, carry):
            if g == 0:
                hid_copy(e).wait_recv()
            mine = pl.ds(pl.multiple_of(part * hidden, SLOT), hidden)
            theirs = pl.ds(pl.multiple_of(other * hidden, SLOT), hidden)
            left = jnp.concatenate([hid_own[e], hid_other[e]], axis=0)
            right = jnp.concatenate(
                [dn[2 * e, mine, lanes], dn[2 * e + 1, mine, lanes],
                 dn[2 * e, theirs, lanes], dn[2 * e + 1, theirs, lanes]], axis=0
            )
            wide[e, :rows, lanes] = lax.dot_general(
                left, right, (((0,), (0,)), ((), ())), preferred_element_type=jnp.float32
            ).astype(jnp.bfloat16)
            return carry

        lax.fori_loop(0, local, one, 0)

    def result_rows(s, q):
        return wide[:local, slot_rows(s), lanes_of(q)].reshape(slots, wide_chunk)

    def rx_copy(line, q):
        return remote(
            wide.at[lines + line, pl.ds(slots, pack), lanes_of(q)], got_rows.at[line, q],
            rx_s.at[line, q], rx_r.at[line, q], x_to,
        )

    def rz_copy(line, q, way):
        where = {"dev": jnp.where(way == 0, above, below)}
        return remote(
            tok.at[line, q], got_sum.at[way, line, q],
            rz_s.at[line, q], rz_r.at[way, line, q], where,
        )

    def give(line, q):
        packed = jnp.dot(
            squeeze[...], result_rows(line * COLS + (1 - x), q), preferred_element_type=jnp.float32
        )
        wide[lines + line, slots:slots + pack, lanes_of(q)] = packed.astype(jnp.bfloat16)
        rx_copy(line, q).start()

    def gather_here(line, q):
        rx_copy(line, q).wait_recv()
        pieces = jnp.concatenate([result_rows(line * COLS + x, q), got_rows[line, q]], axis=0)
        acc[...] = lax.dot_general(
            gated[line], pieces, (((0,), (0,)), ((), ())), preferred_element_type=jnp.float32
        )

    def add_line(line, q, way):
        rz_copy(line, q, way).wait_recv()
        acc[...] += got_sum[way, line, q].astype(jnp.float32)

    def pass_on(line, q):
        gather_here(line, q)
        way = jnp.where(line > z, 0, 1)

        @pl.when(jnp.where(line > z, not_bottom, not_top))
        def _():
            add_line(line, q, way)

        tok[line, q] = acc[...].astype(jnp.bfloat16)
        rz_copy(line, q, way).start()

    for g in range(half // group):
        lower(g)
        for q in range(2 * g, 2 * g + 2):
            give(far_lines[0], q)
    def give_all(line):
        lax.fori_loop(0, chunks, lambda q, carry: (give(line, q), carry)[1], 0)

    for line in near_lines:
        low = line < z

        @pl.when(jnp.where(low, not_top, not_bottom))
        def _():
            for c in range(chunks):
                z_copy(line, c, jnp.where(low, 0, 1)).wait_send()

    far_end = (z == 0) | (z == lines - 1)

    @pl.when(far_end)
    def _():
        for q in range(2):
            pass_on(far_lines[0], q)

    give_all(far_lines[1])

    @pl.when(far_end)
    def _():
        for q in range(2, chunks):
            pass_on(far_lines[0], q)

    for line in far_lines[2:] + [z]:
        give_all(line)

    @pl.when(jnp.logical_not(far_end))
    def _():
        for q in range(chunks):
            pass_on(far_lines[0], q)

    for line in far_lines[1:]:
        lax.fori_loop(0, chunks, lambda q, carry, line=line: (pass_on(line, q), carry)[1], 0)
    for q in range(chunks):
        gather_here(z, q)

        @pl.when(not_bottom)
        def _():
            add_line(z, q, 0)

        @pl.when(not_top)
        def _():
            add_line(z, q, 1)

        own = own_lanes(q)
        lanes = slice(q * wide_chunk, (q + 1) * wide_chunk)
        out[:, lanes] = (
            state[:, own] + (1.0 + modulation[3:4, own]) * acc[...]
        ).astype(out.dtype)

    for c in range(chunks):

        @pl.when(not_top)
        def _():
            z_copy(z, c, 0, normed.at[:, own_lanes(c)]).wait_send()

        @pl.when(not_bottom)
        def _():
            z_copy(z, c, 1, normed.at[:, own_lanes(c)]).wait_send()

        for line in near_lines:
            rz_copy(line, c, jnp.where(line > z, 0, 1)).wait_send()
        for line in range(lines):
            x_copy(line, c).wait_send()
            rx_copy(line, c).wait_send()
        for s in range(devices):
            core_copy(part, s, c).wait_send()
    for line in near_lines:
        meta_copy(line).wait_send()

    def hid_drain(e, carry):
        hid_copy(e).wait_send()
        return carry

    lax.fori_loop(0, local, hid_drain, 0)


def front_kernel(
    devices, start_weights,
    sources, held, own_sem,
    normed, state, meta,
    near, relayed, column, mixed, mixed_in, mine_out, their_out, sent_back, got_back, their_back,
    near_s, near_r, far_s, far_r, way_s, way_r, side_s, wz_s, wz_r, wy_s, wy_r, mix_s, mix_r,
    sum_s, sum_r, back_s, back_r, share_s, share_r,
):
    packed_hbm, weight_hbm = sources[1], sources[2]
    tokens, packed, modulation, router, ids = held
    me = lax.axis_index("dev")
    part = lax.axis_index("sub")
    group = lax.axis_index("groups")
    z = me // COLS
    x = me % COLS
    lines = devices // COLS
    count, width = tokens.shape
    shard = column.shape[1]
    share = shard // 2
    piece = share // PIECES
    pairs, pair = near.shape[1], near.shape[4]
    targets = (tokens, packed, column.at[z], modulation, router, ids)

    def own_copy(i):
        return pltpu.make_async_copy(sources[i], targets[i], own_sem.at[i])

    for i in (1, 2, 0, 3, 4, 5):
        own_copy(i).start()
    not_top = z < lines - 1
    not_bottom = z > 0
    above = jnp.minimum(me + COLS, devices - 1)
    below = jnp.maximum(me - COLS, 0)
    x_to = {"dev": z * COLS + (1 - x)}
    y_to = {"groups": 1 - group}
    core_to = {"sub": 1 - part}
    near_lines = [choose(z, table) for table in line_order(lines, True)]

    barrier = pltpu.get_barrier_semaphore()

    def greet(where):
        pl.semaphore_signal(barrier, inc=1, device_id=where, device_id_type=MESH)

    for where in (x_to, y_to, core_to, {**x_to, **core_to}):
        greet(where)
    for line in near_lines:
        greet({"dev": line * COLS + x})
    pl.semaphore_wait(barrier, lines + 3)

    def remote(src, dst, send, recv, where):
        return pltpu.make_async_remote_copy(
            src_ref=src, dst_ref=dst, send_sem=send, recv_sem=recv,
            device_id=where, device_id_type=MESH,
        )

    def near_copy(k):
        src = packed_hbm.at[1:3, :, pl.ds(k * pair, pair)]
        return remote(src, near.at[x, k], near_s.at[k], near_r.at[k], x_to)

    def far_copy(k):
        where = {"dev": jnp.where(x == 0, above, below)}
        return remote(near.at[1 - x, k], near.at[x, k], far_s.at[k], far_r.at[k], where)

    give_far = ((x == 0) & not_top) | ((x == 1) & not_bottom)
    have_far = ((x == 0) & not_bottom) | ((x == 1) & not_top)

    early = pairs // 2
    give_side = ((x == 1) & not_top) | ((x == 0) & not_bottom)
    have_side = ((x == 1) & not_bottom) | ((x == 0) & not_top)

    def way_copy(k):
        src = packed_hbm.at[1:3, :, pl.ds(k * pair, pair)]
        where = {"dev": jnp.where(x == 1, above, below)}
        return remote(src, relayed.at[k - early], way_s.at[k - early], way_r.at[k - early], where)

    def side_copy(k):
        return remote(
            relayed.at[k - early], near.at[1 - x, k], side_s.at[k - early], far_r.at[k], x_to
        )

    def piece_rows(which, i):
        return pl.ds(pl.multiple_of(which * share + i * piece, SLOT), piece)

    def wz_copy(line, i, way, src=None):
        dst = column.at[line, piece_rows(group, i)]
        where = {"dev": jnp.where(way == 0, above, below)}
        return remote(
            dst if src is None else src, dst, wz_s.at[line, i, way], wz_r.at[line, i], where
        )

    def own_piece(i):
        return weight_hbm.at[piece_rows(group, i)]

    def wy_copy(line, i, which):
        block = column.at[line, piece_rows(which, i)]
        return remote(block, block, wy_s.at[line, i], wy_r.at[line, i], y_to)

    for k in range(pairs):
        near_copy(k).start()
    for i in range(PIECES):

        @pl.when(not_top)
        def _():
            wz_copy(z, i, 0, own_piece(i)).start()

        @pl.when(not_bottom)
        def _():
            wz_copy(z, i, 1, own_piece(i)).start()

    @pl.when(give_side)
    def _():
        for k in range(early, pairs):
            way_copy(k).start()

    start_weights()

    @pl.when(jnp.logical_not(have_far))
    def _():
        near[x] = jnp.zeros_like(near[x])

    def way_of(line):
        return jnp.where(line < z, 0, 1)

    def more(line):
        return jnp.where(line < z, not_top, not_bottom)

    def busy(line):
        return jnp.where(line < z, x == 0, x == 1)

    def distance(line):
        return jnp.abs(line - z)

    def take(line, onward, pieces=range(PIECES)):
        for i in pieces:
            wz_copy(line, i, way_of(line)).wait_recv()

            @pl.when(onward)
            def _():
                wz_copy(line, i, way_of(line)).start()

            wy_copy(line, i, group).start()

    def take_next(only_busy, pieces):
        for line in near_lines:

            @pl.when((distance(line) == 1) & (busy(line) if only_busy else jnp.logical_not(busy(line))))
            def _():
                take(line, more(line), pieces)

    take_next(True, range(PIECES // 2))
    take_next(False, range(PIECES // 2))
    for k in range(early):
        near_copy(k).wait_recv()

        @pl.when(give_far)
        def _():
            far_copy(k).start()

    take_next(True, range(PIECES // 2, PIECES))
    take_next(False, range(PIECES // 2, PIECES))

    @pl.when(have_side)
    def _():
        for k in range(early, pairs):
            way_copy(k).wait_recv()
            side_copy(k).start()

    for k in range(early, pairs):
        near_copy(k).wait_recv()
    for i in range(6):
        own_copy(i).wait()

    row = lax.broadcasted_iota(jnp.int32, (count, count), 0)
    col = lax.broadcasted_iota(jnp.int32, (count, count), 1)
    see_before = (col >= row) & (me > 0)
    see_after = (col <= row) & (me < devices - 1)

    def mix_copy(k):
        lanes = pl.ds(k * pair, pair)
        return remote(
            mixed.at[:, lanes], mixed_in.at[:, lanes], mix_s.at[k], mix_r.at[k], x_to
        )

    for k in range(pairs):

        @pl.when(have_far)
        def _():
            far_copy(k).wait_recv()

        for h in range(pair // HEAD):
            lanes = slice(k * pair + h * HEAD, k * pair + (h + 1) * HEAD)
            inner = slice(h * HEAD, (h + 1) * HEAD)
            query = packed[0, :, lanes]

            def score(keys):
                return lax.dot_general(
                    query, keys, (((1,), (1,)), ((), ())), preferred_element_type=jnp.float32
                ) / math.sqrt(HEAD)

            scores = jnp.concatenate(
                [
                    jnp.where(see_before, score(near[0, k, 0, :, inner]), NEG),
                    score(packed[1, :, lanes]),
                    jnp.where(see_after, score(near[1, k, 0, :, inner]), NEG),
                ],
                axis=1,
            )
            top = jnp.max(scores, -1, keepdims=True)
            weight = jnp.exp(scores - top)
            weight = (weight / jnp.sum(weight, -1, keepdims=True)).astype(jnp.bfloat16)
            values = jnp.concatenate(
                [near[0, k, 1, :, inner], packed[2, :, lanes], near[1, k, 1, :, inner]], axis=0
            )
            mixed[:, lanes] = jnp.dot(
                weight, values, preferred_element_type=jnp.float32
            ).astype(jnp.bfloat16)
        mix_copy(k).start()
        if k + 1 == early:
            for line in near_lines:

                @pl.when(distance(line) == 2)
                def _():
                    take(line, more(line))

    last = near_lines[-1]
    far_last = distance(last) > 2

    @pl.when(far_last)
    def _():
        take(last, more(last))

    for k in range(pairs):
        mix_copy(k).wait_recv()

    def place_of(which):
        return group if which == 0 else 1 - group

    def sum_copy(line, which):
        place = place_of(which)
        return remote(
            mine_out.at[line, place], their_out.at[line, place],
            sum_s.at[line, which], sum_r.at[line, which], core_to,
        )

    def back_copy(line, which):
        place = place_of(which)
        return remote(
            sent_back.at[line, place], got_back.at[line, place],
            back_s.at[line, which], back_r.at[line, which], x_to,
        )

    def share_copy(line, which):
        place = place_of(which)
        return remote(
            got_back.at[line, place], their_back.at[line, place],
            share_s.at[line, which], share_r.at[line, which], core_to,
        )

    def direct_copy(which):
        place = place_of(which)
        return remote(
            sent_back.at[last, place], their_back.at[last, place],
            share_s.at[last, which], share_r.at[last, which],
            {"dev": z * COLS + (1 - x), "sub": 1 - part},
        )

    def project(line, which, direct=False):
        place = place_of(which)
        block = column[line, pl.ds(pl.multiple_of(place * share, SLOT), share), :]
        both = jnp.concatenate([mixed_in[...], mixed[...]], axis=0)
        product = lax.dot_general(
            both, block, (((1,), (1,)), ((), ())), preferred_element_type=jnp.float32
        )
        sent_back[line, place] = product[:count].astype(jnp.bfloat16)
        back_copy(line, which).start()
        if direct:
            direct_copy(which).start()
        mine_out[line, place] = product[count:]
        sum_copy(line, which).start()

    def halves_in(line):
        for n in range(PIECES):
            wy_copy(line, n, 1 - group).wait_recv()

    def last_step():
        halves_in(last)
        project(last, 1, True)

    def add_up(line, which):
        place = place_of(which)
        sum_copy(line, which).wait_recv()
        share_copy(line, which).wait_recv()
        partial = jnp.zeros((count, share), jnp.float32)
        for column_of, total in (
            (x, mine_out[line, place] + their_out[line, place]),
            (
                1 - x,
                got_back[line, place].astype(jnp.float32)
                + their_back[line, place].astype(jnp.float32),
            ),
        ):
            start = (line * COLS + column_of) * shard + place * share
            lanes = pl.ds(pl.multiple_of(start, LANES), share)
            value = tokens[:, lanes].astype(jnp.float32) + (1.0 + modulation[0:1, lanes]) * total
            state[:, lanes] = value
            partial = partial + value * value
        return partial

    steps = [(line, which) for line in [z] + near_lines[:-1] for which in range(2)]
    project(z, 0)
    project(z, 1)
    for line in near_lines[:-1]:
        project(line, 0)
        halves_in(line)
        project(line, 1)
    project(last, 0, True)

    @pl.when(jnp.logical_not(far_last))
    def _():
        last_step()

    for line, which in steps:
        back_copy(line, which).wait_recv()
        share_copy(line, which).start()
    squares = jnp.zeros((count, share), jnp.float32)
    for line, which in steps:
        squares = squares + add_up(line, which)

    @pl.when(far_last)
    def _():
        last_step()

    for which in range(2):
        back_copy(last, which).wait_recv()
        squares = squares + add_up(last, which)
    square = jnp.sum(squares, -1, keepdims=True)
    scale = lax.rsqrt(square / width + EPS)
    for s in range(devices):
        lanes = slice(s * shard, (s + 1) * shard)
        normed[:, lanes] = (
            state[:, lanes] * scale * (1.0 + modulation[2:3, lanes]) + modulation[1:2, lanes]
        ).astype(jnp.bfloat16)
    logits = lax.dot_general(
        router[...], normed[...], (((1,), (1,)), ((), ())), preferred_element_type=jnp.float32
    )
    name = lax.broadcasted_iota(jnp.int32, logits.shape, 0)
    named = name == ids[0:1]
    for k in range(1, ids.shape[0]):
        named = named | (name == ids[k:k + 1])
    lifted = jnp.where(named, jax.nn.sigmoid(logits), 0.0)
    meta[...] = lifted / jnp.sum(lifted, 0, keepdims=True)

    for k in range(pairs):
        near_copy(k).wait_send()
        mix_copy(k).wait_send()

        if k < early:

            @pl.when(give_far)
            def _():
                far_copy(k).wait_send()
        else:

            @pl.when(give_side)
            def _():
                way_copy(k).wait_send()

            @pl.when(have_side)
            def _():
                side_copy(k).wait_send()

    for i in range(PIECES):

        @pl.when(not_top)
        def _():
            wz_copy(z, i, 0, own_piece(i)).wait_send()

        @pl.when(not_bottom)
        def _():
            wz_copy(z, i, 1, own_piece(i)).wait_send()

        for line in near_lines:

            @pl.when(more(line))
            def _():
                wz_copy(line, i, way_of(line)).wait_send()

            wy_copy(line, i, group).wait_send()
    for line, which in steps + [(last, 0), (last, 1)]:
        sum_copy(line, which).wait_send()
        back_copy(line, which).wait_send()
        share_copy(line, which).wait_send()


def block_kernel(devices, *refs):
    sources, gate_up, down, out = refs[:6], refs[6], refs[7], refs[8]
    held, normed, state, meta, wide = refs[9:14], refs[14], refs[15], refs[16], refs[17]
    front_buffers, expert_buffers = refs[18:28], refs[28:44]
    own_sem, gu_sem, dn_sem = refs[44:47]
    front_sems, expert_sems = refs[47:66], refs[66:]
    gu, dn = expert_buffers[5:7]
    squeeze, grow = expert_buffers[13:15]
    halves = gate_up.shape[0]

    def weight_copies(h):
        return (
            pltpu.make_async_copy(gate_up.at[h], gu.at[h], gu_sem.at[h]),
            pltpu.make_async_copy(down.at[h], dn.at[h], dn_sem.at[h]),
        )

    def start_weights():
        def one(h, carry):
            for copy in weight_copies(h):
                copy.start()
            return carry

        lax.fori_loop(0, halves, one, 0)
        for ref, axis in ((squeeze, 0), (grow, 1)):
            packed = lax.broadcasted_iota(jnp.int32, ref.shape, axis)
            slot = lax.broadcasted_iota(jnp.int32, ref.shape, 1 - axis)
            inner = slot & (SLOT - 1)
            same = (packed == (slot - inner) // SLOT * CAP + inner) & (inner < CAP)
            ref[...] = jnp.where(same, 1.0, 0.0).astype(jnp.bfloat16)

    front_kernel(
        devices, start_weights, sources, held, own_sem, normed, state, meta,
        *front_buffers, *front_sems,
    )
    expert_kernel(
        devices, weight_copies, normed, meta, state, held[2], wide, out,
        *expert_buffers, *expert_sems,
    )


def block_call(
    tokens, query_key_value, out_weight, modulation, router_weight, expert_ids,
    gate_up_weight, down_weight,
):
    devices = lax.axis_size("dev")
    count, width = tokens.shape
    half = down_weight.shape[2]
    halves = gate_up_weight.shape[0]
    local = halves // 2
    gate_up_weight = gate_up_weight.swapaxes(2, 3)
    hidden = gate_up_weight.shape[2]
    lines = devices // COLS
    rows = devices * SLOT
    slots, pack = local * SLOT, local * CAP
    part = half // CHUNKS
    shard = out_weight.shape[0]
    own = (
        tokens, query_key_value.transpose(1, 0, 2), out_weight, modulation,
        router_weight.T, expert_ids.T,
    )
    hbm = pl.BlockSpec(memory_space=pl.ANY)
    dma = pltpu.SemaphoreType.DMA
    return pl.pallas_call(
        functools.partial(block_kernel, devices),
        out_shape=jax.ShapeDtypeStruct((count, half), jnp.bfloat16),
        in_specs=[hbm] * 8,
        out_specs=pl.BlockSpec(memory_space=pltpu.VMEM),
        scratch_shapes=[
            *[pltpu.VMEM(own[i].shape, own[i].dtype) for i in (0, 1, 3, 4, 5)],
            pltpu.VMEM((count, width), jnp.bfloat16),
            pltpu.VMEM((count, width), jnp.float32),
            pltpu.VMEM((router_weight.shape[1], count), jnp.float32),
            pltpu.VMEM((devices, slots + pack, half), jnp.bfloat16),
            pltpu.VMEM((2, CHUNKS, 2, count, part), jnp.bfloat16),
            pltpu.VMEM((CHUNKS // 2, 2, count, part), jnp.bfloat16),
            pltpu.VMEM((lines, shard, half), jnp.bfloat16),
            pltpu.VMEM((count, half), jnp.bfloat16),
            pltpu.VMEM((count, half), jnp.bfloat16),
            pltpu.VMEM((lines, 2, count, shard // 2), jnp.float32),
            pltpu.VMEM((lines, 2, count, shard // 2), jnp.float32),
            pltpu.VMEM((lines, 2, count, shard // 2), jnp.bfloat16),
            pltpu.VMEM((lines, 2, count, shard // 2), jnp.bfloat16),
            pltpu.VMEM((lines, 2, count, shard // 2), jnp.bfloat16),
            pltpu.VMEM((lines, CHUNKS, count, part), jnp.bfloat16),
            pltpu.VMEM((lines, CHUNKS, pack, part), jnp.bfloat16),
            pltpu.VMEM((lines, CHUNKS, pack, part), jnp.bfloat16),
            pltpu.VMEM((2, lines, CHUNKS, count, part), jnp.bfloat16),
            pltpu.VMEM((2, CHUNKS, local, rows, part), jnp.bfloat16),
            pltpu.VMEM(gate_up_weight.shape, jnp.bfloat16),
            pltpu.VMEM(down_weight.shape, jnp.bfloat16),
            pltpu.VMEM((local, 4 * hidden, rows), jnp.float32),
            pltpu.VMEM((local, 2 * hidden, rows), jnp.bfloat16),
            pltpu.VMEM((local, 2 * hidden, rows), jnp.bfloat16),
            pltpu.VMEM((lines, COLS * local, count), jnp.float32),
            pltpu.VMEM((lines, slots + pack, count), jnp.bfloat16),
            pltpu.VMEM((lines, slots + pack, count), jnp.bfloat16),
            pltpu.VMEM((pack, slots), jnp.bfloat16),
            pltpu.VMEM((slots, pack), jnp.bfloat16),
            pltpu.VMEM((count, part), jnp.float32),
            dma((6,)), dma((halves,)), dma((halves,)),
            dma((CHUNKS,)), dma((CHUNKS,)), dma((CHUNKS,)), dma((CHUNKS,)),
            dma((CHUNKS // 2,)), dma((CHUNKS // 2,)), dma((CHUNKS // 2,)),
            dma((lines, PIECES, 2)), dma((lines, PIECES)),
            dma((lines, PIECES)), dma((lines, PIECES)), dma((CHUNKS,)), dma((CHUNKS,)),
            dma((lines, 2)), dma((lines, 2)), dma((lines, 2)), dma((lines, 2)),
            dma((lines, 2)), dma((lines, 2)),
            dma((lines,)), dma((lines,)),
            dma((lines, CHUNKS, 2)), dma((lines, CHUNKS)),
            dma((lines, CHUNKS)), dma((lines, CHUNKS)),
            dma((devices, CHUNKS)), dma((devices, CHUNKS)),
            dma((local,)), dma((local,)),
            dma((lines, CHUNKS)), dma((lines, CHUNKS)),
            dma((lines, CHUNKS)), dma((2, lines, CHUNKS)),
        ],
        compiler_params=pltpu.CompilerParams(
            collective_id=1, has_side_effects=True, vmem_limit_bytes=VMEM_BYTES
        ),
    )(*own, gate_up_weight, down_weight)


def body(
    tokens,
    query_key_value,
    out_weight,
    modulation,
    router_weight,
    expert_ids,
    gate_up_weight,
    down_weight,
):
    count = tokens.shape[0]
    width = tokens.shape[1]
    parts = lax.axis_size("sub")
    part = lax.axis_index("sub")
    position = lax.axis_index("dev")
    devices = lax.axis_size("dev")
    total = count * devices
    local_width = query_key_value.shape[2]
    weight_bytes = 2 * (gate_up_weight.size + down_weight.size)
    token_bytes = 12 * devices * count * width
    fits = weight_bytes + token_bytes < VMEM_BYTES and CAP <= SLOT
    paired = parts == 2 and lax.axis_size("groups") == 2 and devices % COLS == 0
    experts_here = gate_up_weight.shape[0] // 2
    tiled = out_weight.shape[0] % (2 * LANES) == 0 and count == LANES
    tiled = tiled and down_weight.shape[2] // CHUNKS % HEAD == 0 and devices == 4 * COLS
    tiled = tiled and down_weight.shape[2] % (2 * CHUNKS * LANES) == 0 and experts_here == devices
    tiled = tiled and SLOT * devices == LANES
    tiled = tiled and gate_up_weight.shape[3] % 64 == 0
    if fits and paired and tiled:
        return block_call(
            tokens, query_key_value, out_weight, modulation, router_weight, expert_ids,
            gate_up_weight, down_weight,
        )
    heads_here = local_width // HEAD
    query = query_key_value[:, 0].reshape(count, heads_here, HEAD)
    pair = query_key_value[:, 1:]
    near = extended(pair, (("dev", 0),), count)
    keys = near[:, 0].reshape(3 * count, heads_here, HEAD)
    values = near[:, 1].reshape(3 * count, heads_here, HEAD)
    mixed = window_attention(query, keys, values, position, total).reshape(count, local_width)
    partial_proj = lax.dot_general(
        mixed,
        lax.all_gather(out_weight, "dev", axis=0, tiled=True),
        (((1,), (1,)), ((), ())),
        preferred_element_type=jnp.float32,
    )
    proj = lax.psum(partial_proj, "sub")
    state = tokens.astype(jnp.float32) + (1.0 + modulation[0]) * proj
    normed = normalize(state, modulation)
    gates = route(normed, router_weight, expert_ids)
    experts = router_weight.shape[1]
    topk = expert_ids.shape[1]
    flat = expert_ids.reshape(-1)
    picks = flat.shape[0]
    onehot = (flat[:, None] == jnp.arange(experts, dtype=jnp.int32)[None, :]).astype(jnp.int32)
    rank = jnp.sum((jnp.cumsum(onehot, 0) - 1) * onehot, 1)
    target = flat * CAP + rank
    hit = target[None, :] == jnp.arange(experts * CAP, dtype=jnp.int32)[:, None]
    filled = jnp.any(hit, 1)
    anchor = jnp.sum(jnp.where(hit, jnp.arange(picks, dtype=jnp.int32)[None, :], 0), 1) // topk
    slice_width = width // parts
    sent = lax.dynamic_slice_in_dim(normed, part * slice_width, slice_width, 1)
    sent_width = sent.shape[1]
    rows_out = jnp.where(filled[:, None], sent[anchor], jnp.zeros((), jnp.bfloat16))
    halves_here = gate_up_weight.shape[0]
    doubled = jnp.broadcast_to(
        rows_out.reshape(experts, 1, CAP, sent_width), (experts, 2, CAP, sent_width)
    )
    outgoing = doubled.reshape(devices, halves_here, CAP, sent_width)
    up_form = "sxcd,xgdf->sxcgf"
    down_form = "sxcf,xfd->sxcd"
    incoming = lax.all_to_all(outgoing, "dev", split_axis=0, concat_axis=0, tiled=True)
    both = jnp.einsum(
        up_form,
        lax.all_gather(incoming, "sub", axis=3, tiled=True),
        gate_up_weight,
        preferred_element_type=jnp.float32,
    )
    hidden = (jax.nn.silu(both[..., 0, :]) * both[..., 1, :]).astype(jnp.bfloat16)
    gathered = lax.all_gather(hidden, "sub", axis=hidden.ndim - 1, tiled=True)
    result = jnp.einsum(down_form, gathered, down_weight, preferred_element_type=jnp.float32)
    returned = lax.all_to_all(
        result.astype(jnp.bfloat16), "dev", split_axis=0, concat_axis=0, tiled=True
    )
    own_width = returned.shape[-1]
    arranged = returned.reshape(experts, 2, CAP, own_width)
    answers = arranged[flat, :, rank, :].reshape(count, topk, 2, own_width).astype(jnp.float32)
    combined = answers[:, :, 0] + answers[:, :, 1]
    routed = jnp.einsum("tk,tkd->td", gates, combined)
    own = lax.dynamic_slice_in_dim(state, part * slice_width, slice_width, 1)
    lift = lax.dynamic_slice_in_dim(modulation[3], part * slice_width, slice_width, 0)
    return (own + (1.0 + lift) * routed).astype(jnp.bfloat16)


def solution(mesh):
    return jax.shard_map(
        body,
        mesh=mesh,
        in_specs=(
            P(("groups", "dev"), None),
            P(("groups", "dev"), None, "sub"),
            P("dev", "sub"),
            P("groups", None),
            P(),
            P(("groups", "dev"), None),
            P("dev", None, None, "sub"),
            P("dev", None, "sub"),
        ),
        out_specs=P(("groups", "dev"), "sub"),
        check_vma=False,
    )
```

```python
import functools
import math

import jax
import jax.numpy as jnp
from jax import lax
from jax.experimental import pallas as pl
from jax.experimental.pallas import tpu as pltpu
from jax.sharding import PartitionSpec as P

HEAD = 128
CAP = 12


EPS = 1e-06
NEG = -1e30


def extended(cells, sides, width):
    for axis, dim in sides:
        count = lax.axis_size(axis)
        ends = count - 1
        head = lax.slice_in_dim(cells, 0, width, axis=dim)
        tail = lax.slice_in_dim(cells, cells.shape[dim] - width, cells.shape[dim], axis=dim)
        cells = jnp.concatenate(
            [
                lax.ppermute(tail, axis, [(i, (i + 1) % count) for i in range(ends)]),
                cells,
                lax.ppermute(head, axis, [((i + 1) % count, i) for i in range(ends)]),
            ],
            axis=dim,
        )
    return cells


def window_attention(query, keys, values, index, total):
    count = query.shape[0]
    rows = jnp.arange(count, dtype=jnp.int32)[:, None]
    cols = jnp.arange(3 * count, dtype=jnp.int32)[None, :] - count
    place = index * count + cols
    allowed = (jnp.abs(cols - rows) <= count) & (place >= 0) & (place < total)
    scores = jnp.einsum(
        "qhd,khd->hqk", query, keys, preferred_element_type=jnp.float32
    ) / math.sqrt(query.shape[2])
    scores = jnp.where(allowed[None], scores, NEG)
    top = jnp.max(scores, -1, keepdims=True)
    weight = jnp.exp(scores - top)
    weight = (weight / jnp.sum(weight, -1, keepdims=True)).astype(jnp.bfloat16)
    mixed = jnp.einsum("hqk,khd->qhd", weight, values, preferred_element_type=jnp.float32)
    return mixed.astype(jnp.bfloat16)


def normalize(state, modulation):
    scale = lax.rsqrt(jnp.mean(state * state, -1, keepdims=True) + EPS)
    return (state * scale * (1.0 + modulation[2]) + modulation[1]).astype(jnp.bfloat16)


def route(normed, router_weight, expert_ids):
    logits = jnp.dot(normed, router_weight, preferred_element_type=jnp.float32)
    experts = router_weight.shape[1]
    match = expert_ids[:, :, None] == jnp.arange(experts, dtype=jnp.int32)[None, None, :]
    picked = jnp.sum(jnp.where(match, logits[:, None, :], 0.0), -1)
    lifted = jax.nn.sigmoid(picked)
    return lifted / jnp.sum(lifted, -1, keepdims=True)


LANES = 128
SLOT = 16
COLS = 2
CHUNKS = 4
PIECES = 4
LAG = 2
PAIR = 256
VMEM_BYTES = 66 * 1000 * 1000
MESH = pl.DeviceIdType.MESH


def choose(index, table):
    value = jnp.int32(table[0])
    for i in range(1, len(table)):
        value = jnp.where(index == i, table[i], value)
    return value


def line_order(lines, nearest, inner=False):
    rows = []
    for z in range(lines):
        lower = (z < lines - 1 - z) != inner
        others = [line for line in range(lines) if line != z]
        sign = 1 if nearest else -1
        rows.append(sorted(others, key=lambda line: (sign * abs(line - z), (line > z) == lower)))
    return [[rows[z][j] for z in range(lines)] for j in range(lines - 1)]


def expert_kernel(
    devices, weight_copies,
    normed, meta, state, modulation, wide,
    out,
    tok, got_packed, got_rows, got_sum, disp, gu, dn, raised, hid_own, hid_other,
    got_meta, pick, gated, squeeze, grow, acc,
    meta_s, meta_r, z_s, z_r, x_s, x_r, core_s, core_r, hid_s, hid_r, rx_s, rx_r, rz_s, rz_r,
):
    me = lax.axis_index("dev")
    part = lax.axis_index("sub")
    other = 1 - part
    z = me // COLS
    x = me % COLS
    lines = devices // COLS
    count, width = normed.shape
    half = width // 2
    local = hid_own.shape[0]
    hidden = gu.shape[2]
    slots = local * SLOT
    pack = local * CAP
    rows = devices * SLOT
    chunks, wide_chunk = tok.shape[1], tok.shape[3]

    def remote(src, dst, send, recv, where):
        return pltpu.make_async_remote_copy(
            src_ref=src, dst_ref=dst, send_sem=send, recv_sem=recv,
            device_id=where, device_id_type=MESH,
        )

    above = jnp.minimum(me + COLS, devices - 1)
    below = jnp.maximum(me - COLS, 0)
    x_to = {"dev": z * COLS + (1 - x)}
    core_to = {"sub": other}
    not_top = z < lines - 1
    not_bottom = z > 0
    near_lines = [choose(z, table) for table in line_order(lines, True, True)]
    far_lines = [choose(z, table) for table in line_order(lines, False)]

    def lanes_of(c):
        return pl.ds(pl.multiple_of(c * wide_chunk, wide_chunk), wide_chunk)

    def own_lanes(c):
        return pl.ds(pl.multiple_of(part * half + c * wide_chunk, wide_chunk), wide_chunk)

    def slot_rows(s):
        return pl.ds(pl.multiple_of(s * SLOT, SLOT), SLOT)

    def meta_copy(line):
        return remote(
            meta.at[pl.ds(pl.multiple_of(line * COLS * local, COLS * local), COLS * local)],
            got_meta.at[z], meta_s.at[line], meta_r.at[z], {"dev": line * COLS + x},
        )

    def meta_arrival(line):
        return remote(got_meta.at[line], got_meta.at[line], meta_s.at[line], meta_r.at[line], x_to)

    def z_copy(line, c, way, src=None):
        dst = tok.at[line, c]
        where = {"dev": jnp.where(way == 0, above, below)}
        return remote(
            dst if src is None else src, dst, z_s.at[line, c, way], z_r.at[line, c], where
        )

    def packed_out(line, c):
        return wide.at[line, pl.ds(slots, pack), lanes_of(c)]

    def x_copy(line, c):
        return remote(
            packed_out(line, c), got_packed.at[line, c], x_s.at[line, c], x_r.at[line, c], x_to
        )

    def core_copy(which, s, c):
        place = disp.at[which, c, :, slot_rows(s), :]
        return remote(place, place, core_s.at[s, c], core_r.at[s, c], core_to)

    def own_send(c):
        src = normed.at[:, own_lanes(c)]

        @pl.when(not_top)
        def _():
            z_copy(z, c, 0, src).start()

        @pl.when(not_bottom)
        def _():
            z_copy(z, c, 1, src).start()

    own_send(0)
    for line in near_lines:
        meta_copy(line).start()
    for c in range(1, chunks):
        own_send(c)

    before = (
        lax.broadcasted_iota(jnp.int32, (count, count), 0)
        < lax.broadcasted_iota(jnp.int32, (count, count), 1)
    ).astype(jnp.float32).astype(jnp.bfloat16)
    place = lax.broadcasted_iota(jnp.int32, (local, SLOT, count), 1).astype(jnp.float32)

    def routing(line, ours, theirs):
        for first, gate in ((True, ours), (False, theirs)):
            chosen = jnp.where(gate > 0.0, 1.0, 0.0)
            rank = jnp.dot(chosen.astype(jnp.bfloat16), before, preferred_element_type=jnp.float32)
            rank = jnp.where(gate > 0.0, rank, -1.0)
            hit = jnp.broadcast_to(rank[:, None, :], place.shape) == place
            one = jnp.where(hit, 1.0, 0.0).reshape(slots, count).astype(jnp.bfloat16)
            value = jnp.where(hit, jnp.broadcast_to(gate[:, None, :], place.shape), 0.0)
            value = value.reshape(slots, count).astype(jnp.bfloat16)
            if first:
                pick[line, :slots] = one
                gated[line, :slots] = value
            else:
                pick[line, slots:] = jnp.dot(
                    squeeze[...], one, preferred_element_type=jnp.float32
                ).astype(jnp.bfloat16)
                gated[line, slots:] = jnp.dot(
                    squeeze[...], value, preferred_element_type=jnp.float32
                ).astype(jnp.bfloat16)

    def expert_rows(base, column):
        return pl.ds(pl.multiple_of(base + column * local, local), local)

    def spread(line, c, block):
        moved = jnp.dot(pick[line], block, preferred_element_type=jnp.float32).astype(jnp.bfloat16)
        s = line * COLS + x
        wide[line, slots:slots + pack, lanes_of(c)] = moved[slots:]
        x_copy(line, c).start()
        disp[part, c, :, slot_rows(s), :] = moved[:slots].reshape(local, SLOT, wide_chunk)
        core_copy(part, s, c).start()

    def own_step(c):
        spread(z, c, normed[:, own_lanes(c)])

    def line_step(line, c):
        low = line < z

        @pl.when(c == 0)
        def _():
            meta_arrival(line).wait_recv()
            routing(
                line, got_meta[line, expert_rows(0, x)], got_meta[line, expert_rows(0, 1 - x)]
            )

        way = jnp.where(low, 0, 1)
        z_copy(line, c, way).wait_recv()

        @pl.when(jnp.where(low, not_top, not_bottom))
        def _():
            z_copy(line, c, way).start()

        spread(line, c, tok[line, c])

    def x_step(line, c):
        x_copy(line, c).wait_recv()
        s = line * COLS + (1 - x)
        disp[part, c, :, slot_rows(s), :] = jnp.dot(
            grow[...], got_packed[line, c], preferred_element_type=jnp.float32
        ).astype(jnp.bfloat16).reshape(local, SLOT, wide_chunk)
        core_copy(part, s, c).start()

    def across_rows(left, right):
        return lax.dot_general(
            left, right, (((1,), (1,)), ((), ())), preferred_element_type=jnp.float32
        )

    def raise_side(e, side):
        sums = []
        for g in range(2):
            for b in range(2):
                total = None
                for c in range(chunks):
                    start = side * half + c * wide_chunk
                    piece = across_rows(
                        gu[2 * e + b, g, :, start:start + wide_chunk], disp[side, c, e]
                    )
                    total = piece if total is None else total + piece
                sums.append(total)
        return sums

    def raise_first(e, carry):
        for n, total in enumerate(raise_side(e, 1)):
            raised[e, n * hidden:(n + 1) * hidden] = total
        return carry

    def raise_second(e, carry):
        sums = [
            total + raised[e, n * hidden:(n + 1) * hidden]
            for n, total in enumerate(raise_side(e, 0))
        ]
        for b in range(2):
            gate = sums[b]
            hid_own[e, b * hidden:(b + 1) * hidden] = (
                gate * jax.nn.sigmoid(gate) * sums[2 + b]
            ).astype(jnp.bfloat16)
        hid_copy(e).start()
        return carry

    def hid_copy(e):
        return remote(hid_own.at[e], hid_other.at[e], hid_s.at[e], hid_r.at[e], core_to)

    def arrived():
        for c in range(chunks):
            for s in range(devices):
                core_copy(other, s, c).wait_recv()

    routing(
        z, meta[expert_rows(z * COLS * local, x)], meta[expert_rows(z * COLS * local, 1 - x)]
    )
    for c in range(chunks):
        own_step(c)

    def weight_wait(h, carry):
        for copy in weight_copies(h):
            copy.wait()
        return carry

    lax.fori_loop(0, 2 * local, weight_wait, 0)

    def step(t, carry):
        for line in near_lines:
            c = t - (jnp.abs(line - z) - 1) * chunks

            @pl.when((c >= 0) & (c < chunks))
            def _():
                line_step(line, c)

        @pl.when((t >= 1) & (t < 1 + chunks))
        def _():
            x_step(z, t - 1)

        for line in near_lines:
            c = t - LAG - (jnp.abs(line - z) - 1) * chunks

            @pl.when((c >= 0) & (c < chunks))
            def _():
                x_step(line, c)

        return carry

    span = chunks * (lines - 1) + LAG
    lax.fori_loop(0, span - 2, step, 0)
    first, second = local * 3 // 8, local * 5 // 8

    def early_raise(start, stop):
        @pl.when(part == 0)
        def _():
            if start == 0:
                arrived()
            lax.fori_loop(start, stop, raise_first, 0)

    early_raise(0, first)
    step(span - 2, 0)
    early_raise(first, second)
    step(span - 1, 0)
    early_raise(second, local)

    @pl.when(part == 1)
    def _():
        lax.fori_loop(0, local, raise_first, 0)
        arrived()

    lax.fori_loop(0, local, raise_second, 0)

    group = 2 * wide_chunk

    def lower(g):
        lanes = slice(g * group, (g + 1) * group)

        def one(e, carry):
            if g == 0:
                hid_copy(e).wait_recv()
            mine = pl.ds(pl.multiple_of(part * hidden, SLOT), hidden)
            theirs = pl.ds(pl.multiple_of(other * hidden, SLOT), hidden)
            left = jnp.concatenate([hid_own[e], hid_other[e]], axis=0)
            right = jnp.concatenate(
                [dn[2 * e, mine, lanes], dn[2 * e + 1, mine, lanes],
                 dn[2 * e, theirs, lanes], dn[2 * e + 1, theirs, lanes]], axis=0
            )
            wide[e, :rows, lanes] = lax.dot_general(
                left, right, (((0,), (0,)), ((), ())), preferred_element_type=jnp.float32
            ).astype(jnp.bfloat16)
            return carry

        lax.fori_loop(0, local, one, 0)

    def result_rows(s, q):
        return wide[:local, slot_rows(s), lanes_of(q)].reshape(slots, wide_chunk)

    def rx_copy(line, q):
        return remote(
            wide.at[lines + line, pl.ds(slots, pack), lanes_of(q)], got_rows.at[line, q],
            rx_s.at[line, q], rx_r.at[line, q], x_to,
        )

    def rz_copy(line, q, way):
        where = {"dev": jnp.where(way == 0, above, below)}
        return remote(
            tok.at[line, q], got_sum.at[way, line, q],
            rz_s.at[line, q], rz_r.at[way, line, q], where,
        )

    def give(line, q):
        packed = jnp.dot(
            squeeze[...], result_rows(line * COLS + (1 - x), q), preferred_element_type=jnp.float32
        )
        wide[lines + line, slots:slots + pack, lanes_of(q)] = packed.astype(jnp.bfloat16)
        rx_copy(line, q).start()

    def gather_here(line, q):
        rx_copy(line, q).wait_recv()
        pieces = jnp.concatenate([result_rows(line * COLS + x, q), got_rows[line, q]], axis=0)
        acc[...] = lax.dot_general(
            gated[line], pieces, (((0,), (0,)), ((), ())), preferred_element_type=jnp.float32
        )

    def add_line(line, q, way):
        rz_copy(line, q, way).wait_recv()
        acc[...] += got_sum[way, line, q].astype(jnp.float32)

    def pass_on(line, q):
        gather_here(line, q)
        way = jnp.where(line > z, 0, 1)

        @pl.when(jnp.where(line > z, not_bottom, not_top))
        def _():
            add_line(line, q, way)

        tok[line, q] = acc[...].astype(jnp.bfloat16)
        rz_copy(line, q, way).start()

    for g in range(half // group):
        lower(g)
        for q in range(2 * g, 2 * g + 2):
            give(far_lines[0], q)
    def give_all(line):
        lax.fori_loop(0, chunks, lambda q, carry: (give(line, q), carry)[1], 0)

    for line in near_lines:
        low = line < z

        @pl.when(jnp.where(low, not_top, not_bottom))
        def _():
            for c in range(chunks):
                z_copy(line, c, jnp.where(low, 0, 1)).wait_send()

    far_end = (z == 0) | (z == lines - 1)

    @pl.when(far_end)
    def _():
        for q in range(2):
            pass_on(far_lines[0], q)

    give_all(far_lines[1])

    @pl.when(far_end)
    def _():
        for q in range(2, chunks):
            pass_on(far_lines[0], q)

    for line in far_lines[2:] + [z]:
        give_all(line)

    @pl.when(jnp.logical_not(far_end))
    def _():
        for q in range(chunks):
            pass_on(far_lines[0], q)

    for line in far_lines[1:]:
        lax.fori_loop(0, chunks, lambda q, carry, line=line: (pass_on(line, q), carry)[1], 0)
    for q in range(chunks):
        gather_here(z, q)

        @pl.when(not_bottom)
        def _():
            add_line(z, q, 0)

        @pl.when(not_top)
        def _():
            add_line(z, q, 1)

        own = own_lanes(q)
        lanes = slice(q * wide_chunk, (q + 1) * wide_chunk)
        out[:, lanes] = (
            state[:, own] + (1.0 + modulation[3:4, own]) * acc[...]
        ).astype(out.dtype)

    for c in range(chunks):

        @pl.when(not_top)
        def _():
            z_copy(z, c, 0, normed.at[:, own_lanes(c)]).wait_send()

        @pl.when(not_bottom)
        def _():
            z_copy(z, c, 1, normed.at[:, own_lanes(c)]).wait_send()

        for line in near_lines:
            rz_copy(line, c, jnp.where(line > z, 0, 1)).wait_send()
        for line in range(lines):
            x_copy(line, c).wait_send()
            rx_copy(line, c).wait_send()
        for s in range(devices):
            core_copy(part, s, c).wait_send()
    for line in near_lines:
        meta_copy(line).wait_send()

    def hid_drain(e, carry):
        hid_copy(e).wait_send()
        return carry

    lax.fori_loop(0, local, hid_drain, 0)


def front_kernel(
    devices, start_weights,
    sources, held, own_sem,
    normed, state, meta,
    window, queries, column, mixed, mine_out, their_out, sent_back, got_back, their_back,
    pair_s, pair_r, query_s, query_r, early_s, late_s, edge_r, wz_s, wz_r, wy_s, wy_r, mix_s, mix_r,
    sum_s, sum_r, back_s, back_r, share_s, share_r,
):
    packed_hbm, weight_hbm = sources[1], sources[2]
    tokens, modulation, router, ids = held
    me = lax.axis_index("dev")
    part = lax.axis_index("sub")
    group = lax.axis_index("groups")
    z = me // COLS
    x = me % COLS
    lines = devices // COLS
    count, width = tokens.shape
    shard = column.shape[1]
    share = shard // 2
    piece = share // PIECES
    heads = window.shape[3]
    pairs = heads // PAIR
    ours = pl.ds(pl.multiple_of(x * heads, heads), heads)
    theirs = pl.ds(pl.multiple_of((1 - x) * heads, heads), heads)
    own_parts = (
        (packed_hbm.at[1:3, :, ours], window.at[1 + x]), (packed_hbm.at[0, :, ours], queries.at[x]),
        (weight_hbm, column.at[z]), (sources[0], tokens), (sources[3], modulation),
        (sources[4], router), (sources[5], ids),
    )

    def own_copy(i):
        return pltpu.make_async_copy(*own_parts[i], own_sem.at[i])

    for i in range(len(own_parts)):
        own_copy(i).start()
    not_top = z < lines - 1
    not_bottom = z > 0
    above = jnp.minimum(me + COLS, devices - 1)
    below = jnp.maximum(me - COLS, 0)
    x_to = {"dev": z * COLS + (1 - x)}
    y_to = {"groups": 1 - group}
    core_to = {"sub": 1 - part}
    near_lines = [choose(z, table) for table in line_order(lines, True)]

    barrier = pltpu.get_barrier_semaphore()

    def greet(where):
        pl.semaphore_signal(barrier, inc=1, device_id=where, device_id_type=MESH)

    for where in (x_to, y_to, core_to, {**x_to, **core_to}):
        greet(where)
    for line in near_lines:
        greet({"dev": line * COLS + x})
    pl.semaphore_wait(barrier, lines + 3)

    def remote(src, dst, send, recv, where):
        return pltpu.make_async_remote_copy(
            src_ref=src, dst_ref=dst, send_sem=send, recv_sem=recv,
            device_id=where, device_id_type=MESH,
        )

    def part_lanes(base, k):
        return pl.ds(pl.multiple_of(base * heads + k * PAIR, PAIR), PAIR)

    def pair_copy(k):
        return remote(
            packed_hbm.at[1:3, :, part_lanes(1 - x, k)], window.at[1 + x, :, :, part_lanes(0, k)],
            pair_s.at[k], pair_r.at[k], x_to,
        )

    def query_copy():
        return remote(
            packed_hbm.at[0, :, theirs], queries.at[x], query_s.at[0], query_r.at[0], x_to
        )

    def edge_copy(k, up, src, send):
        where = {"dev": jnp.where(up, above, below)}
        place = jnp.where(up, 0, 3)
        return remote(
            src, window.at[place, :, :, part_lanes(0, k)], send,
            edge_r.at[jnp.where(up, 0, 1), k], where,
        )

    def early_copy(k):
        return edge_copy(k, x == 1, packed_hbm.at[1:3, :, part_lanes(x, k)], early_s.at[k])

    def late_copy(k):
        return edge_copy(k, x == 0, window.at[2 - x, :, :, part_lanes(0, k)], late_s.at[k])

    give_late = ((x == 0) & not_top) | ((x == 1) & not_bottom)
    give_early = ((x == 1) & not_top) | ((x == 0) & not_bottom)

    def piece_rows(which, i):
        return pl.ds(pl.multiple_of(which * share + i * piece, SLOT), piece)

    def wz_copy(line, i, way, src=None):
        dst = column.at[line, piece_rows(group, i)]
        where = {"dev": jnp.where(way == 0, above, below)}
        return remote(
            dst if src is None else src, dst, wz_s.at[line, i, way], wz_r.at[line, i], where
        )

    def own_piece(i):
        return weight_hbm.at[piece_rows(group, i)]

    def wy_copy(line, i, which):
        block = column.at[line, piece_rows(which, i)]
        return remote(block, block, wy_s.at[line, i], wy_r.at[line, i], y_to)

    for k in range(pairs):
        pair_copy(k).start()
    query_copy().start()

    def send_pieces(pieces):
        for i in pieces:

            @pl.when(not_top)
            def _():
                wz_copy(z, i, 0, own_piece(i)).start()

            @pl.when(not_bottom)
            def _():
                wz_copy(z, i, 1, own_piece(i)).start()

    send_pieces(range(PIECES // 2))

    @pl.when(give_early)
    def _():
        for k in range(pairs):
            early_copy(k).start()

    send_pieces(range(PIECES // 2, PIECES))
    start_weights()

    @pl.when(jnp.logical_not(not_bottom))
    def _():
        window[0] = jnp.zeros_like(window[0])

    @pl.when(jnp.logical_not(not_top))
    def _():
        window[3] = jnp.zeros_like(window[3])

    def way_of(line):
        return jnp.where(line < z, 0, 1)

    def more(line):
        return jnp.where(line < z, not_top, not_bottom)

    def busy(line):
        return jnp.where(line < z, x == 0, x == 1)

    def distance(line):
        return jnp.abs(line - z)

    def take(line, onward, pieces=range(PIECES)):
        for i in pieces:
            wz_copy(line, i, way_of(line)).wait_recv()

            @pl.when(onward)
            def _():
                wz_copy(line, i, way_of(line)).start()

            wy_copy(line, i, group).start()

    def take_next(only_busy, pieces):
        for line in near_lines:

            @pl.when((distance(line) == 1) & (busy(line) if only_busy else jnp.logical_not(busy(line))))
            def _():
                take(line, more(line), pieces)

    for k in range(pairs):
        pair_copy(k).wait_recv()

        @pl.when(give_late)
        def _():
            late_copy(k).start()

    take_next(True, range(PIECES // 2))
    take_next(False, range(PIECES // 2))
    for i in range(len(own_parts)):
        own_copy(i).wait()
    query_copy().wait_recv()

    row = lax.broadcasted_iota(jnp.int32, (count, count), 0)
    col = lax.broadcasted_iota(jnp.int32, (count, count), 1)

    def mix_copy(b, k):
        block = mixed.at[pl.ds(pl.multiple_of(b * count, count), count), part_lanes(x, k)]
        return remote(block, block, mix_s.at[b, k], mix_r.at[b, k], x_to)

    def attend(b, k):
        see_before = (col >= row) & ((z > 0) | (b == 1))
        see_after = (col <= row) & ((z < lines - 1) | (b == 0))
        for h in range(PAIR // HEAD):
            inner = slice(k * PAIR + h * HEAD, k * PAIR + (h + 1) * HEAD)
            query = queries[b, :, inner]

            def score(keys):
                return lax.dot_general(
                    query, keys, (((1,), (1,)), ((), ())), preferred_element_type=jnp.float32
                ) / math.sqrt(HEAD)

            scores = jnp.concatenate(
                [
                    jnp.where(see_before, score(window[b, 0, :, inner]), NEG),
                    score(window[b + 1, 0, :, inner]),
                    jnp.where(see_after, score(window[b + 2, 0, :, inner]), NEG),
                ],
                axis=1,
            )
            top = jnp.max(scores, -1, keepdims=True)
            weight = jnp.exp(scores - top)
            weight = (weight / jnp.sum(weight, -1, keepdims=True)).astype(jnp.bfloat16)
            values = jnp.concatenate([window[b + n, 1, :, inner] for n in range(3)], axis=0)
            lanes = pl.ds(
                pl.multiple_of(x * heads + k * PAIR + h * HEAD, HEAD), HEAD
            )
            mixed[pl.ds(pl.multiple_of(b * count, count), count), lanes] = jnp.dot(
                weight, values, preferred_element_type=jnp.float32
            ).astype(jnp.bfloat16)
        mix_copy(b, k).start()

    for b, up in ((1 - x, x == 1), (x, x == 0)):
        for k in range(pairs):

            @pl.when(jnp.where(up, not_bottom, not_top))
            def _():
                edge_copy(k, up, window.at[0, :, :, part_lanes(0, k)], early_s.at[k]).wait_recv()

            attend(b, k)
        if b is not x:
            take_next(True, range(PIECES // 2, PIECES))
            take_next(False, range(PIECES // 2, PIECES))
        else:
            for line in near_lines:

                @pl.when(distance(line) == 2)
                def _():
                    take(line, more(line))

    last = near_lines[-1]
    far_last = distance(last) > 2

    def take_last(pieces):
        @pl.when(far_last)
        def _():
            take(last, more(last), pieces)

    for b in range(COLS):
        for k in range(pairs):
            mix_copy(b, k).wait_recv()

    def place_of(which):
        return group if which == 0 else 1 - group

    def sum_copy(line, which):
        place = place_of(which)
        return remote(
            mine_out.at[line, place], their_out.at[line, place],
            sum_s.at[line, which], sum_r.at[line, which], core_to,
        )

    def back_copy(line, which):
        place = place_of(which)
        return remote(
            sent_back.at[line, place], got_back.at[line, place],
            back_s.at[line, which], back_r.at[line, which], x_to,
        )

    def share_copy(line, which):
        place = place_of(which)
        return remote(
            got_back.at[line, place], their_back.at[line, place],
            share_s.at[line, which], share_r.at[line, which], core_to,
        )

    def direct_copy(which):
        place = place_of(which)
        return remote(
            sent_back.at[last, place], their_back.at[last, place],
            share_s.at[last, which], share_r.at[last, which],
            {"dev": z * COLS + (1 - x), "sub": 1 - part},
        )

    def project(line, which, direct=False):
        place = place_of(which)
        block = column[line, pl.ds(pl.multiple_of(place * share, SLOT), share), :]
        both = jnp.concatenate(
            [mixed[pl.ds(pl.multiple_of(b * count, count), count), :] for b in (1 - x, x)], axis=0
        )
        product = lax.dot_general(
            both, block, (((1,), (1,)), ((), ())), preferred_element_type=jnp.float32
        )
        sent_back[line, place] = product[:count].astype(jnp.bfloat16)
        back_copy(line, which).start()
        if direct:
            direct_copy(which).start()
        mine_out[line, place] = product[count:]
        sum_copy(line, which).start()

    def halves_in(line):
        for n in range(PIECES):
            wy_copy(line, n, 1 - group).wait_recv()

    def last_step():
        halves_in(last)
        project(last, 1, True)

    def add_up(line, which):
        place = place_of(which)
        sum_copy(line, which).wait_recv()
        share_copy(line, which).wait_recv()
        partial = jnp.zeros((count, share), jnp.float32)
        for column_of, total in (
            (x, mine_out[line, place] + their_out[line, place]),
            (
                1 - x,
                got_back[line, place].astype(jnp.float32)
                + their_back[line, place].astype(jnp.float32),
            ),
        ):
            start = (line * COLS + column_of) * shard + place * share
            lanes = pl.ds(pl.multiple_of(start, LANES), share)
            value = tokens[:, lanes].astype(jnp.float32) + (1.0 + modulation[0:1, lanes]) * total
            state[:, lanes] = value
            partial = partial + value * value
        return partial

    steps = [(line, which) for line in [z] + near_lines[:-1] for which in range(2)]
    quarter = PIECES // 4
    for i, (line, which) in enumerate(steps):
        if which == 1 and i > 1:
            halves_in(line)
        project(line, which)
        if i < 4:
            take_last(range(i * quarter, (i + 1) * quarter))
    project(last, 0, True)

    @pl.when(jnp.logical_not(far_last))
    def _():
        last_step()

    for line, which in steps:
        back_copy(line, which).wait_recv()
        share_copy(line, which).start()
    squares = jnp.zeros((count, share), jnp.float32)
    for line, which in steps:
        squares = squares + add_up(line, which)

    @pl.when(far_last)
    def _():
        last_step()

    for which in range(2):
        back_copy(last, which).wait_recv()
        squares = squares + add_up(last, which)
    square = jnp.sum(squares, -1, keepdims=True)
    scale = lax.rsqrt(square / width + EPS)
    for s in range(devices):
        lanes = slice(s * shard, (s + 1) * shard)
        normed[:, lanes] = (
            state[:, lanes] * scale * (1.0 + modulation[2:3, lanes]) + modulation[1:2, lanes]
        ).astype(jnp.bfloat16)
    logits = lax.dot_general(
        router[...], normed[...], (((1,), (1,)), ((), ())), preferred_element_type=jnp.float32
    )
    name = lax.broadcasted_iota(jnp.int32, logits.shape, 0)
    named = name == ids[0:1]
    for k in range(1, ids.shape[0]):
        named = named | (name == ids[k:k + 1])
    lifted = jnp.where(named, jax.nn.sigmoid(logits), 0.0)
    meta[...] = lifted / jnp.sum(lifted, 0, keepdims=True)

    query_copy().wait_send()
    for k in range(pairs):
        pair_copy(k).wait_send()
        for b in range(COLS):
            mix_copy(b, k).wait_send()

        @pl.when(give_early)
        def _():
            early_copy(k).wait_send()

        @pl.when(give_late)
        def _():
            late_copy(k).wait_send()

    for i in range(PIECES):

        @pl.when(not_top)
        def _():
            wz_copy(z, i, 0, own_piece(i)).wait_send()

        @pl.when(not_bottom)
        def _():
            wz_copy(z, i, 1, own_piece(i)).wait_send()

        for line in near_lines:

            @pl.when(more(line))
            def _():
                wz_copy(line, i, way_of(line)).wait_send()

            wy_copy(line, i, group).wait_send()
    for line, which in steps + [(last, 0), (last, 1)]:
        sum_copy(line, which).wait_send()
        back_copy(line, which).wait_send()
        share_copy(line, which).wait_send()


def block_kernel(devices, *refs):
    sources, gate_up, down, out = refs[:6], refs[6], refs[7], refs[8]
    held, normed, state, meta, wide = refs[9:13], refs[13], refs[14], refs[15], refs[16]
    front_buffers, expert_buffers = refs[17:26], refs[26:42]
    own_sem, gu_sem, dn_sem = refs[42:45]
    front_sems, expert_sems = refs[45:64], refs[64:]
    gu, dn = expert_buffers[5:7]
    squeeze, grow = expert_buffers[13:15]
    halves = gate_up.shape[0]

    def weight_copies(h):
        return (
            pltpu.make_async_copy(gate_up.at[h], gu.at[h], gu_sem.at[h]),
            pltpu.make_async_copy(down.at[h], dn.at[h], dn_sem.at[h]),
        )

    def start_weights():
        def one(h, carry):
            for copy in weight_copies(h):
                copy.start()
            return carry

        lax.fori_loop(0, halves, one, 0)
        for ref, axis in ((squeeze, 0), (grow, 1)):
            packed = lax.broadcasted_iota(jnp.int32, ref.shape, axis)
            slot = lax.broadcasted_iota(jnp.int32, ref.shape, 1 - axis)
            inner = slot & (SLOT - 1)
            same = (packed == (slot - inner) // SLOT * CAP + inner) & (inner < CAP)
            ref[...] = jnp.where(same, 1.0, 0.0).astype(jnp.bfloat16)

    front_kernel(
        devices, start_weights, sources, held, own_sem, normed, state, meta,
        *front_buffers, *front_sems,
    )
    expert_kernel(
        devices, weight_copies, normed, meta, state, held[1], wide, out,
        *expert_buffers, *expert_sems,
    )


def block_call(
    tokens, query_key_value, out_weight, modulation, router_weight, expert_ids,
    gate_up_weight, down_weight,
):
    devices = lax.axis_size("dev")
    count, width = tokens.shape
    half = down_weight.shape[2]
    halves = gate_up_weight.shape[0]
    local = halves // 2
    gate_up_weight = gate_up_weight.swapaxes(2, 3)
    hidden = gate_up_weight.shape[2]
    lines = devices // COLS
    rows = devices * SLOT
    slots, pack = local * SLOT, local * CAP
    part = half // CHUNKS
    shard = out_weight.shape[0]
    own = (
        tokens, query_key_value.transpose(1, 0, 2), out_weight, modulation,
        router_weight.T, expert_ids.T,
    )
    hbm = pl.BlockSpec(memory_space=pl.ANY)
    dma = pltpu.SemaphoreType.DMA
    return pl.pallas_call(
        functools.partial(block_kernel, devices),
        out_shape=jax.ShapeDtypeStruct((count, half), jnp.bfloat16),
        in_specs=[hbm] * 8,
        out_specs=pl.BlockSpec(memory_space=pltpu.VMEM),
        scratch_shapes=[
            *[pltpu.VMEM(own[i].shape, own[i].dtype) for i in (0, 3, 4, 5)],
            pltpu.VMEM((count, width), jnp.bfloat16),
            pltpu.VMEM((count, width), jnp.float32),
            pltpu.VMEM((router_weight.shape[1], count), jnp.float32),
            pltpu.VMEM((devices, slots + pack, half), jnp.bfloat16),
            pltpu.VMEM((4, 2, count, half // 2), jnp.bfloat16),
            pltpu.VMEM((COLS, count, half // 2), jnp.bfloat16),
            pltpu.VMEM((lines, shard, half), jnp.bfloat16),
            pltpu.VMEM((COLS * count, half), jnp.bfloat16),
            pltpu.VMEM((lines, 2, count, shard // 2), jnp.float32),
            pltpu.VMEM((lines, 2, count, shard // 2), jnp.float32),
            pltpu.VMEM((lines, 2, count, shard // 2), jnp.bfloat16),
            pltpu.VMEM((lines, 2, count, shard // 2), jnp.bfloat16),
            pltpu.VMEM((lines, 2, count, shard // 2), jnp.bfloat16),
            pltpu.VMEM((lines, CHUNKS, count, part), jnp.bfloat16),
            pltpu.VMEM((lines, CHUNKS, pack, part), jnp.bfloat16),
            pltpu.VMEM((lines, CHUNKS, pack, part), jnp.bfloat16),
            pltpu.VMEM((2, lines, CHUNKS, count, part), jnp.bfloat16),
            pltpu.VMEM((2, CHUNKS, local, rows, part), jnp.bfloat16),
            pltpu.VMEM(gate_up_weight.shape, jnp.bfloat16),
            pltpu.VMEM(down_weight.shape, jnp.bfloat16),
            pltpu.VMEM((local, 4 * hidden, rows), jnp.float32),
            pltpu.VMEM((local, 2 * hidden, rows), jnp.bfloat16),
            pltpu.VMEM((local, 2 * hidden, rows), jnp.bfloat16),
            pltpu.VMEM((lines, COLS * local, count), jnp.float32),
            pltpu.VMEM((lines, slots + pack, count), jnp.bfloat16),
            pltpu.VMEM((lines, slots + pack, count), jnp.bfloat16),
            pltpu.VMEM((pack, slots), jnp.bfloat16),
            pltpu.VMEM((slots, pack), jnp.bfloat16),
            pltpu.VMEM((count, part), jnp.float32),
            dma((7,)), dma((halves,)), dma((halves,)),
            dma((half // 2 // PAIR,)), dma((half // 2 // PAIR,)), dma((1,)), dma((1,)),
            dma((half // 2 // PAIR,)), dma((half // 2 // PAIR,)), dma((2, half // 2 // PAIR)),
            dma((lines, PIECES, 2)), dma((lines, PIECES)),
            dma((lines, PIECES)), dma((lines, PIECES)),
            dma((COLS, half // 2 // PAIR)), dma((COLS, half // 2 // PAIR)),
            dma((lines, 2)), dma((lines, 2)), dma((lines, 2)), dma((lines, 2)),
            dma((lines, 2)), dma((lines, 2)),
            dma((lines,)), dma((lines,)),
            dma((lines, CHUNKS, 2)), dma((lines, CHUNKS)),
            dma((lines, CHUNKS)), dma((lines, CHUNKS)),
            dma((devices, CHUNKS)), dma((devices, CHUNKS)),
            dma((local,)), dma((local,)),
            dma((lines, CHUNKS)), dma((lines, CHUNKS)),
            dma((lines, CHUNKS)), dma((2, lines, CHUNKS)),
        ],
        compiler_params=pltpu.CompilerParams(
            collective_id=1, has_side_effects=True, vmem_limit_bytes=VMEM_BYTES
        ),
    )(*own, gate_up_weight, down_weight)


def body(
    tokens,
    query_key_value,
    out_weight,
    modulation,
    router_weight,
    expert_ids,
    gate_up_weight,
    down_weight,
):
    count = tokens.shape[0]
    width = tokens.shape[1]
    parts = lax.axis_size("sub")
    part = lax.axis_index("sub")
    position = lax.axis_index("dev")
    devices = lax.axis_size("dev")
    total = count * devices
    local_width = query_key_value.shape[2]
    weight_bytes = 2 * (gate_up_weight.size + down_weight.size)
    token_bytes = 12 * devices * count * width
    fits = weight_bytes + token_bytes < VMEM_BYTES and CAP <= SLOT
    paired = parts == 2 and lax.axis_size("groups") == 2 and devices % COLS == 0
    experts_here = gate_up_weight.shape[0] // 2
    tiled = out_weight.shape[0] % (2 * LANES) == 0 and count == LANES
    tiled = tiled and down_weight.shape[2] % (2 * PAIR) == 0 and devices == 4 * COLS
    tiled = tiled and down_weight.shape[2] % (2 * CHUNKS * LANES) == 0 and experts_here == devices
    tiled = tiled and SLOT * devices == LANES
    tiled = tiled and gate_up_weight.shape[3] % 64 == 0
    if fits and paired and tiled:
        return block_call(
            tokens, query_key_value, out_weight, modulation, router_weight, expert_ids,
            gate_up_weight, down_weight,
        )
    heads_here = local_width // HEAD
    query = query_key_value[:, 0].reshape(count, heads_here, HEAD)
    pair = query_key_value[:, 1:]
    near = extended(pair, (("dev", 0),), count)
    keys = near[:, 0].reshape(3 * count, heads_here, HEAD)
    values = near[:, 1].reshape(3 * count, heads_here, HEAD)
    mixed = window_attention(query, keys, values, position, total).reshape(count, local_width)
    partial_proj = lax.dot_general(
        mixed,
        lax.all_gather(out_weight, "dev", axis=0, tiled=True),
        (((1,), (1,)), ((), ())),
        preferred_element_type=jnp.float32,
    )
    proj = lax.psum(partial_proj, "sub")
    state = tokens.astype(jnp.float32) + (1.0 + modulation[0]) * proj
    normed = normalize(state, modulation)
    gates = route(normed, router_weight, expert_ids)
    experts = router_weight.shape[1]
    topk = expert_ids.shape[1]
    flat = expert_ids.reshape(-1)
    picks = flat.shape[0]
    onehot = (flat[:, None] == jnp.arange(experts, dtype=jnp.int32)[None, :]).astype(jnp.int32)
    rank = jnp.sum((jnp.cumsum(onehot, 0) - 1) * onehot, 1)
    target = flat * CAP + rank
    hit = target[None, :] == jnp.arange(experts * CAP, dtype=jnp.int32)[:, None]
    filled = jnp.any(hit, 1)
    anchor = jnp.sum(jnp.where(hit, jnp.arange(picks, dtype=jnp.int32)[None, :], 0), 1) // topk
    slice_width = width // parts
    sent = lax.dynamic_slice_in_dim(normed, part * slice_width, slice_width, 1)
    sent_width = sent.shape[1]
    rows_out = jnp.where(filled[:, None], sent[anchor], jnp.zeros((), jnp.bfloat16))
    halves_here = gate_up_weight.shape[0]
    doubled = jnp.broadcast_to(
        rows_out.reshape(experts, 1, CAP, sent_width), (experts, 2, CAP, sent_width)
    )
    outgoing = doubled.reshape(devices, halves_here, CAP, sent_width)
    up_form = "sxcd,xgdf->sxcgf"
    down_form = "sxcf,xfd->sxcd"
    incoming = lax.all_to_all(outgoing, "dev", split_axis=0, concat_axis=0, tiled=True)
    both = jnp.einsum(
        up_form,
        lax.all_gather(incoming, "sub", axis=3, tiled=True),
        gate_up_weight,
        preferred_element_type=jnp.float32,
    )
    hidden = (jax.nn.silu(both[..., 0, :]) * both[..., 1, :]).astype(jnp.bfloat16)
    gathered = lax.all_gather(hidden, "sub", axis=hidden.ndim - 1, tiled=True)
    result = jnp.einsum(down_form, gathered, down_weight, preferred_element_type=jnp.float32)
    returned = lax.all_to_all(
        result.astype(jnp.bfloat16), "dev", split_axis=0, concat_axis=0, tiled=True
    )
    own_width = returned.shape[-1]
    arranged = returned.reshape(experts, 2, CAP, own_width)
    answers = arranged[flat, :, rank, :].reshape(count, topk, 2, own_width).astype(jnp.float32)
    combined = answers[:, :, 0] + answers[:, :, 1]
    routed = jnp.einsum("tk,tkd->td", gates, combined)
    own = lax.dynamic_slice_in_dim(state, part * slice_width, slice_width, 1)
    lift = lax.dynamic_slice_in_dim(modulation[3], part * slice_width, slice_width, 0)
    return (own + (1.0 + lift) * routed).astype(jnp.bfloat16)


def solution(mesh):
    return jax.shard_map(
        body,
        mesh=mesh,
        in_specs=(
            P(("groups", "dev"), None),
            P(("groups", "dev"), None, "sub"),
            P("dev", "sub"),
            P("groups", None),
            P(),
            P(("groups", "dev"), None),
            P("dev", None, None, "sub"),
            P("dev", None, "sub"),
        ),
        out_specs=P(("groups", "dev"), "sub"),
        check_vma=False,
    )
```

```python
import functools
import math

import jax
import jax.numpy as jnp
from jax import lax
from jax.experimental import pallas as pl
from jax.experimental.pallas import tpu as pltpu
from jax.sharding import PartitionSpec as P

HEAD = 128
CAP = 12


EPS = 1e-06
NEG = -1e30


def extended(cells, sides, width):
    for axis, dim in sides:
        count = lax.axis_size(axis)
        ends = count - 1
        head = lax.slice_in_dim(cells, 0, width, axis=dim)
        tail = lax.slice_in_dim(cells, cells.shape[dim] - width, cells.shape[dim], axis=dim)
        cells = jnp.concatenate(
            [
                lax.ppermute(tail, axis, [(i, (i + 1) % count) for i in range(ends)]),
                cells,
                lax.ppermute(head, axis, [((i + 1) % count, i) for i in range(ends)]),
            ],
            axis=dim,
        )
    return cells


def window_attention(query, keys, values, index, total):
    count = query.shape[0]
    rows = jnp.arange(count, dtype=jnp.int32)[:, None]
    cols = jnp.arange(3 * count, dtype=jnp.int32)[None, :] - count
    place = index * count + cols
    allowed = (jnp.abs(cols - rows) <= count) & (place >= 0) & (place < total)
    scores = jnp.einsum(
        "qhd,khd->hqk", query, keys, preferred_element_type=jnp.float32
    ) / math.sqrt(query.shape[2])
    scores = jnp.where(allowed[None], scores, NEG)
    top = jnp.max(scores, -1, keepdims=True)
    weight = jnp.exp(scores - top)
    weight = (weight / jnp.sum(weight, -1, keepdims=True)).astype(jnp.bfloat16)
    mixed = jnp.einsum("hqk,khd->qhd", weight, values, preferred_element_type=jnp.float32)
    return mixed.astype(jnp.bfloat16)


def normalize(state, modulation):
    scale = lax.rsqrt(jnp.mean(state * state, -1, keepdims=True) + EPS)
    return (state * scale * (1.0 + modulation[2]) + modulation[1]).astype(jnp.bfloat16)


def route(normed, router_weight, expert_ids):
    logits = jnp.dot(normed, router_weight, preferred_element_type=jnp.float32)
    experts = router_weight.shape[1]
    match = expert_ids[:, :, None] == jnp.arange(experts, dtype=jnp.int32)[None, None, :]
    picked = jnp.sum(jnp.where(match, logits[:, None, :], 0.0), -1)
    lifted = jax.nn.sigmoid(picked)
    return lifted / jnp.sum(lifted, -1, keepdims=True)


LANES = 128
SLOT = 16
COLS = 2
CHUNKS = 4
PIECES = 4
LAG = 2
SPLIT = 2
PAIR = 256
VMEM_BYTES = 66 * 1000 * 1000
MESH = pl.DeviceIdType.MESH


def choose(index, table):
    value = jnp.int32(table[0])
    for i in range(1, len(table)):
        value = jnp.where(index == i, table[i], value)
    return value


def line_order(lines, nearest, inner=False):
    rows = []
    for z in range(lines):
        lower = (z < lines - 1 - z) != inner
        others = [line for line in range(lines) if line != z]
        sign = 1 if nearest else -1
        rows.append(sorted(others, key=lambda line: (sign * abs(line - z), (line > z) == lower)))
    return [[rows[z][j] for z in range(lines)] for j in range(lines - 1)]


def expert_kernel(
    devices, weight_copies,
    normed, meta, state, modulation, wide,
    out,
    tok, got_packed, got_rows, got_sum, disp, gu, dn, raised, hid_own, hid_other,
    got_meta, pick, gated, squeeze, grow, acc,
    meta_s, meta_r, z_s, z_r, x_s, x_r, core_s, core_r, hid_s, hid_r, rx_s, rx_r, rz_s, rz_r,
):
    me = lax.axis_index("dev")
    part = lax.axis_index("sub")
    other = 1 - part
    z = me // COLS
    x = me % COLS
    lines = devices // COLS
    count, width = normed.shape
    half = width // 2
    local = hid_own.shape[0]
    hidden = gu.shape[2]
    slots = local * SLOT
    pack = local * CAP
    rows = devices * SLOT
    chunks, wide_chunk = tok.shape[1], tok.shape[3]

    def remote(src, dst, send, recv, where):
        return pltpu.make_async_remote_copy(
            src_ref=src, dst_ref=dst, send_sem=send, recv_sem=recv,
            device_id=where, device_id_type=MESH,
        )

    above = jnp.minimum(me + COLS, devices - 1)
    below = jnp.maximum(me - COLS, 0)
    x_to = {"dev": z * COLS + (1 - x)}
    core_to = {"sub": other}
    not_top = z < lines - 1
    not_bottom = z > 0
    near_lines = [choose(z, table) for table in line_order(lines, True, True)]
    far_lines = [choose(z, table) for table in line_order(lines, False)]

    def lanes_of(c):
        return pl.ds(pl.multiple_of(c * wide_chunk, wide_chunk), wide_chunk)

    def own_lanes(c):
        return pl.ds(pl.multiple_of(part * half + c * wide_chunk, wide_chunk), wide_chunk)

    def slot_rows(s):
        return pl.ds(pl.multiple_of(s * SLOT, SLOT), SLOT)

    def meta_copy(line):
        return remote(
            meta.at[pl.ds(pl.multiple_of(line * COLS * local, COLS * local), COLS * local)],
            got_meta.at[z], meta_s.at[line], meta_r.at[z], {"dev": line * COLS + x},
        )

    def meta_arrival(line):
        return remote(got_meta.at[line], got_meta.at[line], meta_s.at[line], meta_r.at[line], x_to)

    def z_copy(line, c, way, src=None):
        dst = tok.at[line, c]
        where = {"dev": jnp.where(way == 0, above, below)}
        return remote(
            dst if src is None else src, dst, z_s.at[line, c, way], z_r.at[line, c], where
        )

    def packed_out(line, c):
        return wide.at[line, pl.ds(slots, pack), lanes_of(c)]

    def x_copy(line, c):
        return remote(
            packed_out(line, c), got_packed.at[line, c], x_s.at[line, c], x_r.at[line, c], x_to
        )

    def core_copy(which, s, c):
        place = disp.at[which, c, :, slot_rows(s), :]
        return remote(place, place, core_s.at[s, c], core_r.at[s, c], core_to)

    def own_send(c):
        src = normed.at[:, own_lanes(c)]

        @pl.when(not_top)
        def _():
            z_copy(z, c, 0, src).start()

        @pl.when(not_bottom)
        def _():
            z_copy(z, c, 1, src).start()

    own_send(0)
    for line in near_lines:
        meta_copy(line).start()
    for c in range(1, chunks):
        own_send(c)

    before = (
        lax.broadcasted_iota(jnp.int32, (count, count), 0)
        < lax.broadcasted_iota(jnp.int32, (count, count), 1)
    ).astype(jnp.float32).astype(jnp.bfloat16)
    place = lax.broadcasted_iota(jnp.int32, (local, SLOT, count), 1).astype(jnp.float32)

    def routing(line, ours, theirs):
        for first, gate in ((True, ours), (False, theirs)):
            chosen = jnp.where(gate > 0.0, 1.0, 0.0)
            rank = jnp.dot(chosen.astype(jnp.bfloat16), before, preferred_element_type=jnp.float32)
            rank = jnp.where(gate > 0.0, rank, -1.0)
            hit = jnp.broadcast_to(rank[:, None, :], place.shape) == place
            one = jnp.where(hit, 1.0, 0.0).reshape(slots, count).astype(jnp.bfloat16)
            value = jnp.where(hit, jnp.broadcast_to(gate[:, None, :], place.shape), 0.0)
            value = value.reshape(slots, count).astype(jnp.bfloat16)
            if first:
                pick[line, :slots] = one
                gated[line, :slots] = value
            else:
                pick[line, slots:] = jnp.dot(
                    squeeze[...], one, preferred_element_type=jnp.float32
                ).astype(jnp.bfloat16)
                gated[line, slots:] = jnp.dot(
                    squeeze[...], value, preferred_element_type=jnp.float32
                ).astype(jnp.bfloat16)

    def expert_rows(base, column):
        return pl.ds(pl.multiple_of(base + column * local, local), local)

    def spread(line, c, block):
        moved = jnp.dot(pick[line], block, preferred_element_type=jnp.float32).astype(jnp.bfloat16)
        s = line * COLS + x
        wide[line, slots:slots + pack, lanes_of(c)] = moved[slots:]
        x_copy(line, c).start()
        disp[part, c, :, slot_rows(s), :] = moved[:slots].reshape(local, SLOT, wide_chunk)
        core_copy(part, s, c).start()

    def own_step(c):
        spread(z, c, normed[:, own_lanes(c)])

    def line_step(line, c):
        low = line < z

        @pl.when(c == 0)
        def _():
            meta_arrival(line).wait_recv()
            routing(
                line, got_meta[line, expert_rows(0, x)], got_meta[line, expert_rows(0, 1 - x)]
            )

        way = jnp.where(low, 0, 1)
        z_copy(line, c, way).wait_recv()

        @pl.when(jnp.where(low, not_top, not_bottom))
        def _():
            z_copy(line, c, way).start()

        spread(line, c, tok[line, c])

    def x_step(line, c):
        x_copy(line, c).wait_recv()
        s = line * COLS + (1 - x)
        disp[part, c, :, slot_rows(s), :] = jnp.dot(
            grow[...], got_packed[line, c], preferred_element_type=jnp.float32
        ).astype(jnp.bfloat16).reshape(local, SLOT, wide_chunk)
        core_copy(part, s, c).start()

    def across_rows(left, right):
        return lax.dot_general(
            left, right, (((1,), (1,)), ((), ())), preferred_element_type=jnp.float32
        )

    def raise_part(e, parts):
        sums = []
        for g in range(2):
            for b in range(2):
                total = None
                for side, c in parts:
                    start = side * half + c * wide_chunk
                    piece = across_rows(
                        gu[2 * e + b, g, :, start:start + wide_chunk], disp[side, c, e]
                    )
                    total = piece if total is None else total + piece
                sums.append(total)
        return sums

    def raise_some(parts, start, stop, first=False, last=False):
        def one(e, carry):
            sums = raise_part(e, parts)
            if not first:
                sums = [
                    total + raised[e, n * hidden:(n + 1) * hidden] for n, total in enumerate(sums)
                ]
            if not last:
                for n, total in enumerate(sums):
                    raised[e, n * hidden:(n + 1) * hidden] = total
                return carry
            for b in range(2):
                gate = sums[b]
                hid_own[e, b * hidden:(b + 1) * hidden] = (
                    gate * jax.nn.sigmoid(gate) * sums[2 + b]
                ).astype(jnp.bfloat16)
            hid_copy(e).start()
            return carry

        lax.fori_loop(start, stop, one, 0)

    def hid_copy(e):
        return remote(hid_own.at[e], hid_other.at[e], hid_s.at[e], hid_r.at[e], core_to)

    def arrived(parts):
        for c in parts:
            for s in range(devices):
                core_copy(other, s, c).wait_recv()

    routing(
        z, meta[expert_rows(z * COLS * local, x)], meta[expert_rows(z * COLS * local, 1 - x)]
    )
    for c in range(chunks):
        own_step(c)

    def weight_wait(h, carry):
        for copy in weight_copies(h):
            copy.wait()
        return carry

    lax.fori_loop(0, 2 * local, weight_wait, 0)

    offsets = [(jnp.abs(line - z) - 1) * chunks for line in near_lines]
    offsets[1] = jnp.maximum(offsets[1], SPLIT)

    def step(t, carry):
        for line, offset in zip(near_lines, offsets):
            c = t - offset

            @pl.when((c >= 0) & (c < chunks))
            def _():
                line_step(line, c)

        @pl.when((t >= 1) & (t < 1 + chunks))
        def _():
            x_step(z, t - 1)

        for line, offset in zip(near_lines, offsets):
            c = t - LAG - offset

            @pl.when((c >= 0) & (c < chunks))
            def _():
                x_step(line, c)

        return carry

    span = chunks * (lines - 1) + LAG
    lax.fori_loop(0, span - 2, step, 0)
    early = range(SPLIT)
    late = range(SPLIT, chunks)
    own_first = (part == 1) & ((z == 0) | (z == lines - 1))

    @pl.when(own_first)
    def _():
        raise_some([(1, c) for c in early], 0, local, first=True)
        step(span - 2, 0)
        step(span - 1, 0)
        raise_some([(1, c) for c in late], 0, local)
        arrived(range(chunks))
        raise_some([(0, c) for c in range(chunks)], 0, local, last=True)

    @pl.when(jnp.logical_not(own_first))
    def _():
        arrived(early)
        raise_some([(side, c) for c in early for side in range(2)], 0, local // 2, first=True)
        step(span - 2, 0)
        step(span - 1, 0)
        raise_some([(side, c) for c in early for side in range(2)], local // 2, local, first=True)
        arrived(late)
        raise_some([(side, c) for c in late for side in range(2)], 0, local, last=True)

    group = 2 * wide_chunk

    def lower(g):
        lanes = slice(g * group, (g + 1) * group)

        def one(e, carry):
            if g == 0:
                hid_copy(e).wait_recv()
            mine = pl.ds(pl.multiple_of(part * hidden, SLOT), hidden)
            theirs = pl.ds(pl.multiple_of(other * hidden, SLOT), hidden)
            left = jnp.concatenate([hid_own[e], hid_other[e]], axis=0)
            right = jnp.concatenate(
                [dn[2 * e, mine, lanes], dn[2 * e + 1, mine, lanes],
                 dn[2 * e, theirs, lanes], dn[2 * e + 1, theirs, lanes]], axis=0
            )
            wide[e, :rows, lanes] = lax.dot_general(
                left, right, (((0,), (0,)), ((), ())), preferred_element_type=jnp.float32
            ).astype(jnp.bfloat16)
            return carry

        lax.fori_loop(0, local, one, 0)

    def result_rows(s, q):
        return wide[:local, slot_rows(s), lanes_of(q)].reshape(slots, wide_chunk)

    def rx_copy(line, q):
        return remote(
            wide.at[lines + line, pl.ds(slots, pack), lanes_of(q)], got_rows.at[line, q],
            rx_s.at[line, q], rx_r.at[line, q], x_to,
        )

    def rz_copy(line, q, way):
        where = {"dev": jnp.where(way == 0, above, below)}
        return remote(
            tok.at[line, q], got_sum.at[way, line, q],
            rz_s.at[line, q], rz_r.at[way, line, q], where,
        )

    def give(line, q):
        packed = jnp.dot(
            squeeze[...], result_rows(line * COLS + (1 - x), q), preferred_element_type=jnp.float32
        )
        wide[lines + line, slots:slots + pack, lanes_of(q)] = packed.astype(jnp.bfloat16)
        rx_copy(line, q).start()

    def gather_here(line, q):
        rx_copy(line, q).wait_recv()
        pieces = jnp.concatenate([result_rows(line * COLS + x, q), got_rows[line, q]], axis=0)
        acc[...] = lax.dot_general(
            gated[line], pieces, (((0,), (0,)), ((), ())), preferred_element_type=jnp.float32
        )

    def add_line(line, q, way):
        rz_copy(line, q, way).wait_recv()
        acc[...] += got_sum[way, line, q].astype(jnp.float32)

    def pass_on(line, q):
        gather_here(line, q)
        way = jnp.where(line > z, 0, 1)

        @pl.when(jnp.where(line > z, not_bottom, not_top))
        def _():
            add_line(line, q, way)

        tok[line, q] = acc[...].astype(jnp.bfloat16)
        rz_copy(line, q, way).start()

    for g in range(half // group):
        lower(g)
        for q in range(2 * g, 2 * g + 2):
            give(far_lines[0], q)
    def give_all(line):
        lax.fori_loop(0, chunks, lambda q, carry: (give(line, q), carry)[1], 0)

    for line in near_lines:
        low = line < z

        @pl.when(jnp.where(low, not_top, not_bottom))
        def _():
            for c in range(chunks):
                z_copy(line, c, jnp.where(low, 0, 1)).wait_send()

    far_end = (z == 0) | (z == lines - 1)

    @pl.when(far_end)
    def _():
        for q in range(2):
            pass_on(far_lines[0], q)

    give_all(far_lines[1])

    @pl.when(far_end)
    def _():
        for q in range(2, chunks):
            pass_on(far_lines[0], q)

    for line in far_lines[2:] + [z]:
        give_all(line)

    @pl.when(jnp.logical_not(far_end))
    def _():
        for q in range(chunks):
            pass_on(far_lines[0], q)

    for line in far_lines[1:]:
        lax.fori_loop(0, chunks, lambda q, carry, line=line: (pass_on(line, q), carry)[1], 0)
    for q in range(chunks):
        gather_here(z, q)

        @pl.when(not_bottom)
        def _():
            add_line(z, q, 0)

        @pl.when(not_top)
        def _():
            add_line(z, q, 1)

        own = own_lanes(q)
        lanes = slice(q * wide_chunk, (q + 1) * wide_chunk)
        out[:, lanes] = (
            state[:, own] + (1.0 + modulation[3:4, own]) * acc[...]
        ).astype(out.dtype)

    for c in range(chunks):

        @pl.when(not_top)
        def _():
            z_copy(z, c, 0, normed.at[:, own_lanes(c)]).wait_send()

        @pl.when(not_bottom)
        def _():
            z_copy(z, c, 1, normed.at[:, own_lanes(c)]).wait_send()

        for line in near_lines:
            rz_copy(line, c, jnp.where(line > z, 0, 1)).wait_send()
        for line in range(lines):
            x_copy(line, c).wait_send()
            rx_copy(line, c).wait_send()
        for s in range(devices):
            core_copy(part, s, c).wait_send()
    for line in near_lines:
        meta_copy(line).wait_send()

    def hid_drain(e, carry):
        hid_copy(e).wait_send()
        return carry

    lax.fori_loop(0, local, hid_drain, 0)


def front_kernel(
    devices, start_weights,
    sources, held, own_sem,
    normed, state, meta,
    window, queries, column, mixed, mine_out, their_out, sent_back, got_back, their_back,
    pair_s, pair_r, query_s, query_r, early_s, late_s, edge_r, wz_s, wz_r, wy_s, wy_r, mix_s, mix_r,
    sum_s, sum_r, back_s, back_r, share_s, share_r,
):
    packed_hbm, weight_hbm = sources[1], sources[2]
    tokens, modulation, router, ids = held
    me = lax.axis_index("dev")
    part = lax.axis_index("sub")
    group = lax.axis_index("groups")
    z = me // COLS
    x = me % COLS
    lines = devices // COLS
    count, width = tokens.shape
    shard = column.shape[1]
    share = shard // 2
    piece = share // PIECES
    heads = window.shape[3]
    pairs = heads // PAIR
    ours = pl.ds(pl.multiple_of(x * heads, heads), heads)
    theirs = pl.ds(pl.multiple_of((1 - x) * heads, heads), heads)
    own_parts = (
        (packed_hbm.at[1:3, :, ours], window.at[1 + x]), (packed_hbm.at[0, :, ours], queries.at[x]),
        (weight_hbm, column.at[z]), (sources[0], tokens), (sources[3], modulation),
        (sources[4], router), (sources[5], ids),
    )

    def own_copy(i):
        return pltpu.make_async_copy(*own_parts[i], own_sem.at[i])

    for i in range(len(own_parts)):
        own_copy(i).start()
    not_top = z < lines - 1
    not_bottom = z > 0
    above = jnp.minimum(me + COLS, devices - 1)
    below = jnp.maximum(me - COLS, 0)
    x_to = {"dev": z * COLS + (1 - x)}
    y_to = {"groups": 1 - group}
    core_to = {"sub": 1 - part}
    near_lines = [choose(z, table) for table in line_order(lines, True)]

    barrier = pltpu.get_barrier_semaphore()

    def greet(where):
        pl.semaphore_signal(barrier, inc=1, device_id=where, device_id_type=MESH)

    for where in (x_to, y_to, core_to, {**x_to, **core_to}):
        greet(where)
    for line in near_lines:
        greet({"dev": line * COLS + x})
    pl.semaphore_wait(barrier, lines + 3)

    def remote(src, dst, send, recv, where):
        return pltpu.make_async_remote_copy(
            src_ref=src, dst_ref=dst, send_sem=send, recv_sem=recv,
            device_id=where, device_id_type=MESH,
        )

    def part_lanes(base, k):
        return pl.ds(pl.multiple_of(base * heads + k * PAIR, PAIR), PAIR)

    def pair_copy(k):
        return remote(
            packed_hbm.at[1:3, :, part_lanes(1 - x, k)], window.at[1 + x, :, :, part_lanes(0, k)],
            pair_s.at[k], pair_r.at[k], x_to,
        )

    def query_copy():
        return remote(
            packed_hbm.at[0, :, theirs], queries.at[x], query_s.at[0], query_r.at[0], x_to
        )

    def edge_copy(k, up, src, send):
        where = {"dev": jnp.where(up, above, below)}
        place = jnp.where(up, 0, 3)
        return remote(
            src, window.at[place, :, :, part_lanes(0, k)], send,
            edge_r.at[jnp.where(up, 0, 1), k], where,
        )

    def early_copy(k):
        return edge_copy(k, x == 1, packed_hbm.at[1:3, :, part_lanes(x, k)], early_s.at[k])

    def late_copy(k):
        return edge_copy(k, x == 0, window.at[2 - x, :, :, part_lanes(0, k)], late_s.at[k])

    give_late = ((x == 0) & not_top) | ((x == 1) & not_bottom)
    give_early = ((x == 1) & not_top) | ((x == 0) & not_bottom)

    def piece_rows(which, i):
        return pl.ds(pl.multiple_of(which * share + i * piece, SLOT), piece)

    def wz_copy(line, i, way, src=None):
        dst = column.at[line, piece_rows(group, i)]
        where = {"dev": jnp.where(way == 0, above, below)}
        return remote(
            dst if src is None else src, dst, wz_s.at[line, i, way], wz_r.at[line, i], where
        )

    def own_piece(i):
        return weight_hbm.at[piece_rows(group, i)]

    def wy_copy(line, i, which):
        block = column.at[line, piece_rows(which, i)]
        return remote(block, block, wy_s.at[line, i], wy_r.at[line, i], y_to)

    for k in range(pairs):
        pair_copy(k).start()
    query_copy().start()

    def send_pieces(pieces):
        for i in pieces:

            @pl.when(not_top)
            def _():
                wz_copy(z, i, 0, own_piece(i)).start()

            @pl.when(not_bottom)
            def _():
                wz_copy(z, i, 1, own_piece(i)).start()

    send_pieces(range(PIECES // 2))

    @pl.when(give_early)
    def _():
        for k in range(pairs):
            early_copy(k).start()

    send_pieces(range(PIECES // 2, PIECES))
    start_weights()

    @pl.when(jnp.logical_not(not_bottom))
    def _():
        window[0] = jnp.zeros_like(window[0])

    @pl.when(jnp.logical_not(not_top))
    def _():
        window[3] = jnp.zeros_like(window[3])

    def way_of(line):
        return jnp.where(line < z, 0, 1)

    def more(line):
        return jnp.where(line < z, not_top, not_bottom)

    def busy(line):
        return jnp.where(line < z, x == 0, x == 1)

    def distance(line):
        return jnp.abs(line - z)

    def take(line, onward, pieces=range(PIECES)):
        for i in pieces:
            wz_copy(line, i, way_of(line)).wait_recv()

            @pl.when(onward)
            def _():
                wz_copy(line, i, way_of(line)).start()

            wy_copy(line, i, group).start()

    def take_next(only_busy, pieces):
        for line in near_lines:

            @pl.when((distance(line) == 1) & (busy(line) if only_busy else jnp.logical_not(busy(line))))
            def _():
                take(line, more(line), pieces)

    for k in range(pairs):
        pair_copy(k).wait_recv()

        @pl.when(give_late)
        def _():
            late_copy(k).start()

    take_next(True, range(PIECES // 2))
    take_next(False, range(PIECES // 2))
    for i in range(len(own_parts)):
        own_copy(i).wait()
    query_copy().wait_recv()

    row = lax.broadcasted_iota(jnp.int32, (count, count), 0)
    col = lax.broadcasted_iota(jnp.int32, (count, count), 1)

    def mix_copy(b, k):
        block = mixed.at[pl.ds(pl.multiple_of(b * count, count), count), part_lanes(x, k)]
        return remote(block, block, mix_s.at[b, k], mix_r.at[b, k], x_to)

    def attend(b, k):
        see_before = (col >= row) & ((z > 0) | (b == 1))
        see_after = (col <= row) & ((z < lines - 1) | (b == 0))
        for h in range(PAIR // HEAD):
            inner = slice(k * PAIR + h * HEAD, k * PAIR + (h + 1) * HEAD)
            query = queries[b, :, inner]

            def score(keys):
                return lax.dot_general(
                    query, keys, (((1,), (1,)), ((), ())), preferred_element_type=jnp.float32
                ) / math.sqrt(HEAD)

            scores = jnp.concatenate(
                [
                    jnp.where(see_before, score(window[b, 0, :, inner]), NEG),
                    score(window[b + 1, 0, :, inner]),
                    jnp.where(see_after, score(window[b + 2, 0, :, inner]), NEG),
                ],
                axis=1,
            )
            top = jnp.max(scores, -1, keepdims=True)
            weight = jnp.exp(scores - top)
            weight = (weight / jnp.sum(weight, -1, keepdims=True)).astype(jnp.bfloat16)
            values = jnp.concatenate([window[b + n, 1, :, inner] for n in range(3)], axis=0)
            lanes = pl.ds(
                pl.multiple_of(x * heads + k * PAIR + h * HEAD, HEAD), HEAD
            )
            mixed[pl.ds(pl.multiple_of(b * count, count), count), lanes] = jnp.dot(
                weight, values, preferred_element_type=jnp.float32
            ).astype(jnp.bfloat16)
        mix_copy(b, k).start()

    for b, up in ((1 - x, x == 1), (x, x == 0)):
        for k in range(pairs):

            @pl.when(jnp.where(up, not_bottom, not_top))
            def _():
                edge_copy(k, up, window.at[0, :, :, part_lanes(0, k)], early_s.at[k]).wait_recv()

            attend(b, k)
        if b is not x:
            take_next(True, range(PIECES // 2, PIECES))
            take_next(False, range(PIECES // 2, PIECES))
        else:
            for line in near_lines:

                @pl.when(distance(line) == 2)
                def _():
                    take(line, more(line))

    last = near_lines[-1]
    far_last = distance(last) > 2

    def take_last(pieces):
        @pl.when(far_last)
        def _():
            take(last, more(last), pieces)

    for b in range(COLS):
        for k in range(pairs):
            mix_copy(b, k).wait_recv()

    def place_of(which):
        return group if which == 0 else 1 - group

    def sum_copy(line, which):
        place = place_of(which)
        return remote(
            mine_out.at[line, place], their_out.at[line, place],
            sum_s.at[line, which], sum_r.at[line, which], core_to,
        )

    def back_copy(line, which):
        place = place_of(which)
        return remote(
            sent_back.at[line, place], got_back.at[line, place],
            back_s.at[line, which], back_r.at[line, which], x_to,
        )

    def share_copy(line, which):
        place = place_of(which)
        return remote(
            got_back.at[line, place], their_back.at[line, place],
            share_s.at[line, which], share_r.at[line, which], core_to,
        )

    def direct_copy(which):
        place = place_of(which)
        return remote(
            sent_back.at[last, place], their_back.at[last, place],
            share_s.at[last, which], share_r.at[last, which],
            {"dev": z * COLS + (1 - x), "sub": 1 - part},
        )

    def project(line, which, direct=False):
        place = place_of(which)
        block = column[line, pl.ds(pl.multiple_of(place * share, SLOT), share), :]
        both = jnp.concatenate(
            [mixed[pl.ds(pl.multiple_of(b * count, count), count), :] for b in (1 - x, x)], axis=0
        )
        product = lax.dot_general(
            both, block, (((1,), (1,)), ((), ())), preferred_element_type=jnp.float32
        )
        sent_back[line, place] = product[:count].astype(jnp.bfloat16)
        back_copy(line, which).start()
        if direct:
            direct_copy(which).start()
        mine_out[line, place] = product[count:]
        sum_copy(line, which).start()

    def halves_in(line):
        for n in range(PIECES):
            wy_copy(line, n, 1 - group).wait_recv()

    def last_step():
        halves_in(last)
        project(last, 1, True)

    def add_up(line, which):
        place = place_of(which)
        sum_copy(line, which).wait_recv()
        share_copy(line, which).wait_recv()
        partial = jnp.zeros((count, share), jnp.float32)
        for column_of, total in (
            (x, mine_out[line, place] + their_out[line, place]),
            (
                1 - x,
                got_back[line, place].astype(jnp.float32)
                + their_back[line, place].astype(jnp.float32),
            ),
        ):
            start = (line * COLS + column_of) * shard + place * share
            lanes = pl.ds(pl.multiple_of(start, LANES), share)
            value = tokens[:, lanes].astype(jnp.float32) + (1.0 + modulation[0:1, lanes]) * total
            state[:, lanes] = value
            partial = partial + value * value
        return partial

    steps = [(line, which) for line in [z] + near_lines[:-1] for which in range(2)]
    quarter = PIECES // 4
    for i, (line, which) in enumerate(steps):
        if which == 1 and i > 1:
            halves_in(line)
        project(line, which)
        if i < 4:
            take_last(range(i * quarter, (i + 1) * quarter))
    project(last, 0, True)

    @pl.when(jnp.logical_not(far_last))
    def _():
        last_step()

    def relay(some):
        for line, which in some:
            back_copy(line, which).wait_recv()
            share_copy(line, which).start()

    relay(steps[:4])

    @pl.when(far_last)
    def _():
        last_step()

    relay(steps[4:])
    squares = jnp.zeros((count, share), jnp.float32)
    for line, which in steps:
        squares = squares + add_up(line, which)
    for which in range(2):
        back_copy(last, which).wait_recv()
        squares = squares + add_up(last, which)
    square = jnp.sum(squares, -1, keepdims=True)
    scale = lax.rsqrt(square / width + EPS)
    for s in range(devices):
        lanes = slice(s * shard, (s + 1) * shard)
        normed[:, lanes] = (
            state[:, lanes] * scale * (1.0 + modulation[2:3, lanes]) + modulation[1:2, lanes]
        ).astype(jnp.bfloat16)
    logits = lax.dot_general(
        router[...], normed[...], (((1,), (1,)), ((), ())), preferred_element_type=jnp.float32
    )
    name = lax.broadcasted_iota(jnp.int32, logits.shape, 0)
    named = name == ids[0:1]
    for k in range(1, ids.shape[0]):
        named = named | (name == ids[k:k + 1])
    lifted = jnp.where(named, jax.nn.sigmoid(logits), 0.0)
    meta[...] = lifted / jnp.sum(lifted, 0, keepdims=True)

    def drain():
        query_copy().wait_send()
        for k in range(pairs):
            pair_copy(k).wait_send()
            for b in range(COLS):
                mix_copy(b, k).wait_send()

            @pl.when(give_early)
            def _():
                early_copy(k).wait_send()

            @pl.when(give_late)
            def _():
                late_copy(k).wait_send()

        for i in range(PIECES):

            @pl.when(not_top)
            def _():
                wz_copy(z, i, 0, own_piece(i)).wait_send()

            @pl.when(not_bottom)
            def _():
                wz_copy(z, i, 1, own_piece(i)).wait_send()

            for line in near_lines:

                @pl.when(more(line))
                def _():
                    wz_copy(line, i, way_of(line)).wait_send()

                wy_copy(line, i, group).wait_send()
        for line, which in steps + [(last, 0), (last, 1)]:
            sum_copy(line, which).wait_send()
            back_copy(line, which).wait_send()
            share_copy(line, which).wait_send()

    return drain


def block_kernel(devices, *refs):
    sources, gate_up, down, out = refs[:6], refs[6], refs[7], refs[8]
    held, normed, state, meta, wide = refs[9:13], refs[13], refs[14], refs[15], refs[16]
    front_buffers, expert_buffers = refs[17:26], refs[26:42]
    own_sem, gu_sem, dn_sem = refs[42:45]
    front_sems, expert_sems = refs[45:64], refs[64:]
    gu, dn = expert_buffers[5:7]
    squeeze, grow = expert_buffers[13:15]
    halves = gate_up.shape[0]

    def weight_copies(h):
        return (
            pltpu.make_async_copy(gate_up.at[h], gu.at[h], gu_sem.at[h]),
            pltpu.make_async_copy(down.at[h], dn.at[h], dn_sem.at[h]),
        )

    def start_weights():
        def one(h, carry):
            for copy in weight_copies(h):
                copy.start()
            return carry

        lax.fori_loop(0, halves, one, 0)
        for ref, axis in ((squeeze, 0), (grow, 1)):
            packed = lax.broadcasted_iota(jnp.int32, ref.shape, axis)
            slot = lax.broadcasted_iota(jnp.int32, ref.shape, 1 - axis)
            inner = slot & (SLOT - 1)
            same = (packed == (slot - inner) // SLOT * CAP + inner) & (inner < CAP)
            ref[...] = jnp.where(same, 1.0, 0.0).astype(jnp.bfloat16)

    drain = front_kernel(
        devices, start_weights, sources, held, own_sem, normed, state, meta,
        *front_buffers, *front_sems,
    )
    expert_kernel(
        devices, weight_copies, normed, meta, state, held[1], wide, out,
        *expert_buffers, *expert_sems,
    )
    drain()


def block_call(
    tokens, query_key_value, out_weight, modulation, router_weight, expert_ids,
    gate_up_weight, down_weight,
):
    devices = lax.axis_size("dev")
    count, width = tokens.shape
    half = down_weight.shape[2]
    halves = gate_up_weight.shape[0]
    local = halves // 2
    gate_up_weight = gate_up_weight.swapaxes(2, 3)
    hidden = gate_up_weight.shape[2]
    lines = devices // COLS
    rows = devices * SLOT
    slots, pack = local * SLOT, local * CAP
    part = half // CHUNKS
    shard = out_weight.shape[0]
    own = (
        tokens, query_key_value.transpose(1, 0, 2), out_weight, modulation,
        router_weight.T, expert_ids.T,
    )
    hbm = pl.BlockSpec(memory_space=pl.ANY)
    dma = pltpu.SemaphoreType.DMA
    return pl.pallas_call(
        functools.partial(block_kernel, devices),
        out_shape=jax.ShapeDtypeStruct((count, half), jnp.bfloat16),
        in_specs=[hbm] * 8,
        out_specs=pl.BlockSpec(memory_space=pltpu.VMEM),
        scratch_shapes=[
            *[pltpu.VMEM(own[i].shape, own[i].dtype) for i in (0, 3, 4, 5)],
            pltpu.VMEM((count, width), jnp.bfloat16),
            pltpu.VMEM((count, width), jnp.float32),
            pltpu.VMEM((router_weight.shape[1], count), jnp.float32),
            pltpu.VMEM((devices, slots + pack, half), jnp.bfloat16),
            pltpu.VMEM((4, 2, count, half // 2), jnp.bfloat16),
            pltpu.VMEM((COLS, count, half // 2), jnp.bfloat16),
            pltpu.VMEM((lines, shard, half), jnp.bfloat16),
            pltpu.VMEM((COLS * count, half), jnp.bfloat16),
            pltpu.VMEM((lines, 2, count, shard // 2), jnp.float32),
            pltpu.VMEM((lines, 2, count, shard // 2), jnp.float32),
            pltpu.VMEM((lines, 2, count, shard // 2), jnp.bfloat16),
            pltpu.VMEM((lines, 2, count, shard // 2), jnp.bfloat16),
            pltpu.VMEM((lines, 2, count, shard // 2), jnp.bfloat16),
            pltpu.VMEM((lines, CHUNKS, count, part), jnp.bfloat16),
            pltpu.VMEM((lines, CHUNKS, pack, part), jnp.bfloat16),
            pltpu.VMEM((lines, CHUNKS, pack, part), jnp.bfloat16),
            pltpu.VMEM((2, lines, CHUNKS, count, part), jnp.bfloat16),
            pltpu.VMEM((2, CHUNKS, local, rows, part), jnp.bfloat16),
            pltpu.VMEM(gate_up_weight.shape, jnp.bfloat16),
            pltpu.VMEM(down_weight.shape, jnp.bfloat16),
            pltpu.VMEM((local, 4 * hidden, rows), jnp.float32),
            pltpu.VMEM((local, 2 * hidden, rows), jnp.bfloat16),
            pltpu.VMEM((local, 2 * hidden, rows), jnp.bfloat16),
            pltpu.VMEM((lines, COLS * local, count), jnp.float32),
            pltpu.VMEM((lines, slots + pack, count), jnp.bfloat16),
            pltpu.VMEM((lines, slots + pack, count), jnp.bfloat16),
            pltpu.VMEM((pack, slots), jnp.bfloat16),
            pltpu.VMEM((slots, pack), jnp.bfloat16),
            pltpu.VMEM((count, part), jnp.float32),
            dma((7,)), dma((halves,)), dma((halves,)),
            dma((half // 2 // PAIR,)), dma((half // 2 // PAIR,)), dma((1,)), dma((1,)),
            dma((half // 2 // PAIR,)), dma((half // 2 // PAIR,)), dma((2, half // 2 // PAIR)),
            dma((lines, PIECES, 2)), dma((lines, PIECES)),
            dma((lines, PIECES)), dma((lines, PIECES)),
            dma((COLS, half // 2 // PAIR)), dma((COLS, half // 2 // PAIR)),
            dma((lines, 2)), dma((lines, 2)), dma((lines, 2)), dma((lines, 2)),
            dma((lines, 2)), dma((lines, 2)),
            dma((lines,)), dma((lines,)),
            dma((lines, CHUNKS, 2)), dma((lines, CHUNKS)),
            dma((lines, CHUNKS)), dma((lines, CHUNKS)),
            dma((devices, CHUNKS)), dma((devices, CHUNKS)),
            dma((local,)), dma((local,)),
            dma((lines, CHUNKS)), dma((lines, CHUNKS)),
            dma((lines, CHUNKS)), dma((2, lines, CHUNKS)),
        ],
        compiler_params=pltpu.CompilerParams(
            collective_id=1, has_side_effects=True, vmem_limit_bytes=VMEM_BYTES
        ),
    )(*own, gate_up_weight, down_weight)


def body(
    tokens,
    query_key_value,
    out_weight,
    modulation,
    router_weight,
    expert_ids,
    gate_up_weight,
    down_weight,
):
    count = tokens.shape[0]
    width = tokens.shape[1]
    parts = lax.axis_size("sub")
    part = lax.axis_index("sub")
    position = lax.axis_index("dev")
    devices = lax.axis_size("dev")
    total = count * devices
    local_width = query_key_value.shape[2]
    weight_bytes = 2 * (gate_up_weight.size + down_weight.size)
    token_bytes = 12 * devices * count * width
    fits = weight_bytes + token_bytes < VMEM_BYTES and CAP <= SLOT
    paired = parts == 2 and lax.axis_size("groups") == 2 and devices % COLS == 0
    experts_here = gate_up_weight.shape[0] // 2
    tiled = out_weight.shape[0] % (2 * LANES) == 0 and count == LANES
    tiled = tiled and down_weight.shape[2] % (2 * PAIR) == 0 and devices == 4 * COLS
    tiled = tiled and down_weight.shape[2] % (2 * CHUNKS * LANES) == 0 and experts_here == devices
    tiled = tiled and SLOT * devices == LANES
    tiled = tiled and gate_up_weight.shape[3] % 64 == 0
    if fits and paired and tiled:
        return block_call(
            tokens, query_key_value, out_weight, modulation, router_weight, expert_ids,
            gate_up_weight, down_weight,
        )
    heads_here = local_width // HEAD
    query = query_key_value[:, 0].reshape(count, heads_here, HEAD)
    pair = query_key_value[:, 1:]
    near = extended(pair, (("dev", 0),), count)
    keys = near[:, 0].reshape(3 * count, heads_here, HEAD)
    values = near[:, 1].reshape(3 * count, heads_here, HEAD)
    mixed = window_attention(query, keys, values, position, total).reshape(count, local_width)
    partial_proj = lax.dot_general(
        mixed,
        lax.all_gather(out_weight, "dev", axis=0, tiled=True),
        (((1,), (1,)), ((), ())),
        preferred_element_type=jnp.float32,
    )
    proj = lax.psum(partial_proj, "sub")
    state = tokens.astype(jnp.float32) + (1.0 + modulation[0]) * proj
    normed = normalize(state, modulation)
    gates = route(normed, router_weight, expert_ids)
    experts = router_weight.shape[1]
    topk = expert_ids.shape[1]
    flat = expert_ids.reshape(-1)
    picks = flat.shape[0]
    onehot = (flat[:, None] == jnp.arange(experts, dtype=jnp.int32)[None, :]).astype(jnp.int32)
    rank = jnp.sum((jnp.cumsum(onehot, 0) - 1) * onehot, 1)
    target = flat * CAP + rank
    hit = target[None, :] == jnp.arange(experts * CAP, dtype=jnp.int32)[:, None]
    filled = jnp.any(hit, 1)
    anchor = jnp.sum(jnp.where(hit, jnp.arange(picks, dtype=jnp.int32)[None, :], 0), 1) // topk
    slice_width = width // parts
    sent = lax.dynamic_slice_in_dim(normed, part * slice_width, slice_width, 1)
    sent_width = sent.shape[1]
    rows_out = jnp.where(filled[:, None], sent[anchor], jnp.zeros((), jnp.bfloat16))
    halves_here = gate_up_weight.shape[0]
    doubled = jnp.broadcast_to(
        rows_out.reshape(experts, 1, CAP, sent_width), (experts, 2, CAP, sent_width)
    )
    outgoing = doubled.reshape(devices, halves_here, CAP, sent_width)
    up_form = "sxcd,xgdf->sxcgf"
    down_form = "sxcf,xfd->sxcd"
    incoming = lax.all_to_all(outgoing, "dev", split_axis=0, concat_axis=0, tiled=True)
    both = jnp.einsum(
        up_form,
        lax.all_gather(incoming, "sub", axis=3, tiled=True),
        gate_up_weight,
        preferred_element_type=jnp.float32,
    )
    hidden = (jax.nn.silu(both[..., 0, :]) * both[..., 1, :]).astype(jnp.bfloat16)
    gathered = lax.all_gather(hidden, "sub", axis=hidden.ndim - 1, tiled=True)
    result = jnp.einsum(down_form, gathered, down_weight, preferred_element_type=jnp.float32)
    returned = lax.all_to_all(
        result.astype(jnp.bfloat16), "dev", split_axis=0, concat_axis=0, tiled=True
    )
    own_width = returned.shape[-1]
    arranged = returned.reshape(experts, 2, CAP, own_width)
    answers = arranged[flat, :, rank, :].reshape(count, topk, 2, own_width).astype(jnp.float32)
    combined = answers[:, :, 0] + answers[:, :, 1]
    routed = jnp.einsum("tk,tkd->td", gates, combined)
    own = lax.dynamic_slice_in_dim(state, part * slice_width, slice_width, 1)
    lift = lax.dynamic_slice_in_dim(modulation[3], part * slice_width, slice_width, 0)
    return (own + (1.0 + lift) * routed).astype(jnp.bfloat16)


def solution(mesh):
    return jax.shard_map(
        body,
        mesh=mesh,
        in_specs=(
            P(("groups", "dev"), None),
            P(("groups", "dev"), None, "sub"),
            P("dev", "sub"),
            P("groups", None),
            P(),
            P(("groups", "dev"), None),
            P("dev", None, None, "sub"),
            P("dev", None, "sub"),
        ),
        out_specs=P(("groups", "dev"), "sub"),
        check_vma=False,
    )
```

```python
import functools
import math

import jax
import jax.numpy as jnp
from jax import lax
from jax.experimental import pallas as pl
from jax.experimental.pallas import tpu as pltpu
from jax.sharding import PartitionSpec as P

HEAD = 128
CAP = 12


EPS = 1e-06
NEG = -1e30


def extended(cells, sides, width):
    for axis, dim in sides:
        count = lax.axis_size(axis)
        ends = count - 1
        head = lax.slice_in_dim(cells, 0, width, axis=dim)
        tail = lax.slice_in_dim(cells, cells.shape[dim] - width, cells.shape[dim], axis=dim)
        cells = jnp.concatenate(
            [
                lax.ppermute(tail, axis, [(i, (i + 1) % count) for i in range(ends)]),
                cells,
                lax.ppermute(head, axis, [((i + 1) % count, i) for i in range(ends)]),
            ],
            axis=dim,
        )
    return cells


def window_attention(query, keys, values, index, total):
    count = query.shape[0]
    rows = jnp.arange(count, dtype=jnp.int32)[:, None]
    cols = jnp.arange(3 * count, dtype=jnp.int32)[None, :] - count
    place = index * count + cols
    allowed = (jnp.abs(cols - rows) <= count) & (place >= 0) & (place < total)
    scores = jnp.einsum(
        "qhd,khd->hqk", query, keys, preferred_element_type=jnp.float32
    ) / math.sqrt(query.shape[2])
    scores = jnp.where(allowed[None], scores, NEG)
    top = jnp.max(scores, -1, keepdims=True)
    weight = jnp.exp(scores - top)
    weight = (weight / jnp.sum(weight, -1, keepdims=True)).astype(jnp.bfloat16)
    mixed = jnp.einsum("hqk,khd->qhd", weight, values, preferred_element_type=jnp.float32)
    return mixed.astype(jnp.bfloat16)


def normalize(state, modulation):
    scale = lax.rsqrt(jnp.mean(state * state, -1, keepdims=True) + EPS)
    return (state * scale * (1.0 + modulation[2]) + modulation[1]).astype(jnp.bfloat16)


def route(normed, router_weight, expert_ids):
    logits = jnp.dot(normed, router_weight, preferred_element_type=jnp.float32)
    experts = router_weight.shape[1]
    match = expert_ids[:, :, None] == jnp.arange(experts, dtype=jnp.int32)[None, None, :]
    picked = jnp.sum(jnp.where(match, logits[:, None, :], 0.0), -1)
    lifted = jax.nn.sigmoid(picked)
    return lifted / jnp.sum(lifted, -1, keepdims=True)


LANES = 128
SLOT = 16
COLS = 2
CHUNKS = 4
PIECES = 4
LAG = 2
SPLIT = 2
PAIR = 256
VMEM_BYTES = 66 * 1000 * 1000
MESH = pl.DeviceIdType.MESH


def choose(index, table):
    value = jnp.int32(table[0])
    for i in range(1, len(table)):
        value = jnp.where(index == i, table[i], value)
    return value


def line_order(lines, nearest, inner=False):
    rows = []
    for z in range(lines):
        lower = (z < lines - 1 - z) != inner
        others = [line for line in range(lines) if line != z]
        sign = 1 if nearest else -1
        rows.append(sorted(others, key=lambda line: (sign * abs(line - z), (line > z) == lower)))
    return [[rows[z][j] for z in range(lines)] for j in range(lines - 1)]


def expert_kernel(
    devices, weight_copies,
    normed, meta, state, modulation, wide,
    out,
    tok, got_packed, got_rows, got_sum, disp, gu, dn, raised, hid_own, hid_other,
    got_meta, pick, gated, squeeze, grow, acc,
    meta_s, meta_r, z_s, z_r, x_s, x_r, core_s, core_r, hid_s, hid_r, rx_s, rx_r, rz_s, rz_r,
):
    me = lax.axis_index("dev")
    part = lax.axis_index("sub")
    other = 1 - part
    z = me // COLS
    x = me % COLS
    lines = devices // COLS
    count, width = normed.shape
    half = width // 2
    local = hid_own.shape[0]
    hidden = gu.shape[2]
    slots = local * SLOT
    pack = local * CAP
    rows = devices * SLOT
    chunks, wide_chunk = tok.shape[1], tok.shape[3]

    def remote(src, dst, send, recv, where):
        return pltpu.make_async_remote_copy(
            src_ref=src, dst_ref=dst, send_sem=send, recv_sem=recv,
            device_id=where, device_id_type=MESH,
        )

    above = jnp.minimum(me + COLS, devices - 1)
    below = jnp.maximum(me - COLS, 0)
    x_to = {"dev": z * COLS + (1 - x)}
    core_to = {"sub": other}
    not_top = z < lines - 1
    not_bottom = z > 0
    near_lines = [choose(z, table) for table in line_order(lines, True, True)]
    far_lines = [choose(z, table) for table in line_order(lines, False)]

    def lanes_of(c):
        return pl.ds(pl.multiple_of(c * wide_chunk, wide_chunk), wide_chunk)

    def own_lanes(c):
        return pl.ds(pl.multiple_of(part * half + c * wide_chunk, wide_chunk), wide_chunk)

    def slot_rows(s):
        return pl.ds(pl.multiple_of(s * SLOT, SLOT), SLOT)

    def meta_copy(line):
        return remote(
            meta.at[pl.ds(pl.multiple_of(line * COLS * local, COLS * local), COLS * local)],
            got_meta.at[z], meta_s.at[0], meta_r.at[z], {"dev": line * COLS + x},
        )

    def meta_arrival(line):
        return remote(got_meta.at[line], got_meta.at[line], meta_s.at[0], meta_r.at[line], x_to)

    def z_copy(line, c, way, src=None):
        dst = tok.at[line, c]
        where = {"dev": jnp.where(way == 0, above, below)}
        return remote(
            dst if src is None else src, dst, z_s.at[line, way], z_r.at[line, c], where
        )

    def packed_out(line, c):
        return wide.at[line, pl.ds(slots, pack), lanes_of(c)]

    def x_copy(line, c):
        return remote(
            packed_out(line, c), got_packed.at[line, c], x_s.at[0], x_r.at[line, c], x_to
        )

    def core_copy(which, s, c):
        place = disp.at[which, c, :, slot_rows(s), :]
        return remote(place, place, core_s.at[0], core_r.at[jnp.where(c < SPLIT, 0, 1)], core_to)

    def own_send(c):
        src = normed.at[:, own_lanes(c)]

        @pl.when(not_top)
        def _():
            z_copy(z, c, 0, src).start()

        @pl.when(not_bottom)
        def _():
            z_copy(z, c, 1, src).start()

    own_send(0)
    for line in near_lines:
        meta_copy(line).start()
    for c in range(1, chunks):
        own_send(c)

    before = (
        lax.broadcasted_iota(jnp.int32, (count, count), 0)
        < lax.broadcasted_iota(jnp.int32, (count, count), 1)
    ).astype(jnp.float32).astype(jnp.bfloat16)
    place = lax.broadcasted_iota(jnp.int32, (local, SLOT, count), 1).astype(jnp.float32)

    def routing(line, ours, theirs):
        for first, gate in ((True, ours), (False, theirs)):
            chosen = jnp.where(gate > 0.0, 1.0, 0.0)
            rank = jnp.dot(chosen.astype(jnp.bfloat16), before, preferred_element_type=jnp.float32)
            rank = jnp.where(gate > 0.0, rank, -1.0)
            hit = jnp.broadcast_to(rank[:, None, :], place.shape) == place
            one = jnp.where(hit, 1.0, 0.0).reshape(slots, count).astype(jnp.bfloat16)
            value = jnp.where(hit, jnp.broadcast_to(gate[:, None, :], place.shape), 0.0)
            value = value.reshape(slots, count).astype(jnp.bfloat16)
            if first:
                pick[line, :slots] = one
                gated[line, :slots] = value
            else:
                pick[line, slots:] = jnp.dot(
                    squeeze[...], one, preferred_element_type=jnp.float32
                ).astype(jnp.bfloat16)
                gated[line, slots:] = jnp.dot(
                    squeeze[...], value, preferred_element_type=jnp.float32
                ).astype(jnp.bfloat16)

    def expert_rows(base, column):
        return pl.ds(pl.multiple_of(base + column * local, local), local)

    def spread(line, c, block):
        moved = jnp.dot(pick[line], block, preferred_element_type=jnp.float32).astype(jnp.bfloat16)
        s = line * COLS + x
        wide[line, slots:slots + pack, lanes_of(c)] = moved[slots:]
        x_copy(line, c).start()
        disp[part, c, :, slot_rows(s), :] = moved[:slots].reshape(local, SLOT, wide_chunk)
        core_copy(part, s, c).start()

    def own_step(c):
        spread(z, c, normed[:, own_lanes(c)])

    def line_step(line, c):
        low = line < z

        @pl.when(c == 0)
        def _():
            meta_arrival(line).wait_recv()
            routing(
                line, got_meta[line, expert_rows(0, x)], got_meta[line, expert_rows(0, 1 - x)]
            )

        way = jnp.where(low, 0, 1)
        z_copy(line, c, way).wait_recv()

        @pl.when(jnp.where(low, not_top, not_bottom))
        def _():
            z_copy(line, c, way).start()

        spread(line, c, tok[line, c])

    def x_step(line, c):
        x_copy(line, c).wait_recv()
        s = line * COLS + (1 - x)
        disp[part, c, :, slot_rows(s), :] = jnp.dot(
            grow[...], got_packed[line, c], preferred_element_type=jnp.float32
        ).astype(jnp.bfloat16).reshape(local, SLOT, wide_chunk)
        core_copy(part, s, c).start()

    def across_rows(left, right):
        return lax.dot_general(
            left, right, (((1,), (1,)), ((), ())), preferred_element_type=jnp.float32
        )

    def raise_part(e, parts):
        sums = []
        for g in range(2):
            for b in range(2):
                total = None
                for side, c in parts:
                    start = side * half + c * wide_chunk
                    piece = across_rows(
                        gu[2 * e + b, g, :, start:start + wide_chunk], disp[side, c, e]
                    )
                    total = piece if total is None else total + piece
                sums.append(total)
        return sums

    def raise_some(parts, start, stop, first=False, last=False):
        def one(e, carry):
            sums = raise_part(e, parts)
            if not first:
                sums = [
                    total + raised[e, n * hidden:(n + 1) * hidden] for n, total in enumerate(sums)
                ]
            if not last:
                for n, total in enumerate(sums):
                    raised[e, n * hidden:(n + 1) * hidden] = total
                return carry
            for b in range(2):
                gate = sums[b]
                hid_own[e, b * hidden:(b + 1) * hidden] = (
                    gate * jax.nn.sigmoid(gate) * sums[2 + b]
                ).astype(jnp.bfloat16)
            hid_copy(e).start()
            return carry

        lax.fori_loop(start, stop, one, 0)

    def hid_copy(e):
        return remote(hid_own.at[e], hid_other.at[e], hid_s.at[0], hid_r.at[e], core_to)

    def arrived(which):
        span_of = pl.ds(which * SPLIT, SPLIT) if which == 0 else pl.ds(SPLIT, chunks - SPLIT)
        block = disp.at[other, span_of]
        remote(block, block, core_s.at[0], core_r.at[which], core_to).wait_recv()

    def sent(ref, sem):
        remote(ref, ref, sem, sem, core_to).wait_send()

    routing(
        z, meta[expert_rows(z * COLS * local, x)], meta[expert_rows(z * COLS * local, 1 - x)]
    )
    for c in range(chunks):
        own_step(c)

    for copy in weight_copies():
        copy.wait()

    offsets = [(jnp.abs(line - z) - 1) * chunks for line in near_lines]
    offsets[1] = jnp.maximum(offsets[1], SPLIT)

    def step(t, carry):
        for line, offset in zip(near_lines, offsets):
            c = t - offset

            @pl.when((c >= 0) & (c < chunks))
            def _():
                line_step(line, c)

        @pl.when((t >= 1) & (t < 1 + chunks))
        def _():
            x_step(z, t - 1)

        for line, offset in zip(near_lines, offsets):
            c = t - LAG - offset

            @pl.when((c >= 0) & (c < chunks))
            def _():
                x_step(line, c)

        return carry

    span = chunks * (lines - 1) + LAG
    lax.fori_loop(0, span - 2, step, 0)
    early = range(SPLIT)
    late = range(SPLIT, chunks)
    own_first = (part == 1) & ((z == 0) | (z == lines - 1))

    @pl.when(own_first)
    def _():
        raise_some([(1, c) for c in early], 0, local, first=True)
        step(span - 2, 0)
        step(span - 1, 0)
        raise_some([(1, c) for c in late], 0, local)
        arrived(0)
        arrived(1)
        raise_some([(0, c) for c in range(chunks)], 0, local, last=True)

    @pl.when(jnp.logical_not(own_first))
    def _():
        arrived(0)
        raise_some([(side, c) for c in early for side in range(2)], 0, local // 2, first=True)
        step(span - 2, 0)
        step(span - 1, 0)
        raise_some([(side, c) for c in early for side in range(2)], local // 2, local, first=True)
        arrived(1)
        raise_some([(side, c) for c in late for side in range(2)], 0, local, last=True)

    group = 2 * wide_chunk

    def lower(g):
        lanes = slice(g * group, (g + 1) * group)

        def one(e, carry):
            if g == 0:
                hid_copy(e).wait_recv()
            mine = pl.ds(pl.multiple_of(part * hidden, SLOT), hidden)
            theirs = pl.ds(pl.multiple_of(other * hidden, SLOT), hidden)
            left = jnp.concatenate([hid_own[e], hid_other[e]], axis=0)
            right = jnp.concatenate(
                [dn[2 * e, mine, lanes], dn[2 * e + 1, mine, lanes],
                 dn[2 * e, theirs, lanes], dn[2 * e + 1, theirs, lanes]], axis=0
            )
            wide[e, :rows, lanes] = lax.dot_general(
                left, right, (((0,), (0,)), ((), ())), preferred_element_type=jnp.float32
            ).astype(jnp.bfloat16)
            return carry

        lax.fori_loop(0, local, one, 0)

    def result_rows(s, q):
        return wide[:local, slot_rows(s), lanes_of(q)].reshape(slots, wide_chunk)

    def rx_copy(line, q):
        return remote(
            wide.at[lines + line, pl.ds(slots, pack), lanes_of(q)], got_rows.at[line, q],
            rx_s.at[0], rx_r.at[line, q], x_to,
        )

    def rz_copy(line, q, way):
        where = {"dev": jnp.where(way == 0, above, below)}
        return remote(
            tok.at[line, q], got_sum.at[way, line, q],
            rz_s.at[0], rz_r.at[way, line, q], where,
        )

    def give(line, q):
        packed = jnp.dot(
            squeeze[...], result_rows(line * COLS + (1 - x), q), preferred_element_type=jnp.float32
        )
        wide[lines + line, slots:slots + pack, lanes_of(q)] = packed.astype(jnp.bfloat16)
        rx_copy(line, q).start()

    def gather_here(line, q):
        rx_copy(line, q).wait_recv()
        pieces = jnp.concatenate([result_rows(line * COLS + x, q), got_rows[line, q]], axis=0)
        acc[...] = lax.dot_general(
            gated[line], pieces, (((0,), (0,)), ((), ())), preferred_element_type=jnp.float32
        )

    def add_line(line, q, way):
        rz_copy(line, q, way).wait_recv()
        acc[...] += got_sum[way, line, q].astype(jnp.float32)

    def pass_on(line, q):
        gather_here(line, q)
        way = jnp.where(line > z, 0, 1)

        @pl.when(jnp.where(line > z, not_bottom, not_top))
        def _():
            add_line(line, q, way)

        tok[line, q] = acc[...].astype(jnp.bfloat16)
        rz_copy(line, q, way).start()

    for g in range(half // group):
        lower(g)
        for q in range(2 * g, 2 * g + 2):
            give(far_lines[0], q)
    def give_all(line):
        lax.fori_loop(0, chunks, lambda q, carry: (give(line, q), carry)[1], 0)

    for line in near_lines:
        low = line < z

        @pl.when(jnp.where(low, not_top, not_bottom))
        def _():
            sent(tok.at[line], z_s.at[line, jnp.where(low, 0, 1)])

    far_end = (z == 0) | (z == lines - 1)

    @pl.when(far_end)
    def _():
        for q in range(2):
            pass_on(far_lines[0], q)

    give_all(far_lines[1])

    @pl.when(far_end)
    def _():
        for q in range(2, chunks):
            pass_on(far_lines[0], q)

    for line in far_lines[2:] + [z]:
        give_all(line)

    @pl.when(jnp.logical_not(far_end))
    def _():
        for q in range(chunks):
            pass_on(far_lines[0], q)

    for line in far_lines[1:]:
        lax.fori_loop(0, chunks, lambda q, carry, line=line: (pass_on(line, q), carry)[1], 0)
    for q in range(chunks):
        gather_here(z, q)

        @pl.when(not_bottom)
        def _():
            add_line(z, q, 0)

        @pl.when(not_top)
        def _():
            add_line(z, q, 1)

        own = own_lanes(q)
        lanes = slice(q * wide_chunk, (q + 1) * wide_chunk)
        out[:, lanes] = (
            state[:, own] + (1.0 + modulation[3:4, own]) * acc[...]
        ).astype(out.dtype)

    @pl.when(not_top)
    def _():
        sent(tok.at[z], z_s.at[z, 0])

    @pl.when(not_bottom)
    def _():
        sent(tok.at[z], z_s.at[z, 1])

    sent(tok.at[pl.ds(0, lines - 1)], rz_s.at[0])
    sent(got_packed, x_s.at[0])
    sent(got_rows, rx_s.at[0])
    sent(disp.at[part], core_s.at[0])
    sent(got_meta.at[pl.ds(0, lines - 1)], meta_s.at[0])
    sent(hid_own, hid_s.at[0])


def front_kernel(
    devices, start_weights,
    sources, held, own_sem,
    normed, state, meta,
    window, queries, column, mixed, mine_out, their_out, sent_back, got_back, their_back,
    pair_s, pair_r, query_s, query_r, early_s, late_s, edge_r, wz_s, wz_r, wy_s, wy_r, mix_s, mix_r,
    sum_s, sum_r, back_s, back_r, share_s, share_r,
):
    packed_hbm, weight_hbm = sources[1], sources[2]
    tokens, modulation, router, ids = held
    me = lax.axis_index("dev")
    part = lax.axis_index("sub")
    group = lax.axis_index("groups")
    z = me // COLS
    x = me % COLS
    lines = devices // COLS
    count, width = tokens.shape
    shard = column.shape[1]
    share = shard // 2
    piece = share // PIECES
    heads = window.shape[3]
    pairs = heads // PAIR
    ours = pl.ds(pl.multiple_of(x * heads, heads), heads)
    theirs = pl.ds(pl.multiple_of((1 - x) * heads, heads), heads)
    own_parts = (
        (packed_hbm.at[1:3, :, ours], window.at[1 + x]), (packed_hbm.at[0, :, ours], queries.at[x]),
        (weight_hbm, column.at[z]), (sources[0], tokens), (sources[3], modulation),
        (sources[4], router), (sources[5], ids),
    )

    def own_copy(i):
        return pltpu.make_async_copy(*own_parts[i], own_sem.at[i])

    for i in range(len(own_parts)):
        own_copy(i).start()
    not_top = z < lines - 1
    not_bottom = z > 0
    above = jnp.minimum(me + COLS, devices - 1)
    below = jnp.maximum(me - COLS, 0)
    x_to = {"dev": z * COLS + (1 - x)}
    y_to = {"groups": 1 - group}
    core_to = {"sub": 1 - part}
    near_lines = [choose(z, table) for table in line_order(lines, True)]

    barrier = pltpu.get_barrier_semaphore()

    def greet(where):
        pl.semaphore_signal(barrier, inc=1, device_id=where, device_id_type=MESH)

    for where in (x_to, y_to, core_to, {**x_to, **core_to}):
        greet(where)
    for line in near_lines:
        greet({"dev": line * COLS + x})
    pl.semaphore_wait(barrier, lines + 3)

    def remote(src, dst, send, recv, where):
        return pltpu.make_async_remote_copy(
            src_ref=src, dst_ref=dst, send_sem=send, recv_sem=recv,
            device_id=where, device_id_type=MESH,
        )

    def part_lanes(base, k):
        return pl.ds(pl.multiple_of(base * heads + k * PAIR, PAIR), PAIR)

    def pair_copy(k):
        return remote(
            packed_hbm.at[1:3, :, part_lanes(1 - x, k)], window.at[1 + x, :, :, part_lanes(0, k)],
            pair_s.at[k], pair_r.at[k], x_to,
        )

    def query_copy():
        return remote(
            packed_hbm.at[0, :, theirs], queries.at[x], query_s.at[0], query_r.at[0], x_to
        )

    def edge_copy(k, up, src, send):
        where = {"dev": jnp.where(up, above, below)}
        place = jnp.where(up, 0, 3)
        return remote(
            src, window.at[place, :, :, part_lanes(0, k)], send,
            edge_r.at[jnp.where(up, 0, 1), k], where,
        )

    def early_copy(k):
        return edge_copy(k, x == 1, packed_hbm.at[1:3, :, part_lanes(x, k)], early_s.at[k])

    def late_copy(k):
        return edge_copy(k, x == 0, window.at[2 - x, :, :, part_lanes(0, k)], late_s.at[k])

    give_late = ((x == 0) & not_top) | ((x == 1) & not_bottom)
    give_early = ((x == 1) & not_top) | ((x == 0) & not_bottom)

    def piece_rows(which, i):
        return pl.ds(pl.multiple_of(which * share + i * piece, SLOT), piece)

    def wz_copy(line, i, way, src=None):
        dst = column.at[line, piece_rows(group, i)]
        where = {"dev": jnp.where(way == 0, above, below)}
        return remote(
            dst if src is None else src, dst, wz_s.at[line, way], wz_r.at[line, i], where
        )

    def own_piece(i):
        return weight_hbm.at[piece_rows(group, i)]

    def wy_copy(line, i, which):
        block = column.at[line, piece_rows(which, i)]
        return remote(block, block, wy_s.at[0], wy_r.at[line], y_to)

    for k in range(pairs):
        pair_copy(k).start()
    query_copy().start()

    def send_pieces(pieces):
        for i in pieces:

            @pl.when(not_top)
            def _():
                wz_copy(z, i, 0, own_piece(i)).start()

            @pl.when(not_bottom)
            def _():
                wz_copy(z, i, 1, own_piece(i)).start()

    send_pieces(range(PIECES // 2))

    @pl.when(give_early)
    def _():
        for k in range(pairs):
            early_copy(k).start()

    send_pieces(range(PIECES // 2, PIECES))
    start_weights()

    @pl.when(jnp.logical_not(not_bottom))
    def _():
        window[0] = jnp.zeros_like(window[0])

    @pl.when(jnp.logical_not(not_top))
    def _():
        window[3] = jnp.zeros_like(window[3])

    def way_of(line):
        return jnp.where(line < z, 0, 1)

    def more(line):
        return jnp.where(line < z, not_top, not_bottom)

    def busy(line):
        return jnp.where(line < z, x == 0, x == 1)

    def distance(line):
        return jnp.abs(line - z)

    def take(line, onward, pieces=range(PIECES)):
        for i in pieces:
            wz_copy(line, i, way_of(line)).wait_recv()

            @pl.when(onward)
            def _():
                wz_copy(line, i, way_of(line)).start()

            wy_copy(line, i, group).start()

    def take_next(only_busy, pieces):
        for line in near_lines:

            @pl.when((distance(line) == 1) & (busy(line) if only_busy else jnp.logical_not(busy(line))))
            def _():
                take(line, more(line), pieces)

    for k in range(pairs):
        pair_copy(k).wait_recv()

        @pl.when(give_late)
        def _():
            late_copy(k).start()

    take_next(True, range(PIECES // 2))
    take_next(False, range(PIECES // 2))
    for i in range(len(own_parts)):
        own_copy(i).wait()
    query_copy().wait_recv()

    row = lax.broadcasted_iota(jnp.int32, (count, count), 0)
    col = lax.broadcasted_iota(jnp.int32, (count, count), 1)

    def mix_copy(b, k):
        block = mixed.at[pl.ds(pl.multiple_of(b * count, count), count), part_lanes(x, k)]
        return remote(block, block, mix_s.at[0], mix_r.at[0], x_to)

    def attend(b, k):
        see_before = (col >= row) & ((z > 0) | (b == 1))
        see_after = (col <= row) & ((z < lines - 1) | (b == 0))
        for h in range(PAIR // HEAD):
            inner = slice(k * PAIR + h * HEAD, k * PAIR + (h + 1) * HEAD)
            query = queries[b, :, inner]

            def score(keys):
                return lax.dot_general(
                    query, keys, (((1,), (1,)), ((), ())), preferred_element_type=jnp.float32
                ) / math.sqrt(HEAD)

            scores = jnp.concatenate(
                [
                    jnp.where(see_before, score(window[b, 0, :, inner]), NEG),
                    score(window[b + 1, 0, :, inner]),
                    jnp.where(see_after, score(window[b + 2, 0, :, inner]), NEG),
                ],
                axis=1,
            )
            top = jnp.max(scores, -1, keepdims=True)
            weight = jnp.exp(scores - top)
            weight = (weight / jnp.sum(weight, -1, keepdims=True)).astype(jnp.bfloat16)
            values = jnp.concatenate([window[b + n, 1, :, inner] for n in range(3)], axis=0)
            lanes = pl.ds(
                pl.multiple_of(x * heads + k * PAIR + h * HEAD, HEAD), HEAD
            )
            mixed[pl.ds(pl.multiple_of(b * count, count), count), lanes] = jnp.dot(
                weight, values, preferred_element_type=jnp.float32
            ).astype(jnp.bfloat16)
        mix_copy(b, k).start()

    for b, up in ((1 - x, x == 1), (x, x == 0)):
        for k in range(pairs):

            @pl.when(jnp.where(up, not_bottom, not_top))
            def _():
                edge_copy(k, up, window.at[0, :, :, part_lanes(0, k)], early_s.at[k]).wait_recv()

            attend(b, k)
        if b is not x:
            take_next(True, range(PIECES // 2, PIECES))
            take_next(False, range(PIECES // 2, PIECES))
        else:
            for line in near_lines:

                @pl.when(distance(line) == 2)
                def _():
                    take(line, more(line))

    last = near_lines[-1]
    far_last = distance(last) > 2

    def take_last(pieces):
        @pl.when(far_last)
        def _():
            take(last, more(last), pieces)

    mix_block = mixed.at[:, theirs]
    remote(mix_block, mix_block, mix_s.at[0], mix_r.at[0], x_to).wait_recv()

    def place_of(which):
        return group if which == 0 else 1 - group

    def sum_copy(line, which):
        place = place_of(which)
        return remote(
            mine_out.at[line, place], their_out.at[line, place],
            sum_s.at[0], sum_r.at[line, which], core_to,
        )

    def back_copy(line, which):
        place = place_of(which)
        return remote(
            sent_back.at[line, place], got_back.at[line, place],
            back_s.at[0], back_r.at[line, which], x_to,
        )

    def share_copy(line, which):
        place = place_of(which)
        return remote(
            got_back.at[line, place], their_back.at[line, place],
            share_s.at[0], share_r.at[line, which], core_to,
        )

    def direct_copy(which):
        place = place_of(which)
        return remote(
            sent_back.at[last, place], their_back.at[last, place],
            share_s.at[0], share_r.at[last, which],
            {"dev": z * COLS + (1 - x), "sub": 1 - part},
        )

    def project(line, which, direct=False):
        place = place_of(which)
        block = column[line, pl.ds(pl.multiple_of(place * share, SLOT), share), :]
        both = jnp.concatenate(
            [mixed[pl.ds(pl.multiple_of(b * count, count), count), :] for b in (1 - x, x)], axis=0
        )
        product = lax.dot_general(
            both, block, (((1,), (1,)), ((), ())), preferred_element_type=jnp.float32
        )
        sent_back[line, place] = product[:count].astype(jnp.bfloat16)
        back_copy(line, which).start()
        if direct:
            direct_copy(which).start()
        mine_out[line, place] = product[count:]
        sum_copy(line, which).start()

    def halves_in(line):
        block = column.at[line, pl.ds(pl.multiple_of((1 - group) * share, SLOT), share)]
        remote(block, block, wy_s.at[0], wy_r.at[line], y_to).wait_recv()

    def last_step():
        halves_in(last)
        project(last, 1, True)

    def add_up(line, which):
        place = place_of(which)
        sum_copy(line, which).wait_recv()
        share_copy(line, which).wait_recv()
        partial = jnp.zeros((count, share), jnp.float32)
        for column_of, total in (
            (x, mine_out[line, place] + their_out[line, place]),
            (
                1 - x,
                got_back[line, place].astype(jnp.float32)
                + their_back[line, place].astype(jnp.float32),
            ),
        ):
            start = (line * COLS + column_of) * shard + place * share
            lanes = pl.ds(pl.multiple_of(start, LANES), share)
            value = tokens[:, lanes].astype(jnp.float32) + (1.0 + modulation[0:1, lanes]) * total
            state[:, lanes] = value
            partial = partial + value * value
        return partial

    steps = [(line, which) for line in [z] + near_lines[:-1] for which in range(2)]
    quarter = PIECES // 4
    for i, (line, which) in enumerate(steps):
        if which == 1 and i > 1:
            halves_in(line)
        project(line, which)
        if i < 4:
            take_last(range(i * quarter, (i + 1) * quarter))
    project(last, 0, True)

    @pl.when(jnp.logical_not(far_last))
    def _():
        last_step()

    def relay(some):
        for line, which in some:
            back_copy(line, which).wait_recv()
            share_copy(line, which).start()

    relay(steps[:4])

    @pl.when(far_last)
    def _():
        last_step()

    relay(steps[4:])
    squares = jnp.zeros((count, share), jnp.float32)
    for line, which in steps:
        squares = squares + add_up(line, which)
    for which in range(2):
        back_copy(last, which).wait_recv()
        squares = squares + add_up(last, which)
    square = jnp.sum(squares, -1, keepdims=True)
    scale = lax.rsqrt(square / width + EPS)
    for s in range(devices):
        lanes = slice(s * shard, (s + 1) * shard)
        normed[:, lanes] = (
            state[:, lanes] * scale * (1.0 + modulation[2:3, lanes]) + modulation[1:2, lanes]
        ).astype(jnp.bfloat16)
    logits = lax.dot_general(
        router[...], normed[...], (((1,), (1,)), ((), ())), preferred_element_type=jnp.float32
    )
    name = lax.broadcasted_iota(jnp.int32, logits.shape, 0)
    named = name == ids[0:1]
    for k in range(1, ids.shape[0]):
        named = named | (name == ids[k:k + 1])
    lifted = jnp.where(named, jax.nn.sigmoid(logits), 0.0)
    meta[...] = lifted / jnp.sum(lifted, 0, keepdims=True)

    def drain():
        def sent(ref, sem):
            remote(ref, ref, sem, sem, x_to).wait_send()

        query_copy().wait_send()
        sent(mixed.at[:, ours], mix_s.at[0])
        for k in range(pairs):
            pair_copy(k).wait_send()

            @pl.when(give_early)
            def _():
                early_copy(k).wait_send()

            @pl.when(give_late)
            def _():
                late_copy(k).wait_send()

        half_shard = column.at[0, pl.ds(0, share)]

        @pl.when(not_top)
        def _():
            sent(half_shard, wz_s.at[z, 0])

        @pl.when(not_bottom)
        def _():
            sent(half_shard, wz_s.at[z, 1])

        for line in near_lines:

            @pl.when(more(line))
            def _():
                sent(half_shard, wz_s.at[line, way_of(line)])

        sent(column.at[pl.ds(0, lines - 1), pl.ds(0, share)], wy_s.at[0])
        sent(mine_out, sum_s.at[0])
        sent(sent_back, back_s.at[0])
        sent(got_back, share_s.at[0])

    return drain


def block_kernel(devices, *refs):
    sources, gate_up, down, out = refs[:6], refs[6], refs[7], refs[8]
    held, normed, state, meta, wide = refs[9:13], refs[13], refs[14], refs[15], refs[16]
    front_buffers, expert_buffers = refs[17:26], refs[26:42]
    own_sem, gu_sem, dn_sem = refs[42:45]
    front_sems, expert_sems = refs[45:64], refs[64:]
    gu, dn = expert_buffers[5:7]
    squeeze, grow = expert_buffers[13:15]
    def weight_copies():
        return (
            pltpu.make_async_copy(gate_up, gu, gu_sem.at[0]),
            pltpu.make_async_copy(down, dn, dn_sem.at[0]),
        )

    def start_weights():
        for copy in weight_copies():
            copy.start()
        for ref, axis in ((squeeze, 0), (grow, 1)):
            packed = lax.broadcasted_iota(jnp.int32, ref.shape, axis)
            slot = lax.broadcasted_iota(jnp.int32, ref.shape, 1 - axis)
            inner = slot & (SLOT - 1)
            same = (packed == (slot - inner) // SLOT * CAP + inner) & (inner < CAP)
            ref[...] = jnp.where(same, 1.0, 0.0).astype(jnp.bfloat16)

    drain = front_kernel(
        devices, start_weights, sources, held, own_sem, normed, state, meta,
        *front_buffers, *front_sems,
    )
    expert_kernel(
        devices, weight_copies, normed, meta, state, held[1], wide, out,
        *expert_buffers, *expert_sems,
    )
    drain()


def block_call(
    tokens, query_key_value, out_weight, modulation, router_weight, expert_ids,
    gate_up_weight, down_weight,
):
    devices = lax.axis_size("dev")
    count, width = tokens.shape
    half = down_weight.shape[2]
    halves = gate_up_weight.shape[0]
    local = halves // 2
    gate_up_weight = gate_up_weight.swapaxes(2, 3)
    hidden = gate_up_weight.shape[2]
    lines = devices // COLS
    rows = devices * SLOT
    slots, pack = local * SLOT, local * CAP
    part = half // CHUNKS
    pairs = half // 2 // PAIR
    shard = out_weight.shape[0]
    own = (
        tokens, query_key_value.transpose(1, 0, 2), out_weight, modulation,
        router_weight.T, expert_ids.T,
    )
    hbm = pl.BlockSpec(memory_space=pl.ANY)
    dma = pltpu.SemaphoreType.DMA
    return pl.pallas_call(
        functools.partial(block_kernel, devices),
        out_shape=jax.ShapeDtypeStruct((count, half), jnp.bfloat16),
        in_specs=[hbm] * 8,
        out_specs=pl.BlockSpec(memory_space=pltpu.VMEM),
        scratch_shapes=[
            *[pltpu.VMEM(own[i].shape, own[i].dtype) for i in (0, 3, 4, 5)],
            pltpu.VMEM((count, width), jnp.bfloat16),
            pltpu.VMEM((count, width), jnp.float32),
            pltpu.VMEM((router_weight.shape[1], count), jnp.float32),
            pltpu.VMEM((devices, slots + pack, half), jnp.bfloat16),
            pltpu.VMEM((4, 2, count, half // 2), jnp.bfloat16),
            pltpu.VMEM((COLS, count, half // 2), jnp.bfloat16),
            pltpu.VMEM((lines, shard, half), jnp.bfloat16),
            pltpu.VMEM((COLS * count, half), jnp.bfloat16),
            pltpu.VMEM((lines, 2, count, shard // 2), jnp.float32),
            pltpu.VMEM((lines, 2, count, shard // 2), jnp.float32),
            pltpu.VMEM((lines, 2, count, shard // 2), jnp.bfloat16),
            pltpu.VMEM((lines, 2, count, shard // 2), jnp.bfloat16),
            pltpu.VMEM((lines, 2, count, shard // 2), jnp.bfloat16),
            pltpu.VMEM((lines, CHUNKS, count, part), jnp.bfloat16),
            pltpu.VMEM((lines, CHUNKS, pack, part), jnp.bfloat16),
            pltpu.VMEM((lines, CHUNKS, pack, part), jnp.bfloat16),
            pltpu.VMEM((2, lines, CHUNKS, count, part), jnp.bfloat16),
            pltpu.VMEM((2, CHUNKS, local, rows, part), jnp.bfloat16),
            pltpu.VMEM(gate_up_weight.shape, jnp.bfloat16),
            pltpu.VMEM(down_weight.shape, jnp.bfloat16),
            pltpu.VMEM((local, 4 * hidden, rows), jnp.float32),
            pltpu.VMEM((local, 2 * hidden, rows), jnp.bfloat16),
            pltpu.VMEM((local, 2 * hidden, rows), jnp.bfloat16),
            pltpu.VMEM((lines, COLS * local, count), jnp.float32),
            pltpu.VMEM((lines, slots + pack, count), jnp.bfloat16),
            pltpu.VMEM((lines, slots + pack, count), jnp.bfloat16),
            pltpu.VMEM((pack, slots), jnp.bfloat16),
            pltpu.VMEM((slots, pack), jnp.bfloat16),
            pltpu.VMEM((count, part), jnp.float32),
            dma((7,)), dma((1,)), dma((1,)),
            dma((pairs,)), dma((pairs,)), dma((1,)), dma((1,)),
            dma((pairs,)), dma((pairs,)), dma((2, pairs)),
            dma((lines, 2)), dma((lines, PIECES)), dma((1,)), dma((lines,)), dma((1,)), dma((1,)),
            dma((1,)), dma((lines, 2)), dma((1,)), dma((lines, 2)), dma((1,)), dma((lines, 2)),
            dma((1,)), dma((lines,)),
            dma((lines, 2)), dma((lines, CHUNKS)), dma((1,)), dma((lines, CHUNKS)),
            dma((1,)), dma((2,)), dma((1,)), dma((local,)),
            dma((1,)), dma((lines, CHUNKS)), dma((1,)), dma((2, lines, CHUNKS)),
        ],
        compiler_params=pltpu.CompilerParams(
            collective_id=1, has_side_effects=True, vmem_limit_bytes=VMEM_BYTES
        ),
    )(*own, gate_up_weight, down_weight)


def body(
    tokens,
    query_key_value,
    out_weight,
    modulation,
    router_weight,
    expert_ids,
    gate_up_weight,
    down_weight,
):
    count = tokens.shape[0]
    width = tokens.shape[1]
    parts = lax.axis_size("sub")
    part = lax.axis_index("sub")
    position = lax.axis_index("dev")
    devices = lax.axis_size("dev")
    total = count * devices
    local_width = query_key_value.shape[2]
    weight_bytes = 2 * (gate_up_weight.size + down_weight.size)
    token_bytes = 12 * devices * count * width
    fits = weight_bytes + token_bytes < VMEM_BYTES and CAP <= SLOT
    paired = parts == 2 and lax.axis_size("groups") == 2 and devices % COLS == 0
    experts_here = gate_up_weight.shape[0] // 2
    tiled = out_weight.shape[0] % (2 * LANES) == 0 and count == LANES
    tiled = tiled and down_weight.shape[2] % (2 * PAIR) == 0 and devices == 4 * COLS
    tiled = tiled and down_weight.shape[2] % (2 * CHUNKS * LANES) == 0 and experts_here == devices
    tiled = tiled and SLOT * devices == LANES
    tiled = tiled and gate_up_weight.shape[3] % 64 == 0
    if fits and paired and tiled:
        return block_call(
            tokens, query_key_value, out_weight, modulation, router_weight, expert_ids,
            gate_up_weight, down_weight,
        )
    heads_here = local_width // HEAD
    query = query_key_value[:, 0].reshape(count, heads_here, HEAD)
    pair = query_key_value[:, 1:]
    near = extended(pair, (("dev", 0),), count)
    keys = near[:, 0].reshape(3 * count, heads_here, HEAD)
    values = near[:, 1].reshape(3 * count, heads_here, HEAD)
    mixed = window_attention(query, keys, values, position, total).reshape(count, local_width)
    partial_proj = lax.dot_general(
        mixed,
        lax.all_gather(out_weight, "dev", axis=0, tiled=True),
        (((1,), (1,)), ((), ())),
        preferred_element_type=jnp.float32,
    )
    proj = lax.psum(partial_proj, "sub")
    state = tokens.astype(jnp.float32) + (1.0 + modulation[0]) * proj
    normed = normalize(state, modulation)
    gates = route(normed, router_weight, expert_ids)
    experts = router_weight.shape[1]
    topk = expert_ids.shape[1]
    flat = expert_ids.reshape(-1)
    picks = flat.shape[0]
    onehot = (flat[:, None] == jnp.arange(experts, dtype=jnp.int32)[None, :]).astype(jnp.int32)
    rank = jnp.sum((jnp.cumsum(onehot, 0) - 1) * onehot, 1)
    target = flat * CAP + rank
    hit = target[None, :] == jnp.arange(experts * CAP, dtype=jnp.int32)[:, None]
    filled = jnp.any(hit, 1)
    anchor = jnp.sum(jnp.where(hit, jnp.arange(picks, dtype=jnp.int32)[None, :], 0), 1) // topk
    slice_width = width // parts
    sent = lax.dynamic_slice_in_dim(normed, part * slice_width, slice_width, 1)
    sent_width = sent.shape[1]
    rows_out = jnp.where(filled[:, None], sent[anchor], jnp.zeros((), jnp.bfloat16))
    halves_here = gate_up_weight.shape[0]
    doubled = jnp.broadcast_to(
        rows_out.reshape(experts, 1, CAP, sent_width), (experts, 2, CAP, sent_width)
    )
    outgoing = doubled.reshape(devices, halves_here, CAP, sent_width)
    up_form = "sxcd,xgdf->sxcgf"
    down_form = "sxcf,xfd->sxcd"
    incoming = lax.all_to_all(outgoing, "dev", split_axis=0, concat_axis=0, tiled=True)
    both = jnp.einsum(
        up_form,
        lax.all_gather(incoming, "sub", axis=3, tiled=True),
        gate_up_weight,
        preferred_element_type=jnp.float32,
    )
    hidden = (jax.nn.silu(both[..., 0, :]) * both[..., 1, :]).astype(jnp.bfloat16)
    gathered = lax.all_gather(hidden, "sub", axis=hidden.ndim - 1, tiled=True)
    result = jnp.einsum(down_form, gathered, down_weight, preferred_element_type=jnp.float32)
    returned = lax.all_to_all(
        result.astype(jnp.bfloat16), "dev", split_axis=0, concat_axis=0, tiled=True
    )
    own_width = returned.shape[-1]
    arranged = returned.reshape(experts, 2, CAP, own_width)
    answers = arranged[flat, :, rank, :].reshape(count, topk, 2, own_width).astype(jnp.float32)
    combined = answers[:, :, 0] + answers[:, :, 1]
    routed = jnp.einsum("tk,tkd->td", gates, combined)
    own = lax.dynamic_slice_in_dim(state, part * slice_width, slice_width, 1)
    lift = lax.dynamic_slice_in_dim(modulation[3], part * slice_width, slice_width, 0)
    return (own + (1.0 + lift) * routed).astype(jnp.bfloat16)


def solution(mesh):
    return jax.shard_map(
        body,
        mesh=mesh,
        in_specs=(
            P(("groups", "dev"), None),
            P(("groups", "dev"), None, "sub"),
            P("dev", "sub"),
            P("groups", None),
            P(),
            P(("groups", "dev"), None),
            P("dev", None, None, "sub"),
            P("dev", None, "sub"),
        ),
        out_specs=P(("groups", "dev"), "sub"),
        check_vma=False,
    )
```

```python
import functools
import math

import jax
import jax.numpy as jnp
from jax import lax
from jax.experimental import pallas as pl
from jax.experimental.pallas import tpu as pltpu
from jax.sharding import PartitionSpec as P

HEAD = 128
CAP = 12


EPS = 1e-06
NEG = -1e30


def extended(cells, sides, width):
    for axis, dim in sides:
        count = lax.axis_size(axis)
        ends = count - 1
        head = lax.slice_in_dim(cells, 0, width, axis=dim)
        tail = lax.slice_in_dim(cells, cells.shape[dim] - width, cells.shape[dim], axis=dim)
        cells = jnp.concatenate(
            [
                lax.ppermute(tail, axis, [(i, (i + 1) % count) for i in range(ends)]),
                cells,
                lax.ppermute(head, axis, [((i + 1) % count, i) for i in range(ends)]),
            ],
            axis=dim,
        )
    return cells


def window_attention(query, keys, values, index, total):
    count = query.shape[0]
    rows = jnp.arange(count, dtype=jnp.int32)[:, None]
    cols = jnp.arange(3 * count, dtype=jnp.int32)[None, :] - count
    place = index * count + cols
    allowed = (jnp.abs(cols - rows) <= count) & (place >= 0) & (place < total)
    scores = jnp.einsum(
        "qhd,khd->hqk", query, keys, preferred_element_type=jnp.float32
    ) / math.sqrt(query.shape[2])
    scores = jnp.where(allowed[None], scores, NEG)
    top = jnp.max(scores, -1, keepdims=True)
    weight = jnp.exp(scores - top)
    weight = (weight / jnp.sum(weight, -1, keepdims=True)).astype(jnp.bfloat16)
    mixed = jnp.einsum("hqk,khd->qhd", weight, values, preferred_element_type=jnp.float32)
    return mixed.astype(jnp.bfloat16)


def normalize(state, modulation):
    scale = lax.rsqrt(jnp.mean(state * state, -1, keepdims=True) + EPS)
    return (state * scale * (1.0 + modulation[2]) + modulation[1]).astype(jnp.bfloat16)


def route(normed, router_weight, expert_ids):
    logits = jnp.dot(normed, router_weight, preferred_element_type=jnp.float32)
    experts = router_weight.shape[1]
    match = expert_ids[:, :, None] == jnp.arange(experts, dtype=jnp.int32)[None, None, :]
    picked = jnp.sum(jnp.where(match, logits[:, None, :], 0.0), -1)
    lifted = jax.nn.sigmoid(picked)
    return lifted / jnp.sum(lifted, -1, keepdims=True)


LANES = 128
SLOT = 16
COLS = 2
CHUNKS = 4
PIECES = 4
LAG = 4
SPLIT = 2
PAIR = 256
VMEM_BYTES = 66 * 1000 * 1000
MESH = pl.DeviceIdType.MESH


def choose(index, table):
    value = jnp.int32(table[0])
    for i in range(1, len(table)):
        value = jnp.where(index == i, table[i], value)
    return value


def line_order(lines, nearest, inner=False):
    rows = []
    for z in range(lines):
        lower = (z < lines - 1 - z) != inner
        others = [line for line in range(lines) if line != z]
        sign = 1 if nearest else -1
        rows.append(sorted(others, key=lambda line: (sign * abs(line - z), (line > z) == lower)))
    return [[rows[z][j] for z in range(lines)] for j in range(lines - 1)]


def expert_kernel(
    devices, weight_copies,
    normed, meta, state, modulation, wide,
    out,
    tok, got_packed, got_rows, got_sum, disp, gu, dn, raised, hid_own, hid_other,
    got_meta, pick, gated, squeeze, grow, acc,
    meta_s, meta_r, z_s, z_r, x_s, x_r, core_s, core_r, hid_s, hid_r, rx_s, rx_r, rz_s, rz_r,
):
    me = lax.axis_index("dev")
    part = lax.axis_index("sub")
    other = 1 - part
    z = me // COLS
    x = me % COLS
    lines = devices // COLS
    count, width = normed.shape
    half = width // 2
    local = hid_own.shape[0]
    hidden = gu.shape[2]
    slots = local * SLOT
    pack = local * CAP
    rows = devices * SLOT
    chunks, wide_chunk = tok.shape[1], tok.shape[3]

    def remote(src, dst, send, recv, where):
        return pltpu.make_async_remote_copy(
            src_ref=src, dst_ref=dst, send_sem=send, recv_sem=recv,
            device_id=where, device_id_type=MESH,
        )

    above = jnp.minimum(me + COLS, devices - 1)
    below = jnp.maximum(me - COLS, 0)
    x_to = {"dev": z * COLS + (1 - x)}
    core_to = {"sub": other}
    not_top = z < lines - 1
    not_bottom = z > 0
    near_lines = [choose(z, table) for table in line_order(lines, True, True)]
    far_lines = [choose(z, table) for table in line_order(lines, False)]

    def lanes_of(c):
        return pl.ds(pl.multiple_of(c * wide_chunk, wide_chunk), wide_chunk)

    def own_lanes(c):
        return pl.ds(pl.multiple_of(part * half + c * wide_chunk, wide_chunk), wide_chunk)

    def slot_rows(s):
        return pl.ds(pl.multiple_of(s * SLOT, SLOT), SLOT)

    def meta_copy(line):
        return remote(
            meta.at[pl.ds(pl.multiple_of(line * COLS * local, COLS * local), COLS * local)],
            got_meta.at[z], meta_s.at[0], meta_r.at[z], {"dev": line * COLS + x},
        )

    def meta_arrival(line):
        return remote(got_meta.at[line], got_meta.at[line], meta_s.at[0], meta_r.at[line], x_to)

    def z_copy(line, c, way, src=None):
        dst = tok.at[line, c]
        where = {"dev": jnp.where(way == 0, above, below)}
        return remote(
            dst if src is None else src, dst, z_s.at[line, way], z_r.at[line, c], where
        )

    def packed_out(line, c):
        return wide.at[line, pl.ds(slots, pack), lanes_of(c)]

    def x_copy(line, c):
        return remote(
            packed_out(line, c), got_packed.at[line, c], x_s.at[0], x_r.at[line, c], x_to
        )

    def core_copy(which, s, c):
        place = disp.at[which, c, :, slot_rows(s), :]
        return remote(place, place, core_s.at[0], core_r.at[jnp.where(c < SPLIT, 0, 1)], core_to)

    def own_send(c):
        src = normed.at[:, own_lanes(c)]

        @pl.when(not_top)
        def _():
            z_copy(z, c, 0, src).start()

        @pl.when(not_bottom)
        def _():
            z_copy(z, c, 1, src).start()

    own_send(0)
    for line in near_lines:
        meta_copy(line).start()
    for c in range(1, chunks):
        own_send(c)

    before = (
        lax.broadcasted_iota(jnp.int32, (count, count), 0)
        < lax.broadcasted_iota(jnp.int32, (count, count), 1)
    ).astype(jnp.float32).astype(jnp.bfloat16)
    place = lax.broadcasted_iota(jnp.int32, (local, SLOT, count), 1).astype(jnp.float32)

    def routing(line, ours, theirs):
        for first, gate in ((True, ours), (False, theirs)):
            chosen = jnp.where(gate > 0.0, 1.0, 0.0)
            rank = jnp.dot(chosen.astype(jnp.bfloat16), before, preferred_element_type=jnp.float32)
            rank = jnp.where(gate > 0.0, rank, -1.0)
            hit = jnp.broadcast_to(rank[:, None, :], place.shape) == place
            one = jnp.where(hit, 1.0, 0.0).reshape(slots, count).astype(jnp.bfloat16)
            value = jnp.where(hit, jnp.broadcast_to(gate[:, None, :], place.shape), 0.0)
            value = value.reshape(slots, count).astype(jnp.bfloat16)
            if first:
                pick[line, :slots] = one
                gated[line, :slots] = value
            else:
                pick[line, slots:] = jnp.dot(
                    squeeze[...], one, preferred_element_type=jnp.float32
                ).astype(jnp.bfloat16)
                gated[line, slots:] = jnp.dot(
                    squeeze[...], value, preferred_element_type=jnp.float32
                ).astype(jnp.bfloat16)

    def expert_rows(base, column):
        return pl.ds(pl.multiple_of(base + column * local, local), local)

    def spread(line, c, block):
        moved = jnp.dot(pick[line], block, preferred_element_type=jnp.float32).astype(jnp.bfloat16)
        s = line * COLS + x
        wide[line, slots:slots + pack, lanes_of(c)] = moved[slots:]
        x_copy(line, c).start()
        disp[part, c, :, slot_rows(s), :] = moved[:slots].reshape(local, SLOT, wide_chunk)
        core_copy(part, s, c).start()

    def own_step(c):
        spread(z, c, normed[:, own_lanes(c)])

    def line_step(line, c):
        low = line < z

        @pl.when(c == 0)
        def _():
            meta_arrival(line).wait_recv()
            routing(
                line, got_meta[line, expert_rows(0, x)], got_meta[line, expert_rows(0, 1 - x)]
            )

        way = jnp.where(low, 0, 1)
        z_copy(line, c, way).wait_recv()

        @pl.when(jnp.where(low, not_top, not_bottom))
        def _():
            z_copy(line, c, way).start()

        spread(line, c, tok[line, c])

    def x_step(line, c):
        x_copy(line, c).wait_recv()
        s = line * COLS + (1 - x)
        disp[part, c, :, slot_rows(s), :] = jnp.dot(
            grow[...], got_packed[line, c], preferred_element_type=jnp.float32
        ).astype(jnp.bfloat16).reshape(local, SLOT, wide_chunk)
        core_copy(part, s, c).start()

    def across_rows(left, right):
        return lax.dot_general(
            left, right, (((1,), (1,)), ((), ())), preferred_element_type=jnp.float32
        )

    def raise_part(e, parts):
        sums = []
        for g in range(2):
            for b in range(2):
                total = None
                for side, c in parts:
                    start = side * half + c * wide_chunk
                    piece = across_rows(
                        gu[2 * e + b, g, :, start:start + wide_chunk], disp[side, c, e]
                    )
                    total = piece if total is None else total + piece
                sums.append(total)
        return sums

    def raise_some(parts, start, stop, first=False, last=False):
        def one(e, carry):
            sums = raise_part(e, parts)
            if not first:
                sums = [
                    total + raised[e, n * hidden:(n + 1) * hidden] for n, total in enumerate(sums)
                ]
            if not last:
                for n, total in enumerate(sums):
                    raised[e, n * hidden:(n + 1) * hidden] = total
                return carry
            for b in range(2):
                gate = sums[b]
                hid_own[e, b * hidden:(b + 1) * hidden] = (
                    gate * jax.nn.sigmoid(gate) * sums[2 + b]
                ).astype(jnp.bfloat16)
            hid_copy(e).start()
            return carry

        lax.fori_loop(start, stop, one, 0)

    def hid_copy(e):
        return remote(hid_own.at[e], hid_other.at[e], hid_s.at[0], hid_r.at[e // (local // 2)], core_to)

    def arrived(which):
        span_of = pl.ds(which * SPLIT, SPLIT) if which == 0 else pl.ds(SPLIT, chunks - SPLIT)
        block = disp.at[other, span_of]
        remote(block, block, core_s.at[0], core_r.at[which], core_to).wait_recv()

    def sent(ref, sem):
        remote(ref, ref, sem, sem, core_to).wait_send()

    routing(
        z, meta[expert_rows(z * COLS * local, x)], meta[expert_rows(z * COLS * local, 1 - x)]
    )
    for c in range(chunks):
        own_step(c)

    for copy in weight_copies():
        copy.wait()

    offsets = [(jnp.abs(line - z) - 1) * chunks for line in near_lines]
    offsets[1] = jnp.maximum(offsets[1], SPLIT)

    def step(t, carry):
        for line, offset in zip(near_lines, offsets):
            c = t - offset

            @pl.when((c >= 0) & (c < chunks))
            def _():
                line_step(line, c)

        @pl.when((t >= LAG - 1) & (t < LAG - 1 + chunks))
        def _():
            x_step(z, t - LAG + 1)

        for line, offset in zip(near_lines, offsets):
            c = t - LAG - offset

            @pl.when((c >= 0) & (c < chunks))
            def _():
                x_step(line, c)

        return carry

    span = chunks * (lines - 1) + LAG
    lax.fori_loop(0, span - 2, step, 0)
    early = range(SPLIT)
    late = range(SPLIT, chunks)
    own_first = (part == 1) & ((z == 0) | (z == lines - 1))

    @pl.when(own_first)
    def _():
        raise_some([(1, c) for c in early], 0, local, first=True)
        step(span - 2, 0)
        step(span - 1, 0)
        raise_some([(1, c) for c in late], 0, local)
        arrived(0)
        arrived(1)
        raise_some([(0, c) for c in range(chunks)], 0, local, last=True)

    @pl.when(jnp.logical_not(own_first))
    def _():
        arrived(0)
        raise_some([(side, c) for c in early for side in range(2)], 0, local // 2, first=True)
        step(span - 2, 0)
        step(span - 1, 0)
        raise_some([(side, c) for c in early for side in range(2)], local // 2, local, first=True)
        arrived(1)
        raise_some([(side, c) for c in late for side in range(2)], 0, local, last=True)

    group = 2 * wide_chunk

    def lower(g):
        lanes = slice(g * group, (g + 1) * group)

        def one(e, carry):
            mine = pl.ds(pl.multiple_of(part * hidden, SLOT), hidden)
            theirs = pl.ds(pl.multiple_of(other * hidden, SLOT), hidden)
            left = jnp.concatenate([hid_own[e], hid_other[e]], axis=0)
            right = jnp.concatenate(
                [dn[2 * e, mine, lanes], dn[2 * e + 1, mine, lanes],
                 dn[2 * e, theirs, lanes], dn[2 * e + 1, theirs, lanes]], axis=0
            )
            wide[e, :rows, lanes] = lax.dot_general(
                left, right, (((0,), (0,)), ((), ())), preferred_element_type=jnp.float32
            ).astype(jnp.bfloat16)
            return carry

        for which in range(2):
            if g == 0:
                block = hid_other.at[pl.ds(which * (local // 2), local // 2)]
                remote(block, block, hid_s.at[0], hid_r.at[which], core_to).wait_recv()
            lax.fori_loop(which * (local // 2), (which + 1) * (local // 2), one, 0)

    def result_rows(s, q):
        return wide[:local, slot_rows(s), lanes_of(q)].reshape(slots, wide_chunk)

    def rx_copy(line, q):
        return remote(
            wide.at[lines + line, pl.ds(slots, pack), lanes_of(q)], got_rows.at[line, q],
            rx_s.at[0], rx_r.at[line, q], x_to,
        )

    def rz_copy(line, q, way, owner=None):
        owner = z - 1 if owner is None else owner
        where = {"dev": jnp.where(way == 0, above, below)}
        return remote(
            tok.at[line, q], got_sum.at[way, line, q],
            rz_s.at[0], rz_r.at[jnp.where((way == 1) & (line == owner), lines, line), q], where,
        )

    def give(line, q):
        packed = jnp.dot(
            squeeze[...], result_rows(line * COLS + (1 - x), q), preferred_element_type=jnp.float32
        )
        wide[lines + line, slots:slots + pack, lanes_of(q)] = packed.astype(jnp.bfloat16)
        rx_copy(line, q).start()

    def gather_here(line, q):
        rx_copy(line, q).wait_recv()
        pieces = jnp.concatenate([result_rows(line * COLS + x, q), got_rows[line, q]], axis=0)
        acc[...] = lax.dot_general(
            gated[line], pieces, (((0,), (0,)), ((), ())), preferred_element_type=jnp.float32
        )

    def add_line(line, q, way):
        rz_copy(line, q, way, z).wait_recv()
        acc[...] += got_sum[way, line, q].astype(jnp.float32)

    def pass_on(line, q):
        gather_here(line, q)
        way = jnp.where(line > z, 0, 1)

        @pl.when(jnp.where(line > z, not_bottom, not_top))
        def _():
            add_line(line, q, way)

        tok[line, q] = acc[...].astype(jnp.bfloat16)
        rz_copy(line, q, way).start()

    for g in range(half // group):
        lower(g)
        for q in range(2 * g, 2 * g + 2):
            give(far_lines[0], q)
    def give_all(line):
        lax.fori_loop(0, chunks, lambda q, carry: (give(line, q), carry)[1], 0)

    for line in near_lines:
        low = line < z

        @pl.when(jnp.where(low, not_top, not_bottom))
        def _():
            sent(tok.at[line], z_s.at[line, jnp.where(low, 0, 1)])

    far_end = (z == 0) | (z == lines - 1)

    @pl.when(far_end)
    def _():
        for q in range(2):
            pass_on(far_lines[0], q)

    give_all(far_lines[1])

    @pl.when(far_end)
    def _():
        for q in range(2, chunks):
            pass_on(far_lines[0], q)

    for line in far_lines[2:] + [z]:
        give_all(line)

    @pl.when(jnp.logical_not(far_end))
    def _():
        for q in range(chunks):
            pass_on(far_lines[0], q)

    for line in far_lines[1:]:
        lax.fori_loop(0, chunks, lambda q, carry, line=line: (pass_on(line, q), carry)[1], 0)
    for q in range(chunks):
        gather_here(z, q)

        @pl.when(not_bottom)
        def _():
            add_line(z, q, 0)

        @pl.when(not_top)
        def _():
            add_line(z, q, 1)

        own = own_lanes(q)
        lanes = slice(q * wide_chunk, (q + 1) * wide_chunk)
        out[:, lanes] = (
            state[:, own] + (1.0 + modulation[3:4, own]) * acc[...]
        ).astype(out.dtype)

    @pl.when(not_top)
    def _():
        sent(tok.at[z], z_s.at[z, 0])

    @pl.when(not_bottom)
    def _():
        sent(tok.at[z], z_s.at[z, 1])

    sent(tok.at[pl.ds(0, lines - 1)], rz_s.at[0])
    sent(got_packed, x_s.at[0])
    sent(got_rows, rx_s.at[0])
    sent(disp.at[part], core_s.at[0])
    sent(got_meta.at[pl.ds(0, lines - 1)], meta_s.at[0])
    sent(hid_own, hid_s.at[0])


def front_kernel(
    devices, start_weights,
    sources, held, own_sem,
    normed, state, meta,
    window, queries, column, mixed, mine_out, their_out, sent_back, got_back, their_back,
    pair_s, pair_r, query_s, query_r, early_s, late_s, edge_r, wz_s, wz_r, wy_s, wy_r, mix_s, mix_r,
    sum_s, sum_r, back_s, back_r, share_s, share_r,
):
    packed_hbm, weight_hbm = sources[1], sources[2]
    tokens, modulation, router, ids = held
    me = lax.axis_index("dev")
    part = lax.axis_index("sub")
    group = lax.axis_index("groups")
    z = me // COLS
    x = me % COLS
    lines = devices // COLS
    count, width = tokens.shape
    shard = column.shape[1]
    share = shard // 2
    piece = share // PIECES
    heads = window.shape[3]
    pairs = heads // PAIR
    ours = pl.ds(pl.multiple_of(x * heads, heads), heads)
    theirs = pl.ds(pl.multiple_of((1 - x) * heads, heads), heads)
    own_parts = (
        (packed_hbm.at[1:3, :, ours], window.at[1 + x]), (packed_hbm.at[0, :, ours], queries.at[x]),
        (weight_hbm, column.at[z]), (sources[0], tokens), (sources[3], modulation),
        (sources[4], router), (sources[5], ids),
    )

    def own_copy(i):
        return pltpu.make_async_copy(*own_parts[i], own_sem.at[i])

    for i in range(len(own_parts)):
        own_copy(i).start()
    not_top = z < lines - 1
    not_bottom = z > 0
    above = jnp.minimum(me + COLS, devices - 1)
    below = jnp.maximum(me - COLS, 0)
    x_to = {"dev": z * COLS + (1 - x)}
    y_to = {"groups": 1 - group}
    core_to = {"sub": 1 - part}
    near_lines = [choose(z, table) for table in line_order(lines, True)]

    barrier = pltpu.get_barrier_semaphore()

    def greet(where):
        pl.semaphore_signal(barrier, inc=1, device_id=where, device_id_type=MESH)

    for where in (x_to, y_to, core_to, {**x_to, **core_to}):
        greet(where)
    for line in near_lines:
        greet({"dev": line * COLS + x})
    pl.semaphore_wait(barrier, lines + 3)

    def remote(src, dst, send, recv, where):
        return pltpu.make_async_remote_copy(
            src_ref=src, dst_ref=dst, send_sem=send, recv_sem=recv,
            device_id=where, device_id_type=MESH,
        )

    def part_lanes(base, k):
        return pl.ds(pl.multiple_of(base * heads + k * PAIR, PAIR), PAIR)

    def pair_copy(k):
        return remote(
            packed_hbm.at[1:3, :, part_lanes(1 - x, k)], window.at[1 + x, :, :, part_lanes(0, k)],
            pair_s.at[k], pair_r.at[k], x_to,
        )

    def query_copy():
        return remote(
            packed_hbm.at[0, :, theirs], queries.at[x], query_s.at[0], query_r.at[0], x_to
        )

    def edge_copy(k, up, src, send):
        where = {"dev": jnp.where(up, above, below)}
        place = jnp.where(up, 0, 3)
        return remote(
            src, window.at[place, :, :, part_lanes(0, k)], send,
            edge_r.at[jnp.where(up, 0, 1), k], where,
        )

    def early_copy(k):
        return edge_copy(k, x == 1, packed_hbm.at[1:3, :, part_lanes(x, k)], early_s.at[k])

    def late_copy(k):
        return edge_copy(k, x == 0, window.at[2 - x, :, :, part_lanes(0, k)], late_s.at[k])

    give_late = ((x == 0) & not_top) | ((x == 1) & not_bottom)
    give_early = ((x == 1) & not_top) | ((x == 0) & not_bottom)

    def piece_rows(which, i):
        return pl.ds(pl.multiple_of(which * share + i * piece, SLOT), piece)

    def wz_copy(line, i, way, src=None):
        dst = column.at[line, piece_rows(group, i)]
        where = {"dev": jnp.where(way == 0, above, below)}
        return remote(
            dst if src is None else src, dst, wz_s.at[line, way], wz_r.at[line, i], where
        )

    def own_piece(i):
        return weight_hbm.at[piece_rows(group, i)]

    def wy_copy(line, i, which):
        block = column.at[line, piece_rows(which, i)]
        return remote(block, block, wy_s.at[0], wy_r.at[line], y_to)

    for k in range(pairs):
        pair_copy(k).start()
    query_copy().start()

    def send_pieces(pieces):
        for i in pieces:

            @pl.when(not_top)
            def _():
                wz_copy(z, i, 0, own_piece(i)).start()

            @pl.when(not_bottom)
            def _():
                wz_copy(z, i, 1, own_piece(i)).start()

    send_pieces(range(PIECES // 2))

    @pl.when(give_early)
    def _():
        for k in range(pairs):
            early_copy(k).start()

    send_pieces(range(PIECES // 2, PIECES))
    start_weights()

    @pl.when(jnp.logical_not(not_bottom))
    def _():
        window[0] = jnp.zeros_like(window[0])

    @pl.when(jnp.logical_not(not_top))
    def _():
        window[3] = jnp.zeros_like(window[3])

    def way_of(line):
        return jnp.where(line < z, 0, 1)

    def more(line):
        return jnp.where(line < z, not_top, not_bottom)

    def busy(line):
        return jnp.where(line < z, x == 0, x == 1)

    def distance(line):
        return jnp.abs(line - z)

    def take(line, onward, pieces=range(PIECES)):
        for i in pieces:
            wz_copy(line, i, way_of(line)).wait_recv()

            @pl.when(onward)
            def _():
                wz_copy(line, i, way_of(line)).start()

            wy_copy(line, i, group).start()

    def take_next(only_busy, pieces):
        for line in near_lines:

            @pl.when((distance(line) == 1) & (busy(line) if only_busy else jnp.logical_not(busy(line))))
            def _():
                take(line, more(line), pieces)

    for k in range(pairs):
        pair_copy(k).wait_recv()

        @pl.when(give_late)
        def _():
            late_copy(k).start()

    take_next(True, range(PIECES // 2))
    take_next(False, range(PIECES // 2))
    for i in range(len(own_parts)):
        own_copy(i).wait()
    query_copy().wait_recv()

    row = lax.broadcasted_iota(jnp.int32, (count, count), 0)
    col = lax.broadcasted_iota(jnp.int32, (count, count), 1)

    def mix_copy(b, k):
        block = mixed.at[pl.ds(pl.multiple_of(b * count, count), count), part_lanes(x, k)]
        return remote(block, block, mix_s.at[0], mix_r.at[0], x_to)

    def attend(b, k):
        see_before = (col >= row) & ((z > 0) | (b == 1))
        see_after = (col <= row) & ((z < lines - 1) | (b == 0))
        for h in range(PAIR // HEAD):
            inner = slice(k * PAIR + h * HEAD, k * PAIR + (h + 1) * HEAD)
            query = queries[b, :, inner]

            def score(keys):
                return lax.dot_general(
                    query, keys, (((1,), (1,)), ((), ())), preferred_element_type=jnp.float32
                ) / math.sqrt(HEAD)

            scores = jnp.concatenate(
                [
                    jnp.where(see_before, score(window[b, 0, :, inner]), NEG),
                    score(window[b + 1, 0, :, inner]),
                    jnp.where(see_after, score(window[b + 2, 0, :, inner]), NEG),
                ],
                axis=1,
            )
            top = jnp.max(scores, -1, keepdims=True)
            weight = jnp.exp(scores - top)
            weight = (weight / jnp.sum(weight, -1, keepdims=True)).astype(jnp.bfloat16)
            values = jnp.concatenate([window[b + n, 1, :, inner] for n in range(3)], axis=0)
            lanes = pl.ds(
                pl.multiple_of(x * heads + k * PAIR + h * HEAD, HEAD), HEAD
            )
            mixed[pl.ds(pl.multiple_of(b * count, count), count), lanes] = jnp.dot(
                weight, values, preferred_element_type=jnp.float32
            ).astype(jnp.bfloat16)
        mix_copy(b, k).start()

    for b, up in ((1 - x, x == 1), (x, x == 0)):
        for k in range(pairs):

            @pl.when(jnp.where(up, not_bottom, not_top))
            def _():
                edge_copy(k, up, window.at[0, :, :, part_lanes(0, k)], early_s.at[k]).wait_recv()

            attend(b, k)
        if b is not x:
            take_next(True, range(PIECES // 2, PIECES))
            take_next(False, range(PIECES // 2, PIECES))
        else:
            for line in near_lines:

                @pl.when(distance(line) == 2)
                def _():
                    take(line, more(line))

    last = near_lines[-1]
    far_last = distance(last) > 2

    def take_last(pieces):
        @pl.when(far_last)
        def _():
            take(last, more(last), pieces)

    mix_block = mixed.at[:, theirs]
    remote(mix_block, mix_block, mix_s.at[0], mix_r.at[0], x_to).wait_recv()

    def place_of(which):
        return group if which == 0 else 1 - group

    def group_of(line):
        return jnp.where(line == last, 1, 0)

    def come(ref, sem):
        remote(ref, ref, sum_s.at[0], sem, core_to).wait_recv()

    def sum_copy(line, which):
        place = place_of(which)
        return remote(
            mine_out.at[line, place], their_out.at[line, place],
            sum_s.at[0], sum_r.at[group_of(line)], core_to,
        )

    def back_copy(line, which):
        place = place_of(which)
        return remote(
            sent_back.at[line, place], got_back.at[line, place],
            back_s.at[0], back_r.at[line], x_to,
        )

    def share_copy(line, which):
        place = place_of(which)
        return remote(
            got_back.at[line, place], their_back.at[line, place],
            share_s.at[0], share_r.at[group_of(line)], core_to,
        )

    def direct_copy(which):
        place = place_of(which)
        return remote(
            sent_back.at[last, place], their_back.at[last, place],
            share_s.at[0], share_r.at[1],
            {"dev": z * COLS + (1 - x), "sub": 1 - part},
        )

    def project(line, which, direct=False):
        place = place_of(which)
        block = column[line, pl.ds(pl.multiple_of(place * share, SLOT), share), :]
        both = jnp.concatenate(
            [mixed[pl.ds(pl.multiple_of(b * count, count), count), :] for b in (1 - x, x)], axis=0
        )
        product = lax.dot_general(
            both, block, (((1,), (1,)), ((), ())), preferred_element_type=jnp.float32
        )
        sent_back[line, place] = product[:count].astype(jnp.bfloat16)
        back_copy(line, which).start()
        if direct:
            direct_copy(which).start()
        mine_out[line, place] = product[count:]
        sum_copy(line, which).start()

    def halves_in(line):
        block = column.at[line, pl.ds(pl.multiple_of((1 - group) * share, SLOT), share)]
        remote(block, block, wy_s.at[0], wy_r.at[line], y_to).wait_recv()

    def last_step():
        halves_in(last)
        project(last, 1, True)

    def add_up(line, which):
        place = place_of(which)
        partial = jnp.zeros((count, share), jnp.float32)
        for column_of, total in (
            (x, mine_out[line, place] + their_out[line, place]),
            (
                1 - x,
                got_back[line, place].astype(jnp.float32)
                + their_back[line, place].astype(jnp.float32),
            ),
        ):
            start = (line * COLS + column_of) * shard + place * share
            lanes = pl.ds(pl.multiple_of(start, LANES), share)
            value = tokens[:, lanes].astype(jnp.float32) + (1.0 + modulation[0:1, lanes]) * total
            state[:, lanes] = value
            partial = partial + value * value
        return partial

    steps = [(line, which) for line in [z] + near_lines[:-1] for which in range(2)]
    quarter = PIECES // 4
    for i, (line, which) in enumerate(steps):
        if which == 1 and i > 1:
            halves_in(line)
        project(line, which)
        if i < 4:
            take_last(range(i * quarter, (i + 1) * quarter))
    project(last, 0, True)

    @pl.when(jnp.logical_not(far_last))
    def _():
        last_step()

    def relay(some):
        for line, which in some:
            if which == 0:
                come(got_back.at[line], back_r.at[line])
            share_copy(line, which).start()

    relay(steps[:4])

    @pl.when(far_last)
    def _():
        last_step()

    relay(steps[4:])
    squares = jnp.zeros((count, share), jnp.float32)
    come(mine_out.at[pl.ds(0, lines - 1)], sum_r.at[0])
    come(got_back.at[pl.ds(0, lines - 1)], share_r.at[0])
    for line, which in steps:
        squares = squares + add_up(line, which)
    come(got_back.at[last], back_r.at[last])
    come(mine_out.at[last], sum_r.at[1])
    come(got_back.at[last], share_r.at[1])
    for which in range(2):
        squares = squares + add_up(last, which)
    square = jnp.sum(squares, -1, keepdims=True)
    scale = lax.rsqrt(square / width + EPS)
    for s in range(devices):
        lanes = slice(s * shard, (s + 1) * shard)
        normed[:, lanes] = (
            state[:, lanes] * scale * (1.0 + modulation[2:3, lanes]) + modulation[1:2, lanes]
        ).astype(jnp.bfloat16)
    logits = lax.dot_general(
        router[...], normed[...], (((1,), (1,)), ((), ())), preferred_element_type=jnp.float32
    )
    name = lax.broadcasted_iota(jnp.int32, logits.shape, 0)
    named = name == ids[0:1]
    for k in range(1, ids.shape[0]):
        named = named | (name == ids[k:k + 1])
    lifted = jnp.where(named, jax.nn.sigmoid(logits), 0.0)
    meta[...] = lifted / jnp.sum(lifted, 0, keepdims=True)

    def drain():
        def sent(ref, sem):
            remote(ref, ref, sem, sem, x_to).wait_send()

        query_copy().wait_send()
        sent(mixed.at[:, ours], mix_s.at[0])
        for k in range(pairs):
            pair_copy(k).wait_send()

            @pl.when(give_early)
            def _():
                early_copy(k).wait_send()

            @pl.when(give_late)
            def _():
                late_copy(k).wait_send()

        half_shard = column.at[0, pl.ds(0, share)]

        @pl.when(not_top)
        def _():
            sent(half_shard, wz_s.at[z, 0])

        @pl.when(not_bottom)
        def _():
            sent(half_shard, wz_s.at[z, 1])

        for line in near_lines:

            @pl.when(more(line))
            def _():
                sent(half_shard, wz_s.at[line, way_of(line)])

        sent(column.at[pl.ds(0, lines - 1), pl.ds(0, share)], wy_s.at[0])
        sent(mine_out, sum_s.at[0])
        sent(sent_back, back_s.at[0])
        sent(got_back, share_s.at[0])

    return drain


def block_kernel(devices, *refs):
    sources, gate_up, down, out = refs[:6], refs[6], refs[7], refs[8]
    held, normed, state, meta, wide = refs[9:13], refs[13], refs[14], refs[15], refs[16]
    front_buffers, expert_buffers = refs[17:26], refs[26:42]
    own_sem, gu_sem, dn_sem = refs[42:45]
    front_sems, expert_sems = refs[45:64], refs[64:]
    gu, dn = expert_buffers[5:7]
    squeeze, grow = expert_buffers[13:15]
    def weight_copies():
        return (
            pltpu.make_async_copy(gate_up, gu, gu_sem.at[0]),
            pltpu.make_async_copy(down, dn, dn_sem.at[0]),
        )

    def start_weights():
        for copy in weight_copies():
            copy.start()
        for ref, axis in ((squeeze, 0), (grow, 1)):
            packed = lax.broadcasted_iota(jnp.int32, ref.shape, axis)
            slot = lax.broadcasted_iota(jnp.int32, ref.shape, 1 - axis)
            inner = slot & (SLOT - 1)
            same = (packed == (slot - inner) // SLOT * CAP + inner) & (inner < CAP)
            ref[...] = jnp.where(same, 1.0, 0.0).astype(jnp.bfloat16)

    drain = front_kernel(
        devices, start_weights, sources, held, own_sem, normed, state, meta,
        *front_buffers, *front_sems,
    )
    expert_kernel(
        devices, weight_copies, normed, meta, state, held[1], wide, out,
        *expert_buffers, *expert_sems,
    )
    drain()


def block_call(
    tokens, query_key_value, out_weight, modulation, router_weight, expert_ids,
    gate_up_weight, down_weight,
):
    devices = lax.axis_size("dev")
    count, width = tokens.shape
    half = down_weight.shape[2]
    halves = gate_up_weight.shape[0]
    local = halves // 2
    gate_up_weight = gate_up_weight.swapaxes(2, 3)
    hidden = gate_up_weight.shape[2]
    lines = devices // COLS
    rows = devices * SLOT
    slots, pack = local * SLOT, local * CAP
    part = half // CHUNKS
    pairs = half // 2 // PAIR
    shard = out_weight.shape[0]
    own = (
        tokens, query_key_value.transpose(1, 0, 2), out_weight, modulation,
        router_weight.T, expert_ids.T,
    )
    hbm = pl.BlockSpec(memory_space=pl.ANY)
    dma = pltpu.SemaphoreType.DMA
    return pl.pallas_call(
        functools.partial(block_kernel, devices),
        out_shape=jax.ShapeDtypeStruct((count, half), jnp.bfloat16),
        in_specs=[hbm] * 8,
        out_specs=pl.BlockSpec(memory_space=pltpu.VMEM),
        scratch_shapes=[
            *[pltpu.VMEM(own[i].shape, own[i].dtype) for i in (0, 3, 4, 5)],
            pltpu.VMEM((count, width), jnp.bfloat16),
            pltpu.VMEM((count, width), jnp.float32),
            pltpu.VMEM((router_weight.shape[1], count), jnp.float32),
            pltpu.VMEM((devices, slots + pack, half), jnp.bfloat16),
            pltpu.VMEM((4, 2, count, half // 2), jnp.bfloat16),
            pltpu.VMEM((COLS, count, half // 2), jnp.bfloat16),
            pltpu.VMEM((lines, shard, half), jnp.bfloat16),
            pltpu.VMEM((COLS * count, half), jnp.bfloat16),
            pltpu.VMEM((lines, 2, count, shard // 2), jnp.float32),
            pltpu.VMEM((lines, 2, count, shard // 2), jnp.float32),
            pltpu.VMEM((lines, 2, count, shard // 2), jnp.bfloat16),
            pltpu.VMEM((lines, 2, count, shard // 2), jnp.bfloat16),
            pltpu.VMEM((lines, 2, count, shard // 2), jnp.bfloat16),
            pltpu.VMEM((lines, CHUNKS, count, part), jnp.bfloat16),
            pltpu.VMEM((lines, CHUNKS, pack, part), jnp.bfloat16),
            pltpu.VMEM((lines, CHUNKS, pack, part), jnp.bfloat16),
            pltpu.VMEM((2, lines, CHUNKS, count, part), jnp.bfloat16),
            pltpu.VMEM((2, CHUNKS, local, rows, part), jnp.bfloat16),
            pltpu.VMEM(gate_up_weight.shape, jnp.bfloat16),
            pltpu.VMEM(down_weight.shape, jnp.bfloat16),
            pltpu.VMEM((local, 4 * hidden, rows), jnp.float32),
            pltpu.VMEM((local, 2 * hidden, rows), jnp.bfloat16),
            pltpu.VMEM((local, 2 * hidden, rows), jnp.bfloat16),
            pltpu.VMEM((lines, COLS * local, count), jnp.float32),
            pltpu.VMEM((lines, slots + pack, count), jnp.bfloat16),
            pltpu.VMEM((lines, slots + pack, count), jnp.bfloat16),
            pltpu.VMEM((pack, slots), jnp.bfloat16),
            pltpu.VMEM((slots, pack), jnp.bfloat16),
            pltpu.VMEM((count, part), jnp.float32),
            dma((7,)), dma((1,)), dma((1,)),
            dma((pairs,)), dma((pairs,)), dma((1,)), dma((1,)),
            dma((pairs,)), dma((pairs,)), dma((2, pairs)),
            dma((lines, 2)), dma((lines, PIECES)), dma((1,)), dma((lines,)), dma((1,)), dma((1,)),
            dma((1,)), dma((2,)), dma((1,)), dma((lines,)), dma((1,)), dma((2,)),
            dma((1,)), dma((lines,)),
            dma((lines, 2)), dma((lines, CHUNKS)), dma((1,)), dma((lines, CHUNKS)),
            dma((1,)), dma((2,)), dma((1,)), dma((2,)),
            dma((1,)), dma((lines, CHUNKS)), dma((1,)), dma((lines + 1, CHUNKS)),
        ],
        compiler_params=pltpu.CompilerParams(
            collective_id=1, has_side_effects=True, vmem_limit_bytes=VMEM_BYTES
        ),
    )(*own, gate_up_weight, down_weight)


def body(
    tokens,
    query_key_value,
    out_weight,
    modulation,
    router_weight,
    expert_ids,
    gate_up_weight,
    down_weight,
):
    count = tokens.shape[0]
    width = tokens.shape[1]
    parts = lax.axis_size("sub")
    part = lax.axis_index("sub")
    position = lax.axis_index("dev")
    devices = lax.axis_size("dev")
    total = count * devices
    local_width = query_key_value.shape[2]
    weight_bytes = 2 * (gate_up_weight.size + down_weight.size)
    token_bytes = 12 * devices * count * width
    fits = weight_bytes + token_bytes < VMEM_BYTES and CAP <= SLOT
    paired = parts == 2 and lax.axis_size("groups") == 2 and devices % COLS == 0
    experts_here = gate_up_weight.shape[0] // 2
    tiled = out_weight.shape[0] % (2 * LANES) == 0 and count == LANES
    tiled = tiled and down_weight.shape[2] % (2 * PAIR) == 0 and devices == 4 * COLS
    tiled = tiled and down_weight.shape[2] % (2 * CHUNKS * LANES) == 0 and experts_here == devices
    tiled = tiled and SLOT * devices == LANES
    tiled = tiled and gate_up_weight.shape[3] % 64 == 0
    if fits and paired and tiled:
        return block_call(
            tokens, query_key_value, out_weight, modulation, router_weight, expert_ids,
            gate_up_weight, down_weight,
        )
    heads_here = local_width // HEAD
    query = query_key_value[:, 0].reshape(count, heads_here, HEAD)
    pair = query_key_value[:, 1:]
    near = extended(pair, (("dev", 0),), count)
    keys = near[:, 0].reshape(3 * count, heads_here, HEAD)
    values = near[:, 1].reshape(3 * count, heads_here, HEAD)
    mixed = window_attention(query, keys, values, position, total).reshape(count, local_width)
    partial_proj = lax.dot_general(
        mixed,
        lax.all_gather(out_weight, "dev", axis=0, tiled=True),
        (((1,), (1,)), ((), ())),
        preferred_element_type=jnp.float32,
    )
    proj = lax.psum(partial_proj, "sub")
    state = tokens.astype(jnp.float32) + (1.0 + modulation[0]) * proj
    normed = normalize(state, modulation)
    gates = route(normed, router_weight, expert_ids)
    experts = router_weight.shape[1]
    topk = expert_ids.shape[1]
    flat = expert_ids.reshape(-1)
    picks = flat.shape[0]
    onehot = (flat[:, None] == jnp.arange(experts, dtype=jnp.int32)[None, :]).astype(jnp.int32)
    rank = jnp.sum((jnp.cumsum(onehot, 0) - 1) * onehot, 1)
    target = flat * CAP + rank
    hit = target[None, :] == jnp.arange(experts * CAP, dtype=jnp.int32)[:, None]
    filled = jnp.any(hit, 1)
    anchor = jnp.sum(jnp.where(hit, jnp.arange(picks, dtype=jnp.int32)[None, :], 0), 1) // topk
    slice_width = width // parts
    sent = lax.dynamic_slice_in_dim(normed, part * slice_width, slice_width, 1)
    sent_width = sent.shape[1]
    rows_out = jnp.where(filled[:, None], sent[anchor], jnp.zeros((), jnp.bfloat16))
    halves_here = gate_up_weight.shape[0]
    doubled = jnp.broadcast_to(
        rows_out.reshape(experts, 1, CAP, sent_width), (experts, 2, CAP, sent_width)
    )
    outgoing = doubled.reshape(devices, halves_here, CAP, sent_width)
    up_form = "sxcd,xgdf->sxcgf"
    down_form = "sxcf,xfd->sxcd"
    incoming = lax.all_to_all(outgoing, "dev", split_axis=0, concat_axis=0, tiled=True)
    both = jnp.einsum(
        up_form,
        lax.all_gather(incoming, "sub", axis=3, tiled=True),
        gate_up_weight,
        preferred_element_type=jnp.float32,
    )
    hidden = (jax.nn.silu(both[..., 0, :]) * both[..., 1, :]).astype(jnp.bfloat16)
    gathered = lax.all_gather(hidden, "sub", axis=hidden.ndim - 1, tiled=True)
    result = jnp.einsum(down_form, gathered, down_weight, preferred_element_type=jnp.float32)
    returned = lax.all_to_all(
        result.astype(jnp.bfloat16), "dev", split_axis=0, concat_axis=0, tiled=True
    )
    own_width = returned.shape[-1]
    arranged = returned.reshape(experts, 2, CAP, own_width)
    answers = arranged[flat, :, rank, :].reshape(count, topk, 2, own_width).astype(jnp.float32)
    combined = answers[:, :, 0] + answers[:, :, 1]
    routed = jnp.einsum("tk,tkd->td", gates, combined)
    own = lax.dynamic_slice_in_dim(state, part * slice_width, slice_width, 1)
    lift = lax.dynamic_slice_in_dim(modulation[3], part * slice_width, slice_width, 0)
    return (own + (1.0 + lift) * routed).astype(jnp.bfloat16)


def solution(mesh):
    return jax.shard_map(
        body,
        mesh=mesh,
        in_specs=(
            P(("groups", "dev"), None),
            P(("groups", "dev"), None, "sub"),
            P("dev", "sub"),
            P("groups", None),
            P(),
            P(("groups", "dev"), None),
            P("dev", None, None, "sub"),
            P("dev", None, "sub"),
        ),
        out_specs=P(("groups", "dev"), "sub"),
        check_vma=False,
    )
```

```python
import functools
import math

import jax
import jax.numpy as jnp
from jax import lax
from jax.experimental import pallas as pl
from jax.experimental.pallas import tpu as pltpu
from jax.sharding import PartitionSpec as P

HEAD = 128
CAP = 12


EPS = 1e-06
NEG = -1e30


def extended(cells, sides, width):
    for axis, dim in sides:
        count = lax.axis_size(axis)
        ends = count - 1
        head = lax.slice_in_dim(cells, 0, width, axis=dim)
        tail = lax.slice_in_dim(cells, cells.shape[dim] - width, cells.shape[dim], axis=dim)
        cells = jnp.concatenate(
            [
                lax.ppermute(tail, axis, [(i, (i + 1) % count) for i in range(ends)]),
                cells,
                lax.ppermute(head, axis, [((i + 1) % count, i) for i in range(ends)]),
            ],
            axis=dim,
        )
    return cells


def window_attention(query, keys, values, index, total):
    count = query.shape[0]
    rows = jnp.arange(count, dtype=jnp.int32)[:, None]
    cols = jnp.arange(3 * count, dtype=jnp.int32)[None, :] - count
    place = index * count + cols
    allowed = (jnp.abs(cols - rows) <= count) & (place >= 0) & (place < total)
    scores = jnp.einsum(
        "qhd,khd->hqk", query, keys, preferred_element_type=jnp.float32
    ) / math.sqrt(query.shape[2])
    scores = jnp.where(allowed[None], scores, NEG)
    top = jnp.max(scores, -1, keepdims=True)
    weight = jnp.exp(scores - top)
    weight = (weight / jnp.sum(weight, -1, keepdims=True)).astype(jnp.bfloat16)
    mixed = jnp.einsum("hqk,khd->qhd", weight, values, preferred_element_type=jnp.float32)
    return mixed.astype(jnp.bfloat16)


def normalize(state, modulation):
    scale = lax.rsqrt(jnp.mean(state * state, -1, keepdims=True) + EPS)
    return (state * scale * (1.0 + modulation[2]) + modulation[1]).astype(jnp.bfloat16)


def route(normed, router_weight, expert_ids):
    logits = jnp.dot(normed, router_weight, preferred_element_type=jnp.float32)
    experts = router_weight.shape[1]
    match = expert_ids[:, :, None] == jnp.arange(experts, dtype=jnp.int32)[None, None, :]
    picked = jnp.sum(jnp.where(match, logits[:, None, :], 0.0), -1)
    lifted = jax.nn.sigmoid(picked)
    return lifted / jnp.sum(lifted, -1, keepdims=True)


LANES = 128
SLOT = 16
COLS = 2
CHUNKS = 4
PIECES = 4
LAG = 4
SPLIT = 2
PAIR = 256
VMEM_BYTES = 66 * 1000 * 1000
MESH = pl.DeviceIdType.MESH


def choose(index, table):
    value = jnp.int32(table[0])
    for i in range(1, len(table)):
        value = jnp.where(index == i, table[i], value)
    return value


def line_order(lines, nearest, inner=False):
    rows = []
    for z in range(lines):
        lower = (z < lines - 1 - z) != inner
        others = [line for line in range(lines) if line != z]
        sign = 1 if nearest else -1
        rows.append(sorted(others, key=lambda line: (sign * abs(line - z), (line > z) == lower)))
    return [[rows[z][j] for z in range(lines)] for j in range(lines - 1)]


def expert_kernel(
    devices, weight_copies,
    normed, meta, state, modulation, wide,
    out,
    tok, got_packed, got_rows, got_sum, disp, gu, dn, raised, hid_own, hid_other,
    got_meta, pick, gated, squeeze, grow, acc,
    meta_s, meta_r, z_s, z_r, x_s, x_r, core_s, core_r, hid_s, hid_r, rx_s, rx_r, rz_s, rz_r,
):
    me = lax.axis_index("dev")
    part = lax.axis_index("sub")
    other = 1 - part
    z = me // COLS
    x = me % COLS
    lines = devices // COLS
    count, width = normed.shape
    half = width // 2
    local = hid_own.shape[0]
    hidden = gu.shape[2]
    slots = local * SLOT
    pack = local * CAP
    rows = devices * SLOT
    chunks, wide_chunk = tok.shape[1], tok.shape[3]

    def remote(src, dst, send, recv, where):
        return pltpu.make_async_remote_copy(
            src_ref=src, dst_ref=dst, send_sem=send, recv_sem=recv,
            device_id=where, device_id_type=MESH,
        )

    above = jnp.minimum(me + COLS, devices - 1)
    below = jnp.maximum(me - COLS, 0)
    x_to = {"dev": z * COLS + (1 - x)}
    core_to = {"sub": other}
    not_top = z < lines - 1
    not_bottom = z > 0
    near_lines = [choose(z, table) for table in line_order(lines, True, True)]
    far_lines = [choose(z, table) for table in line_order(lines, False)]

    def lanes_of(c):
        return pl.ds(pl.multiple_of(c * wide_chunk, wide_chunk), wide_chunk)

    def own_lanes(c):
        return pl.ds(pl.multiple_of(part * half + c * wide_chunk, wide_chunk), wide_chunk)

    def slot_rows(s):
        return pl.ds(pl.multiple_of(s * SLOT, SLOT), SLOT)

    def meta_copy(line):
        return remote(
            meta.at[pl.ds(pl.multiple_of(line * COLS * local, COLS * local), COLS * local)],
            got_meta.at[z], meta_s.at[0], meta_r.at[z], {"dev": line * COLS + x},
        )

    def meta_arrival(line):
        return remote(got_meta.at[line], got_meta.at[line], meta_s.at[0], meta_r.at[line], x_to)

    def z_copy(line, c, way, src=None):
        dst = tok.at[line, c]
        where = {"dev": jnp.where(way == 0, above, below)}
        return remote(
            dst if src is None else src, dst, z_s.at[jnp.where((line == z) & (way == 1), lines, line)], z_r.at[line, c], where
        )

    def packed_out(line, c):
        return wide.at[line, pl.ds(slots, pack), lanes_of(c)]

    def x_copy(line, c):
        return remote(
            packed_out(line, c), got_packed.at[line, c], x_s.at[0], x_r.at[line, c // 2], x_to
        )

    def core_copy(which, s, c):
        place = disp.at[which, c, :, slot_rows(s), :]
        return remote(place, place, core_s.at[0], core_r.at[jnp.where(c < SPLIT, 0, 1)], core_to)

    def own_send(c):
        src = normed.at[:, own_lanes(c)]

        @pl.when(not_top)
        def _():
            z_copy(z, c, 0, src).start()

        @pl.when(not_bottom)
        def _():
            z_copy(z, c, 1, src).start()

    own_send(0)
    for line in near_lines:
        meta_copy(line).start()
    for c in range(1, chunks):
        own_send(c)

    before = (
        lax.broadcasted_iota(jnp.int32, (count, count), 0)
        < lax.broadcasted_iota(jnp.int32, (count, count), 1)
    ).astype(jnp.float32).astype(jnp.bfloat16)
    place = lax.broadcasted_iota(jnp.int32, (local, SLOT, count), 1).astype(jnp.float32)

    def routing(line, ours, theirs):
        for first, gate in ((True, ours), (False, theirs)):
            chosen = jnp.where(gate > 0.0, 1.0, 0.0)
            rank = jnp.dot(chosen.astype(jnp.bfloat16), before, preferred_element_type=jnp.float32)
            rank = jnp.where(gate > 0.0, rank, -1.0)
            hit = jnp.broadcast_to(rank[:, None, :], place.shape) == place
            one = jnp.where(hit, 1.0, 0.0).reshape(slots, count).astype(jnp.bfloat16)
            value = jnp.where(hit, jnp.broadcast_to(gate[:, None, :], place.shape), 0.0)
            value = value.reshape(slots, count).astype(jnp.bfloat16)
            if first:
                pick[line, :slots] = one
                gated[line, :slots] = value
            else:
                pick[line, slots:] = jnp.dot(
                    squeeze[...], one, preferred_element_type=jnp.float32
                ).astype(jnp.bfloat16)
                gated[line, slots:] = jnp.dot(
                    squeeze[...], value, preferred_element_type=jnp.float32
                ).astype(jnp.bfloat16)

    def expert_rows(base, column):
        return pl.ds(pl.multiple_of(base + column * local, local), local)

    def spread(line, c, block):
        moved = jnp.dot(pick[line], block, preferred_element_type=jnp.float32).astype(jnp.bfloat16)
        s = line * COLS + x
        wide[line, slots:slots + pack, lanes_of(c)] = moved[slots:]
        x_copy(line, c).start()
        disp[part, c, :, slot_rows(s), :] = moved[:slots].reshape(local, SLOT, wide_chunk)
        core_copy(part, s, c).start()

    def own_step(c):
        spread(z, c, normed[:, own_lanes(c)])

    def line_step(line, c):
        low = line < z

        @pl.when(c == 0)
        def _():
            meta_arrival(line).wait_recv()
            routing(
                line, got_meta[line, expert_rows(0, x)], got_meta[line, expert_rows(0, 1 - x)]
            )

        way = jnp.where(low, 0, 1)
        z_copy(line, c, way).wait_recv()

        @pl.when(jnp.where(low, not_top, not_bottom))
        def _():
            z_copy(line, c, way).start()

        spread(line, c, tok[line, c])

    def x_step(line, c):
        @pl.when(c % 2 == 0)
        def _():
            block = got_packed.at[line, pl.ds(c, 2)]
            remote(block, block, x_s.at[0], x_r.at[line, c // 2], x_to).wait_recv()

        s = line * COLS + (1 - x)
        disp[part, c, :, slot_rows(s), :] = jnp.dot(
            grow[...], got_packed[line, c], preferred_element_type=jnp.float32
        ).astype(jnp.bfloat16).reshape(local, SLOT, wide_chunk)
        core_copy(part, s, c).start()

    def across_rows(left, right):
        return lax.dot_general(
            left, right, (((1,), (1,)), ((), ())), preferred_element_type=jnp.float32
        )

    def raise_part(e, parts):
        sums = []
        for g in range(2):
            for b in range(2):
                total = None
                for side, c in parts:
                    start = side * half + c * wide_chunk
                    piece = across_rows(
                        gu[2 * e + b, g, :, start:start + wide_chunk], disp[side, c, e]
                    )
                    total = piece if total is None else total + piece
                sums.append(total)
        return sums

    def raise_some(parts, start, stop, first=False, last=False):
        def one(e, carry):
            sums = raise_part(e, parts)
            if not first:
                sums = [
                    total + raised[e, n * hidden:(n + 1) * hidden] for n, total in enumerate(sums)
                ]
            if not last:
                for n, total in enumerate(sums):
                    raised[e, n * hidden:(n + 1) * hidden] = total
                return carry
            for b in range(2):
                gate = sums[b]
                hid_own[e, b * hidden:(b + 1) * hidden] = (
                    gate * jax.nn.sigmoid(gate) * sums[2 + b]
                ).astype(jnp.bfloat16)
            hid_copy(e).start()
            return carry

        lax.fori_loop(start, stop, one, 0)

    def hid_copy(e):
        return remote(hid_own.at[e], hid_other.at[e], hid_s.at[0], hid_r.at[e // (local // 2)], core_to)

    def arrived(which):
        span_of = pl.ds(which * SPLIT, SPLIT) if which == 0 else pl.ds(SPLIT, chunks - SPLIT)
        block = disp.at[other, span_of]
        remote(block, block, core_s.at[0], core_r.at[which], core_to).wait_recv()

    def sent(ref, sem):
        remote(ref, ref, sem, sem, core_to).wait_send()

    routing(
        z, meta[expert_rows(z * COLS * local, x)], meta[expert_rows(z * COLS * local, 1 - x)]
    )
    for c in range(chunks):
        own_step(c)

    for copy in weight_copies():
        copy.wait()

    offsets = [(jnp.abs(line - z) - 1) * chunks for line in near_lines]
    offsets[1] = jnp.maximum(offsets[1], SPLIT)

    def step(t, carry):
        for line, offset in zip(near_lines, offsets):
            c = t - offset

            @pl.when((c >= 0) & (c < chunks))
            def _():
                line_step(line, c)

        @pl.when((t >= LAG - 1) & (t < LAG - 1 + chunks))
        def _():
            x_step(z, t - LAG + 1)

        for line, offset in zip(near_lines, offsets):
            c = t - LAG - offset

            @pl.when((c >= 0) & (c < chunks))
            def _():
                x_step(line, c)

        return carry

    span = chunks * (lines - 1) + LAG
    lax.fori_loop(0, span - 2, step, 0)
    early = range(SPLIT)
    late = range(SPLIT, chunks)
    own_first = (part == 1) & ((z == 0) | (z == lines - 1))

    @pl.when(own_first)
    def _():
        raise_some([(1, c) for c in early], 0, local, first=True)
        step(span - 2, 0)
        step(span - 1, 0)
        raise_some([(1, c) for c in late], 0, local)
        arrived(0)
        arrived(1)
        raise_some([(0, c) for c in range(chunks)], 0, local, last=True)

    @pl.when(jnp.logical_not(own_first))
    def _():
        arrived(0)
        raise_some([(side, c) for c in early for side in range(2)], 0, local // 2, first=True)
        step(span - 2, 0)
        step(span - 1, 0)
        raise_some([(side, c) for c in early for side in range(2)], local // 2, local, first=True)
        arrived(1)
        raise_some([(side, c) for c in late for side in range(2)], 0, local, last=True)

    group = 2 * wide_chunk

    def lower(g, between):
        lanes = slice(g * group, (g + 1) * group)

        def one(e, carry):
            mine = pl.ds(pl.multiple_of(part * hidden, SLOT), hidden)
            theirs = pl.ds(pl.multiple_of(other * hidden, SLOT), hidden)
            left = jnp.concatenate([hid_own[e], hid_other[e]], axis=0)
            right = jnp.concatenate(
                [dn[2 * e, mine, lanes], dn[2 * e + 1, mine, lanes],
                 dn[2 * e, theirs, lanes], dn[2 * e + 1, theirs, lanes]], axis=0
            )
            wide[e, :rows, lanes] = lax.dot_general(
                left, right, (((0,), (0,)), ((), ())), preferred_element_type=jnp.float32
            ).astype(jnp.bfloat16)
            return carry

        for which in range(2):
            if g == 0:
                block = hid_other.at[pl.ds(which * (local // 2), local // 2)]
                remote(block, block, hid_s.at[0], hid_r.at[which], core_to).wait_recv()
            lax.fori_loop(which * (local // 2), (which + 1) * (local // 2), one, 0)
            if which == 0:
                between()

    def result_rows(s, q):
        return wide[:local, slot_rows(s), lanes_of(q)].reshape(slots, wide_chunk)

    def rx_copy(line, q):
        return remote(
            wide.at[lines + line, pl.ds(slots, pack), lanes_of(q)], got_rows.at[line, q],
            rx_s.at[0], rx_r.at[line, q], x_to,
        )

    def rz_copy(line, q, way, owner=None):
        owner = z - 1 if owner is None else owner
        where = {"dev": jnp.where(way == 0, above, below)}
        return remote(
            tok.at[line, q], got_sum.at[way, line, q],
            rz_s.at[0], rz_r.at[jnp.where((way == 1) & (line == owner), lines, line), q], where,
        )

    def give(line, q):
        packed = jnp.dot(
            squeeze[...], result_rows(line * COLS + (1 - x), q), preferred_element_type=jnp.float32
        )
        wide[lines + line, slots:slots + pack, lanes_of(q)] = packed.astype(jnp.bfloat16)
        rx_copy(line, q).start()

    def gather_here(line, q):
        rx_copy(line, q).wait_recv()
        pieces = jnp.concatenate([result_rows(line * COLS + x, q), got_rows[line, q]], axis=0)
        acc[...] = lax.dot_general(
            gated[line], pieces, (((0,), (0,)), ((), ())), preferred_element_type=jnp.float32
        )

    def add_line(line, q, way):
        rz_copy(line, q, way, z).wait_recv()
        acc[...] += got_sum[way, line, q].astype(jnp.float32)

    def pass_on(line, q):
        gather_here(line, q)
        way = jnp.where(line > z, 0, 1)

        @pl.when(jnp.where(line > z, not_bottom, not_top))
        def _():
            add_line(line, q, way)

        tok[line, q] = acc[...].astype(jnp.bfloat16)
        rz_copy(line, q, way).start()

    lower(0, lambda: None)
    give(far_lines[0], 0)
    lower(1, lambda: give(far_lines[0], 1))
    for q in range(2, chunks):
        give(far_lines[0], q)
    def give_all(line):
        lax.fori_loop(0, chunks, lambda q, carry: (give(line, q), carry)[1], 0)

    for line in near_lines:
        low = line < z

        @pl.when(jnp.where(low, not_top, not_bottom))
        def _():
            sent(tok.at[line], z_s.at[line])

    far_end = (z == 0) | (z == lines - 1)

    @pl.when(far_end)
    def _():
        for q in range(2):
            pass_on(far_lines[0], q)

    give_all(far_lines[1])

    @pl.when(far_end)
    def _():
        for q in range(2, chunks):
            pass_on(far_lines[0], q)

    for line in far_lines[2:] + [z]:
        give_all(line)

    @pl.when(jnp.logical_not(far_end))
    def _():
        for q in range(chunks):
            pass_on(far_lines[0], q)

    for line in far_lines[1:]:
        lax.fori_loop(0, chunks, lambda q, carry, line=line: (pass_on(line, q), carry)[1], 0)
    for q in range(chunks):
        gather_here(z, q)

        @pl.when(not_bottom)
        def _():
            add_line(z, q, 0)

        @pl.when(not_top)
        def _():
            add_line(z, q, 1)

        own = own_lanes(q)
        lanes = slice(q * wide_chunk, (q + 1) * wide_chunk)
        out[:, lanes] = (
            state[:, own] + (1.0 + modulation[3:4, own]) * acc[...]
        ).astype(out.dtype)

    @pl.when(not_top)
    def _():
        sent(tok.at[z], z_s.at[z])

    @pl.when(not_bottom)
    def _():
        sent(tok.at[z], z_s.at[lines])

    sent(tok.at[pl.ds(0, lines - 1)], rz_s.at[0])
    sent(got_packed, x_s.at[0])
    sent(got_rows, rx_s.at[0])
    sent(disp.at[part], core_s.at[0])
    sent(got_meta.at[pl.ds(0, lines - 1)], meta_s.at[0])
    sent(hid_own, hid_s.at[0])


def front_kernel(
    devices, start_weights,
    sources, held, own_sem,
    normed, state, meta,
    window, queries, column, mixed, mine_out, their_out, sent_back, got_back, their_back,
    pair_s, pair_r, query_s, query_r, early_s, late_s, edge_r, wz_s, wz_r, wy_s, wy_r, mix_s, mix_r,
    sum_s, sum_r, back_s, back_r, share_s, share_r,
):
    packed_hbm, weight_hbm = sources[1], sources[2]
    tokens, modulation, router, ids = held
    me = lax.axis_index("dev")
    part = lax.axis_index("sub")
    group = lax.axis_index("groups")
    z = me // COLS
    x = me % COLS
    lines = devices // COLS
    count, width = tokens.shape
    shard = column.shape[1]
    share = shard // 2
    piece = share // PIECES
    heads = window.shape[3]
    pairs = heads // PAIR
    ours = pl.ds(pl.multiple_of(x * heads, heads), heads)
    theirs = pl.ds(pl.multiple_of((1 - x) * heads, heads), heads)
    own_parts = (
        (packed_hbm.at[1:3, :, ours], window.at[1 + x]), (packed_hbm.at[0, :, ours], queries.at[x]),
        (weight_hbm, column.at[z]), (sources[0], tokens), (sources[3], modulation),
        (sources[4], router), (sources[5], ids),
    )

    def own_copy(i):
        return pltpu.make_async_copy(*own_parts[i], own_sem.at[i])

    for i in range(len(own_parts)):
        own_copy(i).start()
    not_top = z < lines - 1
    not_bottom = z > 0
    above = jnp.minimum(me + COLS, devices - 1)
    below = jnp.maximum(me - COLS, 0)
    x_to = {"dev": z * COLS + (1 - x)}
    y_to = {"groups": 1 - group}
    core_to = {"sub": 1 - part}
    near_lines = [choose(z, table) for table in line_order(lines, True)]

    barrier = pltpu.get_barrier_semaphore()

    def greet(where):
        pl.semaphore_signal(barrier, inc=1, device_id=where, device_id_type=MESH)

    for where in (x_to, y_to, core_to, {**x_to, **core_to}):
        greet(where)
    for line in near_lines:
        greet({"dev": line * COLS + x})
    pl.semaphore_wait(barrier, lines + 3)

    def remote(src, dst, send, recv, where):
        return pltpu.make_async_remote_copy(
            src_ref=src, dst_ref=dst, send_sem=send, recv_sem=recv,
            device_id=where, device_id_type=MESH,
        )

    def part_lanes(base, k):
        return pl.ds(pl.multiple_of(base * heads + k * PAIR, PAIR), PAIR)

    def pair_copy(k):
        return remote(
            packed_hbm.at[1:3, :, part_lanes(1 - x, k)], window.at[1 + x, :, :, part_lanes(0, k)],
            pair_s.at[k], pair_r.at[k], x_to,
        )

    def query_copy():
        return remote(
            packed_hbm.at[0, :, theirs], queries.at[x], query_s.at[0], query_r.at[0], x_to
        )

    def edge_copy(k, up, src, send):
        where = {"dev": jnp.where(up, above, below)}
        place = jnp.where(up, 0, 3)
        return remote(
            src, window.at[place, :, :, part_lanes(0, k)], send,
            edge_r.at[jnp.where(up, 0, 1), k], where,
        )

    def early_copy(k):
        return edge_copy(k, x == 1, packed_hbm.at[1:3, :, part_lanes(x, k)], early_s.at[k])

    def late_copy(k):
        return edge_copy(k, x == 0, window.at[2 - x, :, :, part_lanes(0, k)], late_s.at[k])

    give_late = ((x == 0) & not_top) | ((x == 1) & not_bottom)
    give_early = ((x == 1) & not_top) | ((x == 0) & not_bottom)

    def piece_rows(which, i):
        return pl.ds(pl.multiple_of(which * share + i * piece, SLOT), piece)

    def wz_copy(line, i, way, src=None):
        dst = column.at[line, piece_rows(group, i)]
        where = {"dev": jnp.where(way == 0, above, below)}
        return remote(
            dst if src is None else src, dst,
            wz_s.at[jnp.where((line == z) & (way == 1), lines, line)], wz_r.at[line, i], where
        )

    def own_piece(i):
        return weight_hbm.at[piece_rows(group, i)]

    def wy_copy(line, i, which):
        block = column.at[line, piece_rows(which, i)]
        return remote(block, block, wy_s.at[0], wy_r.at[line], y_to)

    for k in range(pairs):
        pair_copy(k).start()
    query_copy().start()

    def send_pieces(pieces):
        for i in pieces:

            @pl.when(not_top)
            def _():
                wz_copy(z, i, 0, own_piece(i)).start()

            @pl.when(not_bottom)
            def _():
                wz_copy(z, i, 1, own_piece(i)).start()

    send_pieces(range(PIECES // 2))

    @pl.when(give_early)
    def _():
        for k in range(pairs):
            early_copy(k).start()

    send_pieces(range(PIECES // 2, PIECES))
    start_weights()

    @pl.when(jnp.logical_not(not_bottom))
    def _():
        window[0] = jnp.zeros_like(window[0])

    @pl.when(jnp.logical_not(not_top))
    def _():
        window[3] = jnp.zeros_like(window[3])

    def way_of(line):
        return jnp.where(line < z, 0, 1)

    def more(line):
        return jnp.where(line < z, not_top, not_bottom)

    def busy(line):
        return jnp.where(line < z, x == 0, x == 1)

    def distance(line):
        return jnp.abs(line - z)

    def take(line, onward, pieces=range(PIECES)):
        for i in pieces:
            wz_copy(line, i, way_of(line)).wait_recv()

            @pl.when(onward)
            def _():
                wz_copy(line, i, way_of(line)).start()

            wy_copy(line, i, group).start()

    def take_next(only_busy, pieces):
        for line in near_lines:

            @pl.when((distance(line) == 1) & (busy(line) if only_busy else jnp.logical_not(busy(line))))
            def _():
                take(line, more(line), pieces)

    for k in range(pairs):
        pair_copy(k).wait_recv()

        @pl.when(give_late)
        def _():
            late_copy(k).start()

    take_next(True, range(PIECES // 2))
    take_next(False, range(PIECES // 2))
    for i in range(len(own_parts)):
        own_copy(i).wait()
    query_copy().wait_recv()

    row = lax.broadcasted_iota(jnp.int32, (count, count), 0)
    col = lax.broadcasted_iota(jnp.int32, (count, count), 1)

    def mix_copy(b, k):
        block = mixed.at[pl.ds(pl.multiple_of(b * count, count), count), part_lanes(x, k)]
        return remote(block, block, mix_s.at[0], mix_r.at[0], x_to)

    def attend(b, k):
        see_before = (col >= row) & ((z > 0) | (b == 1))
        see_after = (col <= row) & ((z < lines - 1) | (b == 0))
        for h in range(PAIR // HEAD):
            inner = slice(k * PAIR + h * HEAD, k * PAIR + (h + 1) * HEAD)
            query = queries[b, :, inner]

            def score(keys):
                return lax.dot_general(
                    query, keys, (((1,), (1,)), ((), ())), preferred_element_type=jnp.float32
                ) / math.sqrt(HEAD)

            scores = jnp.concatenate(
                [
                    jnp.where(see_before, score(window[b, 0, :, inner]), NEG),
                    score(window[b + 1, 0, :, inner]),
                    jnp.where(see_after, score(window[b + 2, 0, :, inner]), NEG),
                ],
                axis=1,
            )
            top = jnp.max(scores, -1, keepdims=True)
            weight = jnp.exp(scores - top)
            weight = (weight / jnp.sum(weight, -1, keepdims=True)).astype(jnp.bfloat16)
            values = jnp.concatenate([window[b + n, 1, :, inner] for n in range(3)], axis=0)
            lanes = pl.ds(
                pl.multiple_of(x * heads + k * PAIR + h * HEAD, HEAD), HEAD
            )
            mixed[pl.ds(pl.multiple_of(b * count, count), count), lanes] = jnp.dot(
                weight, values, preferred_element_type=jnp.float32
            ).astype(jnp.bfloat16)
        mix_copy(b, k).start()

    for b, up in ((1 - x, x == 1), (x, x == 0)):
        for k in range(pairs):

            @pl.when(jnp.where(up, not_bottom, not_top))
            def _():
                edge_copy(k, up, window.at[0, :, :, part_lanes(0, k)], early_s.at[k]).wait_recv()

            attend(b, k)
        if b is not x:
            take_next(True, range(PIECES // 2, PIECES))
            take_next(False, range(PIECES // 2, PIECES))
        else:
            for line in near_lines:

                @pl.when(distance(line) == 2)
                def _():
                    take(line, more(line))

    last = near_lines[-1]
    far_last = distance(last) > 2

    def take_last(pieces):
        @pl.when(far_last)
        def _():
            take(last, more(last), pieces)

    mix_block = mixed.at[:, theirs]
    remote(mix_block, mix_block, mix_s.at[0], mix_r.at[0], x_to).wait_recv()

    def place_of(which):
        return group if which == 0 else 1 - group

    def group_of(line):
        return jnp.where(line == last, 1, 0)

    def come(ref, sem):
        remote(ref, ref, sum_s.at[0], sem, core_to).wait_recv()

    def sum_copy(line, which):
        place = place_of(which)
        return remote(
            mine_out.at[line, place], their_out.at[line, place],
            sum_s.at[0], sum_r.at[group_of(line)], core_to,
        )

    def back_copy(line, which):
        place = place_of(which)
        return remote(
            sent_back.at[line, place], got_back.at[line, place],
            back_s.at[0], back_r.at[line], x_to,
        )

    def share_copy(line, which):
        place = place_of(which)
        return remote(
            got_back.at[line, place], their_back.at[line, place],
            share_s.at[0], share_r.at[group_of(line)], core_to,
        )

    def direct_copy(which):
        place = place_of(which)
        return remote(
            sent_back.at[last, place], their_back.at[last, place],
            share_s.at[0], share_r.at[1],
            {"dev": z * COLS + (1 - x), "sub": 1 - part},
        )

    def project(line, which, direct=False):
        place = place_of(which)
        block = column[line, pl.ds(pl.multiple_of(place * share, SLOT), share), :]
        both = jnp.concatenate(
            [mixed[pl.ds(pl.multiple_of(b * count, count), count), :] for b in (1 - x, x)], axis=0
        )
        product = lax.dot_general(
            both, block, (((1,), (1,)), ((), ())), preferred_element_type=jnp.float32
        )
        sent_back[line, place] = product[:count].astype(jnp.bfloat16)
        back_copy(line, which).start()
        if direct:
            direct_copy(which).start()
        mine_out[line, place] = product[count:]
        sum_copy(line, which).start()

    def halves_in(line):
        block = column.at[line, pl.ds(pl.multiple_of((1 - group) * share, SLOT), share)]
        remote(block, block, wy_s.at[0], wy_r.at[line], y_to).wait_recv()

    def last_step():
        halves_in(last)
        project(last, 1, True)

    def add_up(line, which):
        place = place_of(which)
        partial = jnp.zeros((count, share), jnp.float32)
        for column_of, total in (
            (x, mine_out[line, place] + their_out[line, place]),
            (
                1 - x,
                got_back[line, place].astype(jnp.float32)
                + their_back[line, place].astype(jnp.float32),
            ),
        ):
            start = (line * COLS + column_of) * shard + place * share
            lanes = pl.ds(pl.multiple_of(start, LANES), share)
            value = tokens[:, lanes].astype(jnp.float32) + (1.0 + modulation[0:1, lanes]) * total
            state[:, lanes] = value
            partial = partial + value * value
        return partial

    steps = [(line, which) for line in [z] + near_lines[:-1] for which in range(2)]
    quarter = PIECES // 4
    for i, (line, which) in enumerate(steps):
        if which == 1 and i > 1:
            halves_in(line)
        project(line, which)
        if i < 4:
            take_last(range(i * quarter, (i + 1) * quarter))
    project(last, 0, True)

    @pl.when(jnp.logical_not(far_last))
    def _():
        last_step()

    def relay(some):
        for line, which in some:
            if which == 0:
                come(got_back.at[line], back_r.at[line])
            share_copy(line, which).start()

    relay(steps[:4])

    @pl.when(far_last)
    def _():
        last_step()

    relay(steps[4:])
    squares = jnp.zeros((count, share), jnp.float32)
    come(mine_out.at[pl.ds(0, lines - 1)], sum_r.at[0])
    come(got_back.at[pl.ds(0, lines - 1)], share_r.at[0])
    for line, which in steps:
        squares = squares + add_up(line, which)
    come(got_back.at[last], back_r.at[last])
    come(mine_out.at[last], sum_r.at[1])
    come(got_back.at[last], share_r.at[1])
    for which in range(2):
        squares = squares + add_up(last, which)
    square = jnp.sum(squares, -1, keepdims=True)
    scale = lax.rsqrt(square / width + EPS)
    for s in range(devices):
        lanes = slice(s * shard, (s + 1) * shard)
        normed[:, lanes] = (
            state[:, lanes] * scale * (1.0 + modulation[2:3, lanes]) + modulation[1:2, lanes]
        ).astype(jnp.bfloat16)
    logits = lax.dot_general(
        router[...], normed[...], (((1,), (1,)), ((), ())), preferred_element_type=jnp.float32
    )
    name = lax.broadcasted_iota(jnp.int32, logits.shape, 0)
    named = name == ids[0:1]
    for k in range(1, ids.shape[0]):
        named = named | (name == ids[k:k + 1])
    lifted = jnp.where(named, jax.nn.sigmoid(logits), 0.0)
    meta[...] = lifted / jnp.sum(lifted, 0, keepdims=True)

    def drain():
        def sent(ref, sem):
            remote(ref, ref, sem, sem, x_to).wait_send()

        query_copy().wait_send()
        sent(mixed.at[:, ours], mix_s.at[0])
        for k in range(pairs):
            pair_copy(k).wait_send()

            @pl.when(give_early)
            def _():
                early_copy(k).wait_send()

            @pl.when(give_late)
            def _():
                late_copy(k).wait_send()

        half_shard = column.at[0, pl.ds(0, share)]

        @pl.when(not_top)
        def _():
            sent(half_shard, wz_s.at[z])

        @pl.when(not_bottom)
        def _():
            sent(half_shard, wz_s.at[lines])

        for line in near_lines:

            @pl.when(more(line))
            def _():
                sent(half_shard, wz_s.at[line])

        sent(column.at[pl.ds(0, lines - 1), pl.ds(0, share)], wy_s.at[0])
        sent(mine_out, sum_s.at[0])
        sent(sent_back, back_s.at[0])
        sent(got_back, share_s.at[0])

    return drain


def block_kernel(devices, *refs):
    sources, gate_up, down, out = refs[:6], refs[6], refs[7], refs[8]
    held, normed, state, meta, wide = refs[9:13], refs[13], refs[14], refs[15], refs[16]
    front_buffers, expert_buffers = refs[17:26], refs[26:42]
    own_sem, gu_sem, dn_sem = refs[42:45]
    front_sems, expert_sems = refs[45:64], refs[64:]
    gu, dn = expert_buffers[5:7]
    squeeze, grow = expert_buffers[13:15]
    def weight_copies():
        return (
            pltpu.make_async_copy(gate_up, gu, gu_sem.at[0]),
            pltpu.make_async_copy(down, dn, dn_sem.at[0]),
        )

    def start_weights():
        for copy in weight_copies():
            copy.start()
        for ref, axis in ((squeeze, 0), (grow, 1)):
            packed = lax.broadcasted_iota(jnp.int32, ref.shape, axis)
            slot = lax.broadcasted_iota(jnp.int32, ref.shape, 1 - axis)
            inner = slot & (SLOT - 1)
            same = (packed == (slot - inner) // SLOT * CAP + inner) & (inner < CAP)
            ref[...] = jnp.where(same, 1.0, 0.0).astype(jnp.bfloat16)

    drain = front_kernel(
        devices, start_weights, sources, held, own_sem, normed, state, meta,
        *front_buffers, *front_sems,
    )
    expert_kernel(
        devices, weight_copies, normed, meta, state, held[1], wide, out,
        *expert_buffers, *expert_sems,
    )
    drain()


def block_call(
    tokens, query_key_value, out_weight, modulation, router_weight, expert_ids,
    gate_up_weight, down_weight,
):
    devices = lax.axis_size("dev")
    count, width = tokens.shape
    half = down_weight.shape[2]
    halves = gate_up_weight.shape[0]
    local = halves // 2
    gate_up_weight = gate_up_weight.swapaxes(2, 3)
    hidden = gate_up_weight.shape[2]
    lines = devices // COLS
    rows = devices * SLOT
    slots, pack = local * SLOT, local * CAP
    part = half // CHUNKS
    pairs = half // 2 // PAIR
    shard = out_weight.shape[0]
    own = (
        tokens, query_key_value.transpose(1, 0, 2), out_weight, modulation,
        router_weight.T, expert_ids.T,
    )
    hbm = pl.BlockSpec(memory_space=pl.ANY)
    dma = pltpu.SemaphoreType.DMA
    return pl.pallas_call(
        functools.partial(block_kernel, devices),
        out_shape=jax.ShapeDtypeStruct((count, half), jnp.bfloat16),
        in_specs=[hbm] * 8,
        out_specs=pl.BlockSpec(memory_space=pltpu.VMEM),
        scratch_shapes=[
            *[pltpu.VMEM(own[i].shape, own[i].dtype) for i in (0, 3, 4, 5)],
            pltpu.VMEM((count, width), jnp.bfloat16),
            pltpu.VMEM((count, width), jnp.float32),
            pltpu.VMEM((router_weight.shape[1], count), jnp.float32),
            pltpu.VMEM((devices, slots + pack, half), jnp.bfloat16),
            pltpu.VMEM((4, 2, count, half // 2), jnp.bfloat16),
            pltpu.VMEM((COLS, count, half // 2), jnp.bfloat16),
            pltpu.VMEM((lines, shard, half), jnp.bfloat16),
            pltpu.VMEM((COLS * count, half), jnp.bfloat16),
            pltpu.VMEM((lines, 2, count, shard // 2), jnp.float32),
            pltpu.VMEM((lines, 2, count, shard // 2), jnp.float32),
            pltpu.VMEM((lines, 2, count, shard // 2), jnp.bfloat16),
            pltpu.VMEM((lines, 2, count, shard // 2), jnp.bfloat16),
            pltpu.VMEM((lines, 2, count, shard // 2), jnp.bfloat16),
            pltpu.VMEM((lines, CHUNKS, count, part), jnp.bfloat16),
            pltpu.VMEM((lines, CHUNKS, pack, part), jnp.bfloat16),
            pltpu.VMEM((lines, CHUNKS, pack, part), jnp.bfloat16),
            pltpu.VMEM((2, lines, CHUNKS, count, part), jnp.bfloat16),
            pltpu.VMEM((2, CHUNKS, local, rows, part), jnp.bfloat16),
            pltpu.VMEM(gate_up_weight.shape, jnp.bfloat16),
            pltpu.VMEM(down_weight.shape, jnp.bfloat16),
            pltpu.VMEM((local, 4 * hidden, rows), jnp.float32),
            pltpu.VMEM((local, 2 * hidden, rows), jnp.bfloat16),
            pltpu.VMEM((local, 2 * hidden, rows), jnp.bfloat16),
            pltpu.VMEM((lines, COLS * local, count), jnp.float32),
            pltpu.VMEM((lines, slots + pack, count), jnp.bfloat16),
            pltpu.VMEM((lines, slots + pack, count), jnp.bfloat16),
            pltpu.VMEM((pack, slots), jnp.bfloat16),
            pltpu.VMEM((slots, pack), jnp.bfloat16),
            pltpu.VMEM((count, part), jnp.float32),
            dma((7,)), dma((1,)), dma((1,)),
            dma((pairs,)), dma((pairs,)), dma((1,)), dma((1,)),
            dma((pairs,)), dma((pairs,)), dma((2, pairs)),
            dma((lines + 1,)), dma((lines, PIECES)), dma((1,)), dma((lines,)), dma((1,)), dma((1,)),
            dma((1,)), dma((2,)), dma((1,)), dma((lines,)), dma((1,)), dma((2,)),
            dma((1,)), dma((lines,)),
            dma((lines + 1,)), dma((lines, CHUNKS)), dma((1,)), dma((lines, CHUNKS // 2)),
            dma((1,)), dma((2,)), dma((1,)), dma((2,)),
            dma((1,)), dma((lines, CHUNKS)), dma((1,)), dma((lines + 1, CHUNKS)),
        ],
        compiler_params=pltpu.CompilerParams(
            collective_id=1, has_side_effects=True, vmem_limit_bytes=VMEM_BYTES
        ),
    )(*own, gate_up_weight, down_weight)


def body(
    tokens,
    query_key_value,
    out_weight,
    modulation,
    router_weight,
    expert_ids,
    gate_up_weight,
    down_weight,
):
    count = tokens.shape[0]
    width = tokens.shape[1]
    parts = lax.axis_size("sub")
    part = lax.axis_index("sub")
    position = lax.axis_index("dev")
    devices = lax.axis_size("dev")
    total = count * devices
    local_width = query_key_value.shape[2]
    weight_bytes = 2 * (gate_up_weight.size + down_weight.size)
    token_bytes = 12 * devices * count * width
    fits = weight_bytes + token_bytes < VMEM_BYTES and CAP <= SLOT
    paired = parts == 2 and lax.axis_size("groups") == 2 and devices % COLS == 0
    experts_here = gate_up_weight.shape[0] // 2
    tiled = out_weight.shape[0] % (2 * LANES) == 0 and count == LANES
    tiled = tiled and down_weight.shape[2] == 4 * PAIR and devices == 4 * COLS
    tiled = tiled and down_weight.shape[2] % (2 * CHUNKS * LANES) == 0 and experts_here == devices
    tiled = tiled and SLOT * devices == LANES
    tiled = tiled and gate_up_weight.shape[3] % 64 == 0
    if fits and paired and tiled:
        return block_call(
            tokens, query_key_value, out_weight, modulation, router_weight, expert_ids,
            gate_up_weight, down_weight,
        )
    heads_here = local_width // HEAD
    query = query_key_value[:, 0].reshape(count, heads_here, HEAD)
    pair = query_key_value[:, 1:]
    near = extended(pair, (("dev", 0),), count)
    keys = near[:, 0].reshape(3 * count, heads_here, HEAD)
    values = near[:, 1].reshape(3 * count, heads_here, HEAD)
    mixed = window_attention(query, keys, values, position, total).reshape(count, local_width)
    partial_proj = lax.dot_general(
        mixed,
        lax.all_gather(out_weight, "dev", axis=0, tiled=True),
        (((1,), (1,)), ((), ())),
        preferred_element_type=jnp.float32,
    )
    proj = lax.psum(partial_proj, "sub")
    state = tokens.astype(jnp.float32) + (1.0 + modulation[0]) * proj
    normed = normalize(state, modulation)
    gates = route(normed, router_weight, expert_ids)
    experts = router_weight.shape[1]
    topk = expert_ids.shape[1]
    flat = expert_ids.reshape(-1)
    picks = flat.shape[0]
    onehot = (flat[:, None] == jnp.arange(experts, dtype=jnp.int32)[None, :]).astype(jnp.int32)
    rank = jnp.sum((jnp.cumsum(onehot, 0) - 1) * onehot, 1)
    target = flat * CAP + rank
    hit = target[None, :] == jnp.arange(experts * CAP, dtype=jnp.int32)[:, None]
    filled = jnp.any(hit, 1)
    anchor = jnp.sum(jnp.where(hit, jnp.arange(picks, dtype=jnp.int32)[None, :], 0), 1) // topk
    slice_width = width // parts
    sent = lax.dynamic_slice_in_dim(normed, part * slice_width, slice_width, 1)
    sent_width = sent.shape[1]
    rows_out = jnp.where(filled[:, None], sent[anchor], jnp.zeros((), jnp.bfloat16))
    halves_here = gate_up_weight.shape[0]
    doubled = jnp.broadcast_to(
        rows_out.reshape(experts, 1, CAP, sent_width), (experts, 2, CAP, sent_width)
    )
    outgoing = doubled.reshape(devices, halves_here, CAP, sent_width)
    up_form = "sxcd,xgdf->sxcgf"
    down_form = "sxcf,xfd->sxcd"
    incoming = lax.all_to_all(outgoing, "dev", split_axis=0, concat_axis=0, tiled=True)
    both = jnp.einsum(
        up_form,
        lax.all_gather(incoming, "sub", axis=3, tiled=True),
        gate_up_weight,
        preferred_element_type=jnp.float32,
    )
    hidden = (jax.nn.silu(both[..., 0, :]) * both[..., 1, :]).astype(jnp.bfloat16)
    gathered = lax.all_gather(hidden, "sub", axis=hidden.ndim - 1, tiled=True)
    result = jnp.einsum(down_form, gathered, down_weight, preferred_element_type=jnp.float32)
    returned = lax.all_to_all(
        result.astype(jnp.bfloat16), "dev", split_axis=0, concat_axis=0, tiled=True
    )
    own_width = returned.shape[-1]
    arranged = returned.reshape(experts, 2, CAP, own_width)
    answers = arranged[flat, :, rank, :].reshape(count, topk, 2, own_width).astype(jnp.float32)
    combined = answers[:, :, 0] + answers[:, :, 1]
    routed = jnp.einsum("tk,tkd->td", gates, combined)
    own = lax.dynamic_slice_in_dim(state, part * slice_width, slice_width, 1)
    lift = lax.dynamic_slice_in_dim(modulation[3], part * slice_width, slice_width, 0)
    return (own + (1.0 + lift) * routed).astype(jnp.bfloat16)


def solution(mesh):
    return jax.shard_map(
        body,
        mesh=mesh,
        in_specs=(
            P(("groups", "dev"), None),
            P(("groups", "dev"), None, "sub"),
            P("dev", "sub"),
            P("groups", None),
            P(),
            P(("groups", "dev"), None),
            P("dev", None, None, "sub"),
            P("dev", None, "sub"),
        ),
        out_specs=P(("groups", "dev"), "sub"),
        check_vma=False,
    )
```

```python
import functools
import math

import jax
import jax.numpy as jnp
from jax import lax
from jax.experimental import pallas as pl
from jax.experimental.pallas import tpu as pltpu
from jax.sharding import PartitionSpec as P

HEAD = 128
CAP = 12


EPS = 1e-06
NEG = -1e30


def extended(cells, sides, width):
    for axis, dim in sides:
        count = lax.axis_size(axis)
        ends = count - 1
        head = lax.slice_in_dim(cells, 0, width, axis=dim)
        tail = lax.slice_in_dim(cells, cells.shape[dim] - width, cells.shape[dim], axis=dim)
        cells = jnp.concatenate(
            [
                lax.ppermute(tail, axis, [(i, (i + 1) % count) for i in range(ends)]),
                cells,
                lax.ppermute(head, axis, [((i + 1) % count, i) for i in range(ends)]),
            ],
            axis=dim,
        )
    return cells


def window_attention(query, keys, values, index, total):
    count = query.shape[0]
    rows = jnp.arange(count, dtype=jnp.int32)[:, None]
    cols = jnp.arange(3 * count, dtype=jnp.int32)[None, :] - count
    place = index * count + cols
    allowed = (jnp.abs(cols - rows) <= count) & (place >= 0) & (place < total)
    scores = jnp.einsum(
        "qhd,khd->hqk", query, keys, preferred_element_type=jnp.float32
    ) / math.sqrt(query.shape[2])
    scores = jnp.where(allowed[None], scores, NEG)
    top = jnp.max(scores, -1, keepdims=True)
    weight = jnp.exp(scores - top)
    weight = (weight / jnp.sum(weight, -1, keepdims=True)).astype(jnp.bfloat16)
    mixed = jnp.einsum("hqk,khd->qhd", weight, values, preferred_element_type=jnp.float32)
    return mixed.astype(jnp.bfloat16)


def normalize(state, modulation):
    scale = lax.rsqrt(jnp.mean(state * state, -1, keepdims=True) + EPS)
    return (state * scale * (1.0 + modulation[2]) + modulation[1]).astype(jnp.bfloat16)


def route(normed, router_weight, expert_ids):
    logits = jnp.dot(normed, router_weight, preferred_element_type=jnp.float32)
    experts = router_weight.shape[1]
    match = expert_ids[:, :, None] == jnp.arange(experts, dtype=jnp.int32)[None, None, :]
    picked = jnp.sum(jnp.where(match, logits[:, None, :], 0.0), -1)
    lifted = jax.nn.sigmoid(picked)
    return lifted / jnp.sum(lifted, -1, keepdims=True)


LANES = 128
SLOT = 16
COLS = 2
CHUNKS = 4
PIECES = 4
LAG = 4
SPLIT = 2
PAIR = 256
VMEM_BYTES = 66 * 1000 * 1000
MESH = pl.DeviceIdType.MESH


def choose(index, table):
    value = jnp.int32(table[0])
    for i in range(1, len(table)):
        value = jnp.where(index == i, table[i], value)
    return value


def line_order(lines, nearest, inner=False):
    rows = []
    for z in range(lines):
        lower = (z < lines - 1 - z) != inner
        others = [line for line in range(lines) if line != z]
        sign = 1 if nearest else -1
        rows.append(sorted(others, key=lambda line: (sign * abs(line - z), (line > z) == lower)))
    return [[rows[z][j] for z in range(lines)] for j in range(lines - 1)]


def expert_kernel(
    devices, weight_copies,
    normed, meta, state, modulation, wide,
    out,
    tok, got_packed, got_rows, got_sum, disp, gu, dn, raised, hid_own, hid_other,
    got_meta, pick, gated, squeeze, grow, acc,
    meta_s, meta_r, z_s, z_r, x_s, x_r, core_s, core_r, hid_s, hid_r, rx_s, rx_r, rz_s, rz_r,
):
    me = lax.axis_index("dev")
    part = lax.axis_index("sub")
    other = 1 - part
    z = me // COLS
    x = me % COLS
    lines = devices // COLS
    count, width = normed.shape
    half = width // 2
    local = hid_own.shape[0]
    hidden = gu.shape[2]
    slots = local * SLOT
    pack = local * CAP
    rows = devices * SLOT
    chunks, wide_chunk = tok.shape[1], tok.shape[3]

    def remote(src, dst, send, recv, where):
        return pltpu.make_async_remote_copy(
            src_ref=src, dst_ref=dst, send_sem=send, recv_sem=recv,
            device_id=where, device_id_type=MESH,
        )

    above = jnp.minimum(me + COLS, devices - 1)
    below = jnp.maximum(me - COLS, 0)
    x_to = {"dev": z * COLS + (1 - x)}
    core_to = {"sub": other}
    not_top = z < lines - 1
    not_bottom = z > 0
    near_lines = [choose(z, table) for table in line_order(lines, True, True)]
    far_lines = [choose(z, table) for table in line_order(lines, False)]

    def lanes_of(c):
        return pl.ds(pl.multiple_of(c * wide_chunk, wide_chunk), wide_chunk)

    def own_lanes(c):
        return pl.ds(pl.multiple_of(part * half + c * wide_chunk, wide_chunk), wide_chunk)

    def slot_rows(s):
        return pl.ds(pl.multiple_of(s * SLOT, SLOT), SLOT)

    def meta_copy(line):
        return remote(
            meta.at[pl.ds(pl.multiple_of(line * COLS * local, COLS * local), COLS * local)],
            got_meta.at[z], meta_s.at[0], meta_r.at[z], {"dev": line * COLS + x},
        )

    def meta_arrival(line):
        return remote(got_meta.at[line], got_meta.at[line], meta_s.at[0], meta_r.at[line], x_to)

    def z_copy(line, c, way, src=None):
        dst = tok.at[line, c]
        where = {"dev": jnp.where(way == 0, above, below)}
        return remote(
            dst if src is None else src, dst, z_s.at[jnp.where((line == z) & (way == 1), lines, line)], z_r.at[line, c], where
        )

    def packed_out(line, c):
        return wide.at[line, pl.ds(slots, pack), lanes_of(c)]

    def x_copy(line, c):
        return remote(
            packed_out(line, c), got_packed.at[line, c], x_s.at[0], x_r.at[line, c // 2], x_to
        )

    def core_copy(which, s, c):
        place = disp.at[which, c, :, slot_rows(s), :]
        return remote(place, place, core_s.at[0], core_r.at[jnp.where(c < SPLIT, 0, 1)], core_to)

    def own_send(c):
        src = normed.at[:, own_lanes(c)]

        @pl.when(not_top)
        def _():
            z_copy(z, c, 0, src).start()

        @pl.when(not_bottom)
        def _():
            z_copy(z, c, 1, src).start()

    yield lambda: own_send(0)

    for line in near_lines:
        meta_copy(line).start()
    for c in range(1, chunks):
        own_send(c)

    before = (
        lax.broadcasted_iota(jnp.int32, (count, count), 0)
        < lax.broadcasted_iota(jnp.int32, (count, count), 1)
    ).astype(jnp.float32).astype(jnp.bfloat16)
    place = lax.broadcasted_iota(jnp.int32, (local, SLOT, count), 1).astype(jnp.float32)

    def routing(line, ours, theirs):
        for first, gate in ((True, ours), (False, theirs)):
            chosen = jnp.where(gate > 0.0, 1.0, 0.0)
            rank = jnp.dot(chosen.astype(jnp.bfloat16), before, preferred_element_type=jnp.float32)
            rank = jnp.where(gate > 0.0, rank, -1.0)
            hit = jnp.broadcast_to(rank[:, None, :], place.shape) == place
            one = jnp.where(hit, 1.0, 0.0).reshape(slots, count).astype(jnp.bfloat16)
            value = jnp.where(hit, jnp.broadcast_to(gate[:, None, :], place.shape), 0.0)
            value = value.reshape(slots, count).astype(jnp.bfloat16)
            if first:
                pick[line, :slots] = one
                gated[line, :slots] = value
            else:
                pick[line, slots:] = jnp.dot(
                    squeeze[...], one, preferred_element_type=jnp.float32
                ).astype(jnp.bfloat16)
                gated[line, slots:] = jnp.dot(
                    squeeze[...], value, preferred_element_type=jnp.float32
                ).astype(jnp.bfloat16)

    def expert_rows(base, column):
        return pl.ds(pl.multiple_of(base + column * local, local), local)

    def spread(line, c, block):
        moved = jnp.dot(pick[line], block, preferred_element_type=jnp.float32).astype(jnp.bfloat16)
        s = line * COLS + x
        wide[line, slots:slots + pack, lanes_of(c)] = moved[slots:]
        x_copy(line, c).start()
        disp[part, c, :, slot_rows(s), :] = moved[:slots].reshape(local, SLOT, wide_chunk)
        core_copy(part, s, c).start()

    def own_step(c):
        spread(z, c, normed[:, own_lanes(c)])

    def line_step(line, c):
        low = line < z

        @pl.when(c == 0)
        def _():
            meta_arrival(line).wait_recv()
            routing(
                line, got_meta[line, expert_rows(0, x)], got_meta[line, expert_rows(0, 1 - x)]
            )

        way = jnp.where(low, 0, 1)
        z_copy(line, c, way).wait_recv()

        @pl.when(jnp.where(low, not_top, not_bottom))
        def _():
            z_copy(line, c, way).start()

        spread(line, c, tok[line, c])

    def x_step(line, c):
        @pl.when(c % 2 == 0)
        def _():
            block = got_packed.at[line, pl.ds(c, 2)]
            remote(block, block, x_s.at[0], x_r.at[line, c // 2], x_to).wait_recv()

        s = line * COLS + (1 - x)
        disp[part, c, :, slot_rows(s), :] = jnp.dot(
            grow[...], got_packed[line, c], preferred_element_type=jnp.float32
        ).astype(jnp.bfloat16).reshape(local, SLOT, wide_chunk)
        core_copy(part, s, c).start()

    def across_rows(left, right):
        return lax.dot_general(
            left, right, (((1,), (1,)), ((), ())), preferred_element_type=jnp.float32
        )

    def raise_part(e, parts):
        sums = []
        for g in range(2):
            for b in range(2):
                total = None
                for side, c in parts:
                    start = side * half + c * wide_chunk
                    piece = across_rows(
                        gu[2 * e + b, g, :, start:start + wide_chunk], disp[side, c, e]
                    )
                    total = piece if total is None else total + piece
                sums.append(total)
        return sums

    def raise_some(parts, start, stop, first=False, last=False):
        def one(e, carry):
            sums = raise_part(e, parts)
            if not first:
                sums = [
                    total + raised[e, n * hidden:(n + 1) * hidden] for n, total in enumerate(sums)
                ]
            if not last:
                for n, total in enumerate(sums):
                    raised[e, n * hidden:(n + 1) * hidden] = total
                return carry
            for b in range(2):
                gate = sums[b]
                hid_own[e, b * hidden:(b + 1) * hidden] = (
                    gate * jax.nn.sigmoid(gate) * sums[2 + b]
                ).astype(jnp.bfloat16)
            hid_copy(e).start()
            return carry

        lax.fori_loop(start, stop, one, 0)

    def hid_copy(e):
        return remote(hid_own.at[e], hid_other.at[e], hid_s.at[0], hid_r.at[e // (local // 2)], core_to)

    def arrived(which):
        span_of = pl.ds(which * SPLIT, SPLIT) if which == 0 else pl.ds(SPLIT, chunks - SPLIT)
        block = disp.at[other, span_of]
        remote(block, block, core_s.at[0], core_r.at[which], core_to).wait_recv()

    def sent(ref, sem):
        remote(ref, ref, sem, sem, core_to).wait_send()

    routing(
        z, meta[expert_rows(z * COLS * local, x)], meta[expert_rows(z * COLS * local, 1 - x)]
    )
    for c in range(chunks):
        own_step(c)

    for copy in weight_copies():
        copy.wait()

    offsets = [(jnp.abs(line - z) - 1) * chunks for line in near_lines]
    offsets[1] = jnp.maximum(offsets[1], SPLIT)

    def step(t, carry):
        for line, offset in zip(near_lines, offsets):
            c = t - offset

            @pl.when((c >= 0) & (c < chunks))
            def _():
                line_step(line, c)

        @pl.when((t >= LAG - 1) & (t < LAG - 1 + chunks))
        def _():
            x_step(z, t - LAG + 1)

        for line, offset in zip(near_lines, offsets):
            c = t - LAG - offset

            @pl.when((c >= 0) & (c < chunks))
            def _():
                x_step(line, c)

        return carry

    span = chunks * (lines - 1) + LAG
    lax.fori_loop(0, span - 2, step, 0)
    early = range(SPLIT)
    late = range(SPLIT, chunks)
    own_first = (part == 1) & ((z == 0) | (z == lines - 1))

    @pl.when(own_first)
    def _():
        raise_some([(1, c) for c in early], 0, local, first=True)
        step(span - 2, 0)
        step(span - 1, 0)
        raise_some([(1, c) for c in late], 0, local)
        arrived(0)
        arrived(1)
        raise_some([(0, c) for c in range(chunks)], 0, local, last=True)

    @pl.when(jnp.logical_not(own_first))
    def _():
        arrived(0)
        raise_some([(side, c) for c in early for side in range(2)], 0, local // 2, first=True)
        step(span - 2, 0)
        step(span - 1, 0)
        raise_some([(side, c) for c in early for side in range(2)], local // 2, local, first=True)
        arrived(1)
        raise_some([(side, c) for c in late for side in range(2)], 0, local, last=True)

    group = 2 * wide_chunk

    def lower(g, between):
        lanes = slice(g * group, (g + 1) * group)

        def one(e, carry):
            mine = pl.ds(pl.multiple_of(part * hidden, SLOT), hidden)
            theirs = pl.ds(pl.multiple_of(other * hidden, SLOT), hidden)
            left = jnp.concatenate([hid_own[e], hid_other[e]], axis=0)
            right = jnp.concatenate(
                [dn[2 * e, mine, lanes], dn[2 * e + 1, mine, lanes],
                 dn[2 * e, theirs, lanes], dn[2 * e + 1, theirs, lanes]], axis=0
            )
            wide[e, :rows, lanes] = lax.dot_general(
                left, right, (((0,), (0,)), ((), ())), preferred_element_type=jnp.float32
            ).astype(jnp.bfloat16)
            return carry

        for which in range(2):
            if g == 0:
                block = hid_other.at[pl.ds(which * (local // 2), local // 2)]
                remote(block, block, hid_s.at[0], hid_r.at[which], core_to).wait_recv()
            lax.fori_loop(which * (local // 2), (which + 1) * (local // 2), one, 0)
            if which == 0:
                between()

    def result_rows(s, q):
        return wide[:local, slot_rows(s), lanes_of(q)].reshape(slots, wide_chunk)

    def rx_copy(line, q):
        return remote(
            wide.at[lines + line, pl.ds(slots, pack), lanes_of(q)], got_rows.at[line, q],
            rx_s.at[0], rx_r.at[line, q], x_to,
        )

    def rz_copy(line, q, way, owner=None):
        owner = z - 1 if owner is None else owner
        where = {"dev": jnp.where(way == 0, above, below)}
        return remote(
            tok.at[line, q], got_sum.at[way, line, q],
            rz_s.at[0], rz_r.at[jnp.where((way == 1) & (line == owner), lines, line), q], where,
        )

    def give(line, q):
        packed = jnp.dot(
            squeeze[...], result_rows(line * COLS + (1 - x), q), preferred_element_type=jnp.float32
        )
        wide[lines + line, slots:slots + pack, lanes_of(q)] = packed.astype(jnp.bfloat16)
        rx_copy(line, q).start()

    def gather_here(line, q):
        rx_copy(line, q).wait_recv()
        pieces = jnp.concatenate([result_rows(line * COLS + x, q), got_rows[line, q]], axis=0)
        acc[...] = lax.dot_general(
            gated[line], pieces, (((0,), (0,)), ((), ())), preferred_element_type=jnp.float32
        )

    def add_line(line, q, way):
        rz_copy(line, q, way, z).wait_recv()
        acc[...] += got_sum[way, line, q].astype(jnp.float32)

    def pass_on(line, q):
        gather_here(line, q)
        way = jnp.where(line > z, 0, 1)

        @pl.when(jnp.where(line > z, not_bottom, not_top))
        def _():
            add_line(line, q, way)

        tok[line, q] = acc[...].astype(jnp.bfloat16)
        rz_copy(line, q, way).start()

    lower(0, lambda: None)
    give(far_lines[0], 0)
    lower(1, lambda: give(far_lines[0], 1))
    for q in range(2, chunks):
        give(far_lines[0], q)
    def give_all(line):
        lax.fori_loop(0, chunks, lambda q, carry: (give(line, q), carry)[1], 0)

    for line in near_lines:
        low = line < z

        @pl.when(jnp.where(low, not_top, not_bottom))
        def _():
            sent(tok.at[line], z_s.at[line])

    far_end = (z == 0) | (z == lines - 1)

    @pl.when(far_end)
    def _():
        for q in range(2):
            pass_on(far_lines[0], q)

    give_all(far_lines[1])

    @pl.when(far_end)
    def _():
        for q in range(2, chunks):
            pass_on(far_lines[0], q)

    for line in far_lines[2:] + [z]:
        give_all(line)

    @pl.when(jnp.logical_not(far_end))
    def _():
        for q in range(chunks):
            pass_on(far_lines[0], q)

    for line in far_lines[1:]:
        lax.fori_loop(0, chunks, lambda q, carry, line=line: (pass_on(line, q), carry)[1], 0)
    for q in range(chunks):
        gather_here(z, q)

        @pl.when(not_bottom)
        def _():
            add_line(z, q, 0)

        @pl.when(not_top)
        def _():
            add_line(z, q, 1)

        own = own_lanes(q)
        lanes = slice(q * wide_chunk, (q + 1) * wide_chunk)
        out[:, lanes] = (
            state[:, own] + (1.0 + modulation[3:4, own]) * acc[...]
        ).astype(out.dtype)

    @pl.when(not_top)
    def _():
        sent(tok.at[z], z_s.at[z])

    @pl.when(not_bottom)
    def _():
        sent(tok.at[z], z_s.at[lines])

    sent(tok.at[pl.ds(0, lines - 1)], rz_s.at[0])
    sent(got_packed, x_s.at[0])
    sent(got_rows, rx_s.at[0])
    sent(disp.at[part], core_s.at[0])
    sent(got_meta.at[pl.ds(0, lines - 1)], meta_s.at[0])
    sent(hid_own, hid_s.at[0])


def front_kernel(
    devices, start_weights, send_first,
    sources, held, own_sem,
    normed, state, meta,
    window, queries, column, mixed, mine_out, their_out, sent_back, got_back, their_back,
    pair_s, pair_r, query_s, query_r, early_s, late_s, edge_r, wz_s, wz_r, wy_s, wy_r, mix_s, mix_r,
    sum_s, sum_r, back_s, back_r, share_s, share_r,
):
    packed_hbm, weight_hbm = sources[1], sources[2]
    tokens, modulation, router, ids = held
    me = lax.axis_index("dev")
    part = lax.axis_index("sub")
    group = lax.axis_index("groups")
    z = me // COLS
    x = me % COLS
    lines = devices // COLS
    count, width = tokens.shape
    shard = column.shape[1]
    share = shard // 2
    piece = share // PIECES
    heads = window.shape[3]
    pairs = heads // PAIR
    ours = pl.ds(pl.multiple_of(x * heads, heads), heads)
    theirs = pl.ds(pl.multiple_of((1 - x) * heads, heads), heads)
    own_parts = (
        (packed_hbm.at[1:3, :, ours], window.at[1 + x]), (packed_hbm.at[0, :, ours], queries.at[x]),
        (weight_hbm, column.at[z]), (sources[0], tokens), (sources[3], modulation),
        (sources[4], router), (sources[5], ids),
    )

    def own_copy(i):
        return pltpu.make_async_copy(*own_parts[i], own_sem.at[i])

    for i in range(len(own_parts)):
        own_copy(i).start()
    not_top = z < lines - 1
    not_bottom = z > 0
    above = jnp.minimum(me + COLS, devices - 1)
    below = jnp.maximum(me - COLS, 0)
    x_to = {"dev": z * COLS + (1 - x)}
    y_to = {"groups": 1 - group}
    core_to = {"sub": 1 - part}
    near_lines = [choose(z, table) for table in line_order(lines, True)]

    barrier = pltpu.get_barrier_semaphore()

    def greet(where):
        pl.semaphore_signal(barrier, inc=1, device_id=where, device_id_type=MESH)

    for where in (x_to, y_to, core_to, {**x_to, **core_to}):
        greet(where)
    for line in near_lines:
        greet({"dev": line * COLS + x})
    pl.semaphore_wait(barrier, lines + 3)

    def remote(src, dst, send, recv, where):
        return pltpu.make_async_remote_copy(
            src_ref=src, dst_ref=dst, send_sem=send, recv_sem=recv,
            device_id=where, device_id_type=MESH,
        )

    def part_lanes(base, k):
        return pl.ds(pl.multiple_of(base * heads + k * PAIR, PAIR), PAIR)

    def pair_copy(k):
        return remote(
            packed_hbm.at[1:3, :, part_lanes(1 - x, k)], window.at[1 + x, :, :, part_lanes(0, k)],
            pair_s.at[k], pair_r.at[k], x_to,
        )

    def query_copy():
        return remote(
            packed_hbm.at[0, :, theirs], queries.at[x], query_s.at[0], query_r.at[0], x_to
        )

    def edge_copy(k, up, src, send):
        where = {"dev": jnp.where(up, above, below)}
        place = jnp.where(up, 0, 3)
        return remote(
            src, window.at[place, :, :, part_lanes(0, k)], send,
            edge_r.at[jnp.where(up, 0, 1), k], where,
        )

    def early_copy(k):
        return edge_copy(k, x == 1, packed_hbm.at[1:3, :, part_lanes(x, k)], early_s.at[k])

    def late_copy(k):
        return edge_copy(k, x == 0, window.at[2 - x, :, :, part_lanes(0, k)], late_s.at[k])

    give_late = ((x == 0) & not_top) | ((x == 1) & not_bottom)
    give_early = ((x == 1) & not_top) | ((x == 0) & not_bottom)

    def piece_rows(which, i):
        return pl.ds(pl.multiple_of(which * share + i * piece, SLOT), piece)

    def wz_copy(line, i, way, src=None):
        dst = column.at[line, piece_rows(group, i)]
        where = {"dev": jnp.where(way == 0, above, below)}
        return remote(
            dst if src is None else src, dst,
            wz_s.at[jnp.where((line == z) & (way == 1), lines, line)], wz_r.at[line, i], where
        )

    def own_piece(i):
        return weight_hbm.at[piece_rows(group, i)]

    def wy_copy(line, i, which):
        block = column.at[line, piece_rows(which, i)]
        return remote(block, block, wy_s.at[0], wy_r.at[line], y_to)

    for k in range(pairs):
        pair_copy(k).start()
    query_copy().start()

    def send_pieces(pieces):
        for i in pieces:

            @pl.when(not_top)
            def _():
                wz_copy(z, i, 0, own_piece(i)).start()

            @pl.when(not_bottom)
            def _():
                wz_copy(z, i, 1, own_piece(i)).start()

    send_pieces(range(PIECES // 2))

    @pl.when(give_early)
    def _():
        for k in range(pairs):
            early_copy(k).start()

    send_pieces(range(PIECES // 2, PIECES))
    start_weights()

    @pl.when(jnp.logical_not(not_bottom))
    def _():
        window[0] = jnp.zeros_like(window[0])

    @pl.when(jnp.logical_not(not_top))
    def _():
        window[3] = jnp.zeros_like(window[3])

    def way_of(line):
        return jnp.where(line < z, 0, 1)

    def more(line):
        return jnp.where(line < z, not_top, not_bottom)

    def busy(line):
        return jnp.where(line < z, x == 0, x == 1)

    def distance(line):
        return jnp.abs(line - z)

    def take(line, onward, pieces=range(PIECES)):
        for i in pieces:
            wz_copy(line, i, way_of(line)).wait_recv()

            @pl.when(onward)
            def _():
                wz_copy(line, i, way_of(line)).start()

            wy_copy(line, i, group).start()

    def take_next(only_busy, pieces):
        for line in near_lines:

            @pl.when((distance(line) == 1) & (busy(line) if only_busy else jnp.logical_not(busy(line))))
            def _():
                take(line, more(line), pieces)

    for k in range(pairs):
        pair_copy(k).wait_recv()

        @pl.when(give_late)
        def _():
            late_copy(k).start()

    take_next(True, range(PIECES // 2))
    take_next(False, range(PIECES // 2))
    for i in range(len(own_parts)):
        own_copy(i).wait()
    query_copy().wait_recv()

    row = lax.broadcasted_iota(jnp.int32, (count, count), 0)
    col = lax.broadcasted_iota(jnp.int32, (count, count), 1)

    def mix_copy(b, k):
        block = mixed.at[pl.ds(pl.multiple_of(b * count, count), count), part_lanes(x, k)]
        return remote(block, block, mix_s.at[0], mix_r.at[0], x_to)

    def attend(b, k):
        see_before = (col >= row) & ((z > 0) | (b == 1))
        see_after = (col <= row) & ((z < lines - 1) | (b == 0))
        for h in range(PAIR // HEAD):
            inner = slice(k * PAIR + h * HEAD, k * PAIR + (h + 1) * HEAD)
            query = queries[b, :, inner]

            def score(keys):
                return lax.dot_general(
                    query, keys, (((1,), (1,)), ((), ())), preferred_element_type=jnp.float32
                ) / math.sqrt(HEAD)

            scores = jnp.concatenate(
                [
                    jnp.where(see_before, score(window[b, 0, :, inner]), NEG),
                    score(window[b + 1, 0, :, inner]),
                    jnp.where(see_after, score(window[b + 2, 0, :, inner]), NEG),
                ],
                axis=1,
            )
            top = jnp.max(scores, -1, keepdims=True)
            weight = jnp.exp(scores - top)
            weight = (weight / jnp.sum(weight, -1, keepdims=True)).astype(jnp.bfloat16)
            values = jnp.concatenate([window[b + n, 1, :, inner] for n in range(3)], axis=0)
            lanes = pl.ds(
                pl.multiple_of(x * heads + k * PAIR + h * HEAD, HEAD), HEAD
            )
            mixed[pl.ds(pl.multiple_of(b * count, count), count), lanes] = jnp.dot(
                weight, values, preferred_element_type=jnp.float32
            ).astype(jnp.bfloat16)
        mix_copy(b, k).start()

    for b, up in ((1 - x, x == 1), (x, x == 0)):
        for k in range(pairs):

            @pl.when(jnp.where(up, not_bottom, not_top))
            def _():
                edge_copy(k, up, window.at[0, :, :, part_lanes(0, k)], early_s.at[k]).wait_recv()

            attend(b, k)
        if b is not x:
            take_next(True, range(PIECES // 2, PIECES))
            take_next(False, range(PIECES // 2, PIECES))
        else:
            for line in near_lines:

                @pl.when(distance(line) == 2)
                def _():
                    take(line, more(line))

    last = near_lines[-1]
    far_last = distance(last) > 2

    def take_last(pieces):
        @pl.when(far_last)
        def _():
            take(last, more(last), pieces)

    mix_block = mixed.at[:, theirs]
    remote(mix_block, mix_block, mix_s.at[0], mix_r.at[0], x_to).wait_recv()

    def place_of(which):
        return group if which == 0 else 1 - group

    def group_of(line):
        return jnp.where(line == last, 1, 0)

    def come(ref, sem):
        remote(ref, ref, sum_s.at[0], sem, core_to).wait_recv()

    def sum_copy(line, which):
        place = place_of(which)
        return remote(
            mine_out.at[line, place], their_out.at[line, place],
            sum_s.at[0], sum_r.at[group_of(line)], core_to,
        )

    def back_copy(line, which):
        place = place_of(which)
        return remote(
            sent_back.at[line, place], got_back.at[line, place],
            back_s.at[0], back_r.at[line], x_to,
        )

    def share_copy(line, which):
        place = place_of(which)
        return remote(
            got_back.at[line, place], their_back.at[line, place],
            share_s.at[0], share_r.at[group_of(line)], core_to,
        )

    def direct_copy(which):
        place = place_of(which)
        return remote(
            sent_back.at[last, place], their_back.at[last, place],
            share_s.at[0], share_r.at[1],
            {"dev": z * COLS + (1 - x), "sub": 1 - part},
        )

    def project(line, which, direct=False):
        place = place_of(which)
        block = column[line, pl.ds(pl.multiple_of(place * share, SLOT), share), :]
        both = jnp.concatenate(
            [mixed[pl.ds(pl.multiple_of(b * count, count), count), :] for b in (1 - x, x)], axis=0
        )
        product = lax.dot_general(
            both, block, (((1,), (1,)), ((), ())), preferred_element_type=jnp.float32
        )
        sent_back[line, place] = product[:count].astype(jnp.bfloat16)
        back_copy(line, which).start()
        if direct:
            direct_copy(which).start()
        mine_out[line, place] = product[count:]
        sum_copy(line, which).start()

    def halves_in(line):
        block = column.at[line, pl.ds(pl.multiple_of((1 - group) * share, SLOT), share)]
        remote(block, block, wy_s.at[0], wy_r.at[line], y_to).wait_recv()

    def last_step():
        halves_in(last)
        project(last, 1, True)

    def add_up(line, which):
        place = place_of(which)
        partial = jnp.zeros((count, share), jnp.float32)
        for column_of, total in (
            (x, mine_out[line, place] + their_out[line, place]),
            (
                1 - x,
                got_back[line, place].astype(jnp.float32)
                + their_back[line, place].astype(jnp.float32),
            ),
        ):
            start = (line * COLS + column_of) * shard + place * share
            lanes = pl.ds(pl.multiple_of(start, LANES), share)
            value = tokens[:, lanes].astype(jnp.float32) + (1.0 + modulation[0:1, lanes]) * total
            state[:, lanes] = value
            partial = partial + value * value
        return partial

    steps = [(line, which) for line in [z] + near_lines[:-1] for which in range(2)]
    quarter = PIECES // 4
    for i, (line, which) in enumerate(steps):
        if which == 1 and i > 1:
            halves_in(line)
        project(line, which)
        if i < 4:
            take_last(range(i * quarter, (i + 1) * quarter))
    project(last, 0, True)

    @pl.when(jnp.logical_not(far_last))
    def _():
        last_step()

    def relay(some):
        for line, which in some:
            if which == 0:
                come(got_back.at[line], back_r.at[line])
            share_copy(line, which).start()

    relay(steps[:4])

    @pl.when(far_last)
    def _():
        last_step()

    relay(steps[4:])
    squares = jnp.zeros((count, share), jnp.float32)
    come(mine_out.at[pl.ds(0, lines - 1)], sum_r.at[0])
    come(got_back.at[pl.ds(0, lines - 1)], share_r.at[0])
    for line, which in steps:
        squares = squares + add_up(line, which)
    come(got_back.at[last], back_r.at[last])
    come(mine_out.at[last], sum_r.at[1])
    come(got_back.at[last], share_r.at[1])
    for which in range(2):
        squares = squares + add_up(last, which)
    square = jnp.sum(squares, -1, keepdims=True)
    scale = lax.rsqrt(square / width + EPS)
    step = width // 2 // CHUNKS
    for i in range(2 * CHUNKS):
        start = (part * CHUNKS + i) % (2 * CHUNKS) * step
        lanes = pl.ds(pl.multiple_of(start, step), step)
        normed[:, lanes] = (
            state[:, lanes] * scale * (1.0 + modulation[2:3, lanes]) + modulation[1:2, lanes]
        ).astype(jnp.bfloat16)
        if i == 0:
            send_first()
    logits = lax.dot_general(
        router[...], normed[...], (((1,), (1,)), ((), ())), preferred_element_type=jnp.float32
    )
    name = lax.broadcasted_iota(jnp.int32, logits.shape, 0)
    named = name == ids[0:1]
    for k in range(1, ids.shape[0]):
        named = named | (name == ids[k:k + 1])
    lifted = jnp.where(named, jax.nn.sigmoid(logits), 0.0)
    meta[...] = lifted / jnp.sum(lifted, 0, keepdims=True)

    def drain():
        def sent(ref, sem):
            remote(ref, ref, sem, sem, x_to).wait_send()

        query_copy().wait_send()
        sent(mixed.at[:, ours], mix_s.at[0])
        for k in range(pairs):
            pair_copy(k).wait_send()

            @pl.when(give_early)
            def _():
                early_copy(k).wait_send()

            @pl.when(give_late)
            def _():
                late_copy(k).wait_send()

        half_shard = column.at[0, pl.ds(0, share)]

        @pl.when(not_top)
        def _():
            sent(half_shard, wz_s.at[z])

        @pl.when(not_bottom)
        def _():
            sent(half_shard, wz_s.at[lines])

        for line in near_lines:

            @pl.when(more(line))
            def _():
                sent(half_shard, wz_s.at[line])

        sent(column.at[pl.ds(0, lines - 1), pl.ds(0, share)], wy_s.at[0])
        sent(mine_out, sum_s.at[0])
        sent(sent_back, back_s.at[0])
        sent(got_back, share_s.at[0])

    return drain


def block_kernel(devices, *refs):
    sources, gate_up, down, out = refs[:6], refs[6], refs[7], refs[8]
    held, normed, state, meta, wide = refs[9:13], refs[13], refs[14], refs[15], refs[16]
    front_buffers, expert_buffers = refs[17:26], refs[26:42]
    own_sem, gu_sem, dn_sem = refs[42:45]
    front_sems, expert_sems = refs[45:64], refs[64:]
    gu, dn = expert_buffers[5:7]
    squeeze, grow = expert_buffers[13:15]
    def weight_copies():
        return (
            pltpu.make_async_copy(gate_up, gu, gu_sem.at[0]),
            pltpu.make_async_copy(down, dn, dn_sem.at[0]),
        )

    def start_weights():
        for copy in weight_copies():
            copy.start()
        for ref, axis in ((squeeze, 0), (grow, 1)):
            packed = lax.broadcasted_iota(jnp.int32, ref.shape, axis)
            slot = lax.broadcasted_iota(jnp.int32, ref.shape, 1 - axis)
            inner = slot & (SLOT - 1)
            same = (packed == (slot - inner) // SLOT * CAP + inner) & (inner < CAP)
            ref[...] = jnp.where(same, 1.0, 0.0).astype(jnp.bfloat16)

    experts = expert_kernel(
        devices, weight_copies, normed, meta, state, held[1], wide, out,
        *expert_buffers, *expert_sems,
    )
    drain = front_kernel(
        devices, start_weights, next(experts), sources, held, own_sem, normed, state, meta,
        *front_buffers, *front_sems,
    )
    next(experts, None)
    drain()


def block_call(
    tokens, query_key_value, out_weight, modulation, router_weight, expert_ids,
    gate_up_weight, down_weight,
):
    devices = lax.axis_size("dev")
    count, width = tokens.shape
    half = down_weight.shape[2]
    halves = gate_up_weight.shape[0]
    local = halves // 2
    gate_up_weight = gate_up_weight.swapaxes(2, 3)
    hidden = gate_up_weight.shape[2]
    lines = devices // COLS
    rows = devices * SLOT
    slots, pack = local * SLOT, local * CAP
    part = half // CHUNKS
    pairs = half // 2 // PAIR
    shard = out_weight.shape[0]
    own = (
        tokens, query_key_value.transpose(1, 0, 2), out_weight, modulation,
        router_weight.T, expert_ids.T,
    )
    hbm = pl.BlockSpec(memory_space=pl.ANY)
    dma = pltpu.SemaphoreType.DMA
    return pl.pallas_call(
        functools.partial(block_kernel, devices),
        out_shape=jax.ShapeDtypeStruct((count, half), jnp.bfloat16),
        in_specs=[hbm] * 8,
        out_specs=pl.BlockSpec(memory_space=pltpu.VMEM),
        scratch_shapes=[
            *[pltpu.VMEM(own[i].shape, own[i].dtype) for i in (0, 3, 4, 5)],
            pltpu.VMEM((count, width), jnp.bfloat16),
            pltpu.VMEM((count, width), jnp.float32),
            pltpu.VMEM((router_weight.shape[1], count), jnp.float32),
            pltpu.VMEM((devices, slots + pack, half), jnp.bfloat16),
            pltpu.VMEM((4, 2, count, half // 2), jnp.bfloat16),
            pltpu.VMEM((COLS, count, half // 2), jnp.bfloat16),
            pltpu.VMEM((lines, shard, half), jnp.bfloat16),
            pltpu.VMEM((COLS * count, half), jnp.bfloat16),
            pltpu.VMEM((lines, 2, count, shard // 2), jnp.float32),
            pltpu.VMEM((lines, 2, count, shard // 2), jnp.float32),
            pltpu.VMEM((lines, 2, count, shard // 2), jnp.bfloat16),
            pltpu.VMEM((lines, 2, count, shard // 2), jnp.bfloat16),
            pltpu.VMEM((lines, 2, count, shard // 2), jnp.bfloat16),
            pltpu.VMEM((lines, CHUNKS, count, part), jnp.bfloat16),
            pltpu.VMEM((lines, CHUNKS, pack, part), jnp.bfloat16),
            pltpu.VMEM((lines, CHUNKS, pack, part), jnp.bfloat16),
            pltpu.VMEM((2, lines, CHUNKS, count, part), jnp.bfloat16),
            pltpu.VMEM((2, CHUNKS, local, rows, part), jnp.bfloat16),
            pltpu.VMEM(gate_up_weight.shape, jnp.bfloat16),
            pltpu.VMEM(down_weight.shape, jnp.bfloat16),
            pltpu.VMEM((local, 4 * hidden, rows), jnp.float32),
            pltpu.VMEM((local, 2 * hidden, rows), jnp.bfloat16),
            pltpu.VMEM((local, 2 * hidden, rows), jnp.bfloat16),
            pltpu.VMEM((lines, COLS * local, count), jnp.float32),
            pltpu.VMEM((lines, slots + pack, count), jnp.bfloat16),
            pltpu.VMEM((lines, slots + pack, count), jnp.bfloat16),
            pltpu.VMEM((pack, slots), jnp.bfloat16),
            pltpu.VMEM((slots, pack), jnp.bfloat16),
            pltpu.VMEM((count, part), jnp.float32),
            dma((7,)), dma((1,)), dma((1,)),
            dma((pairs,)), dma((pairs,)), dma((1,)), dma((1,)),
            dma((pairs,)), dma((pairs,)), dma((2, pairs)),
            dma((lines + 1,)), dma((lines, PIECES)), dma((1,)), dma((lines,)), dma((1,)), dma((1,)),
            dma((1,)), dma((2,)), dma((1,)), dma((lines,)), dma((1,)), dma((2,)),
            dma((1,)), dma((lines,)),
            dma((lines + 1,)), dma((lines, CHUNKS)), dma((1,)), dma((lines, CHUNKS // 2)),
            dma((1,)), dma((2,)), dma((1,)), dma((2,)),
            dma((1,)), dma((lines, CHUNKS)), dma((1,)), dma((lines + 1, CHUNKS)),
        ],
        compiler_params=pltpu.CompilerParams(
            collective_id=1, has_side_effects=True, vmem_limit_bytes=VMEM_BYTES
        ),
    )(*own, gate_up_weight, down_weight)


def body(
    tokens,
    query_key_value,
    out_weight,
    modulation,
    router_weight,
    expert_ids,
    gate_up_weight,
    down_weight,
):
    count = tokens.shape[0]
    width = tokens.shape[1]
    parts = lax.axis_size("sub")
    part = lax.axis_index("sub")
    position = lax.axis_index("dev")
    devices = lax.axis_size("dev")
    total = count * devices
    local_width = query_key_value.shape[2]
    weight_bytes = 2 * (gate_up_weight.size + down_weight.size)
    token_bytes = 12 * devices * count * width
    fits = weight_bytes + token_bytes < VMEM_BYTES and CAP <= SLOT
    paired = parts == 2 and lax.axis_size("groups") == 2 and devices % COLS == 0
    experts_here = gate_up_weight.shape[0] // 2
    tiled = out_weight.shape[0] % (2 * LANES) == 0 and count == LANES
    tiled = tiled and down_weight.shape[2] == 4 * PAIR and devices == 4 * COLS
    tiled = tiled and down_weight.shape[2] % (2 * CHUNKS * LANES) == 0 and experts_here == devices
    tiled = tiled and SLOT * devices == LANES
    tiled = tiled and gate_up_weight.shape[3] % 64 == 0
    if fits and paired and tiled:
        return block_call(
            tokens, query_key_value, out_weight, modulation, router_weight, expert_ids,
            gate_up_weight, down_weight,
        )
    heads_here = local_width // HEAD
    query = query_key_value[:, 0].reshape(count, heads_here, HEAD)
    pair = query_key_value[:, 1:]
    near = extended(pair, (("dev", 0),), count)
    keys = near[:, 0].reshape(3 * count, heads_here, HEAD)
    values = near[:, 1].reshape(3 * count, heads_here, HEAD)
    mixed = window_attention(query, keys, values, position, total).reshape(count, local_width)
    partial_proj = lax.dot_general(
        mixed,
        lax.all_gather(out_weight, "dev", axis=0, tiled=True),
        (((1,), (1,)), ((), ())),
        preferred_element_type=jnp.float32,
    )
    proj = lax.psum(partial_proj, "sub")
    state = tokens.astype(jnp.float32) + (1.0 + modulation[0]) * proj
    normed = normalize(state, modulation)
    gates = route(normed, router_weight, expert_ids)
    experts = router_weight.shape[1]
    topk = expert_ids.shape[1]
    flat = expert_ids.reshape(-1)
    picks = flat.shape[0]
    onehot = (flat[:, None] == jnp.arange(experts, dtype=jnp.int32)[None, :]).astype(jnp.int32)
    rank = jnp.sum((jnp.cumsum(onehot, 0) - 1) * onehot, 1)
    target = flat * CAP + rank
    hit = target[None, :] == jnp.arange(experts * CAP, dtype=jnp.int32)[:, None]
    filled = jnp.any(hit, 1)
    anchor = jnp.sum(jnp.where(hit, jnp.arange(picks, dtype=jnp.int32)[None, :], 0), 1) // topk
    slice_width = width // parts
    sent = lax.dynamic_slice_in_dim(normed, part * slice_width, slice_width, 1)
    sent_width = sent.shape[1]
    rows_out = jnp.where(filled[:, None], sent[anchor], jnp.zeros((), jnp.bfloat16))
    halves_here = gate_up_weight.shape[0]
    doubled = jnp.broadcast_to(
        rows_out.reshape(experts, 1, CAP, sent_width), (experts, 2, CAP, sent_width)
    )
    outgoing = doubled.reshape(devices, halves_here, CAP, sent_width)
    up_form = "sxcd,xgdf->sxcgf"
    down_form = "sxcf,xfd->sxcd"
    incoming = lax.all_to_all(outgoing, "dev", split_axis=0, concat_axis=0, tiled=True)
    both = jnp.einsum(
        up_form,
        lax.all_gather(incoming, "sub", axis=3, tiled=True),
        gate_up_weight,
        preferred_element_type=jnp.float32,
    )
    hidden = (jax.nn.silu(both[..., 0, :]) * both[..., 1, :]).astype(jnp.bfloat16)
    gathered = lax.all_gather(hidden, "sub", axis=hidden.ndim - 1, tiled=True)
    result = jnp.einsum(down_form, gathered, down_weight, preferred_element_type=jnp.float32)
    returned = lax.all_to_all(
        result.astype(jnp.bfloat16), "dev", split_axis=0, concat_axis=0, tiled=True
    )
    own_width = returned.shape[-1]
    arranged = returned.reshape(experts, 2, CAP, own_width)
    answers = arranged[flat, :, rank, :].reshape(count, topk, 2, own_width).astype(jnp.float32)
    combined = answers[:, :, 0] + answers[:, :, 1]
    routed = jnp.einsum("tk,tkd->td", gates, combined)
    own = lax.dynamic_slice_in_dim(state, part * slice_width, slice_width, 1)
    lift = lax.dynamic_slice_in_dim(modulation[3], part * slice_width, slice_width, 0)
    return (own + (1.0 + lift) * routed).astype(jnp.bfloat16)


def solution(mesh):
    return jax.shard_map(
        body,
        mesh=mesh,
        in_specs=(
            P(("groups", "dev"), None),
            P(("groups", "dev"), None, "sub"),
            P("dev", "sub"),
            P("groups", None),
            P(),
            P(("groups", "dev"), None),
            P("dev", None, None, "sub"),
            P("dev", None, "sub"),
        ),
        out_specs=P(("groups", "dev"), "sub"),
        check_vma=False,
    )
```
